32 devices in a mesh: clip: 16 (over z, x, core), frame: 2 (over y).
Axes of the slice: x: 2, y: 2, z: 4, core: 2. Of those that a mesh axis runs over, the one named last changes fastest.
Arguments:
- inputs: bfloat16 [16, 1500, 768], P('clip', 'frame'), may hold values from -6 to 6
- cotangent: bfloat16 [16, 1500, 768], P('clip', 'frame'), may hold values from -2 to 2
- project_in: float32 [768, 2304], P(('clip', 'frame'))
- project_out: float32 [768, 768], P(('clip', 'frame')), may hold values from -0.1875 to 0.1875
- expand_weight: float32 [768, 3072], P(('clip', 'frame')), may hold values from -0.21875 to 0.21875
- shrink_weight: float32 [3072, 768], P(('clip', 'frame')), may hold values from -0.15625 to 0.15625
- expand_bias: float32 [3072], P(('clip', 'frame')), may hold values from -3 to 3
- vectors: float32 [768, 8], P(('clip', 'frame'))
- moments_in: float32 [2, 768, 2304], P(None, ('clip', 'frame')), as said below
- moments_out: float32 [2, 768, 768], P(None, ('clip', 'frame'))
- moments_expand: float32 [2, 768, 3072], P(None, ('clip', 'frame'))
- moments_shrink: float32 [2, 3072, 768], P(None, ('clip', 'frame'))
- moments_bias: float32 [2, 3072], P(None, ('clip', 'frame'))
- moments_vectors: float32 [2, 768, 8], P(None, ('clip', 'frame'))
Outputs:
- output: bfloat16 [16, 1500, 768], P('clip', 'frame')
- grad_inputs: bfloat16 [16, 1500, 768], P('clip', 'frame')
- grad_project_in: float32 [768, 2304], P(('clip', 'frame'))
- grad_project_out: float32 [768, 768], P(('clip', 'frame'))
- grad_expand: float32 [768, 3072], P(('clip', 'frame'))
- grad_shrink: float32 [3072, 768], P(('clip', 'frame'))
- grad_bias: float32 [3072], P(('clip', 'frame'))
- grad_vectors: float32 [768, 8], P(('clip', 'frame'))
- new_project_in: float32 [768, 2304], P(('clip', 'frame'))
- new_project_out: float32 [768, 768], P(('clip', 'frame'))
- new_expand: float32 [768, 3072], P(('clip', 'frame'))
- new_shrink: float32 [3072, 768], P(('clip', 'frame'))
- new_bias: float32 [3072], P(('clip', 'frame'))
- new_vectors: float32 [768, 8], P(('clip', 'frame'))
- new_moments_in: float32 [2, 768, 2304], P(None, ('clip', 'frame'))
- new_moments_out: float32 [2, 768, 768], P(None, ('clip', 'frame'))
- new_moments_expand: float32 [2, 768, 3072], P(None, ('clip', 'frame'))
- new_moments_shrink: float32 [2, 3072, 768], P(None, ('clip', 'frame'))
- new_moments_bias: float32 [2, 3072], P(None, ('clip', 'frame'))
- new_moments_vectors: float32 [2, 768, 8], P(None, ('clip', 'frame'))
The draws below stay inside these ranges and needn't reach their ends.
Inputs may be any that keep to these rules, and one draw needn't show every extreme that they name: `moments_in`: the first row of each moments array is signed, the second positive.
All inputs are finite; a program needn't handle non-finite values.
Results may differ from the reference program's by a relative error of at most 0.013.
The reference program's roundings to bfloat16 on the way count: a program that leaves them out, or rounds other values in their place, can miss the bound.
Values may be sent and summed in bfloat16 or wider, within the bound.
A program may use at most 192 MiB of HBM per device.

```python
import math
from functools import partial
import jax
import jax.numpy as jnp
from jax import lax

D = 768
HEADS = 12
FF = 3072
CLIP_LEN = 1500
ADAM_STEP = 4
CLIPS = 16
TOKENS = 24000


def moment_pair(key, shape, factor):
    typical = factor * 5.0
    first_key = jax.random.fold_in(key, 11)
    second_key = jax.random.fold_in(key, 12)
    signed_part = typical / 9.0 * jax.random.normal(first_key, shape, jnp.float32)
    spread_part = jax.random.uniform(second_key, shape, jnp.float32, math.log(0.3), math.log(3.0))
    square_part = typical * typical / 99.0 * jnp.exp(spread_part)
    return jnp.stack([signed_part, square_part])


def draw_cotangent(key, part):
    base = jax.random.normal(jax.random.fold_in(key, 41), (CLIPS, CLIP_LEN, D), jnp.float32)
    return (jnp.clip(base, -6.0, 6.0) * (5.0 / math.sqrt(TOKENS))).astype(jnp.bfloat16)


def draw_moments_in(key, part):
    return moment_pair(key, (D, 3 * D), 1.0)


def draw_moments_out(key, part):
    return moment_pair(key, (D, D), 0.7)


def draw_moments_expand(key, part):
    return moment_pair(key, (D, FF), 0.5)


def draw_moments_shrink(key, part):
    return moment_pair(key, (FF, D), 0.7)


def draw_moments_bias(key, part):
    return moment_pair(key, (FF,), 0.5)


def draw_moments_vectors(key, part):
    return moment_pair(key, (D, 8), 1.0)


def draw_project_in(key, part):
    return jax.random.normal(jax.random.fold_in(key, 21), (D, 3 * D), jnp.float32) / math.sqrt(D)


def draw_vectors(key, part):
    gain_first = 1.5 + 0.3 * jax.random.uniform(jax.random.fold_in(key, 31), (D, 1), jnp.float32, -1.0, 1.0)
    gain_second = 1.0 + 0.3 * jax.random.uniform(jax.random.fold_in(key, 33), (D, 1), jnp.float32, -1.0, 1.0)
    biases = 0.3 * jax.random.normal(jax.random.fold_in(key, 32), (D, 6), jnp.float32)
    return jnp.concatenate([gain_first, biases[:, 0:4], gain_second, biases[:, 4:6]], axis=1)


def block_scale(stream_key, dims, pieces, smallest, largest):
    gain = 1.0
    for position, shards_of in pieces:
        steps = jax.random.uniform(jax.random.fold_in(jax.random.fold_in(stream_key, 6), position), (shards_of,), jnp.float32, smallest / len(pieces), largest / len(pieces))
        gain = gain * jnp.repeat(jnp.exp(steps), dims[position] // shards_of).reshape((-1,) + (1,) * (len(dims) - 1 - position))
    return gain


def bell_draw(own_key, shape, scale, most, cuts=(), dtype=jnp.bfloat16):
    level = block_scale(own_key, shape, cuts, -0.22, 0.18) if cuts else 1.0
    values = jax.random.normal(own_key, shape, jnp.float32) * scale * level
    return jnp.minimum(jnp.maximum(values, -most), most).astype(dtype)


def setup_inputs(seed: int = 0) -> dict:
    splits = jax.random.split(jax.random.key(seed), 15)
    inputs = bell_draw(splits[0], (CLIPS, CLIP_LEN, D), 1.0, 6.0, ((0, 16), (1, 2)))
    cotangent = draw_cotangent(jax.random.fold_in(splits[14], 71), 0)
    project_in = draw_project_in(jax.random.fold_in(splits[14], 71), 0)
    project_out = bell_draw(splits[3], (D, D), (4 * D // 3) ** -0.5, 0.1875, ((0, 32),), jnp.float32)
    expand_weight = bell_draw(splits[4], (D, FF), D ** -0.5, 0.21875, ((0, 32),), jnp.float32)
    shrink_weight = bell_draw(splits[5], (FF, D), (FF * 2 // 5) ** -0.5, 0.15625, ((0, 32),), jnp.float32)
    expand_bias = bell_draw(splits[6], (FF,), 0.5, 3.0, ((0, 32),), jnp.float32)
    vectors = draw_vectors(jax.random.fold_in(splits[14], 71), 0)
    moments_in = draw_moments_in(jax.random.fold_in(splits[14], 71), 0)
    moments_out = draw_moments_out(jax.random.fold_in(splits[14], 71), 0)
    moments_expand = draw_moments_expand(jax.random.fold_in(splits[14], 71), 0)
    moments_shrink = draw_moments_shrink(jax.random.fold_in(splits[14], 71), 0)
    moments_bias = draw_moments_bias(jax.random.fold_in(splits[14], 71), 0)
    moments_vectors = draw_moments_vectors(jax.random.fold_in(splits[14], 71), 0)
    return dict(inputs=inputs, cotangent=cotangent, project_in=project_in, project_out=project_out, expand_weight=expand_weight, shrink_weight=shrink_weight, expand_bias=expand_bias, vectors=vectors, moments_in=moments_in, moments_out=moments_out, moments_expand=moments_expand, moments_shrink=moments_shrink, moments_bias=moments_bias, moments_vectors=moments_vectors)


@jax.custom_vjp
def low(v):
    return lax.optimization_barrier(v.astype(jnp.bfloat16)).astype(jnp.float32)

@jax.custom_vjp
def low_back(v):
    return v

def low_keep(v):
    return (low(v), None)

def low_pass(kept, grad):
    return (grad,)

def back_keep(v):
    return (v, None)

def back_low(kept, grad):
    return (low(grad),)
low.defvjp(low_keep, low_pass)
low_back.defvjp(back_keep, back_low)
epsilon_norm = 1e-05
beta_first = 0.9
beta_second = 0.99
learn_rate = 0.03
decay_rate = 0.01
epsilon_adam = 1e-08
root_half = 0.7071067811865476

def matmul_exact(left, right):
    return jnp.dot(left, right, precision=lax.Precision.HIGHEST)

def layer_norm(inputs, norm_gain, norm_shift):
    average = lax.optimization_barrier(jnp.mean(inputs, axis=-1, keepdims=True))
    centered = inputs - average
    spread = lax.optimization_barrier(jnp.mean(centered * centered, axis=-1, keepdims=True))
    return centered * lax.rsqrt(spread + epsilon_norm) * norm_gain + norm_shift

def gelu_exact(inputs):
    return 0.5 * inputs * (1.0 + jax.scipy.special.erf(inputs * root_half))

def clip_forward(params, frames_in):
    project_in, project_out, expand_weight, shrink_weight, expand_bias, vectors = params
    seq_len = frames_in.shape[0]
    model_width = frames_in.shape[1]
    head_size = model_width // HEADS
    normed_one = low(layer_norm(frames_in, vectors[:, 0], vectors[:, 1]))
    bias_in = jnp.concatenate([vectors[:, 2], jnp.zeros((model_width,), jnp.float32), vectors[:, 3]])
    projected = low_back(low(matmul_exact(normed_one, project_in) + bias_in))
    queries = projected[:, :model_width].reshape(seq_len, HEADS, head_size)
    keys = projected[:, model_width:2 * model_width].reshape(seq_len, HEADS, head_size)
    values = projected[:, 2 * model_width:].reshape(seq_len, HEADS, head_size)
    scores = jnp.einsum('qhd,khd->hqk', queries, keys, precision=lax.Precision.HIGHEST)
    scores = low_back(scores * (1.0 / math.sqrt(head_size)))
    highest = lax.optimization_barrier(jnp.max(scores, axis=-1, keepdims=True))
    exponent = jnp.exp(scores - highest)
    probabilities = low(exponent / lax.optimization_barrier(jnp.sum(exponent, axis=-1, keepdims=True)))
    mixed = jnp.einsum('hqk,khd->qhd', probabilities, values, precision=lax.Precision.HIGHEST)
    mixed = low_back(low(mixed.reshape(seq_len, model_width)))
    attended = low_back(matmul_exact(mixed, project_out) + vectors[:, 4])
    residual = frames_in + attended
    normed_two = low(layer_norm(residual, vectors[:, 5], vectors[:, 6]))
    preact = low_back(matmul_exact(normed_two, expand_weight) + expand_bias)
    activated = low(gelu_exact(preact))
    return residual + matmul_exact(activated, shrink_weight) + vectors[:, 7]

def adam_step(weight, moments, gradient):
    first = beta_first * moments[0] + (1.0 - beta_first) * gradient
    second = beta_second * moments[1] + (1.0 - beta_second) * gradient * gradient
    first_hat = first / (1.0 - beta_first ** ADAM_STEP)
    second_hat = second / (1.0 - beta_second ** ADAM_STEP)
    change = -learn_rate * (first_hat / (jnp.sqrt(second_hat) + epsilon_adam) + decay_rate * weight)
    return (change, jnp.stack([first, second]))

def reference(inputs, cotangent, project_in, project_out, expand_weight, shrink_weight, expand_bias, vectors, moments_in, moments_out, moments_expand, moments_shrink, moments_bias, moments_vectors):
    params = (project_in, project_out, expand_weight, shrink_weight, expand_bias, vectors)

    def forward(weights, frames_all):
        rounded = tuple((low(item) for item in weights))
        return lax.map(jax.checkpoint(partial(clip_forward, rounded)), frames_all)
    result, pullback = jax.vjp(forward, params, inputs.astype(jnp.float32))
    grads, grad_inputs = pullback(cotangent.astype(jnp.float32))
    new_in, mom_in = adam_step(project_in, moments_in, grads[0])
    new_out, mom_out = adam_step(project_out, moments_out, grads[1])
    new_expand, mom_expand = adam_step(expand_weight, moments_expand, grads[2])
    new_shrink, mom_shrink = adam_step(shrink_weight, moments_shrink, grads[3])
    new_bias, mom_bias = adam_step(expand_bias, moments_bias, grads[4])
    new_vectors, mom_vectors = adam_step(vectors, moments_vectors, grads[5])
    return (result.astype(jnp.bfloat16), grad_inputs.astype(jnp.bfloat16), grads[0], grads[1], grads[2], grads[3], grads[4], grads[5], new_in, new_out, new_expand, new_shrink, new_bias, new_vectors, mom_in, mom_out, mom_expand, mom_shrink, mom_bias, mom_vectors)
```

```python
import math

import jax
import jax.numpy as jnp
from jax import lax
from jax.sharding import PartitionSpec as P

HEADS = 12
ADAM_STEP = 4


epsilon_norm = 1e-05
beta_first = 0.9
beta_second = 0.99
learn_rate = 0.03
decay_rate = 0.01
epsilon_adam = 1e-08
root_half = 0.7071067811865476
inv_root_two_pi = 0.3989422804014327


def norm_parts(inputs, norm_gain, norm_shift):
    average = jnp.mean(inputs, axis=-1, keepdims=True)
    centered = inputs - average
    spread = jnp.mean(centered * centered, axis=-1, keepdims=True)
    inv_std = lax.rsqrt(spread + epsilon_norm)
    normed = centered * inv_std
    return (normed * norm_gain + norm_shift, normed, inv_std)


def norm_backward(grad_normed, normed, inv_std, norm_gain):
    grad_gain = jnp.sum(grad_normed * normed, axis=0)
    grad_shift = jnp.sum(grad_normed, axis=0)
    scaled = grad_normed * norm_gain
    grad_input = inv_std * (
        scaled
        - jnp.mean(scaled, axis=-1, keepdims=True)
        - normed * jnp.mean(scaled * normed, axis=-1, keepdims=True)
    )
    return (grad_input, grad_gain, grad_shift)


def gelu_exact(inputs):
    return 0.5 * inputs * (1.0 + jax.scipy.special.erf(inputs * root_half))


def gelu_slope(inputs):
    return (
        0.5 * (1.0 + jax.scipy.special.erf(inputs * root_half))
        + inputs * jnp.exp(-0.5 * inputs * inputs) * inv_root_two_pi
    )


def attend_forward(queries, keys_values, head_count):
    model_width = queries.shape[2]
    head_size = model_width // head_count
    score_scale = 1.0 / math.sqrt(head_size)

    def one_head(head_index):
        offset = head_index * head_size
        query_block = lax.dynamic_slice_in_dim(queries, offset, head_size, 2)
        key_block = lax.dynamic_slice_in_dim(keys_values, offset, head_size, 2)
        value_block = lax.dynamic_slice_in_dim(keys_values, model_width + offset, head_size, 2)
        scores = (
            jnp.einsum("cqd,ckd->cqk", query_block, key_block, preferred_element_type=jnp.float32)
            * score_scale
        )
        highest = jnp.max(scores, axis=-1, keepdims=True)
        exponent = jnp.exp(scores - highest)
        denominator = jnp.sum(exponent, axis=-1, keepdims=True)
        weights_soft = (exponent / denominator).astype(jnp.bfloat16)
        mixed = jnp.einsum(
            "cqk,ckd->cqd", weights_soft, value_block, preferred_element_type=jnp.float32
        )
        return (mixed, (highest + jnp.log(denominator))[..., 0])

    mixed, log_totals = lax.map(one_head, jnp.arange(head_count))
    clip_count, frame_count = (queries.shape[0], queries.shape[1])
    mixed = jnp.transpose(mixed, (1, 2, 0, 3)).reshape(clip_count, frame_count, model_width)
    return (mixed, log_totals)


def attend_backward(queries, keys_values, grad_mixed, log_totals, head_count):
    model_width = queries.shape[2]
    head_size = model_width // head_count
    score_scale = 1.0 / math.sqrt(head_size)

    def one_head_back(head_index):
        offset = head_index * head_size
        query_block = lax.dynamic_slice_in_dim(queries, offset, head_size, 2)
        key_block = lax.dynamic_slice_in_dim(keys_values, offset, head_size, 2)
        value_block = lax.dynamic_slice_in_dim(keys_values, model_width + offset, head_size, 2)
        grad_block = lax.dynamic_slice_in_dim(grad_mixed, offset, head_size, 2)
        totals = lax.dynamic_index_in_dim(log_totals, head_index, 0, keepdims=False)
        scores = (
            jnp.einsum("cqd,ckd->cqk", query_block, key_block, preferred_element_type=jnp.float32)
            * score_scale
        )
        weights_soft = jnp.exp(scores - totals[..., None])
        grad_weights = jnp.einsum(
            "cqd,ckd->cqk", grad_block, value_block, preferred_element_type=jnp.float32
        )
        delta = jnp.sum(weights_soft * grad_weights, axis=-1, keepdims=True)
        grad_scores = (weights_soft * (grad_weights - delta)).astype(jnp.bfloat16)
        grad_query = (
            jnp.einsum("cqk,ckd->cqd", grad_scores, key_block, preferred_element_type=jnp.float32)
            * score_scale
        )
        grad_key = (
            jnp.einsum("cqk,cqd->ckd", grad_scores, query_block, preferred_element_type=jnp.float32)
            * score_scale
        )
        grad_value = jnp.einsum(
            "cqk,cqd->ckd",
            weights_soft.astype(jnp.bfloat16),
            grad_block,
            preferred_element_type=jnp.float32,
        )
        return (grad_query, delta[..., 0], grad_key, grad_value)

    pieces = lax.map(one_head_back, jnp.arange(head_count))
    clip_count, frame_count = (queries.shape[0], queries.shape[1])
    clip_frames = keys_values.shape[1]
    grad_query = jnp.transpose(pieces[0], (1, 2, 0, 3)).reshape(
        clip_count, frame_count, model_width
    )
    grad_key = jnp.transpose(pieces[2], (1, 2, 0, 3)).reshape(clip_count, clip_frames, model_width)
    grad_value = jnp.transpose(pieces[3], (1, 2, 0, 3)).reshape(
        clip_count, clip_frames, model_width
    )
    return (grad_query, pieces[1], jnp.concatenate([grad_key, grad_value], axis=2))


def adam_step(weight, moments, gradient):
    first = beta_first * moments[0] + (1.0 - beta_first) * gradient
    second = beta_second * moments[1] + (1.0 - beta_second) * gradient * gradient
    first_hat = first / (1.0 - beta_first**ADAM_STEP)
    second_hat = second / (1.0 - beta_second**ADAM_STEP)
    change = -learn_rate * (first_hat / (jnp.sqrt(second_hat) + epsilon_adam) + decay_rate * weight)
    return (change, jnp.stack([first, second]))


def body(
    inputs,
    cotangent,
    project_in,
    project_out,
    expand_weight,
    shrink_weight,
    expand_bias,
    vectors,
    moments_in,
    moments_out,
    moments_expand,
    moments_shrink,
    moments_bias,
    moments_vectors,
):
    clip_count, frame_count, model_width = inputs.shape
    row_count = clip_count * frame_count
    head_count = HEADS
    shard_rows = project_in.shape[0]
    wide_in = project_in.shape[1]
    ff_width = expand_weight.shape[1]
    swap = [(0, 1), (1, 0)]
    everyone = ("clip", "frame")

    small = jnp.concatenate(
        [
            vectors,
            expand_bias.reshape(shard_rows, -1),
            jnp.zeros((shard_rows, 128 - vectors.shape[1] - expand_bias.shape[0] // shard_rows), jnp.float32),
        ],
        axis=1,
    )
    first_pack = jnp.concatenate([project_in, small], axis=1).astype(jnp.bfloat16)
    second_pack = jnp.concatenate(
        [project_out, expand_weight, shrink_weight.reshape(shard_rows, -1)], axis=1
    ).astype(jnp.bfloat16)
    first_full = lax.all_gather(first_pack, everyone, axis=0, tiled=True)
    second_full = lax.all_gather(second_pack, everyone, axis=0, tiled=True)
    full_in = first_full[:, :wide_in]
    small_full = first_full[:, wide_in:].astype(jnp.float32)
    column_set = small_full[:, : vectors.shape[1]]
    full_bias = small_full[:, vectors.shape[1] : vectors.shape[1] + ff_width // model_width].reshape(-1)
    full_out = second_full[:, :model_width]
    full_expand = second_full[:, model_width : model_width + ff_width]
    full_shrink = second_full[:, model_width + ff_width :].reshape(ff_width, model_width)

    frames_rows = inputs.reshape(row_count, model_width).astype(jnp.float32)
    normed_first, plain_first, inv_first = norm_parts(
        frames_rows, column_set[:, 0], column_set[:, 1]
    )
    hidden_first = normed_first.astype(jnp.bfloat16)
    hidden_partner = lax.ppermute(hidden_first, "frame", swap)
    bias_in = jnp.concatenate(
        [column_set[:, 2], jnp.zeros((model_width,), jnp.float32), column_set[:, 3]]
    )
    projected = (
        jnp.dot(hidden_first, full_in, preferred_element_type=jnp.float32) + bias_in
    ).astype(jnp.bfloat16)
    partner_pairs = (
        jnp.dot(hidden_partner, full_in[:, model_width:], preferred_element_type=jnp.float32)
        + bias_in[model_width:]
    ).astype(jnp.bfloat16)
    queries = projected[:, :model_width].reshape(clip_count, frame_count, model_width)
    clip_pairs = jnp.concatenate([projected[:, model_width:], partner_pairs], axis=0).reshape(
        clip_count, 2 * frame_count, 2 * model_width
    )
    mixed, log_totals = attend_forward(queries, clip_pairs, head_count)
    mixed_low = mixed.reshape(row_count, model_width).astype(jnp.bfloat16)
    attended = jnp.dot(mixed_low, full_out, preferred_element_type=jnp.float32) + column_set[:, 4]
    residual = frames_rows + attended
    normed_second, plain_second, inv_second = norm_parts(
        residual, column_set[:, 5], column_set[:, 6]
    )
    hidden_second = normed_second.astype(jnp.bfloat16)
    preact = jnp.dot(hidden_second, full_expand, preferred_element_type=jnp.float32) + full_bias
    activated = gelu_exact(preact).astype(jnp.bfloat16)
    result = (
        residual
        + jnp.dot(activated, full_shrink, preferred_element_type=jnp.float32)
        + column_set[:, 7]
    )
    output = result.astype(jnp.bfloat16).reshape(inputs.shape)

    grad_result = cotangent.reshape(row_count, model_width)
    grad_shrink_term = jnp.dot(activated.T, grad_result, preferred_element_type=jnp.float32)
    grad_down_bias = jnp.sum(grad_result.astype(jnp.float32), axis=0)
    grad_activated = jnp.dot(grad_result, full_shrink.T, preferred_element_type=jnp.float32)
    grad_preact = (grad_activated * gelu_slope(preact)).astype(jnp.bfloat16)
    grad_expand_term = jnp.dot(hidden_second.T, grad_preact, preferred_element_type=jnp.float32)
    grad_bias_term = jnp.sum(grad_preact.astype(jnp.float32), axis=0)
    grad_hidden_second = jnp.dot(grad_preact, full_expand.T, preferred_element_type=jnp.float32)
    norm_term_second, gain_second, shift_second = norm_backward(
        grad_hidden_second, plain_second, inv_second, column_set[:, 5]
    )
    grad_residual = grad_result.astype(jnp.float32) + norm_term_second
    grad_attended = grad_residual.astype(jnp.bfloat16)
    grad_out_term = jnp.dot(mixed_low.T, grad_attended, preferred_element_type=jnp.float32)
    grad_out_bias = jnp.sum(grad_attended.astype(jnp.float32), axis=0)
    owned_late = lax.psum_scatter(
        jnp.concatenate(
            [grad_shrink_term.reshape(model_width, -1), grad_expand_term, grad_out_term], axis=1
        ),
        everyone,
        scatter_dimension=0,
        tiled=True,
    )
    grad_mixed = jnp.dot(grad_attended, full_out.T, preferred_element_type=jnp.float32).astype(
        jnp.bfloat16
    )
    grad_mixed = grad_mixed.reshape(clip_count, frame_count, model_width)
    grad_query, delta_rows, grad_pairs_terms = attend_backward(
        queries, clip_pairs, grad_mixed, log_totals, head_count
    )
    partner_terms = grad_pairs_terms[:, frame_count:].astype(jnp.bfloat16)
    returned_terms = lax.ppermute(partner_terms, "frame", swap)
    grad_pairs = grad_pairs_terms[:, :frame_count] + returned_terms.astype(jnp.float32)
    grad_projected = (
        jnp.concatenate([grad_query, grad_pairs], axis=2)
        .reshape(row_count, 3 * model_width)
        .astype(jnp.bfloat16)
    )
    grad_in_term = jnp.dot(hidden_first.T, grad_projected, preferred_element_type=jnp.float32)
    projected_sums = jnp.sum(grad_projected.astype(jnp.float32), axis=0)
    grad_query_bias = projected_sums[:model_width]
    grad_value_bias = projected_sums[2 * model_width :]
    grad_hidden_first = jnp.dot(grad_projected, full_in.T, preferred_element_type=jnp.float32)
    norm_term_first, gain_first, shift_first = norm_backward(
        grad_hidden_first, plain_first, inv_first, column_set[:, 0]
    )
    grad_inputs = (grad_residual + norm_term_first).astype(jnp.bfloat16).reshape(inputs.shape)
    grad_columns = jnp.stack(
        [
            gain_first,
            shift_first,
            grad_query_bias,
            grad_value_bias,
            grad_out_bias,
            gain_second,
            shift_second,
            grad_down_bias,
        ],
        axis=1,
    )
    small_grads = jnp.concatenate(
        [
            grad_columns,
            grad_bias_term.reshape(model_width, -1),
            jnp.zeros((model_width, 128 - grad_columns.shape[1] - ff_width // model_width), jnp.float32),
        ],
        axis=1,
    )
    owned_in = lax.psum_scatter(grad_in_term, everyone, scatter_dimension=0, tiled=True)
    owned_small = lax.psum_scatter(small_grads, everyone, scatter_dimension=0, tiled=True)
    owned_vectors = owned_small[:, : vectors.shape[1]]
    owned_bias = owned_small[
        :, vectors.shape[1] : vectors.shape[1] + ff_width // model_width
    ].reshape(-1)
    owned_shrink = owned_late[:, :ff_width].reshape(shrink_weight.shape)
    owned_expand = owned_late[:, ff_width : 2 * ff_width]
    owned_out = owned_late[:, 2 * ff_width :]
    new_in, mom_in = adam_step(project_in, moments_in, owned_in)
    new_out, mom_out = adam_step(project_out, moments_out, owned_out)
    new_expand, mom_expand = adam_step(expand_weight, moments_expand, owned_expand)
    new_shrink, mom_shrink = adam_step(shrink_weight, moments_shrink, owned_shrink)
    new_bias, mom_bias = adam_step(expand_bias, moments_bias, owned_bias)
    new_vectors, mom_vectors = adam_step(vectors, moments_vectors, owned_vectors)
    return (
        output,
        grad_inputs,
        owned_in,
        owned_out,
        owned_expand,
        owned_shrink,
        owned_bias,
        owned_vectors,
        new_in,
        new_out,
        new_expand,
        new_shrink,
        new_bias,
        new_vectors,
        mom_in,
        mom_out,
        mom_expand,
        mom_shrink,
        mom_bias,
        mom_vectors,
    )


def solution(mesh):
    in_specs = (
        P("clip", "frame", None),
        P("clip", "frame", None),
        P(("clip", "frame"), None),
        P(("clip", "frame"), None),
        P(("clip", "frame"), None),
        P(("clip", "frame"), None),
        P(("clip", "frame")),
        P(("clip", "frame"), None),
        P(None, ("clip", "frame"), None),
        P(None, ("clip", "frame"), None),
        P(None, ("clip", "frame"), None),
        P(None, ("clip", "frame"), None),
        P(None, ("clip", "frame")),
        P(None, ("clip", "frame"), None),
    )
    out_specs = (
        P("clip", "frame", None),
        P("clip", "frame", None),
        P(("clip", "frame"), None),
        P(("clip", "frame"), None),
        P(("clip", "frame"), None),
        P(("clip", "frame"), None),
        P(("clip", "frame")),
        P(("clip", "frame"), None),
        P(("clip", "frame"), None),
        P(("clip", "frame"), None),
        P(("clip", "frame"), None),
        P(("clip", "frame"), None),
        P(("clip", "frame")),
        P(("clip", "frame"), None),
        P(None, ("clip", "frame"), None),
        P(None, ("clip", "frame"), None),
        P(None, ("clip", "frame"), None),
        P(None, ("clip", "frame"), None),
        P(None, ("clip", "frame")),
        P(None, ("clip", "frame"), None),
    )
    return jax.shard_map(body, mesh=mesh, in_specs=in_specs, out_specs=out_specs, check_vma=False)
```

```python
import math

import jax
import jax.numpy as jnp
from jax import lax
from jax.sharding import PartitionSpec as P

HEADS = 12
ADAM_STEP = 4


epsilon_norm = 1e-05
beta_first = 0.9
beta_second = 0.99
learn_rate = 0.03
decay_rate = 0.01
epsilon_adam = 1e-08
root_half = 0.7071067811865476
inv_root_two_pi = 0.3989422804014327


def norm_parts(inputs, norm_gain, norm_shift):
    average = jnp.mean(inputs, axis=-1, keepdims=True)
    centered = inputs - average
    spread = jnp.mean(centered * centered, axis=-1, keepdims=True)
    inv_std = lax.rsqrt(spread + epsilon_norm)
    normed = centered * inv_std
    return (normed * norm_gain + norm_shift, normed, inv_std)


def norm_backward(grad_normed, normed, inv_std, norm_gain):
    grad_gain = jnp.sum(grad_normed * normed, axis=0)
    grad_shift = jnp.sum(grad_normed, axis=0)
    scaled = grad_normed * norm_gain
    grad_input = inv_std * (
        scaled
        - jnp.mean(scaled, axis=-1, keepdims=True)
        - normed * jnp.mean(scaled * normed, axis=-1, keepdims=True)
    )
    return (grad_input, grad_gain, grad_shift)


def gelu_exact(inputs):
    return 0.5 * inputs * (1.0 + jax.scipy.special.erf(inputs * root_half))


def gelu_slope(inputs):
    return (
        0.5 * (1.0 + jax.scipy.special.erf(inputs * root_half))
        + inputs * jnp.exp(-0.5 * inputs * inputs) * inv_root_two_pi
    )


def attend_forward(queries, keys_values, head_count):
    model_width = queries.shape[2]
    head_size = model_width // head_count
    score_scale = 1.0 / math.sqrt(head_size)

    def one_head(head_index):
        offset = head_index * head_size
        query_block = lax.dynamic_slice_in_dim(queries, offset, head_size, 2)
        key_block = lax.dynamic_slice_in_dim(keys_values, offset, head_size, 2)
        value_block = lax.dynamic_slice_in_dim(keys_values, model_width + offset, head_size, 2)
        scores = (
            jnp.einsum("cqd,ckd->cqk", query_block, key_block, preferred_element_type=jnp.float32)
            * score_scale
        )
        highest = jnp.max(scores, axis=-1, keepdims=True)
        exponent = jnp.exp(scores - highest)
        denominator = jnp.sum(exponent, axis=-1, keepdims=True)
        weights_soft = (exponent / denominator).astype(jnp.bfloat16)
        mixed = jnp.einsum(
            "cqk,ckd->cqd", weights_soft, value_block, preferred_element_type=jnp.float32
        )
        return (mixed, (highest + jnp.log(denominator))[..., 0])

    mixed, log_totals = lax.map(one_head, jnp.arange(head_count))
    clip_count, frame_count = (queries.shape[0], queries.shape[1])
    mixed = jnp.transpose(mixed, (1, 2, 0, 3)).reshape(clip_count, frame_count, model_width)
    return (mixed, log_totals)


def attend_backward(queries, keys_values, grad_mixed, log_totals, head_count):
    model_width = queries.shape[2]
    head_size = model_width // head_count
    score_scale = 1.0 / math.sqrt(head_size)

    def one_head_back(head_index):
        offset = head_index * head_size
        query_block = lax.dynamic_slice_in_dim(queries, offset, head_size, 2)
        key_block = lax.dynamic_slice_in_dim(keys_values, offset, head_size, 2)
        value_block = lax.dynamic_slice_in_dim(keys_values, model_width + offset, head_size, 2)
        grad_block = lax.dynamic_slice_in_dim(grad_mixed, offset, head_size, 2)
        totals = lax.dynamic_index_in_dim(log_totals, head_index, 0, keepdims=False)
        scores = (
            jnp.einsum("cqd,ckd->cqk", query_block, key_block, preferred_element_type=jnp.float32)
            * score_scale
        )
        weights_soft = jnp.exp(scores - totals[..., None])
        grad_weights = jnp.einsum(
            "cqd,ckd->cqk", grad_block, value_block, preferred_element_type=jnp.float32
        )
        delta = jnp.sum(weights_soft * grad_weights, axis=-1, keepdims=True)
        grad_scores = (weights_soft * (grad_weights - delta)).astype(jnp.bfloat16)
        grad_query = (
            jnp.einsum("cqk,ckd->cqd", grad_scores, key_block, preferred_element_type=jnp.float32)
            * score_scale
        )
        grad_key = (
            jnp.einsum("cqk,cqd->ckd", grad_scores, query_block, preferred_element_type=jnp.float32)
            * score_scale
        )
        grad_value = jnp.einsum(
            "cqk,cqd->ckd",
            weights_soft.astype(jnp.bfloat16),
            grad_block,
            preferred_element_type=jnp.float32,
        )
        return (grad_query, delta[..., 0], grad_key, grad_value)

    pieces = lax.map(one_head_back, jnp.arange(head_count))
    clip_count, frame_count = (queries.shape[0], queries.shape[1])
    clip_frames = keys_values.shape[1]
    grad_query = jnp.transpose(pieces[0], (1, 2, 0, 3)).reshape(
        clip_count, frame_count, model_width
    )
    grad_key = jnp.transpose(pieces[2], (1, 2, 0, 3)).reshape(clip_count, clip_frames, model_width)
    grad_value = jnp.transpose(pieces[3], (1, 2, 0, 3)).reshape(
        clip_count, clip_frames, model_width
    )
    return (grad_query, pieces[1], jnp.concatenate([grad_key, grad_value], axis=2))


def adam_step(weight, moments, gradient):
    first = beta_first * moments[0] + (1.0 - beta_first) * gradient
    second = beta_second * moments[1] + (1.0 - beta_second) * gradient * gradient
    first_hat = first / (1.0 - beta_first**ADAM_STEP)
    second_hat = second / (1.0 - beta_second**ADAM_STEP)
    change = -learn_rate * (first_hat / (jnp.sqrt(second_hat) + epsilon_adam) + decay_rate * weight)
    return (change, jnp.stack([first, second]))


def body(
    inputs,
    cotangent,
    project_in,
    project_out,
    expand_weight,
    shrink_weight,
    expand_bias,
    vectors,
    moments_in,
    moments_out,
    moments_expand,
    moments_shrink,
    moments_bias,
    moments_vectors,
):
    clip_count, frame_count, model_width = inputs.shape
    row_count = clip_count * frame_count
    head_count = HEADS
    shard_rows = project_in.shape[0]
    wide_in = project_in.shape[1]
    ff_width = expand_weight.shape[1]
    swap = [(0, 1), (1, 0)]
    everyone = ("clip", "frame")

    small = jnp.concatenate(
        [
            vectors,
            expand_bias.reshape(shard_rows, -1),
            jnp.zeros((shard_rows, 128 - vectors.shape[1] - expand_bias.shape[0] // shard_rows), jnp.float32),
        ],
        axis=1,
    )
    first_pack = jnp.concatenate([project_in, small], axis=1).astype(jnp.bfloat16)
    second_pack = jnp.concatenate(
        [project_out, expand_weight, shrink_weight.reshape(shard_rows, -1)], axis=1
    ).astype(jnp.bfloat16)
    first_full = lax.all_gather(first_pack, everyone, axis=0, tiled=True)
    second_full = lax.all_gather(second_pack, everyone, axis=0, tiled=True)
    full_in = first_full[:, :wide_in]
    small_full = first_full[:, wide_in:].astype(jnp.float32)
    column_set = small_full[:, : vectors.shape[1]]
    full_bias = small_full[:, vectors.shape[1] : vectors.shape[1] + ff_width // model_width].reshape(-1)
    full_out = second_full[:, :model_width]
    full_expand = second_full[:, model_width : model_width + ff_width]
    full_shrink = second_full[:, model_width + ff_width :].reshape(ff_width, model_width)

    frames_rows = inputs.reshape(row_count, model_width).astype(jnp.float32)
    normed_first, plain_first, inv_first = norm_parts(
        frames_rows, column_set[:, 0], column_set[:, 1]
    )
    hidden_first = normed_first.astype(jnp.bfloat16)
    hidden_partner = lax.ppermute(hidden_first, "frame", swap)
    bias_in = jnp.concatenate(
        [column_set[:, 2], jnp.zeros((model_width,), jnp.float32), column_set[:, 3]]
    )
    projected = (
        jnp.dot(hidden_first, full_in, preferred_element_type=jnp.float32) + bias_in
    ).astype(jnp.bfloat16)
    partner_pairs = (
        jnp.dot(hidden_partner, full_in[:, model_width:], preferred_element_type=jnp.float32)
        + bias_in[model_width:]
    ).astype(jnp.bfloat16)
    queries = projected[:, :model_width].reshape(clip_count, frame_count, model_width)
    clip_pairs = jnp.concatenate([projected[:, model_width:], partner_pairs], axis=0).reshape(
        clip_count, 2 * frame_count, 2 * model_width
    )
    mixed, log_totals = attend_forward(queries, clip_pairs, head_count)
    mixed_low = mixed.reshape(row_count, model_width).astype(jnp.bfloat16)
    attended = jnp.dot(mixed_low, full_out, preferred_element_type=jnp.float32) + column_set[:, 4]
    residual = frames_rows + attended
    normed_second, plain_second, inv_second = norm_parts(
        residual, column_set[:, 5], column_set[:, 6]
    )
    hidden_second = normed_second.astype(jnp.bfloat16)
    preact = jnp.dot(hidden_second, full_expand, preferred_element_type=jnp.float32) + full_bias
    activated = gelu_exact(preact).astype(jnp.bfloat16)
    result = (
        residual
        + jnp.dot(activated, full_shrink, preferred_element_type=jnp.float32)
        + column_set[:, 7]
    )
    output = result.astype(jnp.bfloat16).reshape(inputs.shape)

    grad_result = cotangent.reshape(row_count, model_width)
    grad_shrink_term = jnp.dot(activated.T, grad_result, preferred_element_type=jnp.float32)
    grad_down_bias = jnp.sum(grad_result.astype(jnp.float32), axis=0)
    grad_activated = jnp.dot(grad_result, full_shrink.T, preferred_element_type=jnp.float32)
    grad_preact = (grad_activated * gelu_slope(preact)).astype(jnp.bfloat16)
    grad_expand_term = jnp.dot(hidden_second.T, grad_preact, preferred_element_type=jnp.float32)
    grad_bias_term = jnp.sum(grad_preact.astype(jnp.float32), axis=0)
    grad_hidden_second = jnp.dot(grad_preact, full_expand.T, preferred_element_type=jnp.float32)
    norm_term_second, gain_second, shift_second = norm_backward(
        grad_hidden_second, plain_second, inv_second, column_set[:, 5]
    )
    grad_residual = grad_result.astype(jnp.float32) + norm_term_second
    grad_attended = grad_residual.astype(jnp.bfloat16)
    grad_out_term = jnp.dot(mixed_low.T, grad_attended, preferred_element_type=jnp.float32)
    grad_out_bias = jnp.sum(grad_attended.astype(jnp.float32), axis=0)
    owned_late = lax.psum_scatter(
        jnp.concatenate(
            [grad_shrink_term.reshape(model_width, -1), grad_expand_term, grad_out_term], axis=1
        ),
        everyone,
        scatter_dimension=0,
        tiled=True,
    )
    grad_mixed = jnp.dot(grad_attended, full_out.T, preferred_element_type=jnp.float32).astype(
        jnp.bfloat16
    )
    grad_mixed = grad_mixed.reshape(clip_count, frame_count, model_width)
    grad_query, delta_rows, grad_pairs_terms = attend_backward(
        queries, clip_pairs, grad_mixed, log_totals, head_count
    )
    partner_terms = grad_pairs_terms[:, frame_count:].astype(jnp.bfloat16)
    returned_terms = lax.ppermute(partner_terms, "frame", swap)
    grad_pairs = grad_pairs_terms[:, :frame_count] + returned_terms.astype(jnp.float32)
    grad_projected = (
        jnp.concatenate([grad_query, grad_pairs], axis=2)
        .reshape(row_count, 3 * model_width)
        .astype(jnp.bfloat16)
    )
    grad_in_term = jnp.dot(hidden_first.T, grad_projected, preferred_element_type=jnp.float32)
    projected_sums = jnp.sum(grad_projected.astype(jnp.float32), axis=0)
    grad_query_bias = projected_sums[:model_width]
    grad_value_bias = projected_sums[2 * model_width :]
    grad_hidden_first = jnp.dot(grad_projected, full_in.T, preferred_element_type=jnp.float32)
    norm_term_first, gain_first, shift_first = norm_backward(
        grad_hidden_first, plain_first, inv_first, column_set[:, 0]
    )
    grad_inputs = (grad_residual + norm_term_first).astype(jnp.bfloat16).reshape(inputs.shape)
    grad_columns = jnp.stack(
        [
            gain_first,
            shift_first,
            grad_query_bias,
            grad_value_bias,
            grad_out_bias,
            gain_second,
            shift_second,
            grad_down_bias,
        ],
        axis=1,
    )
    small_grads = jnp.concatenate(
        [
            grad_columns,
            grad_bias_term.reshape(model_width, -1),
            jnp.zeros((model_width, 256 - 12), jnp.float32),
        ],
        axis=1,
    )
    first_terms, owned_late = lax.optimization_barrier(
        (jnp.concatenate([grad_in_term, small_grads], axis=1), owned_late)
    )
    owned_first = lax.psum_scatter(first_terms, everyone, scatter_dimension=0, tiled=True)
    owned_in = owned_first[:, :wide_in]
    owned_vectors = owned_first[:, wide_in : wide_in + vectors.shape[1]]
    owned_bias = owned_first[:, wide_in + vectors.shape[1] : wide_in + 12].reshape(-1)
    owned_shrink = owned_late[:, :ff_width].reshape(shrink_weight.shape)
    owned_expand = owned_late[:, ff_width : 2 * ff_width]
    owned_out = owned_late[:, 2 * ff_width :]
    new_in, mom_in = adam_step(project_in, moments_in, owned_in)
    new_out, mom_out = adam_step(project_out, moments_out, owned_out)
    new_expand, mom_expand = adam_step(expand_weight, moments_expand, owned_expand)
    new_shrink, mom_shrink = adam_step(shrink_weight, moments_shrink, owned_shrink)
    new_bias, mom_bias = adam_step(expand_bias, moments_bias, owned_bias)
    new_vectors, mom_vectors = adam_step(vectors, moments_vectors, owned_vectors)
    return (
        output,
        grad_inputs,
        owned_in,
        owned_out,
        owned_expand,
        owned_shrink,
        owned_bias,
        owned_vectors,
        new_in,
        new_out,
        new_expand,
        new_shrink,
        new_bias,
        new_vectors,
        mom_in,
        mom_out,
        mom_expand,
        mom_shrink,
        mom_bias,
        mom_vectors,
    )


def solution(mesh):
    in_specs = (
        P("clip", "frame", None),
        P("clip", "frame", None),
        P(("clip", "frame"), None),
        P(("clip", "frame"), None),
        P(("clip", "frame"), None),
        P(("clip", "frame"), None),
        P(("clip", "frame")),
        P(("clip", "frame"), None),
        P(None, ("clip", "frame"), None),
        P(None, ("clip", "frame"), None),
        P(None, ("clip", "frame"), None),
        P(None, ("clip", "frame"), None),
        P(None, ("clip", "frame")),
        P(None, ("clip", "frame"), None),
    )
    out_specs = (
        P("clip", "frame", None),
        P("clip", "frame", None),
        P(("clip", "frame"), None),
        P(("clip", "frame"), None),
        P(("clip", "frame"), None),
        P(("clip", "frame"), None),
        P(("clip", "frame")),
        P(("clip", "frame"), None),
        P(("clip", "frame"), None),
        P(("clip", "frame"), None),
        P(("clip", "frame"), None),
        P(("clip", "frame"), None),
        P(("clip", "frame")),
        P(("clip", "frame"), None),
        P(None, ("clip", "frame"), None),
        P(None, ("clip", "frame"), None),
        P(None, ("clip", "frame"), None),
        P(None, ("clip", "frame"), None),
        P(None, ("clip", "frame")),
        P(None, ("clip", "frame"), None),
    )
    return jax.shard_map(body, mesh=mesh, in_specs=in_specs, out_specs=out_specs, check_vma=False)
```

```python
import math

import jax
import jax.numpy as jnp
from jax import lax
from jax.experimental import pallas as pl
from jax.experimental.pallas import tpu as pltpu
from jax.sharding import PartitionSpec as P

HEADS = 12
ADAM_STEP = 4


epsilon_norm = 1e-05
beta_first = 0.9
beta_second = 0.99
learn_rate = 0.03
decay_rate = 0.01
epsilon_adam = 1e-08
root_half = 0.7071067811865476
inv_root_two_pi = 0.3989422804014327


def norm_parts(inputs, norm_gain, norm_shift):
    average = jnp.mean(inputs, axis=-1, keepdims=True)
    centered = inputs - average
    spread = jnp.mean(centered * centered, axis=-1, keepdims=True)
    inv_std = lax.rsqrt(spread + epsilon_norm)
    normed = centered * inv_std
    return (normed * norm_gain + norm_shift, normed, inv_std)


def norm_backward(grad_normed, normed, inv_std, norm_gain):
    grad_gain = jnp.sum(grad_normed * normed, axis=0)
    grad_shift = jnp.sum(grad_normed, axis=0)
    scaled = grad_normed * norm_gain
    grad_input = inv_std * (
        scaled
        - jnp.mean(scaled, axis=-1, keepdims=True)
        - normed * jnp.mean(scaled * normed, axis=-1, keepdims=True)
    )
    return (grad_input, grad_gain, grad_shift)


def gelu_exact(inputs):
    return 0.5 * inputs * (1.0 + jax.scipy.special.erf(inputs * root_half))


def gelu_slope(inputs):
    return (
        0.5 * (1.0 + jax.scipy.special.erf(inputs * root_half))
        + inputs * jnp.exp(-0.5 * inputs * inputs) * inv_root_two_pi
    )


QUERY_CHUNK = 256
MASKED = -1e30


def attention_forward_kernel(q_ref, k_ref, v_ref, kbias_ref, o_ref, l_ref):
    head_size = q_ref.shape[1] // 2
    rows = q_ref.shape[0]
    kbias = kbias_ref[...]
    lane = lax.broadcasted_iota(jnp.int32, (QUERY_CHUNK, 2 * head_size), 1)
    for chunk in range(rows // QUERY_CHUNK):
        span = pl.ds(chunk * QUERY_CHUNK, QUERY_CHUNK)
        mixed_parts = []
        totals = []
        for half in range(2):
            cols = pl.ds(half * head_size, head_size)
            query = q_ref[span, cols]
            key = k_ref[:, cols]
            value = v_ref[:, cols]
            scores = (
                lax.dot_general(
                    query, key, (((1,), (1,)), ((), ())), preferred_element_type=jnp.float32
                )
                + kbias
            )
            highest = jnp.max(scores, axis=1, keepdims=True)
            exponent = jnp.exp(scores - highest)
            denominator = jnp.sum(exponent, axis=1, keepdims=True)
            weights = (exponent * (1.0 / denominator)).astype(jnp.bfloat16)
            mixed_parts.append(jnp.dot(weights, value, preferred_element_type=jnp.float32))
            totals.append(highest + jnp.log(denominator))
        o_ref[span, :] = jnp.concatenate(mixed_parts, axis=1).astype(o_ref.dtype)
        l_ref[span, :] = jnp.where(lane < head_size, totals[0], totals[1])


def attention_backward_kernel(
    q_ref, k_ref, v_ref, do_ref, l_ref, kbias_ref, dq_ref, dk_ref, dv_ref
):
    head_size = q_ref.shape[1] // 2
    rows = q_ref.shape[0]
    kbias = kbias_ref[...]
    for half in range(2):
        cols = pl.ds(half * head_size, head_size)
        key = k_ref[:, cols]
        value = v_ref[:, cols]
        grad_key = None
        grad_value = None
        for chunk in range(rows // QUERY_CHUNK):
            span = pl.ds(chunk * QUERY_CHUNK, QUERY_CHUNK)
            query = q_ref[span, cols]
            grad_out = do_ref[span, cols]
            total = l_ref[span, pl.ds(half * head_size, 1)]
            scores = (
                lax.dot_general(
                    query, key, (((1,), (1,)), ((), ())), preferred_element_type=jnp.float32
                )
                + kbias
            )
            weights = jnp.exp(scores - total)
            grad_weights = lax.dot_general(
                grad_out, value, (((1,), (1,)), ((), ())), preferred_element_type=jnp.float32
            )
            delta = jnp.sum(weights * grad_weights, axis=1, keepdims=True)
            grad_scores = (weights * (grad_weights - delta)).astype(jnp.bfloat16)
            dq_ref[span, cols] = jnp.dot(
                grad_scores, key, preferred_element_type=jnp.float32
            ).astype(dq_ref.dtype)
            key_part = lax.dot_general(
                grad_scores, query, (((0,), (0,)), ((), ())), preferred_element_type=jnp.float32
            )
            value_part = lax.dot_general(
                weights.astype(jnp.bfloat16),
                grad_out,
                (((0,), (0,)), ((), ())),
                preferred_element_type=jnp.float32,
            )
            grad_key = key_part if grad_key is None else grad_key + key_part
            grad_value = value_part if grad_value is None else grad_value + value_part
        dk_ref[:, cols] = grad_key
        dv_ref[:, cols] = grad_value


def pad_rows(values, rows):
    return jnp.pad(values, ((0, rows - values.shape[0]), (0, 0)))


def attention_pallas(queries, pairs, grad_out=None, totals=None):
    query_rows, model_width = queries.shape
    key_rows = pairs.shape[0]
    padded_q = -(-query_rows // QUERY_CHUNK) * QUERY_CHUNK
    padded_k = -(-key_rows // 128) * 128
    pair_count = model_width // 128
    q_pad = pad_rows(queries, padded_q)
    kv_pad = pad_rows(pairs, padded_k)
    kbias = jnp.where(jnp.arange(padded_k) < key_rows, 0.0, MASKED).astype(jnp.float32)[None, :]
    q_spec = pl.BlockSpec((padded_q, 128), lambda j: (0, j))
    k_spec = pl.BlockSpec((padded_k, 128), lambda j: (0, j))
    v_spec = pl.BlockSpec((padded_k, 128), lambda j: (0, j + pair_count))
    b_spec = pl.BlockSpec((1, padded_k), lambda j: (0, 0))
    params = pltpu.CompilerParams(vmem_limit_bytes=48 * 1024 * 1024)
    if grad_out is None:
        mixed, log_totals = pl.pallas_call(
            attention_forward_kernel,
            grid=(pair_count,),
            in_specs=[q_spec, k_spec, v_spec, b_spec],
            out_specs=[q_spec, q_spec],
            out_shape=[
                jax.ShapeDtypeStruct((padded_q, model_width), jnp.bfloat16),
                jax.ShapeDtypeStruct((padded_q, model_width), jnp.float32),
            ],
            compiler_params=params,
        )(q_pad, kv_pad, kv_pad, kbias)
        return mixed[:query_rows], log_totals
    do_pad = pad_rows(grad_out, padded_q)
    dq, dk, dv = pl.pallas_call(
        attention_backward_kernel,
        grid=(pair_count,),
        in_specs=[q_spec, k_spec, v_spec, q_spec, q_spec, b_spec],
        out_specs=[q_spec, k_spec, k_spec],
        out_shape=[
            jax.ShapeDtypeStruct((padded_q, model_width), jnp.float32),
            jax.ShapeDtypeStruct((padded_k, model_width), jnp.float32),
            jax.ShapeDtypeStruct((padded_k, model_width), jnp.float32),
        ],
        compiler_params=params,
    )(q_pad, kv_pad, kv_pad, do_pad, totals, kbias)
    return dq[:query_rows], dk[:key_rows], dv[:key_rows]


def attend_forward(queries, keys_values, head_count):
    model_width = queries.shape[2]
    head_size = model_width // head_count
    score_scale = 1.0 / math.sqrt(head_size)

    def one_head(head_index):
        offset = head_index * head_size
        query_block = lax.dynamic_slice_in_dim(queries, offset, head_size, 2)
        key_block = lax.dynamic_slice_in_dim(keys_values, offset, head_size, 2)
        value_block = lax.dynamic_slice_in_dim(keys_values, model_width + offset, head_size, 2)
        scores = (
            jnp.einsum("cqd,ckd->cqk", query_block, key_block, preferred_element_type=jnp.float32)
            * score_scale
        )
        highest = jnp.max(scores, axis=-1, keepdims=True)
        exponent = jnp.exp(scores - highest)
        denominator = jnp.sum(exponent, axis=-1, keepdims=True)
        weights_soft = (exponent / denominator).astype(jnp.bfloat16)
        mixed = jnp.einsum(
            "cqk,ckd->cqd", weights_soft, value_block, preferred_element_type=jnp.float32
        )
        return (mixed, (highest + jnp.log(denominator))[..., 0])

    mixed, log_totals = lax.map(one_head, jnp.arange(head_count))
    clip_count, frame_count = (queries.shape[0], queries.shape[1])
    mixed = jnp.transpose(mixed, (1, 2, 0, 3)).reshape(clip_count, frame_count, model_width)
    return (mixed, log_totals)


def attend_backward(queries, keys_values, grad_mixed, log_totals, head_count):
    model_width = queries.shape[2]
    head_size = model_width // head_count
    score_scale = 1.0 / math.sqrt(head_size)

    def one_head_back(head_index):
        offset = head_index * head_size
        query_block = lax.dynamic_slice_in_dim(queries, offset, head_size, 2)
        key_block = lax.dynamic_slice_in_dim(keys_values, offset, head_size, 2)
        value_block = lax.dynamic_slice_in_dim(keys_values, model_width + offset, head_size, 2)
        grad_block = lax.dynamic_slice_in_dim(grad_mixed, offset, head_size, 2)
        totals = lax.dynamic_index_in_dim(log_totals, head_index, 0, keepdims=False)
        scores = (
            jnp.einsum("cqd,ckd->cqk", query_block, key_block, preferred_element_type=jnp.float32)
            * score_scale
        )
        weights_soft = jnp.exp(scores - totals[..., None])
        grad_weights = jnp.einsum(
            "cqd,ckd->cqk", grad_block, value_block, preferred_element_type=jnp.float32
        )
        delta = jnp.sum(weights_soft * grad_weights, axis=-1, keepdims=True)
        grad_scores = (weights_soft * (grad_weights - delta)).astype(jnp.bfloat16)
        grad_query = (
            jnp.einsum("cqk,ckd->cqd", grad_scores, key_block, preferred_element_type=jnp.float32)
            * score_scale
        )
        grad_key = (
            jnp.einsum("cqk,cqd->ckd", grad_scores, query_block, preferred_element_type=jnp.float32)
            * score_scale
        )
        grad_value = jnp.einsum(
            "cqk,cqd->ckd",
            weights_soft.astype(jnp.bfloat16),
            grad_block,
            preferred_element_type=jnp.float32,
        )
        return (grad_query, delta[..., 0], grad_key, grad_value)

    pieces = lax.map(one_head_back, jnp.arange(head_count))
    clip_count, frame_count = (queries.shape[0], queries.shape[1])
    clip_frames = keys_values.shape[1]
    grad_query = jnp.transpose(pieces[0], (1, 2, 0, 3)).reshape(
        clip_count, frame_count, model_width
    )
    grad_key = jnp.transpose(pieces[2], (1, 2, 0, 3)).reshape(clip_count, clip_frames, model_width)
    grad_value = jnp.transpose(pieces[3], (1, 2, 0, 3)).reshape(
        clip_count, clip_frames, model_width
    )
    return (grad_query, pieces[1], jnp.concatenate([grad_key, grad_value], axis=2))


def adam_step(weight, moments, gradient):
    first = beta_first * moments[0] + (1.0 - beta_first) * gradient
    second = beta_second * moments[1] + (1.0 - beta_second) * gradient * gradient
    first_hat = first / (1.0 - beta_first**ADAM_STEP)
    second_hat = second / (1.0 - beta_second**ADAM_STEP)
    change = -learn_rate * (first_hat / (jnp.sqrt(second_hat) + epsilon_adam) + decay_rate * weight)
    return (change, jnp.stack([first, second]))


def body(
    inputs,
    cotangent,
    project_in,
    project_out,
    expand_weight,
    shrink_weight,
    expand_bias,
    vectors,
    moments_in,
    moments_out,
    moments_expand,
    moments_shrink,
    moments_bias,
    moments_vectors,
):
    clip_count, frame_count, model_width = inputs.shape
    row_count = clip_count * frame_count
    head_count = HEADS
    shard_rows = project_in.shape[0]
    wide_in = project_in.shape[1]
    ff_width = expand_weight.shape[1]
    swap = [(0, 1), (1, 0)]
    everyone = ("clip", "frame")

    small = jnp.concatenate(
        [
            vectors,
            expand_bias.reshape(shard_rows, -1),
            jnp.zeros((shard_rows, 128 - vectors.shape[1] - expand_bias.shape[0] // shard_rows), jnp.float32),
        ],
        axis=1,
    )
    first_pack = jnp.concatenate([project_in, small], axis=1).astype(jnp.bfloat16)
    second_pack = jnp.concatenate(
        [project_out, expand_weight, shrink_weight.reshape(shard_rows, -1)], axis=1
    ).astype(jnp.bfloat16)
    first_full = lax.all_gather(first_pack, everyone, axis=0, tiled=True)
    second_full = lax.all_gather(second_pack, everyone, axis=0, tiled=True)
    full_in = first_full[:, :wide_in]
    small_full = first_full[:, wide_in:].astype(jnp.float32)
    column_set = small_full[:, : vectors.shape[1]]
    full_bias = small_full[:, vectors.shape[1] : vectors.shape[1] + ff_width // model_width].reshape(-1)
    full_out = second_full[:, :model_width]
    full_expand = second_full[:, model_width : model_width + ff_width]
    full_shrink = second_full[:, model_width + ff_width :].reshape(ff_width, model_width)

    frames_rows = inputs.reshape(row_count, model_width).astype(jnp.float32)
    normed_first, plain_first, inv_first = norm_parts(
        frames_rows, column_set[:, 0], column_set[:, 1]
    )
    hidden_first = normed_first.astype(jnp.bfloat16)
    hidden_partner = lax.ppermute(hidden_first, "frame", swap)
    bias_in = jnp.concatenate(
        [column_set[:, 2], jnp.zeros((model_width,), jnp.float32), column_set[:, 3]]
    )
    projected = (
        jnp.dot(hidden_first, full_in, preferred_element_type=jnp.float32) + bias_in
    ).astype(jnp.bfloat16)
    partner_pairs = (
        jnp.dot(hidden_partner, full_in[:, model_width:], preferred_element_type=jnp.float32)
        + bias_in[model_width:]
    ).astype(jnp.bfloat16)
    queries = projected[:, :model_width].reshape(clip_count, frame_count, model_width)
    clip_pairs = jnp.concatenate([projected[:, model_width:], partner_pairs], axis=0).reshape(
        clip_count, 2 * frame_count, 2 * model_width
    )
    score_scale = 1.0 / math.sqrt(model_width // head_count)
    scaled_queries = (projected[:, :model_width] * score_scale).astype(jnp.bfloat16)
    pair_rows = clip_pairs.reshape(2 * row_count, 2 * model_width)
    mixed_low, log_totals = attention_pallas(scaled_queries, pair_rows)
    attended = jnp.dot(mixed_low, full_out, preferred_element_type=jnp.float32) + column_set[:, 4]
    residual = frames_rows + attended
    normed_second, plain_second, inv_second = norm_parts(
        residual, column_set[:, 5], column_set[:, 6]
    )
    hidden_second = normed_second.astype(jnp.bfloat16)
    preact = jnp.dot(hidden_second, full_expand, preferred_element_type=jnp.float32) + full_bias
    activated = gelu_exact(preact).astype(jnp.bfloat16)
    result = (
        residual
        + jnp.dot(activated, full_shrink, preferred_element_type=jnp.float32)
        + column_set[:, 7]
    )
    output = result.astype(jnp.bfloat16).reshape(inputs.shape)

    grad_result = cotangent.reshape(row_count, model_width)
    grad_shrink_term = jnp.dot(activated.T, grad_result, preferred_element_type=jnp.float32)
    grad_down_bias = jnp.sum(grad_result.astype(jnp.float32), axis=0)
    grad_activated = jnp.dot(grad_result, full_shrink.T, preferred_element_type=jnp.float32)
    grad_preact = (grad_activated * gelu_slope(preact)).astype(jnp.bfloat16)
    grad_expand_term = jnp.dot(hidden_second.T, grad_preact, preferred_element_type=jnp.float32)
    grad_bias_term = jnp.sum(grad_preact.astype(jnp.float32), axis=0)
    grad_hidden_second = jnp.dot(grad_preact, full_expand.T, preferred_element_type=jnp.float32)
    norm_term_second, gain_second, shift_second = norm_backward(
        grad_hidden_second, plain_second, inv_second, column_set[:, 5]
    )
    grad_residual = grad_result.astype(jnp.float32) + norm_term_second
    grad_attended = grad_residual.astype(jnp.bfloat16)
    grad_out_term = jnp.dot(mixed_low.T, grad_attended, preferred_element_type=jnp.float32)
    grad_out_bias = jnp.sum(grad_attended.astype(jnp.float32), axis=0)
    owned_late = lax.psum_scatter(
        jnp.concatenate(
            [grad_shrink_term.reshape(model_width, -1), grad_expand_term, grad_out_term], axis=1
        ),
        everyone,
        scatter_dimension=0,
        tiled=True,
    )
    grad_mixed = jnp.dot(grad_attended, full_out.T, preferred_element_type=jnp.float32).astype(
        jnp.bfloat16
    )
    grad_query, grad_keys, grad_values = attention_pallas(
        scaled_queries, pair_rows, grad_mixed, log_totals
    )
    grad_pairs_terms = jnp.concatenate([grad_keys, grad_values], axis=1)
    partner_terms = grad_pairs_terms[row_count:].astype(jnp.bfloat16)
    returned_terms = lax.ppermute(partner_terms, "frame", swap)
    grad_pairs = grad_pairs_terms[:row_count] + returned_terms.astype(jnp.float32)
    grad_projected = jnp.concatenate(
        [(grad_query * score_scale).astype(jnp.bfloat16), grad_pairs.astype(jnp.bfloat16)], axis=1
    )
    grad_in_term = jnp.dot(hidden_first.T, grad_projected, preferred_element_type=jnp.float32)
    projected_sums = jnp.sum(grad_projected.astype(jnp.float32), axis=0)
    grad_query_bias = projected_sums[:model_width]
    grad_value_bias = projected_sums[2 * model_width :]
    grad_hidden_first = jnp.dot(grad_projected, full_in.T, preferred_element_type=jnp.float32)
    norm_term_first, gain_first, shift_first = norm_backward(
        grad_hidden_first, plain_first, inv_first, column_set[:, 0]
    )
    grad_inputs = (grad_residual + norm_term_first).astype(jnp.bfloat16).reshape(inputs.shape)
    grad_columns = jnp.stack(
        [
            gain_first,
            shift_first,
            grad_query_bias,
            grad_value_bias,
            grad_out_bias,
            gain_second,
            shift_second,
            grad_down_bias,
        ],
        axis=1,
    )
    small_grads = jnp.concatenate(
        [
            grad_columns,
            grad_bias_term.reshape(model_width, -1),
            jnp.zeros((model_width, 256 - 12), jnp.float32),
        ],
        axis=1,
    )
    first_terms, owned_late = lax.optimization_barrier(
        (jnp.concatenate([grad_in_term, small_grads], axis=1), owned_late)
    )
    owned_first = lax.psum_scatter(first_terms, everyone, scatter_dimension=0, tiled=True)
    owned_in = owned_first[:, :wide_in]
    owned_vectors = owned_first[:, wide_in : wide_in + vectors.shape[1]]
    owned_bias = owned_first[:, wide_in + vectors.shape[1] : wide_in + 12].reshape(-1)
    owned_shrink = owned_late[:, :ff_width].reshape(shrink_weight.shape)
    owned_expand = owned_late[:, ff_width : 2 * ff_width]
    owned_out = owned_late[:, 2 * ff_width :]
    new_in, mom_in = adam_step(project_in, moments_in, owned_in)
    new_out, mom_out = adam_step(project_out, moments_out, owned_out)
    new_expand, mom_expand = adam_step(expand_weight, moments_expand, owned_expand)
    new_shrink, mom_shrink = adam_step(shrink_weight, moments_shrink, owned_shrink)
    new_bias, mom_bias = adam_step(expand_bias, moments_bias, owned_bias)
    new_vectors, mom_vectors = adam_step(vectors, moments_vectors, owned_vectors)
    return (
        output,
        grad_inputs,
        owned_in,
        owned_out,
        owned_expand,
        owned_shrink,
        owned_bias,
        owned_vectors,
        new_in,
        new_out,
        new_expand,
        new_shrink,
        new_bias,
        new_vectors,
        mom_in,
        mom_out,
        mom_expand,
        mom_shrink,
        mom_bias,
        mom_vectors,
    )


def solution(mesh):
    in_specs = (
        P("clip", "frame", None),
        P("clip", "frame", None),
        P(("clip", "frame"), None),
        P(("clip", "frame"), None),
        P(("clip", "frame"), None),
        P(("clip", "frame"), None),
        P(("clip", "frame")),
        P(("clip", "frame"), None),
        P(None, ("clip", "frame"), None),
        P(None, ("clip", "frame"), None),
        P(None, ("clip", "frame"), None),
        P(None, ("clip", "frame"), None),
        P(None, ("clip", "frame")),
        P(None, ("clip", "frame"), None),
    )
    out_specs = (
        P("clip", "frame", None),
        P("clip", "frame", None),
        P(("clip", "frame"), None),
        P(("clip", "frame"), None),
        P(("clip", "frame"), None),
        P(("clip", "frame"), None),
        P(("clip", "frame")),
        P(("clip", "frame"), None),
        P(("clip", "frame"), None),
        P(("clip", "frame"), None),
        P(("clip", "frame"), None),
        P(("clip", "frame"), None),
        P(("clip", "frame")),
        P(("clip", "frame"), None),
        P(None, ("clip", "frame"), None),
        P(None, ("clip", "frame"), None),
        P(None, ("clip", "frame"), None),
        P(None, ("clip", "frame"), None),
        P(None, ("clip", "frame")),
        P(None, ("clip", "frame"), None),
    )
    return jax.shard_map(body, mesh=mesh, in_specs=in_specs, out_specs=out_specs, check_vma=False)
```

```python
import math

import jax
import jax.numpy as jnp
from jax import lax
from jax.experimental import pallas as pl
from jax.experimental.pallas import tpu as pltpu
from jax.sharding import PartitionSpec as P

HEADS = 12
ADAM_STEP = 4


epsilon_norm = 1e-05
beta_first = 0.9
beta_second = 0.99
learn_rate = 0.03
decay_rate = 0.01
epsilon_adam = 1e-08
root_half = 0.7071067811865476
inv_root_two_pi = 0.3989422804014327


def norm_parts(inputs, norm_gain, norm_shift):
    average = jnp.mean(inputs, axis=-1, keepdims=True)
    centered = inputs - average
    spread = jnp.mean(centered * centered, axis=-1, keepdims=True)
    inv_std = lax.rsqrt(spread + epsilon_norm)
    normed = centered * inv_std
    return (normed * norm_gain + norm_shift, normed, inv_std)


def norm_backward(grad_normed, normed, inv_std, norm_gain):
    grad_gain = jnp.sum(grad_normed * normed, axis=0)
    grad_shift = jnp.sum(grad_normed, axis=0)
    scaled = grad_normed * norm_gain
    grad_input = inv_std * (
        scaled
        - jnp.mean(scaled, axis=-1, keepdims=True)
        - normed * jnp.mean(scaled * normed, axis=-1, keepdims=True)
    )
    return (grad_input, grad_gain, grad_shift)


def gelu_exact(inputs):
    return 0.5 * inputs * (1.0 + jax.scipy.special.erf(inputs * root_half))


def gelu_slope(inputs):
    return (
        0.5 * (1.0 + jax.scipy.special.erf(inputs * root_half))
        + inputs * jnp.exp(-0.5 * inputs * inputs) * inv_root_two_pi
    )


QUERY_CHUNK = 256
MASKED = -1e30


def attention_forward_kernel(q_ref, k_ref, v_ref, kbias_ref, o_ref, l_ref):
    head_size = q_ref.shape[1] // 2
    rows = q_ref.shape[0]
    kbias = kbias_ref[...]
    lane = lax.broadcasted_iota(jnp.int32, (QUERY_CHUNK, 2 * head_size), 1)
    for chunk in range(rows // QUERY_CHUNK):
        span = pl.ds(chunk * QUERY_CHUNK, QUERY_CHUNK)
        mixed_parts = []
        totals = []
        for half in range(2):
            cols = pl.ds(half * head_size, head_size)
            query = q_ref[span, cols]
            key = k_ref[:, cols]
            value = v_ref[:, cols]
            scores = (
                lax.dot_general(
                    query, key, (((1,), (1,)), ((), ())), preferred_element_type=jnp.float32
                )
                + kbias
            )
            highest = jnp.max(scores, axis=1, keepdims=True)
            exponent = jnp.exp(scores - highest)
            denominator = jnp.sum(exponent, axis=1, keepdims=True)
            weights = (exponent * (1.0 / denominator)).astype(jnp.bfloat16)
            mixed_parts.append(jnp.dot(weights, value, preferred_element_type=jnp.float32))
            totals.append(highest + jnp.log(denominator))
        o_ref[span, :] = jnp.concatenate(mixed_parts, axis=1).astype(o_ref.dtype)
        l_ref[span, :] = jnp.where(lane < head_size, totals[0], totals[1])


def attention_backward_kernel(
    q_ref, k_ref, v_ref, do_ref, l_ref, kbias_ref, dq_ref, dk_ref, dv_ref
):
    head_size = q_ref.shape[1] // 2
    rows = q_ref.shape[0]
    kbias = kbias_ref[...]
    for half in range(2):
        cols = pl.ds(half * head_size, head_size)
        key = k_ref[:, cols]
        value = v_ref[:, cols]
        grad_key = None
        grad_value = None
        for chunk in range(rows // QUERY_CHUNK):
            span = pl.ds(chunk * QUERY_CHUNK, QUERY_CHUNK)
            query = q_ref[span, cols]
            grad_out = do_ref[span, cols]
            total = l_ref[span, pl.ds(half * head_size, 1)]
            scores = (
                lax.dot_general(
                    query, key, (((1,), (1,)), ((), ())), preferred_element_type=jnp.float32
                )
                + kbias
            )
            weights = jnp.exp(scores - total)
            grad_weights = lax.dot_general(
                grad_out, value, (((1,), (1,)), ((), ())), preferred_element_type=jnp.float32
            )
            delta = jnp.sum(weights * grad_weights, axis=1, keepdims=True)
            grad_scores = (weights * (grad_weights - delta)).astype(jnp.bfloat16)
            dq_ref[span, cols] = jnp.dot(
                grad_scores, key, preferred_element_type=jnp.float32
            ).astype(dq_ref.dtype)
            key_part = lax.dot_general(
                grad_scores, query, (((0,), (0,)), ((), ())), preferred_element_type=jnp.float32
            )
            value_part = lax.dot_general(
                weights.astype(jnp.bfloat16),
                grad_out,
                (((0,), (0,)), ((), ())),
                preferred_element_type=jnp.float32,
            )
            grad_key = key_part if grad_key is None else grad_key + key_part
            grad_value = value_part if grad_value is None else grad_value + value_part
        dk_ref[:, cols] = grad_key
        dv_ref[:, cols] = grad_value


def pad_rows(values, rows):
    return jnp.pad(values, ((0, rows - values.shape[0]), (0, 0)))


def attention_pallas(queries, pairs, grad_out=None, totals=None):
    query_rows, model_width = queries.shape
    key_rows = pairs.shape[0]
    padded_q = -(-query_rows // QUERY_CHUNK) * QUERY_CHUNK
    padded_k = -(-key_rows // 128) * 128
    pair_count = model_width // 128
    q_pad = pad_rows(queries, padded_q)
    kv_pad = pad_rows(pairs, padded_k)
    kbias = jnp.where(jnp.arange(padded_k) < key_rows, 0.0, MASKED).astype(jnp.float32)[None, :]
    q_spec = pl.BlockSpec((padded_q, 128), lambda j: (0, j))
    k_spec = pl.BlockSpec((padded_k, 128), lambda j: (0, j))
    v_spec = pl.BlockSpec((padded_k, 128), lambda j: (0, j + pair_count))
    b_spec = pl.BlockSpec((1, padded_k), lambda j: (0, 0))
    params = pltpu.CompilerParams(vmem_limit_bytes=48 * 1024 * 1024)
    if grad_out is None:
        mixed, log_totals = pl.pallas_call(
            attention_forward_kernel,
            grid=(pair_count,),
            in_specs=[q_spec, k_spec, v_spec, b_spec],
            out_specs=[q_spec, q_spec],
            out_shape=[
                jax.ShapeDtypeStruct((padded_q, model_width), jnp.bfloat16),
                jax.ShapeDtypeStruct((padded_q, model_width), jnp.float32),
            ],
            compiler_params=params,
        )(q_pad, kv_pad, kv_pad, kbias)
        return mixed[:query_rows], log_totals
    do_pad = pad_rows(grad_out, padded_q)
    dq, dk, dv = pl.pallas_call(
        attention_backward_kernel,
        grid=(pair_count,),
        in_specs=[q_spec, k_spec, v_spec, q_spec, q_spec, b_spec],
        out_specs=[q_spec, k_spec, k_spec],
        out_shape=[
            jax.ShapeDtypeStruct((padded_q, model_width), jnp.float32),
            jax.ShapeDtypeStruct((padded_k, model_width), jnp.float32),
            jax.ShapeDtypeStruct((padded_k, model_width), jnp.float32),
        ],
        compiler_params=params,
    )(q_pad, kv_pad, kv_pad, do_pad, totals, kbias)
    return dq[:query_rows], dk[:key_rows], dv[:key_rows]


def attend_forward(queries, keys_values, head_count):
    model_width = queries.shape[2]
    head_size = model_width // head_count
    score_scale = 1.0 / math.sqrt(head_size)

    def one_head(head_index):
        offset = head_index * head_size
        query_block = lax.dynamic_slice_in_dim(queries, offset, head_size, 2)
        key_block = lax.dynamic_slice_in_dim(keys_values, offset, head_size, 2)
        value_block = lax.dynamic_slice_in_dim(keys_values, model_width + offset, head_size, 2)
        scores = (
            jnp.einsum("cqd,ckd->cqk", query_block, key_block, preferred_element_type=jnp.float32)
            * score_scale
        )
        highest = jnp.max(scores, axis=-1, keepdims=True)
        exponent = jnp.exp(scores - highest)
        denominator = jnp.sum(exponent, axis=-1, keepdims=True)
        weights_soft = (exponent / denominator).astype(jnp.bfloat16)
        mixed = jnp.einsum(
            "cqk,ckd->cqd", weights_soft, value_block, preferred_element_type=jnp.float32
        )
        return (mixed, (highest + jnp.log(denominator))[..., 0])

    mixed, log_totals = lax.map(one_head, jnp.arange(head_count))
    clip_count, frame_count = (queries.shape[0], queries.shape[1])
    mixed = jnp.transpose(mixed, (1, 2, 0, 3)).reshape(clip_count, frame_count, model_width)
    return (mixed, log_totals)


def attend_backward(queries, keys_values, grad_mixed, log_totals, head_count):
    model_width = queries.shape[2]
    head_size = model_width // head_count
    score_scale = 1.0 / math.sqrt(head_size)

    def one_head_back(head_index):
        offset = head_index * head_size
        query_block = lax.dynamic_slice_in_dim(queries, offset, head_size, 2)
        key_block = lax.dynamic_slice_in_dim(keys_values, offset, head_size, 2)
        value_block = lax.dynamic_slice_in_dim(keys_values, model_width + offset, head_size, 2)
        grad_block = lax.dynamic_slice_in_dim(grad_mixed, offset, head_size, 2)
        totals = lax.dynamic_index_in_dim(log_totals, head_index, 0, keepdims=False)
        scores = (
            jnp.einsum("cqd,ckd->cqk", query_block, key_block, preferred_element_type=jnp.float32)
            * score_scale
        )
        weights_soft = jnp.exp(scores - totals[..., None])
        grad_weights = jnp.einsum(
            "cqd,ckd->cqk", grad_block, value_block, preferred_element_type=jnp.float32
        )
        delta = jnp.sum(weights_soft * grad_weights, axis=-1, keepdims=True)
        grad_scores = (weights_soft * (grad_weights - delta)).astype(jnp.bfloat16)
        grad_query = (
            jnp.einsum("cqk,ckd->cqd", grad_scores, key_block, preferred_element_type=jnp.float32)
            * score_scale
        )
        grad_key = (
            jnp.einsum("cqk,cqd->ckd", grad_scores, query_block, preferred_element_type=jnp.float32)
            * score_scale
        )
        grad_value = jnp.einsum(
            "cqk,cqd->ckd",
            weights_soft.astype(jnp.bfloat16),
            grad_block,
            preferred_element_type=jnp.float32,
        )
        return (grad_query, delta[..., 0], grad_key, grad_value)

    pieces = lax.map(one_head_back, jnp.arange(head_count))
    clip_count, frame_count = (queries.shape[0], queries.shape[1])
    clip_frames = keys_values.shape[1]
    grad_query = jnp.transpose(pieces[0], (1, 2, 0, 3)).reshape(
        clip_count, frame_count, model_width
    )
    grad_key = jnp.transpose(pieces[2], (1, 2, 0, 3)).reshape(clip_count, clip_frames, model_width)
    grad_value = jnp.transpose(pieces[3], (1, 2, 0, 3)).reshape(
        clip_count, clip_frames, model_width
    )
    return (grad_query, pieces[1], jnp.concatenate([grad_key, grad_value], axis=2))


def adam_step(weight, moments, gradient):
    first = beta_first * moments[0] + (1.0 - beta_first) * gradient
    second = beta_second * moments[1] + (1.0 - beta_second) * gradient * gradient
    first_hat = first / (1.0 - beta_first**ADAM_STEP)
    second_hat = second / (1.0 - beta_second**ADAM_STEP)
    change = -learn_rate * (first_hat / (jnp.sqrt(second_hat) + epsilon_adam) + decay_rate * weight)
    return (change, jnp.stack([first, second]))


def body(
    inputs,
    cotangent,
    project_in,
    project_out,
    expand_weight,
    shrink_weight,
    expand_bias,
    vectors,
    moments_in,
    moments_out,
    moments_expand,
    moments_shrink,
    moments_bias,
    moments_vectors,
):
    clip_count, frame_count, model_width = inputs.shape
    row_count = clip_count * frame_count
    head_count = HEADS
    shard_rows = project_in.shape[0]
    wide_in = project_in.shape[1]
    ff_width = expand_weight.shape[1]
    swap = [(0, 1), (1, 0)]
    everyone = ("clip", "frame")

    small = jnp.concatenate(
        [
            vectors,
            expand_bias.reshape(shard_rows, -1),
            jnp.zeros((shard_rows, 128 - vectors.shape[1] - expand_bias.shape[0] // shard_rows), jnp.float32),
        ],
        axis=1,
    )
    first_pack = jnp.concatenate([project_in, small], axis=1).astype(jnp.bfloat16)
    second_pack = jnp.concatenate(
        [project_out, expand_weight, shrink_weight.reshape(shard_rows, -1)], axis=1
    ).astype(jnp.bfloat16)
    first_full = lax.all_gather(first_pack, everyone, axis=0, tiled=True)
    second_full = lax.all_gather(second_pack, everyone, axis=0, tiled=True)
    full_in = first_full[:, :wide_in]
    small_full = first_full[:, wide_in:].astype(jnp.float32)
    column_set = small_full[:, : vectors.shape[1]]
    full_bias = small_full[:, vectors.shape[1] : vectors.shape[1] + ff_width // model_width].reshape(-1)
    full_out = second_full[:, :model_width]
    full_expand = second_full[:, model_width : model_width + ff_width]
    full_shrink = second_full[:, model_width + ff_width :].reshape(ff_width, model_width)

    frames_rows = inputs.reshape(row_count, model_width).astype(jnp.float32)
    normed_first, plain_first, inv_first = norm_parts(
        frames_rows, column_set[:, 0], column_set[:, 1]
    )
    hidden_first = normed_first.astype(jnp.bfloat16)
    hidden_partner = lax.ppermute(hidden_first, "frame", swap)
    bias_in = jnp.concatenate(
        [column_set[:, 2], jnp.zeros((model_width,), jnp.float32), column_set[:, 3]]
    )
    projected = (
        jnp.dot(hidden_first, full_in, preferred_element_type=jnp.float32) + bias_in
    ).astype(jnp.bfloat16)
    partner_pairs = (
        jnp.dot(hidden_partner, full_in[:, model_width:], preferred_element_type=jnp.float32)
        + bias_in[model_width:]
    ).astype(jnp.bfloat16)
    queries = projected[:, :model_width].reshape(clip_count, frame_count, model_width)
    clip_pairs = jnp.concatenate([projected[:, model_width:], partner_pairs], axis=0).reshape(
        clip_count, 2 * frame_count, 2 * model_width
    )
    score_scale = 1.0 / math.sqrt(model_width // head_count)
    scaled_queries = (projected[:, :model_width] * score_scale).astype(jnp.bfloat16)
    pair_rows = clip_pairs.reshape(2 * row_count, 2 * model_width)
    mixed_low, log_totals = attention_pallas(scaled_queries, pair_rows)
    attended = jnp.dot(mixed_low, full_out, preferred_element_type=jnp.float32) + column_set[:, 4]
    residual = frames_rows + attended
    normed_second, plain_second, inv_second = norm_parts(
        residual, column_set[:, 5], column_set[:, 6]
    )
    hidden_second = normed_second.astype(jnp.bfloat16)
    preact = jnp.dot(hidden_second, full_expand, preferred_element_type=jnp.float32) + full_bias
    activated = gelu_exact(preact).astype(jnp.bfloat16)
    result = (
        residual
        + jnp.dot(activated, full_shrink, preferred_element_type=jnp.float32)
        + column_set[:, 7]
    )
    output = result.astype(jnp.bfloat16).reshape(inputs.shape)

    grad_result = cotangent.reshape(row_count, model_width)
    grad_shrink_term = jnp.dot(activated.T, grad_result, preferred_element_type=jnp.float32)
    grad_down_bias = jnp.sum(grad_result.astype(jnp.float32), axis=0)
    grad_activated = jnp.dot(grad_result, full_shrink.T, preferred_element_type=jnp.float32)
    grad_preact = (grad_activated * gelu_slope(preact)).astype(jnp.bfloat16)
    grad_expand_term = jnp.dot(hidden_second.T, grad_preact, preferred_element_type=jnp.float32)
    grad_bias_term = jnp.sum(grad_preact.astype(jnp.float32), axis=0)
    grad_hidden_second = jnp.dot(grad_preact, full_expand.T, preferred_element_type=jnp.float32)
    norm_term_second, gain_second, shift_second = norm_backward(
        grad_hidden_second, plain_second, inv_second, column_set[:, 5]
    )
    grad_residual = grad_result.astype(jnp.float32) + norm_term_second
    grad_attended = grad_residual.astype(jnp.bfloat16)
    grad_out_term = jnp.dot(mixed_low.T, grad_attended, preferred_element_type=jnp.float32)
    grad_out_bias = jnp.sum(grad_attended.astype(jnp.float32), axis=0)
    owned_late = lax.psum_scatter(
        jnp.concatenate(
            [grad_shrink_term.reshape(model_width, -1), grad_expand_term, grad_out_term], axis=1
        ).astype(jnp.bfloat16),
        everyone,
        scatter_dimension=0,
        tiled=True,
    ).astype(jnp.float32)
    grad_mixed = jnp.dot(grad_attended, full_out.T, preferred_element_type=jnp.float32).astype(
        jnp.bfloat16
    )
    grad_query, grad_keys, grad_values = attention_pallas(
        scaled_queries, pair_rows, grad_mixed, log_totals
    )
    grad_pairs_terms = jnp.concatenate([grad_keys, grad_values], axis=1)
    partner_terms = grad_pairs_terms[row_count:].astype(jnp.bfloat16)
    returned_terms = lax.ppermute(partner_terms, "frame", swap)
    grad_pairs = grad_pairs_terms[:row_count] + returned_terms.astype(jnp.float32)
    grad_projected = jnp.concatenate(
        [(grad_query * score_scale).astype(jnp.bfloat16), grad_pairs.astype(jnp.bfloat16)], axis=1
    )
    grad_in_term = jnp.dot(hidden_first.T, grad_projected, preferred_element_type=jnp.float32)
    projected_sums = jnp.sum(grad_projected.astype(jnp.float32), axis=0)
    grad_query_bias = projected_sums[:model_width]
    grad_value_bias = projected_sums[2 * model_width :]
    grad_hidden_first = jnp.dot(grad_projected, full_in.T, preferred_element_type=jnp.float32)
    norm_term_first, gain_first, shift_first = norm_backward(
        grad_hidden_first, plain_first, inv_first, column_set[:, 0]
    )
    grad_inputs = (grad_residual + norm_term_first).astype(jnp.bfloat16).reshape(inputs.shape)
    grad_columns = jnp.stack(
        [
            gain_first,
            shift_first,
            grad_query_bias,
            grad_value_bias,
            grad_out_bias,
            gain_second,
            shift_second,
            grad_down_bias,
        ],
        axis=1,
    )
    small_grads = jnp.concatenate(
        [
            grad_columns,
            grad_bias_term.reshape(model_width, -1),
            jnp.zeros((model_width, 256 - 12), jnp.float32),
        ],
        axis=1,
    )
    first_terms, owned_late = lax.optimization_barrier(
        (jnp.concatenate([grad_in_term, small_grads], axis=1), owned_late)
    )
    owned_first = lax.psum_scatter(
        first_terms.astype(jnp.bfloat16), everyone, scatter_dimension=0, tiled=True
    ).astype(jnp.float32)
    owned_in = owned_first[:, :wide_in]
    owned_vectors = owned_first[:, wide_in : wide_in + vectors.shape[1]]
    owned_bias = owned_first[:, wide_in + vectors.shape[1] : wide_in + 12].reshape(-1)
    owned_shrink = owned_late[:, :ff_width].reshape(shrink_weight.shape)
    owned_expand = owned_late[:, ff_width : 2 * ff_width]
    owned_out = owned_late[:, 2 * ff_width :]
    new_in, mom_in = adam_step(project_in, moments_in, owned_in)
    new_out, mom_out = adam_step(project_out, moments_out, owned_out)
    new_expand, mom_expand = adam_step(expand_weight, moments_expand, owned_expand)
    new_shrink, mom_shrink = adam_step(shrink_weight, moments_shrink, owned_shrink)
    new_bias, mom_bias = adam_step(expand_bias, moments_bias, owned_bias)
    new_vectors, mom_vectors = adam_step(vectors, moments_vectors, owned_vectors)
    return (
        output,
        grad_inputs,
        owned_in,
        owned_out,
        owned_expand,
        owned_shrink,
        owned_bias,
        owned_vectors,
        new_in,
        new_out,
        new_expand,
        new_shrink,
        new_bias,
        new_vectors,
        mom_in,
        mom_out,
        mom_expand,
        mom_shrink,
        mom_bias,
        mom_vectors,
    )


def solution(mesh):
    in_specs = (
        P("clip", "frame", None),
        P("clip", "frame", None),
        P(("clip", "frame"), None),
        P(("clip", "frame"), None),
        P(("clip", "frame"), None),
        P(("clip", "frame"), None),
        P(("clip", "frame")),
        P(("clip", "frame"), None),
        P(None, ("clip", "frame"), None),
        P(None, ("clip", "frame"), None),
        P(None, ("clip", "frame"), None),
        P(None, ("clip", "frame"), None),
        P(None, ("clip", "frame")),
        P(None, ("clip", "frame"), None),
    )
    out_specs = (
        P("clip", "frame", None),
        P("clip", "frame", None),
        P(("clip", "frame"), None),
        P(("clip", "frame"), None),
        P(("clip", "frame"), None),
        P(("clip", "frame"), None),
        P(("clip", "frame")),
        P(("clip", "frame"), None),
        P(("clip", "frame"), None),
        P(("clip", "frame"), None),
        P(("clip", "frame"), None),
        P(("clip", "frame"), None),
        P(("clip", "frame")),
        P(("clip", "frame"), None),
        P(None, ("clip", "frame"), None),
        P(None, ("clip", "frame"), None),
        P(None, ("clip", "frame"), None),
        P(None, ("clip", "frame"), None),
        P(None, ("clip", "frame")),
        P(None, ("clip", "frame"), None),
    )
    return jax.shard_map(body, mesh=mesh, in_specs=in_specs, out_specs=out_specs, check_vma=False)
```

```python
import math

import jax
import jax.numpy as jnp
from jax import lax
from jax.experimental import pallas as pl
from jax.experimental.pallas import tpu as pltpu
from jax.sharding import PartitionSpec as P

HEADS = 12
ADAM_STEP = 4


epsilon_norm = 1e-05
beta_first = 0.9
beta_second = 0.99
learn_rate = 0.03
decay_rate = 0.01
epsilon_adam = 1e-08
root_half = 0.7071067811865476
inv_root_two_pi = 0.3989422804014327


def norm_parts(inputs, norm_gain, norm_shift):
    average = jnp.mean(inputs, axis=-1, keepdims=True)
    centered = inputs - average
    spread = jnp.mean(centered * centered, axis=-1, keepdims=True)
    inv_std = lax.rsqrt(spread + epsilon_norm)
    normed = centered * inv_std
    return (normed * norm_gain + norm_shift, normed, inv_std)


def norm_backward(grad_normed, normed, inv_std, norm_gain):
    grad_gain = jnp.sum(grad_normed * normed, axis=0)
    grad_shift = jnp.sum(grad_normed, axis=0)
    scaled = grad_normed * norm_gain
    grad_input = inv_std * (
        scaled
        - jnp.mean(scaled, axis=-1, keepdims=True)
        - normed * jnp.mean(scaled * normed, axis=-1, keepdims=True)
    )
    return (grad_input, grad_gain, grad_shift)


def gelu_exact(inputs):
    return 0.5 * inputs * (1.0 + jax.scipy.special.erf(inputs * root_half))


def gelu_slope(inputs):
    return (
        0.5 * (1.0 + jax.scipy.special.erf(inputs * root_half))
        + inputs * jnp.exp(-0.5 * inputs * inputs) * inv_root_two_pi
    )


QUERY_CHUNK = 256
MASKED = -1e30


def attention_forward_kernel(q_ref, k_ref, v_ref, kbias_ref, o_ref, l_ref):
    head_size = q_ref.shape[1] // 2
    rows = q_ref.shape[0]
    kbias = kbias_ref[...]
    lane = lax.broadcasted_iota(jnp.int32, (QUERY_CHUNK, 2 * head_size), 1)
    for chunk in range(rows // QUERY_CHUNK):
        span = pl.ds(chunk * QUERY_CHUNK, QUERY_CHUNK)
        mixed_parts = []
        totals = []
        for half in range(2):
            cols = pl.ds(half * head_size, head_size)
            query = q_ref[span, cols]
            key = k_ref[:, cols]
            value = v_ref[:, cols]
            scores = (
                lax.dot_general(
                    query, key, (((1,), (1,)), ((), ())), preferred_element_type=jnp.float32
                )
                + kbias
            )
            highest = jnp.max(scores, axis=1, keepdims=True)
            exponent = jnp.exp(scores - highest)
            denominator = jnp.sum(exponent, axis=1, keepdims=True)
            weights = (exponent * (1.0 / denominator)).astype(jnp.bfloat16)
            mixed_parts.append(jnp.dot(weights, value, preferred_element_type=jnp.float32))
            totals.append(highest + jnp.log(denominator))
        o_ref[span, :] = jnp.concatenate(mixed_parts, axis=1).astype(o_ref.dtype)
        l_ref[span, :] = jnp.where(lane < head_size, totals[0], totals[1])


def attention_backward_kernel(
    q_ref, k_ref, v_ref, do_ref, l_ref, kbias_ref, dq_ref, dk_ref, dv_ref
):
    head_size = q_ref.shape[1] // 2
    rows = q_ref.shape[0]
    kbias = kbias_ref[...]
    for half in range(2):
        cols = pl.ds(half * head_size, head_size)
        key = k_ref[:, cols]
        value = v_ref[:, cols]
        grad_key = None
        grad_value = None
        for chunk in range(rows // QUERY_CHUNK):
            span = pl.ds(chunk * QUERY_CHUNK, QUERY_CHUNK)
            query = q_ref[span, cols]
            grad_out = do_ref[span, cols]
            total = l_ref[span, pl.ds(half * head_size, 1)]
            scores = (
                lax.dot_general(
                    query, key, (((1,), (1,)), ((), ())), preferred_element_type=jnp.float32
                )
                + kbias
            )
            weights = jnp.exp(scores - total)
            grad_weights = lax.dot_general(
                grad_out, value, (((1,), (1,)), ((), ())), preferred_element_type=jnp.float32
            )
            delta = jnp.sum(weights * grad_weights, axis=1, keepdims=True)
            grad_scores = (weights * (grad_weights - delta)).astype(jnp.bfloat16)
            dq_ref[span, cols] = jnp.dot(
                grad_scores, key, preferred_element_type=jnp.float32
            ).astype(dq_ref.dtype)
            key_part = lax.dot_general(
                grad_scores, query, (((0,), (0,)), ((), ())), preferred_element_type=jnp.float32
            )
            value_part = lax.dot_general(
                weights.astype(jnp.bfloat16),
                grad_out,
                (((0,), (0,)), ((), ())),
                preferred_element_type=jnp.float32,
            )
            grad_key = key_part if grad_key is None else grad_key + key_part
            grad_value = value_part if grad_value is None else grad_value + value_part
        dk_ref[:, cols] = grad_key
        dv_ref[:, cols] = grad_value


def pad_rows(values, rows):
    return jnp.pad(values, ((0, rows - values.shape[0]), (0, 0)))


def attention_pallas(queries, pairs, grad_out=None, totals=None, first_pair=0, pair_span=None):
    query_rows, model_width = queries.shape
    key_rows = pairs.shape[0]
    padded_q = -(-query_rows // QUERY_CHUNK) * QUERY_CHUNK
    padded_k = -(-key_rows // 128) * 128
    pair_count = model_width // 128
    q_pad = pad_rows(queries, padded_q)
    kv_pad = pad_rows(pairs, padded_k)
    kbias = jnp.where(jnp.arange(padded_k) < key_rows, 0.0, MASKED).astype(jnp.float32)[None, :]
    q_spec = pl.BlockSpec((padded_q, 128), lambda j: (0, j))
    k_spec = pl.BlockSpec((padded_k, 128), lambda j: (0, j))
    v_spec = pl.BlockSpec((padded_k, 128), lambda j: (0, j + pair_count))
    b_spec = pl.BlockSpec((1, padded_k), lambda j: (0, 0))
    params = pltpu.CompilerParams(vmem_limit_bytes=48 * 1024 * 1024)
    if grad_out is None:
        mixed, log_totals = pl.pallas_call(
            attention_forward_kernel,
            grid=(pair_count,),
            in_specs=[q_spec, k_spec, v_spec, b_spec],
            out_specs=[q_spec, q_spec],
            out_shape=[
                jax.ShapeDtypeStruct((padded_q, model_width), jnp.bfloat16),
                jax.ShapeDtypeStruct((padded_q, model_width), jnp.float32),
            ],
            compiler_params=params,
        )(q_pad, kv_pad, kv_pad, kbias)
        return mixed[:query_rows], log_totals
    do_pad = pad_rows(grad_out, padded_q)
    span = pair_count if pair_span is None else pair_span
    qi_spec = pl.BlockSpec((padded_q, 128), lambda j: (0, j + first_pair))
    ki_spec = pl.BlockSpec((padded_k, 128), lambda j: (0, j + first_pair))
    vi_spec = pl.BlockSpec((padded_k, 128), lambda j: (0, j + first_pair + pair_count))
    qo_spec = pl.BlockSpec((padded_q, 128), lambda j: (0, j))
    ko_spec = pl.BlockSpec((padded_k, 128), lambda j: (0, j))
    dq, dk, dv = pl.pallas_call(
        attention_backward_kernel,
        grid=(span,),
        in_specs=[qi_spec, ki_spec, vi_spec, qi_spec, qi_spec, b_spec],
        out_specs=[qo_spec, ko_spec, ko_spec],
        out_shape=[
            jax.ShapeDtypeStruct((padded_q, 128 * span), jnp.float32),
            jax.ShapeDtypeStruct((padded_k, 128 * span), jnp.float32),
            jax.ShapeDtypeStruct((padded_k, 128 * span), jnp.float32),
        ],
        compiler_params=params,
    )(q_pad, kv_pad, kv_pad, do_pad, totals, kbias)
    return dq[:query_rows], dk[:key_rows], dv[:key_rows]


def attend_forward(queries, keys_values, head_count):
    model_width = queries.shape[2]
    head_size = model_width // head_count
    score_scale = 1.0 / math.sqrt(head_size)

    def one_head(head_index):
        offset = head_index * head_size
        query_block = lax.dynamic_slice_in_dim(queries, offset, head_size, 2)
        key_block = lax.dynamic_slice_in_dim(keys_values, offset, head_size, 2)
        value_block = lax.dynamic_slice_in_dim(keys_values, model_width + offset, head_size, 2)
        scores = (
            jnp.einsum("cqd,ckd->cqk", query_block, key_block, preferred_element_type=jnp.float32)
            * score_scale
        )
        highest = jnp.max(scores, axis=-1, keepdims=True)
        exponent = jnp.exp(scores - highest)
        denominator = jnp.sum(exponent, axis=-1, keepdims=True)
        weights_soft = (exponent / denominator).astype(jnp.bfloat16)
        mixed = jnp.einsum(
            "cqk,ckd->cqd", weights_soft, value_block, preferred_element_type=jnp.float32
        )
        return (mixed, (highest + jnp.log(denominator))[..., 0])

    mixed, log_totals = lax.map(one_head, jnp.arange(head_count))
    clip_count, frame_count = (queries.shape[0], queries.shape[1])
    mixed = jnp.transpose(mixed, (1, 2, 0, 3)).reshape(clip_count, frame_count, model_width)
    return (mixed, log_totals)


def attend_backward(queries, keys_values, grad_mixed, log_totals, head_count):
    model_width = queries.shape[2]
    head_size = model_width // head_count
    score_scale = 1.0 / math.sqrt(head_size)

    def one_head_back(head_index):
        offset = head_index * head_size
        query_block = lax.dynamic_slice_in_dim(queries, offset, head_size, 2)
        key_block = lax.dynamic_slice_in_dim(keys_values, offset, head_size, 2)
        value_block = lax.dynamic_slice_in_dim(keys_values, model_width + offset, head_size, 2)
        grad_block = lax.dynamic_slice_in_dim(grad_mixed, offset, head_size, 2)
        totals = lax.dynamic_index_in_dim(log_totals, head_index, 0, keepdims=False)
        scores = (
            jnp.einsum("cqd,ckd->cqk", query_block, key_block, preferred_element_type=jnp.float32)
            * score_scale
        )
        weights_soft = jnp.exp(scores - totals[..., None])
        grad_weights = jnp.einsum(
            "cqd,ckd->cqk", grad_block, value_block, preferred_element_type=jnp.float32
        )
        delta = jnp.sum(weights_soft * grad_weights, axis=-1, keepdims=True)
        grad_scores = (weights_soft * (grad_weights - delta)).astype(jnp.bfloat16)
        grad_query = (
            jnp.einsum("cqk,ckd->cqd", grad_scores, key_block, preferred_element_type=jnp.float32)
            * score_scale
        )
        grad_key = (
            jnp.einsum("cqk,cqd->ckd", grad_scores, query_block, preferred_element_type=jnp.float32)
            * score_scale
        )
        grad_value = jnp.einsum(
            "cqk,cqd->ckd",
            weights_soft.astype(jnp.bfloat16),
            grad_block,
            preferred_element_type=jnp.float32,
        )
        return (grad_query, delta[..., 0], grad_key, grad_value)

    pieces = lax.map(one_head_back, jnp.arange(head_count))
    clip_count, frame_count = (queries.shape[0], queries.shape[1])
    clip_frames = keys_values.shape[1]
    grad_query = jnp.transpose(pieces[0], (1, 2, 0, 3)).reshape(
        clip_count, frame_count, model_width
    )
    grad_key = jnp.transpose(pieces[2], (1, 2, 0, 3)).reshape(clip_count, clip_frames, model_width)
    grad_value = jnp.transpose(pieces[3], (1, 2, 0, 3)).reshape(
        clip_count, clip_frames, model_width
    )
    return (grad_query, pieces[1], jnp.concatenate([grad_key, grad_value], axis=2))


def adam_step(weight, moments, gradient):
    first = beta_first * moments[0] + (1.0 - beta_first) * gradient
    second = beta_second * moments[1] + (1.0 - beta_second) * gradient * gradient
    first_hat = first / (1.0 - beta_first**ADAM_STEP)
    second_hat = second / (1.0 - beta_second**ADAM_STEP)
    change = -learn_rate * (first_hat / (jnp.sqrt(second_hat) + epsilon_adam) + decay_rate * weight)
    return (change, jnp.stack([first, second]))


def body(
    inputs,
    cotangent,
    project_in,
    project_out,
    expand_weight,
    shrink_weight,
    expand_bias,
    vectors,
    moments_in,
    moments_out,
    moments_expand,
    moments_shrink,
    moments_bias,
    moments_vectors,
):
    clip_count, frame_count, model_width = inputs.shape
    row_count = clip_count * frame_count
    head_count = HEADS
    shard_rows = project_in.shape[0]
    wide_in = project_in.shape[1]
    ff_width = expand_weight.shape[1]
    swap = [(0, 1), (1, 0)]
    everyone = ("clip", "frame")

    small = jnp.concatenate(
        [
            vectors,
            expand_bias.reshape(shard_rows, -1),
            jnp.zeros((shard_rows, 128 - vectors.shape[1] - expand_bias.shape[0] // shard_rows), jnp.float32),
        ],
        axis=1,
    )
    first_pack = jnp.concatenate([project_in, small], axis=1).astype(jnp.bfloat16)
    second_pack = jnp.concatenate(
        [project_out, expand_weight, shrink_weight.reshape(shard_rows, -1)], axis=1
    ).astype(jnp.bfloat16)
    first_full = lax.all_gather(first_pack, everyone, axis=0, tiled=True)
    second_full = lax.all_gather(second_pack, everyone, axis=0, tiled=True)
    full_in = first_full[:, :wide_in]
    small_full = first_full[:, wide_in:].astype(jnp.float32)
    column_set = small_full[:, : vectors.shape[1]]
    full_bias = small_full[:, vectors.shape[1] : vectors.shape[1] + ff_width // model_width].reshape(-1)
    full_out = second_full[:, :model_width]
    full_expand = second_full[:, model_width : model_width + ff_width]
    full_shrink = second_full[:, model_width + ff_width :].reshape(ff_width, model_width)

    frames_rows = inputs.reshape(row_count, model_width).astype(jnp.float32)
    normed_first, plain_first, inv_first = norm_parts(
        frames_rows, column_set[:, 0], column_set[:, 1]
    )
    hidden_first = normed_first.astype(jnp.bfloat16)
    partner_rows = lax.ppermute(inputs, "frame", swap).reshape(row_count, model_width)
    hidden_partner = norm_parts(
        partner_rows.astype(jnp.float32), column_set[:, 0], column_set[:, 1]
    )[0].astype(jnp.bfloat16)
    bias_in = jnp.concatenate(
        [column_set[:, 2], jnp.zeros((model_width,), jnp.float32), column_set[:, 3]]
    )
    projected = (
        jnp.dot(hidden_first, full_in, preferred_element_type=jnp.float32) + bias_in
    ).astype(jnp.bfloat16)
    partner_pairs = (
        jnp.dot(hidden_partner, full_in[:, model_width:], preferred_element_type=jnp.float32)
        + bias_in[model_width:]
    ).astype(jnp.bfloat16)
    queries = projected[:, :model_width].reshape(clip_count, frame_count, model_width)
    clip_pairs = jnp.concatenate([projected[:, model_width:], partner_pairs], axis=0).reshape(
        clip_count, 2 * frame_count, 2 * model_width
    )
    score_scale = 1.0 / math.sqrt(model_width // head_count)
    scaled_queries = (projected[:, :model_width] * score_scale).astype(jnp.bfloat16)
    pair_rows = clip_pairs.reshape(2 * row_count, 2 * model_width)
    mixed_low, log_totals = attention_pallas(scaled_queries, pair_rows)
    attended = jnp.dot(mixed_low, full_out, preferred_element_type=jnp.float32) + column_set[:, 4]
    residual = frames_rows + attended
    normed_second, plain_second, inv_second = norm_parts(
        residual, column_set[:, 5], column_set[:, 6]
    )
    hidden_second = normed_second.astype(jnp.bfloat16)
    preact = jnp.dot(hidden_second, full_expand, preferred_element_type=jnp.float32) + full_bias
    activated = gelu_exact(preact).astype(jnp.bfloat16)
    result = (
        residual
        + jnp.dot(activated, full_shrink, preferred_element_type=jnp.float32)
        + column_set[:, 7]
    )
    output = result.astype(jnp.bfloat16).reshape(inputs.shape)

    grad_result = cotangent.reshape(row_count, model_width)
    grad_shrink_term = jnp.dot(activated.T, grad_result, preferred_element_type=jnp.float32)
    grad_down_bias = jnp.sum(grad_result.astype(jnp.float32), axis=0)
    grad_activated = jnp.dot(grad_result, full_shrink.T, preferred_element_type=jnp.float32)
    grad_preact = (grad_activated * gelu_slope(preact)).astype(jnp.bfloat16)
    grad_expand_term = jnp.dot(hidden_second.T, grad_preact, preferred_element_type=jnp.float32)
    grad_bias_term = jnp.sum(grad_preact.astype(jnp.float32), axis=0)
    grad_hidden_second = jnp.dot(grad_preact, full_expand.T, preferred_element_type=jnp.float32)
    norm_term_second, gain_second, shift_second = norm_backward(
        grad_hidden_second, plain_second, inv_second, column_set[:, 5]
    )
    grad_residual = grad_result.astype(jnp.float32) + norm_term_second
    grad_attended = grad_residual.astype(jnp.bfloat16)
    grad_out_term = jnp.dot(mixed_low.T, grad_attended, preferred_element_type=jnp.float32)
    grad_out_bias = jnp.sum(grad_attended.astype(jnp.float32), axis=0)
    owned_late = lax.psum_scatter(
        jnp.concatenate(
            [grad_shrink_term.reshape(model_width, -1), grad_expand_term, grad_out_term], axis=1
        ).astype(jnp.bfloat16),
        everyone,
        scatter_dimension=0,
        tiled=True,
    ).astype(jnp.float32)
    grad_mixed = jnp.dot(grad_attended, full_out.T, preferred_element_type=jnp.float32).astype(
        jnp.bfloat16
    )
    halves = []
    half_pairs = model_width // 256
    for first_pair in (0, half_pairs):
        grad_query, grad_keys, grad_values = attention_pallas(
            scaled_queries, pair_rows, grad_mixed, log_totals, first_pair, half_pairs
        )
        terms = jnp.concatenate([grad_keys, grad_values], axis=1)
        returned = lax.ppermute(terms[row_count:].astype(jnp.bfloat16), "frame", swap)
        halves.append((grad_query, terms[:row_count] + returned.astype(jnp.float32)))
    half_width = model_width // 2
    grad_projected = jnp.concatenate(
        [
            (jnp.concatenate([halves[0][0], halves[1][0]], axis=1) * score_scale).astype(jnp.bfloat16),
            jnp.concatenate(
                [
                    halves[0][1][:, :half_width],
                    halves[1][1][:, :half_width],
                    halves[0][1][:, half_width:],
                    halves[1][1][:, half_width:],
                ],
                axis=1,
            ).astype(jnp.bfloat16),
        ],
        axis=1,
    )
    grad_in_term = jnp.dot(hidden_first.T, grad_projected, preferred_element_type=jnp.float32)
    projected_sums = jnp.sum(grad_projected.astype(jnp.float32), axis=0)
    grad_query_bias = projected_sums[:model_width]
    grad_value_bias = projected_sums[2 * model_width :]
    grad_hidden_first = jnp.dot(grad_projected, full_in.T, preferred_element_type=jnp.float32)
    norm_term_first, gain_first, shift_first = norm_backward(
        grad_hidden_first, plain_first, inv_first, column_set[:, 0]
    )
    grad_inputs = (grad_residual + norm_term_first).astype(jnp.bfloat16).reshape(inputs.shape)
    grad_columns = jnp.stack(
        [
            gain_first,
            shift_first,
            grad_query_bias,
            grad_value_bias,
            grad_out_bias,
            gain_second,
            shift_second,
            grad_down_bias,
        ],
        axis=1,
    )
    small_grads = jnp.concatenate(
        [
            grad_columns,
            grad_bias_term.reshape(model_width, -1),
            jnp.zeros((model_width, 256 - 12), jnp.float32),
        ],
        axis=1,
    )
    first_terms, owned_late = lax.optimization_barrier(
        (jnp.concatenate([grad_in_term, small_grads], axis=1), owned_late)
    )
    owned_first = lax.psum_scatter(
        first_terms.astype(jnp.bfloat16), everyone, scatter_dimension=0, tiled=True
    ).astype(jnp.float32)
    owned_in = owned_first[:, :wide_in]
    owned_vectors = owned_first[:, wide_in : wide_in + vectors.shape[1]]
    owned_bias = owned_first[:, wide_in + vectors.shape[1] : wide_in + 12].reshape(-1)
    owned_shrink = owned_late[:, :ff_width].reshape(shrink_weight.shape)
    owned_expand = owned_late[:, ff_width : 2 * ff_width]
    owned_out = owned_late[:, 2 * ff_width :]
    new_in, mom_in = adam_step(project_in, moments_in, owned_in)
    new_out, mom_out = adam_step(project_out, moments_out, owned_out)
    new_expand, mom_expand = adam_step(expand_weight, moments_expand, owned_expand)
    new_shrink, mom_shrink = adam_step(shrink_weight, moments_shrink, owned_shrink)
    new_bias, mom_bias = adam_step(expand_bias, moments_bias, owned_bias)
    new_vectors, mom_vectors = adam_step(vectors, moments_vectors, owned_vectors)
    return (
        output,
        grad_inputs,
        owned_in,
        owned_out,
        owned_expand,
        owned_shrink,
        owned_bias,
        owned_vectors,
        new_in,
        new_out,
        new_expand,
        new_shrink,
        new_bias,
        new_vectors,
        mom_in,
        mom_out,
        mom_expand,
        mom_shrink,
        mom_bias,
        mom_vectors,
    )


def solution(mesh):
    in_specs = (
        P("clip", "frame", None),
        P("clip", "frame", None),
        P(("clip", "frame"), None),
        P(("clip", "frame"), None),
        P(("clip", "frame"), None),
        P(("clip", "frame"), None),
        P(("clip", "frame")),
        P(("clip", "frame"), None),
        P(None, ("clip", "frame"), None),
        P(None, ("clip", "frame"), None),
        P(None, ("clip", "frame"), None),
        P(None, ("clip", "frame"), None),
        P(None, ("clip", "frame")),
        P(None, ("clip", "frame"), None),
    )
    out_specs = (
        P("clip", "frame", None),
        P("clip", "frame", None),
        P(("clip", "frame"), None),
        P(("clip", "frame"), None),
        P(("clip", "frame"), None),
        P(("clip", "frame"), None),
        P(("clip", "frame")),
        P(("clip", "frame"), None),
        P(("clip", "frame"), None),
        P(("clip", "frame"), None),
        P(("clip", "frame"), None),
        P(("clip", "frame"), None),
        P(("clip", "frame")),
        P(("clip", "frame"), None),
        P(None, ("clip", "frame"), None),
        P(None, ("clip", "frame"), None),
        P(None, ("clip", "frame"), None),
        P(None, ("clip", "frame"), None),
        P(None, ("clip", "frame")),
        P(None, ("clip", "frame"), None),
    )
    return jax.shard_map(body, mesh=mesh, in_specs=in_specs, out_specs=out_specs, check_vma=False)
```

```python
import functools
import math

import jax
import jax.numpy as jnp
from jax import lax
from jax.experimental import pallas as pl
from jax.experimental.pallas import tpu as pltpu
from jax.sharding import PartitionSpec as P

HEADS = 12
ADAM_STEP = 4


epsilon_norm = 1e-05
beta_first = 0.9
beta_second = 0.99
learn_rate = 0.03
decay_rate = 0.01
epsilon_adam = 1e-08
root_half = 0.7071067811865476
inv_root_two_pi = 0.3989422804014327


def norm_parts(inputs, norm_gain, norm_shift):
    average = jnp.mean(inputs, axis=-1, keepdims=True)
    centered = inputs - average
    spread = jnp.mean(centered * centered, axis=-1, keepdims=True)
    inv_std = lax.rsqrt(spread + epsilon_norm)
    normed = centered * inv_std
    return (normed * norm_gain + norm_shift, normed, inv_std)


def norm_backward(grad_normed, normed, inv_std, norm_gain):
    grad_gain = jnp.sum(grad_normed * normed, axis=0)
    grad_shift = jnp.sum(grad_normed, axis=0)
    scaled = grad_normed * norm_gain
    grad_input = inv_std * (
        scaled
        - jnp.mean(scaled, axis=-1, keepdims=True)
        - normed * jnp.mean(scaled * normed, axis=-1, keepdims=True)
    )
    return (grad_input, grad_gain, grad_shift)


def gelu_exact(inputs):
    return 0.5 * inputs * (1.0 + jax.scipy.special.erf(inputs * root_half))


def gelu_slope(inputs):
    return (
        0.5 * (1.0 + jax.scipy.special.erf(inputs * root_half))
        + inputs * jnp.exp(-0.5 * inputs * inputs) * inv_root_two_pi
    )


QUERY_CHUNK = 256
MASKED = -1e30


def attention_forward_kernel(q_ref, k_ref, v_ref, kbias_ref, o_ref, l_ref):
    head_size = q_ref.shape[1] // 2
    rows = q_ref.shape[0]
    kbias = kbias_ref[...]
    lane = lax.broadcasted_iota(jnp.int32, (QUERY_CHUNK, 2 * head_size), 1)
    for chunk in range(rows // QUERY_CHUNK):
        span = pl.ds(chunk * QUERY_CHUNK, QUERY_CHUNK)
        mixed_parts = []
        totals = []
        for half in range(2):
            cols = pl.ds(half * head_size, head_size)
            query = q_ref[span, cols]
            key = k_ref[:, cols]
            value = v_ref[:, cols]
            scores = (
                lax.dot_general(
                    query, key, (((1,), (1,)), ((), ())), preferred_element_type=jnp.float32
                )
                + kbias
            )
            highest = jnp.max(scores, axis=1, keepdims=True)
            exponent = jnp.exp(scores - highest)
            denominator = jnp.sum(exponent, axis=1, keepdims=True)
            weights = (exponent * (1.0 / denominator)).astype(jnp.bfloat16)
            mixed_parts.append(jnp.dot(weights, value, preferred_element_type=jnp.float32))
            totals.append(highest + jnp.log(denominator))
        o_ref[span, :] = jnp.concatenate(mixed_parts, axis=1).astype(o_ref.dtype)
        l_ref[span, :] = jnp.where(lane < head_size, totals[0], totals[1])


def attention_backward_kernel(
    q_ref, k_ref, v_ref, do_ref, l_ref, kbias_ref, dq_ref, dk_ref, dv_ref
):
    head_size = q_ref.shape[1] // 2
    rows = q_ref.shape[0]
    kbias = kbias_ref[...]
    for half in range(2):
        cols = pl.ds(half * head_size, head_size)
        key = k_ref[:, cols]
        value = v_ref[:, cols]
        grad_key = None
        grad_value = None
        for chunk in range(rows // QUERY_CHUNK):
            span = pl.ds(chunk * QUERY_CHUNK, QUERY_CHUNK)
            query = q_ref[span, cols]
            grad_out = do_ref[span, cols]
            total = l_ref[span, pl.ds(half * head_size, 1)]
            scores = (
                lax.dot_general(
                    query, key, (((1,), (1,)), ((), ())), preferred_element_type=jnp.float32
                )
                + kbias
            )
            weights = jnp.exp(scores - total)
            grad_weights = lax.dot_general(
                grad_out, value, (((1,), (1,)), ((), ())), preferred_element_type=jnp.float32
            )
            delta = jnp.sum(weights * grad_weights, axis=1, keepdims=True)
            grad_scores = (weights * (grad_weights - delta)).astype(jnp.bfloat16)
            dq_ref[span, cols] = jnp.dot(
                grad_scores, key, preferred_element_type=jnp.float32
            ).astype(dq_ref.dtype)
            key_part = lax.dot_general(
                grad_scores, query, (((0,), (0,)), ((), ())), preferred_element_type=jnp.float32
            )
            value_part = lax.dot_general(
                weights.astype(jnp.bfloat16),
                grad_out,
                (((0,), (0,)), ((), ())),
                preferred_element_type=jnp.float32,
            )
            grad_key = key_part if grad_key is None else grad_key + key_part
            grad_value = value_part if grad_value is None else grad_value + value_part
        dk_ref[:, cols] = grad_key
        dv_ref[:, cols] = grad_value


def pad_rows(values, rows):
    return jnp.pad(values, ((0, rows - values.shape[0]), (0, 0)))


def attention_pallas(queries, pairs, grad_out=None, totals=None, first_pair=0, pair_span=None):
    query_rows, model_width = queries.shape
    key_rows = pairs.shape[0]
    padded_q = -(-query_rows // QUERY_CHUNK) * QUERY_CHUNK
    padded_k = -(-key_rows // 128) * 128
    pair_count = model_width // 128
    q_pad = pad_rows(queries, padded_q)
    kv_pad = pad_rows(pairs, padded_k)
    kbias = jnp.where(jnp.arange(padded_k) < key_rows, 0.0, MASKED).astype(jnp.float32)[None, :]
    q_spec = pl.BlockSpec((padded_q, 128), lambda j: (0, j))
    k_spec = pl.BlockSpec((padded_k, 128), lambda j: (0, j))
    v_spec = pl.BlockSpec((padded_k, 128), lambda j: (0, j + pair_count))
    b_spec = pl.BlockSpec((1, padded_k), lambda j: (0, 0))
    params = pltpu.CompilerParams(vmem_limit_bytes=48 * 1024 * 1024)
    if grad_out is None:
        mixed, log_totals = pl.pallas_call(
            attention_forward_kernel,
            grid=(pair_count,),
            in_specs=[q_spec, k_spec, v_spec, b_spec],
            out_specs=[q_spec, q_spec],
            out_shape=[
                jax.ShapeDtypeStruct((padded_q, model_width), jnp.bfloat16),
                jax.ShapeDtypeStruct((padded_q, model_width), jnp.float32),
            ],
            compiler_params=params,
        )(q_pad, kv_pad, kv_pad, kbias)
        return mixed[:query_rows], log_totals
    do_pad = pad_rows(grad_out, padded_q)
    span = pair_count if pair_span is None else pair_span
    qi_spec = pl.BlockSpec((padded_q, 128), lambda j: (0, j + first_pair))
    ki_spec = pl.BlockSpec((padded_k, 128), lambda j: (0, j + first_pair))
    vi_spec = pl.BlockSpec((padded_k, 128), lambda j: (0, j + first_pair + pair_count))
    qo_spec = pl.BlockSpec((padded_q, 128), lambda j: (0, j))
    ko_spec = pl.BlockSpec((padded_k, 128), lambda j: (0, j))
    dq, dk, dv = pl.pallas_call(
        attention_backward_kernel,
        grid=(span,),
        in_specs=[qi_spec, ki_spec, vi_spec, qi_spec, qi_spec, b_spec],
        out_specs=[qo_spec, ko_spec, ko_spec],
        out_shape=[
            jax.ShapeDtypeStruct((padded_q, 128 * span), jnp.float32),
            jax.ShapeDtypeStruct((padded_k, 128 * span), jnp.float32),
            jax.ShapeDtypeStruct((padded_k, 128 * span), jnp.float32),
        ],
        compiler_params=params,
    )(q_pad, kv_pad, kv_pad, do_pad, totals, kbias)
    return dq[:query_rows], dk[:key_rows], dv[:key_rows]


def attend_forward(queries, keys_values, head_count):
    model_width = queries.shape[2]
    head_size = model_width // head_count
    score_scale = 1.0 / math.sqrt(head_size)

    def one_head(head_index):
        offset = head_index * head_size
        query_block = lax.dynamic_slice_in_dim(queries, offset, head_size, 2)
        key_block = lax.dynamic_slice_in_dim(keys_values, offset, head_size, 2)
        value_block = lax.dynamic_slice_in_dim(keys_values, model_width + offset, head_size, 2)
        scores = (
            jnp.einsum("cqd,ckd->cqk", query_block, key_block, preferred_element_type=jnp.float32)
            * score_scale
        )
        highest = jnp.max(scores, axis=-1, keepdims=True)
        exponent = jnp.exp(scores - highest)
        denominator = jnp.sum(exponent, axis=-1, keepdims=True)
        weights_soft = (exponent / denominator).astype(jnp.bfloat16)
        mixed = jnp.einsum(
            "cqk,ckd->cqd", weights_soft, value_block, preferred_element_type=jnp.float32
        )
        return (mixed, (highest + jnp.log(denominator))[..., 0])

    mixed, log_totals = lax.map(one_head, jnp.arange(head_count))
    clip_count, frame_count = (queries.shape[0], queries.shape[1])
    mixed = jnp.transpose(mixed, (1, 2, 0, 3)).reshape(clip_count, frame_count, model_width)
    return (mixed, log_totals)


def attend_backward(queries, keys_values, grad_mixed, log_totals, head_count):
    model_width = queries.shape[2]
    head_size = model_width // head_count
    score_scale = 1.0 / math.sqrt(head_size)

    def one_head_back(head_index):
        offset = head_index * head_size
        query_block = lax.dynamic_slice_in_dim(queries, offset, head_size, 2)
        key_block = lax.dynamic_slice_in_dim(keys_values, offset, head_size, 2)
        value_block = lax.dynamic_slice_in_dim(keys_values, model_width + offset, head_size, 2)
        grad_block = lax.dynamic_slice_in_dim(grad_mixed, offset, head_size, 2)
        totals = lax.dynamic_index_in_dim(log_totals, head_index, 0, keepdims=False)
        scores = (
            jnp.einsum("cqd,ckd->cqk", query_block, key_block, preferred_element_type=jnp.float32)
            * score_scale
        )
        weights_soft = jnp.exp(scores - totals[..., None])
        grad_weights = jnp.einsum(
            "cqd,ckd->cqk", grad_block, value_block, preferred_element_type=jnp.float32
        )
        delta = jnp.sum(weights_soft * grad_weights, axis=-1, keepdims=True)
        grad_scores = (weights_soft * (grad_weights - delta)).astype(jnp.bfloat16)
        grad_query = (
            jnp.einsum("cqk,ckd->cqd", grad_scores, key_block, preferred_element_type=jnp.float32)
            * score_scale
        )
        grad_key = (
            jnp.einsum("cqk,cqd->ckd", grad_scores, query_block, preferred_element_type=jnp.float32)
            * score_scale
        )
        grad_value = jnp.einsum(
            "cqk,cqd->ckd",
            weights_soft.astype(jnp.bfloat16),
            grad_block,
            preferred_element_type=jnp.float32,
        )
        return (grad_query, delta[..., 0], grad_key, grad_value)

    pieces = lax.map(one_head_back, jnp.arange(head_count))
    clip_count, frame_count = (queries.shape[0], queries.shape[1])
    clip_frames = keys_values.shape[1]
    grad_query = jnp.transpose(pieces[0], (1, 2, 0, 3)).reshape(
        clip_count, frame_count, model_width
    )
    grad_key = jnp.transpose(pieces[2], (1, 2, 0, 3)).reshape(clip_count, clip_frames, model_width)
    grad_value = jnp.transpose(pieces[3], (1, 2, 0, 3)).reshape(
        clip_count, clip_frames, model_width
    )
    return (grad_query, pieces[1], jnp.concatenate([grad_key, grad_value], axis=2))


def link_plan(mesh):
    devices = list(mesh.devices.reshape(-1))
    bit_count = len(devices).bit_length() - 1
    core_bit = 1
    for bit in range(bit_count):
        first, other = devices[0], devices[1 << bit]
        if getattr(first, "coords", None) is not None and tuple(first.coords) == tuple(other.coords):
            core_bit = bit
    others = [bit for bit in range(bit_count) if bit != core_bit]
    near, far = others[:-1], others[-1:]
    rotated = tuple(tuple(near[k:] + near[:k] + far) for k in range(3))
    inner = [bit for bit in near if bit != 0]
    late = tuple(tuple(inner[k:] + inner[:k] + [0] + far) for k in range(2))
    return bit_count, core_bit, rotated, late


def tree_reduce_scatter(terms, part_columns, orders, plan_bits, hooks=None):
    hooks = dict(hooks or {})
    tied = {}
    bit_count, core_bit = plan_bits
    device = lax.axis_index("clip") * lax.axis_size("frame") + lax.axis_index("frame")
    blocks = 1 << bit_count
    block_rows = terms.shape[0] // blocks
    data = terms.reshape((2,) * bit_count + (block_rows, terms.shape[1]))
    parts = [(data, list(range(bit_count - 1, -1, -1)))]
    plan = [(core_bit,)] + [tuple(order[stage] for order in orders) for stage in range(len(orders[0]))]
    for stage, stage_bits in enumerate(plan):
        if stage == 1:
            whole, bits = parts[0]
            parts = []
            offset = 0
            for width in part_columns:
                parts.append((whole[..., offset : offset + width], bits))
                offset += width
        keeps, sends = [], []
        for (part, part_bits), bit in zip(parts, stage_bits):
            axis = part_bits.index(bit)
            mine = (device >> bit) & 1
            keeps.append(lax.dynamic_index_in_dim(part, mine, axis=axis, keepdims=False))
            sends.append(
                lax.dynamic_index_in_dim(part, 1 - mine, axis=axis, keepdims=False).astype(jnp.bfloat16)
            )
        if stage in hooks:
            sends, tied[stage] = lax.optimization_barrier((sends, hooks[stage](tied)))
        new_parts = []
        for keep, send, (part, part_bits), bit in zip(keeps, sends, parts, stage_bits):
            pairs = [(index, index ^ (1 << bit)) for index in range(blocks)]
            got = lax.ppermute(send, ("clip", "frame"), pairs)
            new_parts.append((keep + got.astype(jnp.float32), [b for b in part_bits if b != bit]))
        parts = new_parts
    return jnp.concatenate([part for part, _ in parts], axis=-1).astype(jnp.float32), tied


def adam_step(weight, moments, gradient):
    first = beta_first * moments[0] + (1.0 - beta_first) * gradient
    second = beta_second * moments[1] + (1.0 - beta_second) * gradient * gradient
    first_hat = first / (1.0 - beta_first**ADAM_STEP)
    second_hat = second / (1.0 - beta_second**ADAM_STEP)
    change = -learn_rate * (first_hat / (jnp.sqrt(second_hat) + epsilon_adam) + decay_rate * weight)
    return (change, jnp.stack([first, second]))


def body(
    plan,
    inputs,
    cotangent,
    project_in,
    project_out,
    expand_weight,
    shrink_weight,
    expand_bias,
    vectors,
    moments_in,
    moments_out,
    moments_expand,
    moments_shrink,
    moments_bias,
    moments_vectors,
):
    clip_count, frame_count, model_width = inputs.shape
    row_count = clip_count * frame_count
    head_count = HEADS
    shard_rows = project_in.shape[0]
    wide_in = project_in.shape[1]
    ff_width = expand_weight.shape[1]
    swap = [(0, 1), (1, 0)]
    everyone = ("clip", "frame")

    small = jnp.concatenate(
        [
            vectors,
            expand_bias.reshape(shard_rows, -1),
            jnp.zeros((shard_rows, 128 - vectors.shape[1] - expand_bias.shape[0] // shard_rows), jnp.float32),
        ],
        axis=1,
    )
    first_pack = jnp.concatenate([project_in, small], axis=1).astype(jnp.bfloat16)
    second_pack = jnp.concatenate(
        [project_out, expand_weight, shrink_weight.reshape(shard_rows, -1)], axis=1
    ).astype(jnp.bfloat16)
    first_full = lax.all_gather(first_pack, everyone, axis=0, tiled=True)
    second_full = lax.all_gather(second_pack, everyone, axis=0, tiled=True)
    full_in = first_full[:, :wide_in]
    small_full = first_full[:, wide_in:].astype(jnp.float32)
    column_set = small_full[:, : vectors.shape[1]]
    full_bias = small_full[:, vectors.shape[1] : vectors.shape[1] + ff_width // model_width].reshape(-1)
    full_out = second_full[:, :model_width]
    full_expand = second_full[:, model_width : model_width + ff_width]
    full_shrink = second_full[:, model_width + ff_width :].reshape(ff_width, model_width)

    frames_rows = inputs.reshape(row_count, model_width).astype(jnp.float32)
    normed_first, plain_first, inv_first = norm_parts(
        frames_rows, column_set[:, 0], column_set[:, 1]
    )
    hidden_first = normed_first.astype(jnp.bfloat16)
    partner_rows = lax.ppermute(inputs, "frame", swap).reshape(row_count, model_width)
    hidden_partner = norm_parts(
        partner_rows.astype(jnp.float32), column_set[:, 0], column_set[:, 1]
    )[0].astype(jnp.bfloat16)
    bias_in = jnp.concatenate(
        [column_set[:, 2], jnp.zeros((model_width,), jnp.float32), column_set[:, 3]]
    )
    projected = (
        jnp.dot(hidden_first, full_in, preferred_element_type=jnp.float32) + bias_in
    ).astype(jnp.bfloat16)
    partner_pairs = (
        jnp.dot(hidden_partner, full_in[:, model_width:], preferred_element_type=jnp.float32)
        + bias_in[model_width:]
    ).astype(jnp.bfloat16)
    queries = projected[:, :model_width].reshape(clip_count, frame_count, model_width)
    clip_pairs = jnp.concatenate([projected[:, model_width:], partner_pairs], axis=0).reshape(
        clip_count, 2 * frame_count, 2 * model_width
    )
    score_scale = 1.0 / math.sqrt(model_width // head_count)
    scaled_queries = (projected[:, :model_width] * score_scale).astype(jnp.bfloat16)
    pair_rows = clip_pairs.reshape(2 * row_count, 2 * model_width)
    mixed_low, log_totals = attention_pallas(scaled_queries, pair_rows)
    attended = jnp.dot(mixed_low, full_out, preferred_element_type=jnp.float32) + column_set[:, 4]
    residual = frames_rows + attended
    normed_second, plain_second, inv_second = norm_parts(
        residual, column_set[:, 5], column_set[:, 6]
    )
    hidden_second = normed_second.astype(jnp.bfloat16)
    preact = jnp.dot(hidden_second, full_expand, preferred_element_type=jnp.float32) + full_bias
    activated = gelu_exact(preact).astype(jnp.bfloat16)
    result = (
        residual
        + jnp.dot(activated, full_shrink, preferred_element_type=jnp.float32)
        + column_set[:, 7]
    )
    output = result.astype(jnp.bfloat16).reshape(inputs.shape)

    grad_result = cotangent.reshape(row_count, model_width)
    grad_shrink_term = jnp.dot(activated.T, grad_result, preferred_element_type=jnp.float32)
    grad_down_bias = jnp.sum(grad_result.astype(jnp.float32), axis=0)
    grad_activated = jnp.dot(grad_result, full_shrink.T, preferred_element_type=jnp.float32)
    grad_preact = (grad_activated * gelu_slope(preact)).astype(jnp.bfloat16)
    grad_expand_term = jnp.dot(hidden_second.T, grad_preact, preferred_element_type=jnp.float32)
    grad_bias_term = jnp.sum(grad_preact.astype(jnp.float32), axis=0)
    grad_hidden_second = jnp.dot(grad_preact, full_expand.T, preferred_element_type=jnp.float32)
    norm_term_second, gain_second, shift_second = norm_backward(
        grad_hidden_second, plain_second, inv_second, column_set[:, 5]
    )
    grad_residual = grad_result.astype(jnp.float32) + norm_term_second
    grad_attended = grad_residual.astype(jnp.bfloat16)
    grad_out_term = jnp.dot(mixed_low.T, grad_attended, preferred_element_type=jnp.float32)
    grad_out_bias = jnp.sum(grad_attended.astype(jnp.float32), axis=0)
    late_terms = jnp.concatenate(
        [grad_shrink_term.reshape(model_width, -1), grad_expand_term, grad_out_term], axis=1
    )
    grad_mixed = jnp.dot(grad_attended, full_out.T, preferred_element_type=jnp.float32).astype(
        jnp.bfloat16
    )
    def first_backward_half(tied):
        mixed_grads = tied[0]
        first = attention_pallas(
            scaled_queries, pair_rows, mixed_grads, log_totals, 0, model_width // 256
        )
        send = jnp.concatenate([first[1], first[2]], axis=1)[row_count:].astype(jnp.bfloat16)
        return (first, send, mixed_grads)

    bit_count, core_bit, rotated_orders, late_orders = plan
    owned_late, tied = tree_reduce_scatter(
        late_terms,
        (3456, 3456),
        late_orders,
        (bit_count, core_bit),
        {0: lambda tied: grad_mixed, 1: first_backward_half},
    )
    first_half, first_send, grad_mixed = tied[1]
    halves = []
    half_pairs = model_width // 256
    for first_pair in (0, half_pairs):
        if first_pair == 0:
            grad_query, grad_keys, grad_values = first_half
            send = first_send
        else:
            grad_query, grad_keys, grad_values = attention_pallas(
                scaled_queries, pair_rows, grad_mixed, log_totals, first_pair, half_pairs
            )
            send = jnp.concatenate([grad_keys, grad_values], axis=1)[row_count:].astype(jnp.bfloat16)
        terms = jnp.concatenate([grad_keys, grad_values], axis=1)
        returned = lax.ppermute(send, "frame", swap)
        halves.append((grad_query, terms[:row_count] + returned.astype(jnp.float32)))
    half_width = model_width // 2
    grad_projected = jnp.concatenate(
        [
            (jnp.concatenate([halves[0][0], halves[1][0]], axis=1) * score_scale).astype(jnp.bfloat16),
            jnp.concatenate(
                [
                    halves[0][1][:, :half_width],
                    halves[1][1][:, :half_width],
                    halves[0][1][:, half_width:],
                    halves[1][1][:, half_width:],
                ],
                axis=1,
            ).astype(jnp.bfloat16),
        ],
        axis=1,
    )
    grad_in_term = jnp.dot(hidden_first.T, grad_projected, preferred_element_type=jnp.float32)
    projected_sums = jnp.sum(grad_projected.astype(jnp.float32), axis=0)
    grad_query_bias = projected_sums[:model_width]
    grad_value_bias = projected_sums[2 * model_width :]
    grad_hidden_first = jnp.dot(grad_projected, full_in.T, preferred_element_type=jnp.float32)
    norm_term_first, gain_first, shift_first = norm_backward(
        grad_hidden_first, plain_first, inv_first, column_set[:, 0]
    )
    grad_inputs = (grad_residual + norm_term_first).astype(jnp.bfloat16).reshape(inputs.shape)
    grad_columns = jnp.stack(
        [
            gain_first,
            shift_first,
            grad_query_bias,
            grad_value_bias,
            grad_out_bias,
            gain_second,
            shift_second,
            grad_down_bias,
        ],
        axis=1,
    )
    small_grads = jnp.concatenate(
        [
            grad_columns,
            grad_bias_term.reshape(model_width, -1),
            jnp.zeros((model_width, 128 - 12), jnp.float32),
        ],
        axis=1,
    )
    owned_first = tree_reduce_scatter(
        jnp.concatenate([grad_in_term, small_grads], axis=1),
        (896, 768, 768),
        rotated_orders,
        (bit_count, core_bit),
    )[0]
    owned_in = owned_first[:, :wide_in]
    owned_vectors = owned_first[:, wide_in : wide_in + vectors.shape[1]]
    owned_bias = owned_first[:, wide_in + vectors.shape[1] : wide_in + 12].reshape(-1)
    owned_shrink = owned_late[:, :ff_width].reshape(shrink_weight.shape)
    owned_expand = owned_late[:, ff_width : 2 * ff_width]
    owned_out = owned_late[:, 2 * ff_width :]
    new_in, mom_in = adam_step(project_in, moments_in, owned_in)
    new_out, mom_out = adam_step(project_out, moments_out, owned_out)
    new_expand, mom_expand = adam_step(expand_weight, moments_expand, owned_expand)
    new_shrink, mom_shrink = adam_step(shrink_weight, moments_shrink, owned_shrink)
    new_bias, mom_bias = adam_step(expand_bias, moments_bias, owned_bias)
    new_vectors, mom_vectors = adam_step(vectors, moments_vectors, owned_vectors)
    return (
        output,
        grad_inputs,
        owned_in,
        owned_out,
        owned_expand,
        owned_shrink,
        owned_bias,
        owned_vectors,
        new_in,
        new_out,
        new_expand,
        new_shrink,
        new_bias,
        new_vectors,
        mom_in,
        mom_out,
        mom_expand,
        mom_shrink,
        mom_bias,
        mom_vectors,
    )


def solution(mesh):
    in_specs = (
        P("clip", "frame", None),
        P("clip", "frame", None),
        P(("clip", "frame"), None),
        P(("clip", "frame"), None),
        P(("clip", "frame"), None),
        P(("clip", "frame"), None),
        P(("clip", "frame")),
        P(("clip", "frame"), None),
        P(None, ("clip", "frame"), None),
        P(None, ("clip", "frame"), None),
        P(None, ("clip", "frame"), None),
        P(None, ("clip", "frame"), None),
        P(None, ("clip", "frame")),
        P(None, ("clip", "frame"), None),
    )
    out_specs = (
        P("clip", "frame", None),
        P("clip", "frame", None),
        P(("clip", "frame"), None),
        P(("clip", "frame"), None),
        P(("clip", "frame"), None),
        P(("clip", "frame"), None),
        P(("clip", "frame")),
        P(("clip", "frame"), None),
        P(("clip", "frame"), None),
        P(("clip", "frame"), None),
        P(("clip", "frame"), None),
        P(("clip", "frame"), None),
        P(("clip", "frame")),
        P(("clip", "frame"), None),
        P(None, ("clip", "frame"), None),
        P(None, ("clip", "frame"), None),
        P(None, ("clip", "frame"), None),
        P(None, ("clip", "frame"), None),
        P(None, ("clip", "frame")),
        P(None, ("clip", "frame"), None),
    )
    return jax.shard_map(
        functools.partial(body, link_plan(mesh)),
        mesh=mesh,
        in_specs=in_specs,
        out_specs=out_specs,
        check_vma=False,
    )
```

```python
import functools
import math

import jax
import jax.numpy as jnp
from jax import lax
from jax.experimental import pallas as pl
from jax.experimental.pallas import tpu as pltpu
from jax.sharding import PartitionSpec as P

HEADS = 12
ADAM_STEP = 4


epsilon_norm = 1e-05
beta_first = 0.9
beta_second = 0.99
learn_rate = 0.03
decay_rate = 0.01
epsilon_adam = 1e-08
root_half = 0.7071067811865476
inv_root_two_pi = 0.3989422804014327


def norm_parts(inputs, norm_gain, norm_shift):
    average = jnp.mean(inputs, axis=-1, keepdims=True)
    centered = inputs - average
    spread = jnp.mean(centered * centered, axis=-1, keepdims=True)
    inv_std = lax.rsqrt(spread + epsilon_norm)
    normed = centered * inv_std
    return (normed * norm_gain + norm_shift, normed, inv_std)


def norm_backward(grad_normed, normed, inv_std, norm_gain):
    grad_gain = jnp.sum(grad_normed * normed, axis=0)
    grad_shift = jnp.sum(grad_normed, axis=0)
    scaled = grad_normed * norm_gain
    grad_input = inv_std * (
        scaled
        - jnp.mean(scaled, axis=-1, keepdims=True)
        - normed * jnp.mean(scaled * normed, axis=-1, keepdims=True)
    )
    return (grad_input, grad_gain, grad_shift)


def gelu_exact(inputs):
    return 0.5 * inputs * (1.0 + jax.scipy.special.erf(inputs * root_half))


def gelu_slope(inputs):
    return (
        0.5 * (1.0 + jax.scipy.special.erf(inputs * root_half))
        + inputs * jnp.exp(-0.5 * inputs * inputs) * inv_root_two_pi
    )


QUERY_CHUNK = 256
MASKED = -1e30


def attention_forward_kernel(q_ref, k_ref, v_ref, kbias_ref, o_ref, l_ref):
    head_size = q_ref.shape[1] // 2
    rows = q_ref.shape[0]
    kbias = kbias_ref[...]
    lane = lax.broadcasted_iota(jnp.int32, (QUERY_CHUNK, 2 * head_size), 1)
    for chunk in range(rows // QUERY_CHUNK):
        span = pl.ds(chunk * QUERY_CHUNK, QUERY_CHUNK)
        mixed_parts = []
        totals = []
        for half in range(2):
            cols = pl.ds(half * head_size, head_size)
            query = q_ref[span, cols]
            key = k_ref[:, cols]
            value = v_ref[:, cols]
            scores = (
                lax.dot_general(
                    query, key, (((1,), (1,)), ((), ())), preferred_element_type=jnp.float32
                )
                + kbias
            )
            highest = jnp.max(scores, axis=1, keepdims=True)
            exponent = jnp.exp(scores - highest)
            denominator = jnp.sum(exponent, axis=1, keepdims=True)
            weights = (exponent * (1.0 / denominator)).astype(jnp.bfloat16)
            mixed_parts.append(jnp.dot(weights, value, preferred_element_type=jnp.float32))
            totals.append(highest + jnp.log(denominator))
        o_ref[span, :] = jnp.concatenate(mixed_parts, axis=1).astype(o_ref.dtype)
        l_ref[span, :] = jnp.where(lane < head_size, totals[0], totals[1])


def attention_backward_kernel(
    q_ref, k_ref, v_ref, do_ref, l_ref, kbias_ref, dq_ref, dk_ref, dv_ref
):
    head_size = q_ref.shape[1] // 2
    rows = q_ref.shape[0]
    kbias = kbias_ref[...]
    for half in range(2):
        cols = pl.ds(half * head_size, head_size)
        key = k_ref[:, cols]
        value = v_ref[:, cols]
        grad_key = None
        grad_value = None
        for chunk in range(rows // QUERY_CHUNK):
            span = pl.ds(chunk * QUERY_CHUNK, QUERY_CHUNK)
            query = q_ref[span, cols]
            grad_out = do_ref[span, cols]
            total = l_ref[span, pl.ds(half * head_size, 1)]
            scores = (
                lax.dot_general(
                    query, key, (((1,), (1,)), ((), ())), preferred_element_type=jnp.float32
                )
                + kbias
            )
            weights = jnp.exp(scores - total)
            grad_weights = lax.dot_general(
                grad_out, value, (((1,), (1,)), ((), ())), preferred_element_type=jnp.float32
            )
            delta = jnp.sum(weights * grad_weights, axis=1, keepdims=True)
            grad_scores = (weights * (grad_weights - delta)).astype(jnp.bfloat16)
            dq_ref[span, cols] = jnp.dot(
                grad_scores, key, preferred_element_type=jnp.float32
            ).astype(dq_ref.dtype)
            key_part = lax.dot_general(
                grad_scores, query, (((0,), (0,)), ((), ())), preferred_element_type=jnp.float32
            )
            value_part = lax.dot_general(
                weights.astype(jnp.bfloat16),
                grad_out,
                (((0,), (0,)), ((), ())),
                preferred_element_type=jnp.float32,
            )
            grad_key = key_part if grad_key is None else grad_key + key_part
            grad_value = value_part if grad_value is None else grad_value + value_part
        dk_ref[:, cols] = grad_key
        dv_ref[:, cols] = grad_value


def pad_rows(values, rows):
    return jnp.pad(values, ((0, rows - values.shape[0]), (0, 0)))


def attention_pallas(queries, pairs, grad_out=None, totals=None, first_pair=0, pair_span=None):
    query_rows, model_width = queries.shape
    key_rows = pairs.shape[0]
    padded_q = -(-query_rows // QUERY_CHUNK) * QUERY_CHUNK
    padded_k = -(-key_rows // 128) * 128
    pair_count = model_width // 128
    q_pad = pad_rows(queries, padded_q)
    kv_pad = pad_rows(pairs, padded_k)
    kbias = jnp.where(jnp.arange(padded_k) < key_rows, 0.0, MASKED).astype(jnp.float32)[None, :]
    q_spec = pl.BlockSpec((padded_q, 128), lambda j: (0, j))
    k_spec = pl.BlockSpec((padded_k, 128), lambda j: (0, j))
    v_spec = pl.BlockSpec((padded_k, 128), lambda j: (0, j + pair_count))
    b_spec = pl.BlockSpec((1, padded_k), lambda j: (0, 0))
    params = pltpu.CompilerParams(vmem_limit_bytes=48 * 1024 * 1024)
    if grad_out is None:
        mixed, log_totals = pl.pallas_call(
            attention_forward_kernel,
            grid=(pair_count,),
            in_specs=[q_spec, k_spec, v_spec, b_spec],
            out_specs=[q_spec, q_spec],
            out_shape=[
                jax.ShapeDtypeStruct((padded_q, model_width), jnp.bfloat16),
                jax.ShapeDtypeStruct((padded_q, model_width), jnp.float32),
            ],
            compiler_params=params,
        )(q_pad, kv_pad, kv_pad, kbias)
        return mixed[:query_rows], log_totals
    do_pad = pad_rows(grad_out, padded_q)
    span = pair_count if pair_span is None else pair_span
    qi_spec = pl.BlockSpec((padded_q, 128), lambda j: (0, j + first_pair))
    ki_spec = pl.BlockSpec((padded_k, 128), lambda j: (0, j + first_pair))
    vi_spec = pl.BlockSpec((padded_k, 128), lambda j: (0, j + first_pair + pair_count))
    qo_spec = pl.BlockSpec((padded_q, 128), lambda j: (0, j))
    ko_spec = pl.BlockSpec((padded_k, 128), lambda j: (0, j))
    dq, dk, dv = pl.pallas_call(
        attention_backward_kernel,
        grid=(span,),
        in_specs=[qi_spec, ki_spec, vi_spec, qi_spec, qi_spec, b_spec],
        out_specs=[qo_spec, ko_spec, ko_spec],
        out_shape=[
            jax.ShapeDtypeStruct((padded_q, 128 * span), jnp.float32),
            jax.ShapeDtypeStruct((padded_k, 128 * span), jnp.float32),
            jax.ShapeDtypeStruct((padded_k, 128 * span), jnp.float32),
        ],
        compiler_params=params,
    )(q_pad, kv_pad, kv_pad, do_pad, totals, kbias)
    return dq[:query_rows], dk[:key_rows], dv[:key_rows]


def attend_forward(queries, keys_values, head_count):
    model_width = queries.shape[2]
    head_size = model_width // head_count
    score_scale = 1.0 / math.sqrt(head_size)

    def one_head(head_index):
        offset = head_index * head_size
        query_block = lax.dynamic_slice_in_dim(queries, offset, head_size, 2)
        key_block = lax.dynamic_slice_in_dim(keys_values, offset, head_size, 2)
        value_block = lax.dynamic_slice_in_dim(keys_values, model_width + offset, head_size, 2)
        scores = (
            jnp.einsum("cqd,ckd->cqk", query_block, key_block, preferred_element_type=jnp.float32)
            * score_scale
        )
        highest = jnp.max(scores, axis=-1, keepdims=True)
        exponent = jnp.exp(scores - highest)
        denominator = jnp.sum(exponent, axis=-1, keepdims=True)
        weights_soft = (exponent / denominator).astype(jnp.bfloat16)
        mixed = jnp.einsum(
            "cqk,ckd->cqd", weights_soft, value_block, preferred_element_type=jnp.float32
        )
        return (mixed, (highest + jnp.log(denominator))[..., 0])

    mixed, log_totals = lax.map(one_head, jnp.arange(head_count))
    clip_count, frame_count = (queries.shape[0], queries.shape[1])
    mixed = jnp.transpose(mixed, (1, 2, 0, 3)).reshape(clip_count, frame_count, model_width)
    return (mixed, log_totals)


def attend_backward(queries, keys_values, grad_mixed, log_totals, head_count):
    model_width = queries.shape[2]
    head_size = model_width // head_count
    score_scale = 1.0 / math.sqrt(head_size)

    def one_head_back(head_index):
        offset = head_index * head_size
        query_block = lax.dynamic_slice_in_dim(queries, offset, head_size, 2)
        key_block = lax.dynamic_slice_in_dim(keys_values, offset, head_size, 2)
        value_block = lax.dynamic_slice_in_dim(keys_values, model_width + offset, head_size, 2)
        grad_block = lax.dynamic_slice_in_dim(grad_mixed, offset, head_size, 2)
        totals = lax.dynamic_index_in_dim(log_totals, head_index, 0, keepdims=False)
        scores = (
            jnp.einsum("cqd,ckd->cqk", query_block, key_block, preferred_element_type=jnp.float32)
            * score_scale
        )
        weights_soft = jnp.exp(scores - totals[..., None])
        grad_weights = jnp.einsum(
            "cqd,ckd->cqk", grad_block, value_block, preferred_element_type=jnp.float32
        )
        delta = jnp.sum(weights_soft * grad_weights, axis=-1, keepdims=True)
        grad_scores = (weights_soft * (grad_weights - delta)).astype(jnp.bfloat16)
        grad_query = (
            jnp.einsum("cqk,ckd->cqd", grad_scores, key_block, preferred_element_type=jnp.float32)
            * score_scale
        )
        grad_key = (
            jnp.einsum("cqk,cqd->ckd", grad_scores, query_block, preferred_element_type=jnp.float32)
            * score_scale
        )
        grad_value = jnp.einsum(
            "cqk,cqd->ckd",
            weights_soft.astype(jnp.bfloat16),
            grad_block,
            preferred_element_type=jnp.float32,
        )
        return (grad_query, delta[..., 0], grad_key, grad_value)

    pieces = lax.map(one_head_back, jnp.arange(head_count))
    clip_count, frame_count = (queries.shape[0], queries.shape[1])
    clip_frames = keys_values.shape[1]
    grad_query = jnp.transpose(pieces[0], (1, 2, 0, 3)).reshape(
        clip_count, frame_count, model_width
    )
    grad_key = jnp.transpose(pieces[2], (1, 2, 0, 3)).reshape(clip_count, clip_frames, model_width)
    grad_value = jnp.transpose(pieces[3], (1, 2, 0, 3)).reshape(
        clip_count, clip_frames, model_width
    )
    return (grad_query, pieces[1], jnp.concatenate([grad_key, grad_value], axis=2))


def link_plan(mesh):
    devices = list(mesh.devices.reshape(-1))
    bit_count = len(devices).bit_length() - 1
    core_bit = 1
    for bit in range(bit_count):
        first, other = devices[0], devices[1 << bit]
        if getattr(first, "coords", None) is not None and tuple(first.coords) == tuple(other.coords):
            core_bit = bit
    others = [bit for bit in range(bit_count) if bit != core_bit]
    near, far = others[:-1], others[-1:]
    rotated = tuple(tuple(near[k:] + near[:k] + far) for k in range(3))
    inner = [bit for bit in near if bit != 0]
    late = tuple(tuple(inner[k:] + inner[:k] + [0] + far) for k in range(2))
    return bit_count, core_bit, rotated, late


def tree_reduce_scatter(terms, part_columns, orders, plan_bits, hooks=None):
    hooks = dict(hooks or {})
    tied = {}
    bit_count, core_bit = plan_bits
    device = lax.axis_index("clip") * lax.axis_size("frame") + lax.axis_index("frame")
    blocks = 1 << bit_count
    block_rows = terms.shape[0] // blocks
    data = terms.reshape((2,) * bit_count + (block_rows, terms.shape[1]))
    parts = [(data, list(range(bit_count - 1, -1, -1)))]
    plan = [(core_bit,)] + [tuple(order[stage] for order in orders) for stage in range(len(orders[0]))]
    for stage, stage_bits in enumerate(plan):
        if stage == 1:
            whole, bits = parts[0]
            parts = []
            offset = 0
            for width in part_columns:
                parts.append((whole[..., offset : offset + width], bits))
                offset += width
        keeps, sends = [], []
        for (part, part_bits), bit in zip(parts, stage_bits):
            axis = part_bits.index(bit)
            mine = (device >> bit) & 1
            keeps.append(lax.dynamic_index_in_dim(part, mine, axis=axis, keepdims=False))
            sends.append(
                lax.dynamic_index_in_dim(part, 1 - mine, axis=axis, keepdims=False).astype(jnp.bfloat16)
            )
        if stage in hooks:
            sends, tied[stage] = lax.optimization_barrier((sends, hooks[stage](tied)))
        new_parts = []
        for keep, send, (part, part_bits), bit in zip(keeps, sends, parts, stage_bits):
            pairs = [(index, index ^ (1 << bit)) for index in range(blocks)]
            got = lax.ppermute(send, ("clip", "frame"), pairs)
            new_parts.append((keep + got.astype(jnp.float32), [b for b in part_bits if b != bit]))
        parts = new_parts
    return jnp.concatenate([part for part, _ in parts], axis=-1).astype(jnp.float32), tied


def adam_step(weight, moments, gradient):
    first = beta_first * moments[0] + (1.0 - beta_first) * gradient
    second = beta_second * moments[1] + (1.0 - beta_second) * gradient * gradient
    first_hat = first / (1.0 - beta_first**ADAM_STEP)
    second_hat = second / (1.0 - beta_second**ADAM_STEP)
    change = -learn_rate * (first_hat / (jnp.sqrt(second_hat) + epsilon_adam) + decay_rate * weight)
    return (change, jnp.stack([first, second]))


def body(
    plan,
    inputs,
    cotangent,
    project_in,
    project_out,
    expand_weight,
    shrink_weight,
    expand_bias,
    vectors,
    moments_in,
    moments_out,
    moments_expand,
    moments_shrink,
    moments_bias,
    moments_vectors,
):
    clip_count, frame_count, model_width = inputs.shape
    row_count = clip_count * frame_count
    head_count = HEADS
    shard_rows = project_in.shape[0]
    wide_in = project_in.shape[1]
    ff_width = expand_weight.shape[1]
    swap = [(0, 1), (1, 0)]
    everyone = ("clip", "frame")

    small = jnp.concatenate(
        [
            vectors,
            expand_bias.reshape(shard_rows, -1),
            jnp.zeros((shard_rows, 128 - vectors.shape[1] - expand_bias.shape[0] // shard_rows), jnp.float32),
        ],
        axis=1,
    )
    first_pack = jnp.concatenate([project_in, small], axis=1).astype(jnp.bfloat16)
    ff_per_row = ff_width // model_width
    expand_local = expand_weight.reshape(shard_rows, model_width, ff_per_row)
    expand_local = jnp.swapaxes(expand_local, 1, 2).reshape(shard_rows, ff_width)
    second_pack = jnp.concatenate(
        [project_out, expand_local, shrink_weight.reshape(shard_rows, -1)], axis=1
    ).astype(jnp.bfloat16)
    first_full = lax.all_gather(first_pack, everyone, axis=0, tiled=True)
    second_full = lax.all_gather(second_pack, everyone, axis=0, tiled=True)
    full_in = first_full[:, :wide_in]
    small_full = first_full[:, wide_in:].astype(jnp.float32)
    column_set = small_full[:, : vectors.shape[1]]
    full_bias = small_full[:, vectors.shape[1] : vectors.shape[1] + ff_width // model_width].T.reshape(-1)
    full_out = second_full[:, :model_width]
    full_expand = second_full[:, model_width : model_width + ff_width]
    shrink_blocks = second_full[:, model_width + ff_width :].reshape(
        model_width, ff_width // model_width, model_width
    )

    frames_rows = inputs.reshape(row_count, model_width).astype(jnp.float32)
    normed_first, plain_first, inv_first = norm_parts(
        frames_rows, column_set[:, 0], column_set[:, 1]
    )
    hidden_first = normed_first.astype(jnp.bfloat16)
    partner_rows = lax.ppermute(inputs, "frame", swap).reshape(row_count, model_width)
    hidden_partner = norm_parts(
        partner_rows.astype(jnp.float32), column_set[:, 0], column_set[:, 1]
    )[0].astype(jnp.bfloat16)
    bias_in = jnp.concatenate(
        [column_set[:, 2], jnp.zeros((model_width,), jnp.float32), column_set[:, 3]]
    )
    projected = (
        jnp.dot(hidden_first, full_in, preferred_element_type=jnp.float32) + bias_in
    ).astype(jnp.bfloat16)
    partner_pairs = (
        jnp.dot(hidden_partner, full_in[:, model_width:], preferred_element_type=jnp.float32)
        + bias_in[model_width:]
    ).astype(jnp.bfloat16)
    queries = projected[:, :model_width].reshape(clip_count, frame_count, model_width)
    clip_pairs = jnp.concatenate([projected[:, model_width:], partner_pairs], axis=0).reshape(
        clip_count, 2 * frame_count, 2 * model_width
    )
    score_scale = 1.0 / math.sqrt(model_width // head_count)
    scaled_queries = (projected[:, :model_width] * score_scale).astype(jnp.bfloat16)
    pair_rows = clip_pairs.reshape(2 * row_count, 2 * model_width)
    mixed_low, log_totals = attention_pallas(scaled_queries, pair_rows)
    attended = jnp.dot(mixed_low, full_out, preferred_element_type=jnp.float32) + column_set[:, 4]
    residual = frames_rows + attended
    normed_second, plain_second, inv_second = norm_parts(
        residual, column_set[:, 5], column_set[:, 6]
    )
    hidden_second = normed_second.astype(jnp.bfloat16)
    preact = jnp.dot(hidden_second, full_expand, preferred_element_type=jnp.float32) + full_bias
    activated = gelu_exact(preact).astype(jnp.bfloat16)
    activated_blocks = activated.reshape(row_count, ff_width // model_width, model_width)
    result = (
        residual
        + jnp.einsum(
            "tjr,rjc->tc", activated_blocks, shrink_blocks, preferred_element_type=jnp.float32
        )
        + column_set[:, 7]
    )
    output = result.astype(jnp.bfloat16).reshape(inputs.shape)

    grad_result = cotangent.reshape(row_count, model_width)
    grad_shrink_term = jnp.einsum(
        "tjr,tc->rjc", activated_blocks, grad_result, preferred_element_type=jnp.float32
    ).astype(jnp.bfloat16)
    grad_down_bias = jnp.sum(grad_result.astype(jnp.float32), axis=0)
    grad_activated = jnp.einsum(
        "tc,rjc->tjr", grad_result, shrink_blocks, preferred_element_type=jnp.float32
    ).reshape(row_count, ff_width)
    grad_preact = (grad_activated * gelu_slope(preact)).astype(jnp.bfloat16)
    grad_expand_term = jnp.dot(
        hidden_second.T, grad_preact, preferred_element_type=jnp.float32
    ).astype(jnp.bfloat16)
    grad_bias_term = jnp.sum(grad_preact.astype(jnp.float32), axis=0)
    grad_hidden_second = jnp.dot(grad_preact, full_expand.T, preferred_element_type=jnp.float32)
    norm_term_second, gain_second, shift_second = norm_backward(
        grad_hidden_second, plain_second, inv_second, column_set[:, 5]
    )
    grad_residual = grad_result.astype(jnp.float32) + norm_term_second
    grad_attended = grad_residual.astype(jnp.bfloat16)
    grad_out_term = jnp.dot(
        mixed_low.T, grad_attended, preferred_element_type=jnp.float32
    ).astype(jnp.bfloat16)
    grad_out_bias = jnp.sum(grad_attended.astype(jnp.float32), axis=0)
    late_terms = jnp.concatenate(
        [grad_shrink_term.reshape(model_width, -1), grad_expand_term, grad_out_term], axis=1
    )
    grad_mixed = jnp.dot(grad_attended, full_out.T, preferred_element_type=jnp.float32).astype(
        jnp.bfloat16
    )
    def first_backward_half(tied):
        mixed_grads = tied[0]
        first = attention_pallas(
            scaled_queries, pair_rows, mixed_grads, log_totals, 0, model_width // 256
        )
        send = jnp.concatenate([first[1], first[2]], axis=1)[row_count:].astype(jnp.bfloat16)
        return (first, send, mixed_grads)

    bit_count, core_bit, rotated_orders, late_orders = plan
    owned_late, tied = tree_reduce_scatter(
        late_terms,
        (3456, 3456),
        late_orders,
        (bit_count, core_bit),
        {0: lambda tied: grad_mixed, 1: first_backward_half},
    )
    first_half, first_send, grad_mixed = tied[1]
    halves = []
    half_pairs = model_width // 256
    for first_pair in (0, half_pairs):
        if first_pair == 0:
            grad_query, grad_keys, grad_values = first_half
            send = first_send
        else:
            grad_query, grad_keys, grad_values = attention_pallas(
                scaled_queries, pair_rows, grad_mixed, log_totals, first_pair, half_pairs
            )
            send = jnp.concatenate([grad_keys, grad_values], axis=1)[row_count:].astype(jnp.bfloat16)
        terms = jnp.concatenate([grad_keys, grad_values], axis=1)
        returned = lax.ppermute(send, "frame", swap)
        halves.append((grad_query, terms[:row_count] + returned.astype(jnp.float32)))
    half_width = model_width // 2
    grad_projected = jnp.concatenate(
        [
            (jnp.concatenate([halves[0][0], halves[1][0]], axis=1) * score_scale).astype(jnp.bfloat16),
            jnp.concatenate(
                [
                    halves[0][1][:, :half_width],
                    halves[1][1][:, :half_width],
                    halves[0][1][:, half_width:],
                    halves[1][1][:, half_width:],
                ],
                axis=1,
            ).astype(jnp.bfloat16),
        ],
        axis=1,
    )
    grad_in_term = jnp.dot(hidden_first.T, grad_projected, preferred_element_type=jnp.float32)
    projected_sums = jnp.sum(grad_projected.astype(jnp.float32), axis=0)
    grad_query_bias = projected_sums[:model_width]
    grad_value_bias = projected_sums[2 * model_width :]
    grad_hidden_first = jnp.dot(grad_projected, full_in.T, preferred_element_type=jnp.float32)
    norm_term_first, gain_first, shift_first = norm_backward(
        grad_hidden_first, plain_first, inv_first, column_set[:, 0]
    )
    grad_inputs = (grad_residual + norm_term_first).astype(jnp.bfloat16).reshape(inputs.shape)
    grad_columns = jnp.stack(
        [
            gain_first,
            shift_first,
            grad_query_bias,
            grad_value_bias,
            grad_out_bias,
            gain_second,
            shift_second,
            grad_down_bias,
        ],
        axis=1,
    )
    small_grads = jnp.concatenate(
        [
            grad_columns,
            grad_bias_term.reshape(-1, model_width).T,
            jnp.zeros((model_width, 128 - 12), jnp.float32),
        ],
        axis=1,
    )
    owned_first = tree_reduce_scatter(
        jnp.concatenate([grad_in_term, small_grads], axis=1),
        (896, 768, 768),
        rotated_orders,
        (bit_count, core_bit),
    )[0]
    owned_in = owned_first[:, :wide_in]
    owned_vectors = owned_first[:, wide_in : wide_in + vectors.shape[1]]
    owned_bias = owned_first[:, wide_in + vectors.shape[1] : wide_in + 12].reshape(-1)
    owned_shrink = owned_late[:, :ff_width].reshape(shrink_weight.shape)
    owned_expand = jnp.swapaxes(
        owned_late[:, ff_width : 2 * ff_width].reshape(shard_rows, ff_per_row, model_width), 1, 2
    ).reshape(shard_rows, ff_width)
    owned_out = owned_late[:, 2 * ff_width :]
    new_in, mom_in = adam_step(project_in, moments_in, owned_in)
    new_out, mom_out = adam_step(project_out, moments_out, owned_out)
    new_expand, mom_expand = adam_step(expand_weight, moments_expand, owned_expand)
    new_shrink, mom_shrink = adam_step(shrink_weight, moments_shrink, owned_shrink)
    new_bias, mom_bias = adam_step(expand_bias, moments_bias, owned_bias)
    new_vectors, mom_vectors = adam_step(vectors, moments_vectors, owned_vectors)
    return (
        output,
        grad_inputs,
        owned_in,
        owned_out,
        owned_expand,
        owned_shrink,
        owned_bias,
        owned_vectors,
        new_in,
        new_out,
        new_expand,
        new_shrink,
        new_bias,
        new_vectors,
        mom_in,
        mom_out,
        mom_expand,
        mom_shrink,
        mom_bias,
        mom_vectors,
    )


def solution(mesh):
    in_specs = (
        P("clip", "frame", None),
        P("clip", "frame", None),
        P(("clip", "frame"), None),
        P(("clip", "frame"), None),
        P(("clip", "frame"), None),
        P(("clip", "frame"), None),
        P(("clip", "frame")),
        P(("clip", "frame"), None),
        P(None, ("clip", "frame"), None),
        P(None, ("clip", "frame"), None),
        P(None, ("clip", "frame"), None),
        P(None, ("clip", "frame"), None),
        P(None, ("clip", "frame")),
        P(None, ("clip", "frame"), None),
    )
    out_specs = (
        P("clip", "frame", None),
        P("clip", "frame", None),
        P(("clip", "frame"), None),
        P(("clip", "frame"), None),
        P(("clip", "frame"), None),
        P(("clip", "frame"), None),
        P(("clip", "frame")),
        P(("clip", "frame"), None),
        P(("clip", "frame"), None),
        P(("clip", "frame"), None),
        P(("clip", "frame"), None),
        P(("clip", "frame"), None),
        P(("clip", "frame")),
        P(("clip", "frame"), None),
        P(None, ("clip", "frame"), None),
        P(None, ("clip", "frame"), None),
        P(None, ("clip", "frame"), None),
        P(None, ("clip", "frame"), None),
        P(None, ("clip", "frame")),
        P(None, ("clip", "frame"), None),
    )
    return jax.shard_map(
        functools.partial(body, link_plan(mesh)),
        mesh=mesh,
        in_specs=in_specs,
        out_specs=out_specs,
        check_vma=False,
    )
```

```python
import functools
import math

import jax
import jax.numpy as jnp
from jax import lax
from jax.experimental import pallas as pl
from jax.experimental.pallas import tpu as pltpu
from jax.sharding import PartitionSpec as P

HEADS = 12
ADAM_STEP = 4


epsilon_norm = 1e-05
beta_first = 0.9
beta_second = 0.99
learn_rate = 0.03
decay_rate = 0.01
epsilon_adam = 1e-08
root_half = 0.7071067811865476
inv_root_two_pi = 0.3989422804014327


def norm_parts(inputs, norm_gain, norm_shift):
    average = jnp.mean(inputs, axis=-1, keepdims=True)
    centered = inputs - average
    spread = jnp.mean(centered * centered, axis=-1, keepdims=True)
    inv_std = lax.rsqrt(spread + epsilon_norm)
    normed = centered * inv_std
    return (normed * norm_gain + norm_shift, normed, inv_std)


def norm_backward(grad_normed, normed, inv_std, norm_gain):
    grad_gain = jnp.sum(grad_normed * normed, axis=0)
    grad_shift = jnp.sum(grad_normed, axis=0)
    scaled = grad_normed * norm_gain
    grad_input = inv_std * (
        scaled
        - jnp.mean(scaled, axis=-1, keepdims=True)
        - normed * jnp.mean(scaled * normed, axis=-1, keepdims=True)
    )
    return (grad_input, grad_gain, grad_shift)


def gelu_exact(inputs):
    return 0.5 * inputs * (1.0 + jax.scipy.special.erf(inputs * root_half))


def gelu_slope(inputs):
    return (
        0.5 * (1.0 + jax.scipy.special.erf(inputs * root_half))
        + inputs * jnp.exp(-0.5 * inputs * inputs) * inv_root_two_pi
    )


QUERY_CHUNK = 256
MASKED = -1e30


def attention_forward_kernel(q_ref, k_ref, v_ref, kbias_ref, o_ref, l_ref):
    head_size = q_ref.shape[1] // 2
    rows = q_ref.shape[0]
    kbias = kbias_ref[...]
    lane = lax.broadcasted_iota(jnp.int32, (QUERY_CHUNK, 2 * head_size), 1)
    for chunk in range(rows // QUERY_CHUNK):
        span = pl.ds(chunk * QUERY_CHUNK, QUERY_CHUNK)
        mixed_parts = []
        totals = []
        for half in range(2):
            cols = pl.ds(half * head_size, head_size)
            query = q_ref[span, cols]
            key = k_ref[:, cols]
            value = v_ref[:, cols]
            scores = (
                lax.dot_general(
                    query, key, (((1,), (1,)), ((), ())), preferred_element_type=jnp.float32
                )
                + kbias
            )
            highest = jnp.max(scores, axis=1, keepdims=True)
            exponent = jnp.exp(scores - highest)
            denominator = jnp.sum(exponent, axis=1, keepdims=True)
            weights = (exponent * (1.0 / denominator)).astype(jnp.bfloat16)
            mixed_parts.append(jnp.dot(weights, value, preferred_element_type=jnp.float32))
            totals.append(highest + jnp.log(denominator))
        o_ref[span, :] = jnp.concatenate(mixed_parts, axis=1).astype(o_ref.dtype)
        l_ref[span, :] = jnp.where(lane < head_size, totals[0], totals[1])


def attention_backward_kernel(
    q_ref, k_ref, v_ref, do_ref, l_ref, kbias_ref, dq_ref, dk_ref, dv_ref
):
    head_size = q_ref.shape[1] // 2
    rows = q_ref.shape[0]
    kbias = kbias_ref[...]
    for half in range(2):
        cols = pl.ds(half * head_size, head_size)
        key = k_ref[:, cols]
        value = v_ref[:, cols]
        grad_key = None
        grad_value = None
        for chunk in range(rows // QUERY_CHUNK):
            span = pl.ds(chunk * QUERY_CHUNK, QUERY_CHUNK)
            query = q_ref[span, cols]
            grad_out = do_ref[span, cols]
            total = l_ref[span, pl.ds(half * head_size, 1)]
            scores = (
                lax.dot_general(
                    query, key, (((1,), (1,)), ((), ())), preferred_element_type=jnp.float32
                )
                + kbias
            )
            weights = jnp.exp(scores - total)
            grad_weights = lax.dot_general(
                grad_out, value, (((1,), (1,)), ((), ())), preferred_element_type=jnp.float32
            )
            delta = jnp.sum(weights * grad_weights, axis=1, keepdims=True)
            grad_scores = (weights * (grad_weights - delta)).astype(jnp.bfloat16)
            dq_ref[span, cols] = jnp.dot(
                grad_scores, key, preferred_element_type=jnp.float32
            ).astype(dq_ref.dtype)
            key_part = lax.dot_general(
                grad_scores, query, (((0,), (0,)), ((), ())), preferred_element_type=jnp.float32
            )
            value_part = lax.dot_general(
                weights.astype(jnp.bfloat16),
                grad_out,
                (((0,), (0,)), ((), ())),
                preferred_element_type=jnp.float32,
            )
            grad_key = key_part if grad_key is None else grad_key + key_part
            grad_value = value_part if grad_value is None else grad_value + value_part
        dk_ref[:, cols] = grad_key
        dv_ref[:, cols] = grad_value


def pad_rows(values, rows):
    return jnp.pad(values, ((0, rows - values.shape[0]), (0, 0)))


def attention_pallas(queries, pairs, grad_out=None, totals=None, first_pair=0, pair_span=None):
    query_rows, model_width = queries.shape
    key_rows = pairs.shape[0]
    padded_q = -(-query_rows // QUERY_CHUNK) * QUERY_CHUNK
    padded_k = -(-key_rows // 128) * 128
    pair_count = model_width // 128
    q_pad = pad_rows(queries, padded_q)
    kv_pad = pad_rows(pairs, padded_k)
    kbias = jnp.where(jnp.arange(padded_k) < key_rows, 0.0, MASKED).astype(jnp.float32)[None, :]
    q_spec = pl.BlockSpec((padded_q, 128), lambda j: (0, j))
    k_spec = pl.BlockSpec((padded_k, 128), lambda j: (0, j))
    v_spec = pl.BlockSpec((padded_k, 128), lambda j: (0, j + pair_count))
    b_spec = pl.BlockSpec((1, padded_k), lambda j: (0, 0))
    params = pltpu.CompilerParams(vmem_limit_bytes=48 * 1024 * 1024)
    if grad_out is None:
        mixed, log_totals = pl.pallas_call(
            attention_forward_kernel,
            grid=(pair_count,),
            in_specs=[q_spec, k_spec, v_spec, b_spec],
            out_specs=[q_spec, q_spec],
            out_shape=[
                jax.ShapeDtypeStruct((padded_q, model_width), jnp.bfloat16),
                jax.ShapeDtypeStruct((padded_q, model_width), jnp.float32),
            ],
            compiler_params=params,
        )(q_pad, kv_pad, kv_pad, kbias)
        return mixed[:query_rows], log_totals
    do_pad = pad_rows(grad_out, padded_q)
    span = pair_count if pair_span is None else pair_span
    qi_spec = pl.BlockSpec((padded_q, 128), lambda j: (0, j + first_pair))
    ki_spec = pl.BlockSpec((padded_k, 128), lambda j: (0, j + first_pair))
    vi_spec = pl.BlockSpec((padded_k, 128), lambda j: (0, j + first_pair + pair_count))
    qo_spec = pl.BlockSpec((padded_q, 128), lambda j: (0, j))
    ko_spec = pl.BlockSpec((padded_k, 128), lambda j: (0, j))
    dq, dk, dv = pl.pallas_call(
        attention_backward_kernel,
        grid=(span,),
        in_specs=[qi_spec, ki_spec, vi_spec, qi_spec, qi_spec, b_spec],
        out_specs=[qo_spec, ko_spec, ko_spec],
        out_shape=[
            jax.ShapeDtypeStruct((padded_q, 128 * span), jnp.float32),
            jax.ShapeDtypeStruct((padded_k, 128 * span), jnp.float32),
            jax.ShapeDtypeStruct((padded_k, 128 * span), jnp.float32),
        ],
        compiler_params=params,
    )(q_pad, kv_pad, kv_pad, do_pad, totals, kbias)
    return dq[:query_rows], dk[:key_rows], dv[:key_rows]


def attend_forward(queries, keys_values, head_count):
    model_width = queries.shape[2]
    head_size = model_width // head_count
    score_scale = 1.0 / math.sqrt(head_size)

    def one_head(head_index):
        offset = head_index * head_size
        query_block = lax.dynamic_slice_in_dim(queries, offset, head_size, 2)
        key_block = lax.dynamic_slice_in_dim(keys_values, offset, head_size, 2)
        value_block = lax.dynamic_slice_in_dim(keys_values, model_width + offset, head_size, 2)
        scores = (
            jnp.einsum("cqd,ckd->cqk", query_block, key_block, preferred_element_type=jnp.float32)
            * score_scale
        )
        highest = jnp.max(scores, axis=-1, keepdims=True)
        exponent = jnp.exp(scores - highest)
        denominator = jnp.sum(exponent, axis=-1, keepdims=True)
        weights_soft = (exponent / denominator).astype(jnp.bfloat16)
        mixed = jnp.einsum(
            "cqk,ckd->cqd", weights_soft, value_block, preferred_element_type=jnp.float32
        )
        return (mixed, (highest + jnp.log(denominator))[..., 0])

    mixed, log_totals = lax.map(one_head, jnp.arange(head_count))
    clip_count, frame_count = (queries.shape[0], queries.shape[1])
    mixed = jnp.transpose(mixed, (1, 2, 0, 3)).reshape(clip_count, frame_count, model_width)
    return (mixed, log_totals)


def attend_backward(queries, keys_values, grad_mixed, log_totals, head_count):
    model_width = queries.shape[2]
    head_size = model_width // head_count
    score_scale = 1.0 / math.sqrt(head_size)

    def one_head_back(head_index):
        offset = head_index * head_size
        query_block = lax.dynamic_slice_in_dim(queries, offset, head_size, 2)
        key_block = lax.dynamic_slice_in_dim(keys_values, offset, head_size, 2)
        value_block = lax.dynamic_slice_in_dim(keys_values, model_width + offset, head_size, 2)
        grad_block = lax.dynamic_slice_in_dim(grad_mixed, offset, head_size, 2)
        totals = lax.dynamic_index_in_dim(log_totals, head_index, 0, keepdims=False)
        scores = (
            jnp.einsum("cqd,ckd->cqk", query_block, key_block, preferred_element_type=jnp.float32)
            * score_scale
        )
        weights_soft = jnp.exp(scores - totals[..., None])
        grad_weights = jnp.einsum(
            "cqd,ckd->cqk", grad_block, value_block, preferred_element_type=jnp.float32
        )
        delta = jnp.sum(weights_soft * grad_weights, axis=-1, keepdims=True)
        grad_scores = (weights_soft * (grad_weights - delta)).astype(jnp.bfloat16)
        grad_query = (
            jnp.einsum("cqk,ckd->cqd", grad_scores, key_block, preferred_element_type=jnp.float32)
            * score_scale
        )
        grad_key = (
            jnp.einsum("cqk,cqd->ckd", grad_scores, query_block, preferred_element_type=jnp.float32)
            * score_scale
        )
        grad_value = jnp.einsum(
            "cqk,cqd->ckd",
            weights_soft.astype(jnp.bfloat16),
            grad_block,
            preferred_element_type=jnp.float32,
        )
        return (grad_query, delta[..., 0], grad_key, grad_value)

    pieces = lax.map(one_head_back, jnp.arange(head_count))
    clip_count, frame_count = (queries.shape[0], queries.shape[1])
    clip_frames = keys_values.shape[1]
    grad_query = jnp.transpose(pieces[0], (1, 2, 0, 3)).reshape(
        clip_count, frame_count, model_width
    )
    grad_key = jnp.transpose(pieces[2], (1, 2, 0, 3)).reshape(clip_count, clip_frames, model_width)
    grad_value = jnp.transpose(pieces[3], (1, 2, 0, 3)).reshape(
        clip_count, clip_frames, model_width
    )
    return (grad_query, pieces[1], jnp.concatenate([grad_key, grad_value], axis=2))


def link_plan(mesh):
    devices = list(mesh.devices.reshape(-1))
    bit_count = len(devices).bit_length() - 1
    core_bit = 1
    for bit in range(bit_count):
        first, other = devices[0], devices[1 << bit]
        if getattr(first, "coords", None) is not None and tuple(first.coords) == tuple(other.coords):
            core_bit = bit
    others = [bit for bit in range(bit_count) if bit != core_bit]
    near, far = others[:-1], others[-1:]
    rotated = tuple(tuple(near[k:] + near[:k] + far) for k in range(3))
    inner = [bit for bit in near if bit != 0]
    late = tuple(tuple(inner[k:] + inner[:k] + [0] + far) for k in range(2))
    return bit_count, core_bit, rotated, late


def tree_reduce_scatter(terms, part_columns, orders, plan_bits, hooks=None):
    hooks = dict(hooks or {})
    tied = {}
    bit_count, core_bit = plan_bits
    device = lax.axis_index("clip") * lax.axis_size("frame") + lax.axis_index("frame")
    blocks = 1 << bit_count
    block_rows = terms.shape[0] // blocks
    data = terms.reshape((2,) * bit_count + (block_rows, terms.shape[1]))
    parts = [(data, list(range(bit_count - 1, -1, -1)))]
    plan = [(core_bit,)] + [tuple(order[stage] for order in orders) for stage in range(len(orders[0]))]
    for stage, stage_bits in enumerate(plan):
        if stage == 1:
            whole, bits = parts[0]
            parts = []
            offset = 0
            for width in part_columns:
                parts.append((whole[..., offset : offset + width], bits))
                offset += width
        keeps, sends = [], []
        for (part, part_bits), bit in zip(parts, stage_bits):
            axis = part_bits.index(bit)
            mine = (device >> bit) & 1
            keeps.append(lax.dynamic_index_in_dim(part, mine, axis=axis, keepdims=False))
            sends.append(
                lax.dynamic_index_in_dim(part, 1 - mine, axis=axis, keepdims=False).astype(jnp.bfloat16)
            )
        if stage in hooks:
            sends, tied[stage] = lax.optimization_barrier((sends, hooks[stage](tied)))
        new_parts = []
        for keep, send, (part, part_bits), bit in zip(keeps, sends, parts, stage_bits):
            pairs = [(index, index ^ (1 << bit)) for index in range(blocks)]
            got = lax.ppermute(send, ("clip", "frame"), pairs)
            new_parts.append((keep + got.astype(jnp.float32), [b for b in part_bits if b != bit]))
        parts = new_parts
    return jnp.concatenate([part for part, _ in parts], axis=-1).astype(jnp.float32), tied


def adam_step(weight, moments, gradient):
    first = beta_first * moments[0] + (1.0 - beta_first) * gradient
    second = beta_second * moments[1] + (1.0 - beta_second) * gradient * gradient
    first_hat = first / (1.0 - beta_first**ADAM_STEP)
    second_hat = second / (1.0 - beta_second**ADAM_STEP)
    change = -learn_rate * (first_hat / (jnp.sqrt(second_hat) + epsilon_adam) + decay_rate * weight)
    return (change, jnp.stack([first, second]))


def body(
    plan,
    inputs,
    cotangent,
    project_in,
    project_out,
    expand_weight,
    shrink_weight,
    expand_bias,
    vectors,
    moments_in,
    moments_out,
    moments_expand,
    moments_shrink,
    moments_bias,
    moments_vectors,
):
    clip_count, frame_count, model_width = inputs.shape
    row_count = clip_count * frame_count
    head_count = HEADS
    shard_rows = project_in.shape[0]
    wide_in = project_in.shape[1]
    ff_width = expand_weight.shape[1]
    swap = [(0, 1), (1, 0)]
    everyone = ("clip", "frame")

    small = jnp.concatenate(
        [
            vectors,
            expand_bias.reshape(shard_rows, -1),
            jnp.zeros((shard_rows, 128 - vectors.shape[1] - expand_bias.shape[0] // shard_rows), jnp.float32),
        ],
        axis=1,
    )
    first_pack = jnp.concatenate([project_in, small], axis=1).astype(jnp.bfloat16)
    second_pack = jnp.concatenate(
        [project_out, expand_weight, shrink_weight.reshape(shard_rows, -1)], axis=1
    ).astype(jnp.bfloat16)
    first_full = lax.all_gather(first_pack, everyone, axis=0, tiled=True)
    second_full = lax.all_gather(second_pack, everyone, axis=0, tiled=True)
    full_in = first_full[:, :wide_in]
    small_full = first_full[:, wide_in:].astype(jnp.float32)
    column_set = small_full[:, : vectors.shape[1]]
    full_bias = small_full[:, vectors.shape[1] : vectors.shape[1] + ff_width // model_width].reshape(-1)
    full_out = second_full[:, :model_width]
    full_expand = second_full[:, model_width : model_width + ff_width]
    full_shrink = second_full[:, model_width + ff_width :].reshape(ff_width, model_width)

    frames_rows = inputs.reshape(row_count, model_width).astype(jnp.float32)
    normed_first, plain_first, inv_first = norm_parts(
        frames_rows, column_set[:, 0], column_set[:, 1]
    )
    hidden_first = normed_first.astype(jnp.bfloat16)
    partner_rows = lax.ppermute(inputs, "frame", swap).reshape(row_count, model_width)
    hidden_partner = norm_parts(
        partner_rows.astype(jnp.float32), column_set[:, 0], column_set[:, 1]
    )[0].astype(jnp.bfloat16)
    bias_in = jnp.concatenate(
        [column_set[:, 2], jnp.zeros((model_width,), jnp.float32), column_set[:, 3]]
    )
    projected = (
        jnp.dot(hidden_first, full_in, preferred_element_type=jnp.float32) + bias_in
    ).astype(jnp.bfloat16)
    partner_pairs = (
        jnp.dot(hidden_partner, full_in[:, model_width:], preferred_element_type=jnp.float32)
        + bias_in[model_width:]
    ).astype(jnp.bfloat16)
    queries = projected[:, :model_width].reshape(clip_count, frame_count, model_width)
    clip_pairs = jnp.concatenate([projected[:, model_width:], partner_pairs], axis=0).reshape(
        clip_count, 2 * frame_count, 2 * model_width
    )
    score_scale = 1.0 / math.sqrt(model_width // head_count)
    scaled_queries = (projected[:, :model_width] * score_scale).astype(jnp.bfloat16)
    pair_rows = clip_pairs.reshape(2 * row_count, 2 * model_width)
    mixed_low, log_totals = attention_pallas(scaled_queries, pair_rows)
    attended = jnp.dot(mixed_low, full_out, preferred_element_type=jnp.float32) + column_set[:, 4]
    residual = frames_rows + attended
    normed_second, plain_second, inv_second = norm_parts(
        residual, column_set[:, 5], column_set[:, 6]
    )
    hidden_second = normed_second.astype(jnp.bfloat16)
    preact = jnp.dot(hidden_second, full_expand, preferred_element_type=jnp.float32) + full_bias
    activated = gelu_exact(preact).astype(jnp.bfloat16)
    result = (
        residual
        + jnp.dot(activated, full_shrink, preferred_element_type=jnp.float32)
        + column_set[:, 7]
    )
    output = result.astype(jnp.bfloat16).reshape(inputs.shape)

    grad_result = cotangent.reshape(row_count, model_width)
    grad_shrink_term = jnp.dot(
        activated.T, grad_result, preferred_element_type=jnp.float32
    ).astype(jnp.bfloat16)
    grad_down_bias = jnp.sum(grad_result.astype(jnp.float32), axis=0)
    grad_activated = jnp.dot(grad_result, full_shrink.T, preferred_element_type=jnp.float32)
    grad_preact = (grad_activated * gelu_slope(preact)).astype(jnp.bfloat16)
    grad_expand_term = jnp.dot(
        hidden_second.T, grad_preact, preferred_element_type=jnp.float32
    ).astype(jnp.bfloat16)
    grad_bias_term = jnp.sum(grad_preact.astype(jnp.float32), axis=0)
    grad_hidden_second = jnp.dot(grad_preact, full_expand.T, preferred_element_type=jnp.float32)
    norm_term_second, gain_second, shift_second = norm_backward(
        grad_hidden_second, plain_second, inv_second, column_set[:, 5]
    )
    grad_residual = grad_result.astype(jnp.float32) + norm_term_second
    grad_attended = grad_residual.astype(jnp.bfloat16)
    grad_out_term = jnp.dot(
        mixed_low.T, grad_attended, preferred_element_type=jnp.float32
    ).astype(jnp.bfloat16)
    grad_out_bias = jnp.sum(grad_attended.astype(jnp.float32), axis=0)
    late_terms = jnp.concatenate(
        [grad_shrink_term.reshape(model_width, -1), grad_expand_term, grad_out_term], axis=1
    )
    grad_mixed = jnp.dot(grad_attended, full_out.T, preferred_element_type=jnp.float32).astype(
        jnp.bfloat16
    )
    def first_backward_half(tied):
        mixed_grads = tied[0]
        first = attention_pallas(
            scaled_queries, pair_rows, mixed_grads, log_totals, 0, model_width // 256
        )
        send = jnp.concatenate([first[1], first[2]], axis=1)[row_count:].astype(jnp.bfloat16)
        return (first, send, mixed_grads)

    bit_count, core_bit, rotated_orders, late_orders = plan
    owned_late, tied = tree_reduce_scatter(
        late_terms,
        (3456, 3456),
        late_orders,
        (bit_count, core_bit),
        {0: lambda tied: grad_mixed, 1: first_backward_half},
    )
    first_half, first_send, grad_mixed = tied[1]
    halves = []
    half_pairs = model_width // 256
    for first_pair in (0, half_pairs):
        if first_pair == 0:
            grad_query, grad_keys, grad_values = first_half
            send = first_send
        else:
            grad_query, grad_keys, grad_values = attention_pallas(
                scaled_queries, pair_rows, grad_mixed, log_totals, first_pair, half_pairs
            )
            send = jnp.concatenate([grad_keys, grad_values], axis=1)[row_count:].astype(jnp.bfloat16)
        terms = jnp.concatenate([grad_keys, grad_values], axis=1)
        returned = lax.ppermute(send, "frame", swap)
        halves.append((grad_query, terms[:row_count] + returned.astype(jnp.float32)))
    half_width = model_width // 2
    grad_projected = jnp.concatenate(
        [
            (jnp.concatenate([halves[0][0], halves[1][0]], axis=1) * score_scale).astype(jnp.bfloat16),
            jnp.concatenate(
                [
                    halves[0][1][:, :half_width],
                    halves[1][1][:, :half_width],
                    halves[0][1][:, half_width:],
                    halves[1][1][:, half_width:],
                ],
                axis=1,
            ).astype(jnp.bfloat16),
        ],
        axis=1,
    )
    grad_in_term = jnp.dot(hidden_first.T, grad_projected, preferred_element_type=jnp.float32)
    projected_sums = jnp.sum(grad_projected.astype(jnp.float32), axis=0)
    grad_query_bias = projected_sums[:model_width]
    grad_value_bias = projected_sums[2 * model_width :]
    grad_hidden_first = jnp.dot(grad_projected, full_in.T, preferred_element_type=jnp.float32)
    norm_term_first, gain_first, shift_first = norm_backward(
        grad_hidden_first, plain_first, inv_first, column_set[:, 0]
    )
    grad_inputs = (grad_residual + norm_term_first).astype(jnp.bfloat16).reshape(inputs.shape)
    grad_columns = jnp.stack(
        [
            gain_first,
            shift_first,
            grad_query_bias,
            grad_value_bias,
            grad_out_bias,
            gain_second,
            shift_second,
            grad_down_bias,
        ],
        axis=1,
    )
    small_grads = jnp.concatenate(
        [
            grad_columns,
            grad_bias_term.reshape(model_width, -1),
            jnp.zeros((model_width, 128 - 12), jnp.float32),
        ],
        axis=1,
    )
    owned_first = tree_reduce_scatter(
        jnp.concatenate([grad_in_term, small_grads], axis=1),
        (896, 768, 768),
        rotated_orders,
        (bit_count, core_bit),
    )[0]
    owned_in = owned_first[:, :wide_in]
    owned_vectors = owned_first[:, wide_in : wide_in + vectors.shape[1]]
    owned_bias = owned_first[:, wide_in + vectors.shape[1] : wide_in + 12].reshape(-1)
    owned_shrink = owned_late[:, :ff_width].reshape(shrink_weight.shape)
    owned_expand = owned_late[:, ff_width : 2 * ff_width]
    owned_out = owned_late[:, 2 * ff_width :]
    new_in, mom_in = adam_step(project_in, moments_in, owned_in)
    new_out, mom_out = adam_step(project_out, moments_out, owned_out)
    new_expand, mom_expand = adam_step(expand_weight, moments_expand, owned_expand)
    new_shrink, mom_shrink = adam_step(shrink_weight, moments_shrink, owned_shrink)
    new_bias, mom_bias = adam_step(expand_bias, moments_bias, owned_bias)
    new_vectors, mom_vectors = adam_step(vectors, moments_vectors, owned_vectors)
    return (
        output,
        grad_inputs,
        owned_in,
        owned_out,
        owned_expand,
        owned_shrink,
        owned_bias,
        owned_vectors,
        new_in,
        new_out,
        new_expand,
        new_shrink,
        new_bias,
        new_vectors,
        mom_in,
        mom_out,
        mom_expand,
        mom_shrink,
        mom_bias,
        mom_vectors,
    )


def solution(mesh):
    in_specs = (
        P("clip", "frame", None),
        P("clip", "frame", None),
        P(("clip", "frame"), None),
        P(("clip", "frame"), None),
        P(("clip", "frame"), None),
        P(("clip", "frame"), None),
        P(("clip", "frame")),
        P(("clip", "frame"), None),
        P(None, ("clip", "frame"), None),
        P(None, ("clip", "frame"), None),
        P(None, ("clip", "frame"), None),
        P(None, ("clip", "frame"), None),
        P(None, ("clip", "frame")),
        P(None, ("clip", "frame"), None),
    )
    out_specs = (
        P("clip", "frame", None),
        P("clip", "frame", None),
        P(("clip", "frame"), None),
        P(("clip", "frame"), None),
        P(("clip", "frame"), None),
        P(("clip", "frame"), None),
        P(("clip", "frame")),
        P(("clip", "frame"), None),
        P(("clip", "frame"), None),
        P(("clip", "frame"), None),
        P(("clip", "frame"), None),
        P(("clip", "frame"), None),
        P(("clip", "frame")),
        P(("clip", "frame"), None),
        P(None, ("clip", "frame"), None),
        P(None, ("clip", "frame"), None),
        P(None, ("clip", "frame"), None),
        P(None, ("clip", "frame"), None),
        P(None, ("clip", "frame")),
        P(None, ("clip", "frame"), None),
    )
    return jax.shard_map(
        functools.partial(body, link_plan(mesh)),
        mesh=mesh,
        in_specs=in_specs,
        out_specs=out_specs,
        check_vma=False,
    )
```

```python
import functools
import math

import jax
import jax.numpy as jnp
from jax import lax
from jax.experimental import pallas as pl
from jax.experimental.pallas import tpu as pltpu
from jax.sharding import PartitionSpec as P

HEADS = 12
ADAM_STEP = 4


epsilon_norm = 1e-05
beta_first = 0.9
beta_second = 0.99
learn_rate = 0.03
decay_rate = 0.01
epsilon_adam = 1e-08
root_half = 0.7071067811865476
inv_root_two_pi = 0.3989422804014327


def norm_parts(inputs, norm_gain, norm_shift):
    average = jnp.mean(inputs, axis=-1, keepdims=True)
    centered = inputs - average
    spread = jnp.mean(centered * centered, axis=-1, keepdims=True)
    inv_std = lax.rsqrt(spread + epsilon_norm)
    normed = centered * inv_std
    return (normed * norm_gain + norm_shift, normed, inv_std)


def norm_backward(grad_normed, normed, inv_std, norm_gain):
    grad_gain = jnp.sum(grad_normed * normed, axis=0)
    grad_shift = jnp.sum(grad_normed, axis=0)
    scaled = grad_normed * norm_gain
    grad_input = inv_std * (
        scaled
        - jnp.mean(scaled, axis=-1, keepdims=True)
        - normed * jnp.mean(scaled * normed, axis=-1, keepdims=True)
    )
    return (grad_input, grad_gain, grad_shift)


def gelu_exact(inputs):
    return 0.5 * inputs * (1.0 + jax.scipy.special.erf(inputs * root_half))


def gelu_slope(inputs):
    return (
        0.5 * (1.0 + jax.scipy.special.erf(inputs * root_half))
        + inputs * jnp.exp(-0.5 * inputs * inputs) * inv_root_two_pi
    )


QUERY_CHUNK = 256
MASKED = -1e30


def attention_forward_kernel(q_ref, k_ref, v_ref, kbias_ref, o_ref, l_ref):
    head_size = q_ref.shape[1] // 2
    rows = q_ref.shape[0]
    kbias = kbias_ref[...]
    lane = lax.broadcasted_iota(jnp.int32, (QUERY_CHUNK, 2 * head_size), 1)
    for chunk in range(rows // QUERY_CHUNK):
        span = pl.ds(chunk * QUERY_CHUNK, QUERY_CHUNK)
        mixed_parts = []
        totals = []
        for half in range(2):
            cols = pl.ds(half * head_size, head_size)
            query = q_ref[span, cols]
            key = k_ref[:, cols]
            value = v_ref[:, cols]
            scores = (
                lax.dot_general(
                    query, key, (((1,), (1,)), ((), ())), preferred_element_type=jnp.float32
                )
                + kbias
            )
            highest = jnp.max(scores, axis=1, keepdims=True)
            exponent = jnp.exp(scores - highest)
            denominator = jnp.sum(exponent, axis=1, keepdims=True)
            weights = (exponent * (1.0 / denominator)).astype(jnp.bfloat16)
            mixed_parts.append(jnp.dot(weights, value, preferred_element_type=jnp.float32))
            totals.append(highest + jnp.log(denominator))
        o_ref[span, :] = jnp.concatenate(mixed_parts, axis=1).astype(o_ref.dtype)
        l_ref[span, :] = jnp.where(lane < head_size, totals[0], totals[1])


def attention_backward_kernel(
    q_ref, k_ref, v_ref, do_ref, l_ref, kbias_ref, dq_ref, dk_ref, dv_ref
):
    head_size = q_ref.shape[1] // 2
    rows = q_ref.shape[0]
    kbias = kbias_ref[...]
    for half in range(2):
        cols = pl.ds(half * head_size, head_size)
        key = k_ref[:, cols]
        value = v_ref[:, cols]
        grad_key = None
        grad_value = None
        for chunk in range(rows // QUERY_CHUNK):
            span = pl.ds(chunk * QUERY_CHUNK, QUERY_CHUNK)
            query = q_ref[span, cols]
            grad_out = do_ref[span, cols]
            total = l_ref[span, pl.ds(half * head_size, 1)]
            scores = (
                lax.dot_general(
                    query, key, (((1,), (1,)), ((), ())), preferred_element_type=jnp.float32
                )
                + kbias
            )
            weights = jnp.exp(scores - total)
            grad_weights = lax.dot_general(
                grad_out, value, (((1,), (1,)), ((), ())), preferred_element_type=jnp.float32
            )
            delta = jnp.sum(weights * grad_weights, axis=1, keepdims=True)
            grad_scores = (weights * (grad_weights - delta)).astype(jnp.bfloat16)
            dq_ref[span, cols] = jnp.dot(
                grad_scores, key, preferred_element_type=jnp.float32
            ).astype(dq_ref.dtype)
            key_part = lax.dot_general(
                grad_scores, query, (((0,), (0,)), ((), ())), preferred_element_type=jnp.float32
            )
            value_part = lax.dot_general(
                weights.astype(jnp.bfloat16),
                grad_out,
                (((0,), (0,)), ((), ())),
                preferred_element_type=jnp.float32,
            )
            grad_key = key_part if grad_key is None else grad_key + key_part
            grad_value = value_part if grad_value is None else grad_value + value_part
        dk_ref[:, cols] = grad_key
        dv_ref[:, cols] = grad_value


def pad_rows(values, rows):
    return jnp.pad(values, ((0, rows - values.shape[0]), (0, 0)))


def attention_pallas(queries, pairs, grad_out=None, totals=None, first_pair=0, pair_span=None):
    query_rows, model_width = queries.shape
    key_rows = pairs.shape[0]
    padded_q = -(-query_rows // QUERY_CHUNK) * QUERY_CHUNK
    padded_k = -(-key_rows // 128) * 128
    pair_count = model_width // 128
    q_pad = pad_rows(queries, padded_q)
    kv_pad = pad_rows(pairs, padded_k)
    kbias = jnp.where(jnp.arange(padded_k) < key_rows, 0.0, MASKED).astype(jnp.float32)[None, :]
    q_spec = pl.BlockSpec((padded_q, 128), lambda j: (0, j))
    k_spec = pl.BlockSpec((padded_k, 128), lambda j: (0, j))
    v_spec = pl.BlockSpec((padded_k, 128), lambda j: (0, j + pair_count))
    b_spec = pl.BlockSpec((1, padded_k), lambda j: (0, 0))
    params = pltpu.CompilerParams(vmem_limit_bytes=48 * 1024 * 1024)
    if grad_out is None:
        mixed, log_totals = pl.pallas_call(
            attention_forward_kernel,
            grid=(pair_count,),
            in_specs=[q_spec, k_spec, v_spec, b_spec],
            out_specs=[q_spec, q_spec],
            out_shape=[
                jax.ShapeDtypeStruct((padded_q, model_width), jnp.bfloat16),
                jax.ShapeDtypeStruct((padded_q, model_width), jnp.float32),
            ],
            compiler_params=params,
        )(q_pad, kv_pad, kv_pad, kbias)
        return mixed[:query_rows], log_totals
    do_pad = pad_rows(grad_out, padded_q)
    span = pair_count if pair_span is None else pair_span
    qi_spec = pl.BlockSpec((padded_q, 128), lambda j: (0, j + first_pair))
    ki_spec = pl.BlockSpec((padded_k, 128), lambda j: (0, j + first_pair))
    vi_spec = pl.BlockSpec((padded_k, 128), lambda j: (0, j + first_pair + pair_count))
    qo_spec = pl.BlockSpec((padded_q, 128), lambda j: (0, j))
    ko_spec = pl.BlockSpec((padded_k, 128), lambda j: (0, j))
    dq, dk, dv = pl.pallas_call(
        attention_backward_kernel,
        grid=(span,),
        in_specs=[qi_spec, ki_spec, vi_spec, qi_spec, qi_spec, b_spec],
        out_specs=[qo_spec, ko_spec, ko_spec],
        out_shape=[
            jax.ShapeDtypeStruct((padded_q, 128 * span), jnp.float32),
            jax.ShapeDtypeStruct((padded_k, 128 * span), jnp.float32),
            jax.ShapeDtypeStruct((padded_k, 128 * span), jnp.float32),
        ],
        compiler_params=params,
    )(q_pad, kv_pad, kv_pad, do_pad, totals, kbias)
    return dq[:query_rows], dk[:key_rows], dv[:key_rows]


def attend_forward(queries, keys_values, head_count):
    model_width = queries.shape[2]
    head_size = model_width // head_count
    score_scale = 1.0 / math.sqrt(head_size)

    def one_head(head_index):
        offset = head_index * head_size
        query_block = lax.dynamic_slice_in_dim(queries, offset, head_size, 2)
        key_block = lax.dynamic_slice_in_dim(keys_values, offset, head_size, 2)
        value_block = lax.dynamic_slice_in_dim(keys_values, model_width + offset, head_size, 2)
        scores = (
            jnp.einsum("cqd,ckd->cqk", query_block, key_block, preferred_element_type=jnp.float32)
            * score_scale
        )
        highest = jnp.max(scores, axis=-1, keepdims=True)
        exponent = jnp.exp(scores - highest)
        denominator = jnp.sum(exponent, axis=-1, keepdims=True)
        weights_soft = (exponent / denominator).astype(jnp.bfloat16)
        mixed = jnp.einsum(
            "cqk,ckd->cqd", weights_soft, value_block, preferred_element_type=jnp.float32
        )
        return (mixed, (highest + jnp.log(denominator))[..., 0])

    mixed, log_totals = lax.map(one_head, jnp.arange(head_count))
    clip_count, frame_count = (queries.shape[0], queries.shape[1])
    mixed = jnp.transpose(mixed, (1, 2, 0, 3)).reshape(clip_count, frame_count, model_width)
    return (mixed, log_totals)


def attend_backward(queries, keys_values, grad_mixed, log_totals, head_count):
    model_width = queries.shape[2]
    head_size = model_width // head_count
    score_scale = 1.0 / math.sqrt(head_size)

    def one_head_back(head_index):
        offset = head_index * head_size
        query_block = lax.dynamic_slice_in_dim(queries, offset, head_size, 2)
        key_block = lax.dynamic_slice_in_dim(keys_values, offset, head_size, 2)
        value_block = lax.dynamic_slice_in_dim(keys_values, model_width + offset, head_size, 2)
        grad_block = lax.dynamic_slice_in_dim(grad_mixed, offset, head_size, 2)
        totals = lax.dynamic_index_in_dim(log_totals, head_index, 0, keepdims=False)
        scores = (
            jnp.einsum("cqd,ckd->cqk", query_block, key_block, preferred_element_type=jnp.float32)
            * score_scale
        )
        weights_soft = jnp.exp(scores - totals[..., None])
        grad_weights = jnp.einsum(
            "cqd,ckd->cqk", grad_block, value_block, preferred_element_type=jnp.float32
        )
        delta = jnp.sum(weights_soft * grad_weights, axis=-1, keepdims=True)
        grad_scores = (weights_soft * (grad_weights - delta)).astype(jnp.bfloat16)
        grad_query = (
            jnp.einsum("cqk,ckd->cqd", grad_scores, key_block, preferred_element_type=jnp.float32)
            * score_scale
        )
        grad_key = (
            jnp.einsum("cqk,cqd->ckd", grad_scores, query_block, preferred_element_type=jnp.float32)
            * score_scale
        )
        grad_value = jnp.einsum(
            "cqk,cqd->ckd",
            weights_soft.astype(jnp.bfloat16),
            grad_block,
            preferred_element_type=jnp.float32,
        )
        return (grad_query, delta[..., 0], grad_key, grad_value)

    pieces = lax.map(one_head_back, jnp.arange(head_count))
    clip_count, frame_count = (queries.shape[0], queries.shape[1])
    clip_frames = keys_values.shape[1]
    grad_query = jnp.transpose(pieces[0], (1, 2, 0, 3)).reshape(
        clip_count, frame_count, model_width
    )
    grad_key = jnp.transpose(pieces[2], (1, 2, 0, 3)).reshape(clip_count, clip_frames, model_width)
    grad_value = jnp.transpose(pieces[3], (1, 2, 0, 3)).reshape(
        clip_count, clip_frames, model_width
    )
    return (grad_query, pieces[1], jnp.concatenate([grad_key, grad_value], axis=2))


def link_plan(mesh):
    devices = list(mesh.devices.reshape(-1))
    bit_count = len(devices).bit_length() - 1
    core_bit = 1
    for bit in range(bit_count):
        first, other = devices[0], devices[1 << bit]
        if getattr(first, "coords", None) is not None and tuple(first.coords) == tuple(other.coords):
            core_bit = bit
    others = [bit for bit in range(bit_count) if bit != core_bit]
    near, far = others[:-1], others[-1:]
    rotated = tuple(tuple(near[k:] + near[:k] + far) for k in range(3))
    inner = [bit for bit in near if bit != 0]
    late = tuple(tuple(inner[k:] + inner[:k] + [0] + far) for k in range(2))
    return bit_count, core_bit, rotated, late


def tree_reduce_scatter(terms, part_columns, orders, plan_bits, hooks=None):
    hooks = dict(hooks or {})
    tied = {}
    bit_count, core_bit = plan_bits
    device = lax.axis_index("clip") * lax.axis_size("frame") + lax.axis_index("frame")
    blocks = 1 << bit_count
    block_rows = terms.shape[0] // blocks
    data = terms.reshape((2,) * bit_count + (block_rows, terms.shape[1]))
    parts = [(data, list(range(bit_count - 1, -1, -1)))]
    plan = [(core_bit,)] + [tuple(order[stage] for order in orders) for stage in range(len(orders[0]))]
    for stage, stage_bits in enumerate(plan):
        if stage == 1:
            whole, bits = parts[0]
            parts = []
            offset = 0
            for width in part_columns:
                parts.append((whole[..., offset : offset + width], bits))
                offset += width
        keeps, sends = [], []
        for (part, part_bits), bit in zip(parts, stage_bits):
            axis = part_bits.index(bit)
            mine = (device >> bit) & 1
            keeps.append(lax.dynamic_index_in_dim(part, mine, axis=axis, keepdims=False))
            sends.append(
                lax.dynamic_index_in_dim(part, 1 - mine, axis=axis, keepdims=False).astype(jnp.bfloat16)
            )
        if stage in hooks:
            sends, tied[stage] = lax.optimization_barrier((sends, hooks[stage](tied)))
        new_parts = []
        for keep, send, (part, part_bits), bit in zip(keeps, sends, parts, stage_bits):
            pairs = [(index, index ^ (1 << bit)) for index in range(blocks)]
            got = lax.ppermute(send, ("clip", "frame"), pairs)
            new_parts.append((keep + got.astype(jnp.float32), [b for b in part_bits if b != bit]))
        parts = new_parts
    return jnp.concatenate([part for part, _ in parts], axis=-1).astype(jnp.float32), tied


def tree_all_gather(local, part_columns, orders, plan_bits):
    bit_count, core_bit = plan_bits
    device = lax.axis_index("clip") * lax.axis_size("frame") + lax.axis_index("frame")
    canonical = list(range(bit_count - 1, -1, -1))

    def double(data, bits, bit):
        mine = (device >> bit) & 1
        pairs = [(index, index ^ (1 << bit)) for index in range(1 << bit_count)]
        got = lax.ppermute(data, ("clip", "frame"), pairs)
        new_bits = sorted(bits + [bit], reverse=True)
        axis = new_bits.index(bit)
        low_first = jnp.stack([data, got], axis=axis)
        high_first = jnp.stack([got, data], axis=axis)
        return jnp.where(mine == 0, low_first, high_first), new_bits

    parts = []
    offset = 0
    for width in part_columns:
        parts.append((local[:, offset : offset + width], []))
        offset += width
    reversed_orders = [list(reversed(order)) for order in orders]
    for stage in range(len(reversed_orders[0])):
        parts = [double(part, bits, order[stage]) for (part, bits), order in zip(parts, reversed_orders)]
    whole = jnp.concatenate([part for part, _ in parts], axis=-1)
    whole, bits = double(whole, parts[0][1], core_bit)
    assert bits == canonical
    return whole.reshape((1 << bit_count) * local.shape[0], local.shape[1])


def adam_step(weight, moments, gradient):
    first = beta_first * moments[0] + (1.0 - beta_first) * gradient
    second = beta_second * moments[1] + (1.0 - beta_second) * gradient * gradient
    first_hat = first / (1.0 - beta_first**ADAM_STEP)
    second_hat = second / (1.0 - beta_second**ADAM_STEP)
    change = -learn_rate * (first_hat / (jnp.sqrt(second_hat) + epsilon_adam) + decay_rate * weight)
    return (change, jnp.stack([first, second]))


def body(
    plan,
    inputs,
    cotangent,
    project_in,
    project_out,
    expand_weight,
    shrink_weight,
    expand_bias,
    vectors,
    moments_in,
    moments_out,
    moments_expand,
    moments_shrink,
    moments_bias,
    moments_vectors,
):
    clip_count, frame_count, model_width = inputs.shape
    row_count = clip_count * frame_count
    head_count = HEADS
    shard_rows = project_in.shape[0]
    wide_in = project_in.shape[1]
    ff_width = expand_weight.shape[1]
    swap = [(0, 1), (1, 0)]
    everyone = ("clip", "frame")

    small = jnp.concatenate(
        [
            vectors,
            expand_bias.reshape(shard_rows, -1),
            jnp.zeros((shard_rows, 128 - vectors.shape[1] - expand_bias.shape[0] // shard_rows), jnp.float32),
        ],
        axis=1,
    )
    first_pack = jnp.concatenate([project_in, small], axis=1).astype(jnp.bfloat16)
    second_pack = jnp.concatenate(
        [project_out, expand_weight, shrink_weight.reshape(shard_rows, -1)], axis=1
    ).astype(jnp.bfloat16)
    bit_count, core_bit, rotated_orders, late_orders = plan
    first_full = tree_all_gather(first_pack, (896, 768, 768), rotated_orders, (bit_count, core_bit))
    second_full = lax.all_gather(second_pack, everyone, axis=0, tiled=True)
    full_in = first_full[:, :wide_in]
    small_full = first_full[:, wide_in:].astype(jnp.float32)
    column_set = small_full[:, : vectors.shape[1]]
    full_bias = small_full[:, vectors.shape[1] : vectors.shape[1] + ff_width // model_width].reshape(-1)
    full_out = second_full[:, :model_width]
    full_expand = second_full[:, model_width : model_width + ff_width]
    full_shrink = second_full[:, model_width + ff_width :].reshape(ff_width, model_width)

    frames_rows = inputs.reshape(row_count, model_width).astype(jnp.float32)
    normed_first, plain_first, inv_first = norm_parts(
        frames_rows, column_set[:, 0], column_set[:, 1]
    )
    hidden_first = normed_first.astype(jnp.bfloat16)
    partner_rows = lax.ppermute(inputs, "frame", swap).reshape(row_count, model_width)
    hidden_partner = norm_parts(
        partner_rows.astype(jnp.float32), column_set[:, 0], column_set[:, 1]
    )[0].astype(jnp.bfloat16)
    bias_in = jnp.concatenate(
        [column_set[:, 2], jnp.zeros((model_width,), jnp.float32), column_set[:, 3]]
    )
    projected = (
        jnp.dot(hidden_first, full_in, preferred_element_type=jnp.float32) + bias_in
    ).astype(jnp.bfloat16)
    partner_pairs = (
        jnp.dot(hidden_partner, full_in[:, model_width:], preferred_element_type=jnp.float32)
        + bias_in[model_width:]
    ).astype(jnp.bfloat16)
    queries = projected[:, :model_width].reshape(clip_count, frame_count, model_width)
    clip_pairs = jnp.concatenate([projected[:, model_width:], partner_pairs], axis=0).reshape(
        clip_count, 2 * frame_count, 2 * model_width
    )
    score_scale = 1.0 / math.sqrt(model_width // head_count)
    scaled_queries = (projected[:, :model_width] * score_scale).astype(jnp.bfloat16)
    pair_rows = clip_pairs.reshape(2 * row_count, 2 * model_width)
    mixed_low, log_totals = attention_pallas(scaled_queries, pair_rows)
    attended = jnp.dot(mixed_low, full_out, preferred_element_type=jnp.float32) + column_set[:, 4]
    residual = frames_rows + attended
    normed_second, plain_second, inv_second = norm_parts(
        residual, column_set[:, 5], column_set[:, 6]
    )
    hidden_second = normed_second.astype(jnp.bfloat16)
    preact = jnp.dot(hidden_second, full_expand, preferred_element_type=jnp.float32) + full_bias
    activated = gelu_exact(preact).astype(jnp.bfloat16)
    result = (
        residual
        + jnp.dot(activated, full_shrink, preferred_element_type=jnp.float32)
        + column_set[:, 7]
    )
    output = result.astype(jnp.bfloat16).reshape(inputs.shape)

    grad_result = cotangent.reshape(row_count, model_width)
    grad_shrink_term = jnp.dot(
        activated.T, grad_result, preferred_element_type=jnp.float32
    ).astype(jnp.bfloat16)
    grad_down_bias = jnp.sum(grad_result.astype(jnp.float32), axis=0)
    grad_activated = jnp.dot(grad_result, full_shrink.T, preferred_element_type=jnp.float32)
    grad_preact = (grad_activated * gelu_slope(preact)).astype(jnp.bfloat16)
    grad_expand_term = jnp.dot(
        hidden_second.T, grad_preact, preferred_element_type=jnp.float32
    ).astype(jnp.bfloat16)
    grad_bias_term = jnp.sum(grad_preact.astype(jnp.float32), axis=0)
    grad_hidden_second = jnp.dot(grad_preact, full_expand.T, preferred_element_type=jnp.float32)
    norm_term_second, gain_second, shift_second = norm_backward(
        grad_hidden_second, plain_second, inv_second, column_set[:, 5]
    )
    grad_residual = grad_result.astype(jnp.float32) + norm_term_second
    grad_attended = grad_residual.astype(jnp.bfloat16)
    grad_out_term = jnp.dot(
        mixed_low.T, grad_attended, preferred_element_type=jnp.float32
    ).astype(jnp.bfloat16)
    grad_out_bias = jnp.sum(grad_attended.astype(jnp.float32), axis=0)
    late_terms = jnp.concatenate(
        [grad_shrink_term.reshape(model_width, -1), grad_expand_term, grad_out_term], axis=1
    )
    grad_mixed = jnp.dot(grad_attended, full_out.T, preferred_element_type=jnp.float32).astype(
        jnp.bfloat16
    )
    def first_backward_half(tied):
        mixed_grads = tied[0]
        first = attention_pallas(
            scaled_queries, pair_rows, mixed_grads, log_totals, 0, model_width // 256
        )
        send = jnp.concatenate([first[1], first[2]], axis=1)[row_count:].astype(jnp.bfloat16)
        return (first, send, mixed_grads)

    owned_late, tied = tree_reduce_scatter(
        late_terms,
        (3456, 3456),
        late_orders,
        (bit_count, core_bit),
        {0: lambda tied: grad_mixed, 1: first_backward_half},
    )
    first_half, first_send, grad_mixed = tied[1]
    halves = []
    half_pairs = model_width // 256
    for first_pair in (0, half_pairs):
        if first_pair == 0:
            grad_query, grad_keys, grad_values = first_half
            send = first_send
        else:
            grad_query, grad_keys, grad_values = attention_pallas(
                scaled_queries, pair_rows, grad_mixed, log_totals, first_pair, half_pairs
            )
            send = jnp.concatenate([grad_keys, grad_values], axis=1)[row_count:].astype(jnp.bfloat16)
        terms = jnp.concatenate([grad_keys, grad_values], axis=1)
        returned = lax.ppermute(send, "frame", swap)
        halves.append((grad_query, terms[:row_count] + returned.astype(jnp.float32)))
    half_width = model_width // 2
    grad_projected = jnp.concatenate(
        [
            (jnp.concatenate([halves[0][0], halves[1][0]], axis=1) * score_scale).astype(jnp.bfloat16),
            jnp.concatenate(
                [
                    halves[0][1][:, :half_width],
                    halves[1][1][:, :half_width],
                    halves[0][1][:, half_width:],
                    halves[1][1][:, half_width:],
                ],
                axis=1,
            ).astype(jnp.bfloat16),
        ],
        axis=1,
    )
    grad_in_term = jnp.dot(hidden_first.T, grad_projected, preferred_element_type=jnp.float32)
    projected_sums = jnp.sum(grad_projected.astype(jnp.float32), axis=0)
    grad_query_bias = projected_sums[:model_width]
    grad_value_bias = projected_sums[2 * model_width :]
    grad_hidden_first = jnp.dot(grad_projected, full_in.T, preferred_element_type=jnp.float32)
    norm_term_first, gain_first, shift_first = norm_backward(
        grad_hidden_first, plain_first, inv_first, column_set[:, 0]
    )
    grad_inputs = (grad_residual + norm_term_first).astype(jnp.bfloat16).reshape(inputs.shape)
    grad_columns = jnp.stack(
        [
            gain_first,
            shift_first,
            grad_query_bias,
            grad_value_bias,
            grad_out_bias,
            gain_second,
            shift_second,
            grad_down_bias,
        ],
        axis=1,
    )
    small_grads = jnp.concatenate(
        [
            grad_columns,
            grad_bias_term.reshape(model_width, -1),
            jnp.zeros((model_width, 128 - 12), jnp.float32),
        ],
        axis=1,
    )
    owned_first = tree_reduce_scatter(
        jnp.concatenate([grad_in_term, small_grads], axis=1),
        (896, 768, 768),
        rotated_orders,
        (bit_count, core_bit),
    )[0]
    owned_in = owned_first[:, :wide_in]
    owned_vectors = owned_first[:, wide_in : wide_in + vectors.shape[1]]
    owned_bias = owned_first[:, wide_in + vectors.shape[1] : wide_in + 12].reshape(-1)
    owned_shrink = owned_late[:, :ff_width].reshape(shrink_weight.shape)
    owned_expand = owned_late[:, ff_width : 2 * ff_width]
    owned_out = owned_late[:, 2 * ff_width :]
    new_in, mom_in = adam_step(project_in, moments_in, owned_in)
    new_out, mom_out = adam_step(project_out, moments_out, owned_out)
    new_expand, mom_expand = adam_step(expand_weight, moments_expand, owned_expand)
    new_shrink, mom_shrink = adam_step(shrink_weight, moments_shrink, owned_shrink)
    new_bias, mom_bias = adam_step(expand_bias, moments_bias, owned_bias)
    new_vectors, mom_vectors = adam_step(vectors, moments_vectors, owned_vectors)
    return (
        output,
        grad_inputs,
        owned_in,
        owned_out,
        owned_expand,
        owned_shrink,
        owned_bias,
        owned_vectors,
        new_in,
        new_out,
        new_expand,
        new_shrink,
        new_bias,
        new_vectors,
        mom_in,
        mom_out,
        mom_expand,
        mom_shrink,
        mom_bias,
        mom_vectors,
    )


def solution(mesh):
    in_specs = (
        P("clip", "frame", None),
        P("clip", "frame", None),
        P(("clip", "frame"), None),
        P(("clip", "frame"), None),
        P(("clip", "frame"), None),
        P(("clip", "frame"), None),
        P(("clip", "frame")),
        P(("clip", "frame"), None),
        P(None, ("clip", "frame"), None),
        P(None, ("clip", "frame"), None),
        P(None, ("clip", "frame"), None),
        P(None, ("clip", "frame"), None),
        P(None, ("clip", "frame")),
        P(None, ("clip", "frame"), None),
    )
    out_specs = (
        P("clip", "frame", None),
        P("clip", "frame", None),
        P(("clip", "frame"), None),
        P(("clip", "frame"), None),
        P(("clip", "frame"), None),
        P(("clip", "frame"), None),
        P(("clip", "frame")),
        P(("clip", "frame"), None),
        P(("clip", "frame"), None),
        P(("clip", "frame"), None),
        P(("clip", "frame"), None),
        P(("clip", "frame"), None),
        P(("clip", "frame")),
        P(("clip", "frame"), None),
        P(None, ("clip", "frame"), None),
        P(None, ("clip", "frame"), None),
        P(None, ("clip", "frame"), None),
        P(None, ("clip", "frame"), None),
        P(None, ("clip", "frame")),
        P(None, ("clip", "frame"), None),
    )
    return jax.shard_map(
        functools.partial(body, link_plan(mesh)),
        mesh=mesh,
        in_specs=in_specs,
        out_specs=out_specs,
        check_vma=False,
    )
```

```python
import functools
import math

import jax
import jax.numpy as jnp
from jax import lax
from jax.experimental import pallas as pl
from jax.experimental.pallas import tpu as pltpu
from jax.sharding import PartitionSpec as P

HEADS = 12
ADAM_STEP = 4


epsilon_norm = 1e-05
beta_first = 0.9
beta_second = 0.99
learn_rate = 0.03
decay_rate = 0.01
epsilon_adam = 1e-08
root_half = 0.7071067811865476
inv_root_two_pi = 0.3989422804014327


def norm_parts(inputs, norm_gain, norm_shift):
    average = jnp.mean(inputs, axis=-1, keepdims=True)
    centered = inputs - average
    spread = jnp.mean(centered * centered, axis=-1, keepdims=True)
    inv_std = lax.rsqrt(spread + epsilon_norm)
    normed = centered * inv_std
    return (normed * norm_gain + norm_shift, normed, inv_std)


def norm_backward(grad_normed, normed, inv_std, norm_gain):
    grad_gain = jnp.sum(grad_normed * normed, axis=0)
    grad_shift = jnp.sum(grad_normed, axis=0)
    scaled = grad_normed * norm_gain
    grad_input = inv_std * (
        scaled
        - jnp.mean(scaled, axis=-1, keepdims=True)
        - normed * jnp.mean(scaled * normed, axis=-1, keepdims=True)
    )
    return (grad_input, grad_gain, grad_shift)


def gelu_exact(inputs):
    return 0.5 * inputs * (1.0 + jax.scipy.special.erf(inputs * root_half))


def gelu_slope(inputs):
    return (
        0.5 * (1.0 + jax.scipy.special.erf(inputs * root_half))
        + inputs * jnp.exp(-0.5 * inputs * inputs) * inv_root_two_pi
    )


QUERY_CHUNK = 256
MASKED = -1e30


def attention_forward_kernel(q_ref, k_ref, v_ref, kbias_ref, o_ref, l_ref):
    head_size = q_ref.shape[1] // 2
    rows = q_ref.shape[0]
    kbias = kbias_ref[...]
    lane = lax.broadcasted_iota(jnp.int32, (QUERY_CHUNK, 2 * head_size), 1)
    for chunk in range(rows // QUERY_CHUNK):
        span = pl.ds(chunk * QUERY_CHUNK, QUERY_CHUNK)
        mixed_parts = []
        totals = []
        for half in range(2):
            cols = pl.ds(half * head_size, head_size)
            query = q_ref[span, cols]
            key = k_ref[:, cols]
            value = v_ref[:, cols]
            scores = (
                lax.dot_general(
                    query, key, (((1,), (1,)), ((), ())), preferred_element_type=jnp.float32
                )
                + kbias
            )
            highest = jnp.max(scores, axis=1, keepdims=True)
            exponent = jnp.exp(scores - highest)
            denominator = jnp.sum(exponent, axis=1, keepdims=True)
            weights = (exponent * (1.0 / denominator)).astype(jnp.bfloat16)
            mixed_parts.append(jnp.dot(weights, value, preferred_element_type=jnp.float32))
            totals.append(highest + jnp.log(denominator))
        o_ref[span, :] = jnp.concatenate(mixed_parts, axis=1).astype(o_ref.dtype)
        l_ref[span, :] = jnp.where(lane < head_size, totals[0], totals[1])


def attention_backward_kernel(
    q_ref, k_ref, v_ref, do_ref, l_ref, kbias_ref, dq_ref, dk_ref, dv_ref
):
    head_size = q_ref.shape[1] // 2
    rows = q_ref.shape[0]
    kbias = kbias_ref[...]
    for half in range(2):
        cols = pl.ds(half * head_size, head_size)
        key = k_ref[:, cols]
        value = v_ref[:, cols]
        grad_key = None
        grad_value = None
        for chunk in range(rows // QUERY_CHUNK):
            span = pl.ds(chunk * QUERY_CHUNK, QUERY_CHUNK)
            query = q_ref[span, cols]
            grad_out = do_ref[span, cols]
            total = l_ref[span, pl.ds(half * head_size, 1)]
            scores = (
                lax.dot_general(
                    query, key, (((1,), (1,)), ((), ())), preferred_element_type=jnp.float32
                )
                + kbias
            )
            weights = jnp.exp(scores - total)
            grad_weights = lax.dot_general(
                grad_out, value, (((1,), (1,)), ((), ())), preferred_element_type=jnp.float32
            )
            delta = jnp.sum(weights * grad_weights, axis=1, keepdims=True)
            grad_scores = (weights * (grad_weights - delta)).astype(jnp.bfloat16)
            dq_ref[span, cols] = jnp.dot(
                grad_scores, key, preferred_element_type=jnp.float32
            ).astype(dq_ref.dtype)
            key_part = lax.dot_general(
                grad_scores, query, (((0,), (0,)), ((), ())), preferred_element_type=jnp.float32
            )
            value_part = lax.dot_general(
                weights.astype(jnp.bfloat16),
                grad_out,
                (((0,), (0,)), ((), ())),
                preferred_element_type=jnp.float32,
            )
            grad_key = key_part if grad_key is None else grad_key + key_part
            grad_value = value_part if grad_value is None else grad_value + value_part
        dk_ref[:, cols] = grad_key
        dv_ref[:, cols] = grad_value


def pad_rows(values, rows):
    return jnp.pad(values, ((0, rows - values.shape[0]), (0, 0)))


def attention_pallas(queries, pairs, grad_out=None, totals=None, first_pair=0, pair_span=None):
    query_rows, model_width = queries.shape
    key_rows = pairs.shape[0]
    padded_q = -(-query_rows // QUERY_CHUNK) * QUERY_CHUNK
    padded_k = -(-key_rows // 128) * 128
    pair_count = model_width // 128
    q_pad = pad_rows(queries, padded_q)
    kv_pad = pad_rows(pairs, padded_k)
    kbias = jnp.where(jnp.arange(padded_k) < key_rows, 0.0, MASKED).astype(jnp.float32)[None, :]
    q_spec = pl.BlockSpec((padded_q, 128), lambda j: (0, j))
    k_spec = pl.BlockSpec((padded_k, 128), lambda j: (0, j))
    v_spec = pl.BlockSpec((padded_k, 128), lambda j: (0, j + pair_count))
    b_spec = pl.BlockSpec((1, padded_k), lambda j: (0, 0))
    params = pltpu.CompilerParams(vmem_limit_bytes=48 * 1024 * 1024)
    if grad_out is None:
        mixed, log_totals = pl.pallas_call(
            attention_forward_kernel,
            grid=(pair_count,),
            in_specs=[q_spec, k_spec, v_spec, b_spec],
            out_specs=[q_spec, q_spec],
            out_shape=[
                jax.ShapeDtypeStruct((padded_q, model_width), jnp.bfloat16),
                jax.ShapeDtypeStruct((padded_q, model_width), jnp.float32),
            ],
            compiler_params=params,
        )(q_pad, kv_pad, kv_pad, kbias)
        return mixed[:query_rows], log_totals
    do_pad = pad_rows(grad_out, padded_q)
    span = pair_count if pair_span is None else pair_span
    qi_spec = pl.BlockSpec((padded_q, 128), lambda j: (0, j + first_pair))
    ki_spec = pl.BlockSpec((padded_k, 128), lambda j: (0, j + first_pair))
    vi_spec = pl.BlockSpec((padded_k, 128), lambda j: (0, j + first_pair + pair_count))
    qo_spec = pl.BlockSpec((padded_q, 128), lambda j: (0, j))
    ko_spec = pl.BlockSpec((padded_k, 128), lambda j: (0, j))
    dq, dk, dv = pl.pallas_call(
        attention_backward_kernel,
        grid=(span,),
        in_specs=[qi_spec, ki_spec, vi_spec, qi_spec, qi_spec, b_spec],
        out_specs=[qo_spec, ko_spec, ko_spec],
        out_shape=[
            jax.ShapeDtypeStruct((padded_q, 128 * span), jnp.float32),
            jax.ShapeDtypeStruct((padded_k, 128 * span), jnp.float32),
            jax.ShapeDtypeStruct((padded_k, 128 * span), jnp.float32),
        ],
        compiler_params=params,
    )(q_pad, kv_pad, kv_pad, do_pad, totals, kbias)
    return dq[:query_rows], dk[:key_rows], dv[:key_rows]


def attend_forward(queries, keys_values, head_count):
    model_width = queries.shape[2]
    head_size = model_width // head_count
    score_scale = 1.0 / math.sqrt(head_size)

    def one_head(head_index):
        offset = head_index * head_size
        query_block = lax.dynamic_slice_in_dim(queries, offset, head_size, 2)
        key_block = lax.dynamic_slice_in_dim(keys_values, offset, head_size, 2)
        value_block = lax.dynamic_slice_in_dim(keys_values, model_width + offset, head_size, 2)
        scores = (
            jnp.einsum("cqd,ckd->cqk", query_block, key_block, preferred_element_type=jnp.float32)
            * score_scale
        )
        highest = jnp.max(scores, axis=-1, keepdims=True)
        exponent = jnp.exp(scores - highest)
        denominator = jnp.sum(exponent, axis=-1, keepdims=True)
        weights_soft = (exponent / denominator).astype(jnp.bfloat16)
        mixed = jnp.einsum(
            "cqk,ckd->cqd", weights_soft, value_block, preferred_element_type=jnp.float32
        )
        return (mixed, (highest + jnp.log(denominator))[..., 0])

    mixed, log_totals = lax.map(one_head, jnp.arange(head_count))
    clip_count, frame_count = (queries.shape[0], queries.shape[1])
    mixed = jnp.transpose(mixed, (1, 2, 0, 3)).reshape(clip_count, frame_count, model_width)
    return (mixed, log_totals)


def attend_backward(queries, keys_values, grad_mixed, log_totals, head_count):
    model_width = queries.shape[2]
    head_size = model_width // head_count
    score_scale = 1.0 / math.sqrt(head_size)

    def one_head_back(head_index):
        offset = head_index * head_size
        query_block = lax.dynamic_slice_in_dim(queries, offset, head_size, 2)
        key_block = lax.dynamic_slice_in_dim(keys_values, offset, head_size, 2)
        value_block = lax.dynamic_slice_in_dim(keys_values, model_width + offset, head_size, 2)
        grad_block = lax.dynamic_slice_in_dim(grad_mixed, offset, head_size, 2)
        totals = lax.dynamic_index_in_dim(log_totals, head_index, 0, keepdims=False)
        scores = (
            jnp.einsum("cqd,ckd->cqk", query_block, key_block, preferred_element_type=jnp.float32)
            * score_scale
        )
        weights_soft = jnp.exp(scores - totals[..., None])
        grad_weights = jnp.einsum(
            "cqd,ckd->cqk", grad_block, value_block, preferred_element_type=jnp.float32
        )
        delta = jnp.sum(weights_soft * grad_weights, axis=-1, keepdims=True)
        grad_scores = (weights_soft * (grad_weights - delta)).astype(jnp.bfloat16)
        grad_query = (
            jnp.einsum("cqk,ckd->cqd", grad_scores, key_block, preferred_element_type=jnp.float32)
            * score_scale
        )
        grad_key = (
            jnp.einsum("cqk,cqd->ckd", grad_scores, query_block, preferred_element_type=jnp.float32)
            * score_scale
        )
        grad_value = jnp.einsum(
            "cqk,cqd->ckd",
            weights_soft.astype(jnp.bfloat16),
            grad_block,
            preferred_element_type=jnp.float32,
        )
        return (grad_query, delta[..., 0], grad_key, grad_value)

    pieces = lax.map(one_head_back, jnp.arange(head_count))
    clip_count, frame_count = (queries.shape[0], queries.shape[1])
    clip_frames = keys_values.shape[1]
    grad_query = jnp.transpose(pieces[0], (1, 2, 0, 3)).reshape(
        clip_count, frame_count, model_width
    )
    grad_key = jnp.transpose(pieces[2], (1, 2, 0, 3)).reshape(clip_count, clip_frames, model_width)
    grad_value = jnp.transpose(pieces[3], (1, 2, 0, 3)).reshape(
        clip_count, clip_frames, model_width
    )
    return (grad_query, pieces[1], jnp.concatenate([grad_key, grad_value], axis=2))


def link_plan(mesh):
    devices = list(mesh.devices.reshape(-1))
    bit_count = len(devices).bit_length() - 1
    core_bit = 1
    for bit in range(bit_count):
        first, other = devices[0], devices[1 << bit]
        if getattr(first, "coords", None) is not None and tuple(first.coords) == tuple(other.coords):
            core_bit = bit
    others = [bit for bit in range(bit_count) if bit != core_bit]
    near, far = others[:-1], others[-1:]
    rotated = tuple(tuple(near[k:] + near[:k] + far) for k in range(3))
    inner = [bit for bit in near if bit != 0]
    late = tuple(tuple(inner[k:] + inner[:k] + [0] + far) for k in range(2))
    return bit_count, core_bit, rotated, late


def tree_reduce_scatter(terms, part_columns, orders, plan_bits, hooks=None):
    hooks = dict(hooks or {})
    tied = {}
    bit_count, core_bit = plan_bits
    device = lax.axis_index("clip") * lax.axis_size("frame") + lax.axis_index("frame")
    blocks = 1 << bit_count
    block_rows = terms.shape[0] // blocks
    data = terms.reshape((2,) * bit_count + (block_rows, terms.shape[1]))
    parts = [(data, list(range(bit_count - 1, -1, -1)))]
    plan = [(core_bit,)] + [tuple(order[stage] for order in orders) for stage in range(len(orders[0]))]
    for stage, stage_bits in enumerate(plan):
        if stage == 1:
            whole, bits = parts[0]
            parts = []
            offset = 0
            for width in part_columns:
                parts.append((whole[..., offset : offset + width], bits))
                offset += width
        keeps, sends = [], []
        for (part, part_bits), bit in zip(parts, stage_bits):
            axis = part_bits.index(bit)
            mine = (device >> bit) & 1
            keeps.append(lax.dynamic_index_in_dim(part, mine, axis=axis, keepdims=False))
            sends.append(
                lax.dynamic_index_in_dim(part, 1 - mine, axis=axis, keepdims=False).astype(jnp.bfloat16)
            )
        new_parts = []
        for keep, send, (part, part_bits), bit in zip(keeps, sends, parts, stage_bits):
            pairs = [(index, index ^ (1 << bit)) for index in range(blocks)]
            got = lax.ppermute(send, ("clip", "frame"), pairs)
            new_parts.append((keep + got.astype(jnp.float32), [b for b in part_bits if b != bit]))
        if stage in hooks:
            values, tied[stage] = lax.optimization_barrier(
                ([part for part, _ in new_parts], hooks[stage](tied))
            )
            new_parts = [(value, part_bits) for value, (_, part_bits) in zip(values, new_parts)]
        parts = new_parts
    return jnp.concatenate([part for part, _ in parts], axis=-1).astype(jnp.float32), tied


def tree_all_gather(local, part_columns, orders, plan_bits):
    bit_count, core_bit = plan_bits
    device = lax.axis_index("clip") * lax.axis_size("frame") + lax.axis_index("frame")
    canonical = list(range(bit_count - 1, -1, -1))

    def double(data, bits, bit):
        mine = (device >> bit) & 1
        pairs = [(index, index ^ (1 << bit)) for index in range(1 << bit_count)]
        got = lax.ppermute(data, ("clip", "frame"), pairs)
        new_bits = sorted(bits + [bit], reverse=True)
        axis = new_bits.index(bit)
        low_first = jnp.stack([data, got], axis=axis)
        high_first = jnp.stack([got, data], axis=axis)
        return jnp.where(mine == 0, low_first, high_first), new_bits

    parts = []
    offset = 0
    for width in part_columns:
        parts.append((local[:, offset : offset + width], []))
        offset += width
    reversed_orders = [list(reversed(order)) for order in orders]
    for stage in range(len(reversed_orders[0])):
        parts = [double(part, bits, order[stage]) for (part, bits), order in zip(parts, reversed_orders)]
    whole = jnp.concatenate([part for part, _ in parts], axis=-1)
    whole, bits = double(whole, parts[0][1], core_bit)
    assert bits == canonical
    return whole.reshape((1 << bit_count) * local.shape[0], local.shape[1])


def adam_step(weight, moments, gradient):
    first = beta_first * moments[0] + (1.0 - beta_first) * gradient
    second = beta_second * moments[1] + (1.0 - beta_second) * gradient * gradient
    first_hat = first / (1.0 - beta_first**ADAM_STEP)
    second_hat = second / (1.0 - beta_second**ADAM_STEP)
    change = -learn_rate * (first_hat / (jnp.sqrt(second_hat) + epsilon_adam) + decay_rate * weight)
    return (change, jnp.stack([first, second]))


def body(
    plan,
    inputs,
    cotangent,
    project_in,
    project_out,
    expand_weight,
    shrink_weight,
    expand_bias,
    vectors,
    moments_in,
    moments_out,
    moments_expand,
    moments_shrink,
    moments_bias,
    moments_vectors,
):
    clip_count, frame_count, model_width = inputs.shape
    row_count = clip_count * frame_count
    head_count = HEADS
    shard_rows = project_in.shape[0]
    wide_in = project_in.shape[1]
    ff_width = expand_weight.shape[1]
    swap = [(0, 1), (1, 0)]
    everyone = ("clip", "frame")

    small = jnp.concatenate(
        [
            vectors,
            expand_bias.reshape(shard_rows, -1),
            jnp.zeros((shard_rows, 128 - vectors.shape[1] - expand_bias.shape[0] // shard_rows), jnp.float32),
        ],
        axis=1,
    )
    first_pack = jnp.concatenate([project_in, small], axis=1).astype(jnp.bfloat16)
    second_pack = jnp.concatenate(
        [project_out, expand_weight, shrink_weight.reshape(shard_rows, -1)], axis=1
    ).astype(jnp.bfloat16)
    bit_count, core_bit, rotated_orders, late_orders = plan
    first_full = tree_all_gather(first_pack, (896, 768, 768), rotated_orders, (bit_count, core_bit))
    second_full = lax.all_gather(second_pack, everyone, axis=0, tiled=True)
    full_in = first_full[:, :wide_in]
    small_full = first_full[:, wide_in:].astype(jnp.float32)
    column_set = small_full[:, : vectors.shape[1]]
    full_bias = small_full[:, vectors.shape[1] : vectors.shape[1] + ff_width // model_width].reshape(-1)
    full_out = second_full[:, :model_width]
    full_expand = second_full[:, model_width : model_width + ff_width]
    full_shrink = second_full[:, model_width + ff_width :].reshape(ff_width, model_width)

    frames_rows = inputs.reshape(row_count, model_width).astype(jnp.float32)
    normed_first, plain_first, inv_first = norm_parts(
        frames_rows, column_set[:, 0], column_set[:, 1]
    )
    hidden_first = normed_first.astype(jnp.bfloat16)
    partner_rows = lax.ppermute(inputs, "frame", swap).reshape(row_count, model_width)
    hidden_partner = norm_parts(
        partner_rows.astype(jnp.float32), column_set[:, 0], column_set[:, 1]
    )[0].astype(jnp.bfloat16)
    bias_in = jnp.concatenate(
        [column_set[:, 2], jnp.zeros((model_width,), jnp.float32), column_set[:, 3]]
    )
    projected = (
        jnp.dot(hidden_first, full_in, preferred_element_type=jnp.float32) + bias_in
    ).astype(jnp.bfloat16)
    partner_pairs = (
        jnp.dot(hidden_partner, full_in[:, model_width:], preferred_element_type=jnp.float32)
        + bias_in[model_width:]
    ).astype(jnp.bfloat16)
    queries = projected[:, :model_width].reshape(clip_count, frame_count, model_width)
    clip_pairs = jnp.concatenate([projected[:, model_width:], partner_pairs], axis=0).reshape(
        clip_count, 2 * frame_count, 2 * model_width
    )
    score_scale = 1.0 / math.sqrt(model_width // head_count)
    scaled_queries = (projected[:, :model_width] * score_scale).astype(jnp.bfloat16)
    pair_rows = clip_pairs.reshape(2 * row_count, 2 * model_width)
    mixed_low, log_totals = attention_pallas(scaled_queries, pair_rows)
    attended = jnp.dot(mixed_low, full_out, preferred_element_type=jnp.float32) + column_set[:, 4]
    residual = frames_rows + attended
    normed_second, plain_second, inv_second = norm_parts(
        residual, column_set[:, 5], column_set[:, 6]
    )
    hidden_second = normed_second.astype(jnp.bfloat16)
    preact = jnp.dot(hidden_second, full_expand, preferred_element_type=jnp.float32) + full_bias
    activated = gelu_exact(preact).astype(jnp.bfloat16)
    result = (
        residual
        + jnp.dot(activated, full_shrink, preferred_element_type=jnp.float32)
        + column_set[:, 7]
    )
    output = result.astype(jnp.bfloat16).reshape(inputs.shape)

    grad_result = cotangent.reshape(row_count, model_width)
    grad_shrink_term = jnp.dot(
        activated.T, grad_result, preferred_element_type=jnp.float32
    ).astype(jnp.bfloat16)
    grad_down_bias = jnp.sum(grad_result.astype(jnp.float32), axis=0)
    grad_activated = jnp.dot(grad_result, full_shrink.T, preferred_element_type=jnp.float32)
    grad_preact = (grad_activated * gelu_slope(preact)).astype(jnp.bfloat16)
    grad_expand_term = jnp.dot(
        hidden_second.T, grad_preact, preferred_element_type=jnp.float32
    ).astype(jnp.bfloat16)
    grad_bias_term = jnp.sum(grad_preact.astype(jnp.float32), axis=0)
    grad_hidden_second = jnp.dot(grad_preact, full_expand.T, preferred_element_type=jnp.float32)
    norm_term_second, gain_second, shift_second = norm_backward(
        grad_hidden_second, plain_second, inv_second, column_set[:, 5]
    )
    grad_residual = grad_result.astype(jnp.float32) + norm_term_second
    grad_attended = grad_residual.astype(jnp.bfloat16)
    grad_out_term = jnp.dot(
        mixed_low.T, grad_attended, preferred_element_type=jnp.float32
    ).astype(jnp.bfloat16)
    grad_out_bias = jnp.sum(grad_attended.astype(jnp.float32), axis=0)
    late_terms = jnp.concatenate(
        [grad_shrink_term.reshape(model_width, -1), grad_expand_term, grad_out_term], axis=1
    )
    grad_mixed = jnp.dot(grad_attended, full_out.T, preferred_element_type=jnp.float32).astype(
        jnp.bfloat16
    )
    piece_pairs = 2
    piece_count = model_width // 128 // piece_pairs

    def run_piece(index, mixed_grads):
        return attention_pallas(
            scaled_queries, pair_rows, mixed_grads, log_totals, index * piece_pairs, piece_pairs
        )

    def piece_hook(index):
        return lambda tied: (run_piece(index, tied[index - 1][1]), tied[index - 1][1])

    hooks = {0: lambda tied: ((), grad_mixed)}
    hooks.update({index: piece_hook(index) for index in range(1, piece_count)})
    pieces = [run_piece(0, grad_mixed)]
    owned_late, tied = tree_reduce_scatter(
        late_terms, (3456, 3456), late_orders, (bit_count, core_bit), hooks
    )
    pieces += [tied[index][0] for index in range(1, piece_count)]
    finished = []
    for grad_query, grad_keys, grad_values in pieces:
        terms = jnp.concatenate([grad_keys, grad_values], axis=1)
        returned = lax.ppermute(terms[row_count:].astype(jnp.bfloat16), "frame", swap)
        finished.append((grad_query, terms[:row_count] + returned.astype(jnp.float32)))
    piece_width = finished[0][0].shape[1]
    grad_projected = jnp.concatenate(
        [
            (jnp.concatenate([query for query, _ in finished], axis=1) * score_scale).astype(
                jnp.bfloat16
            ),
            jnp.concatenate(
                [pair[:, :piece_width] for _, pair in finished]
                + [pair[:, piece_width:] for _, pair in finished],
                axis=1,
            ).astype(jnp.bfloat16),
        ],
        axis=1,
    )
    grad_in_term = jnp.dot(hidden_first.T, grad_projected, preferred_element_type=jnp.float32)
    projected_sums = jnp.sum(grad_projected.astype(jnp.float32), axis=0)
    grad_query_bias = projected_sums[:model_width]
    grad_value_bias = projected_sums[2 * model_width :]
    grad_hidden_first = jnp.dot(grad_projected, full_in.T, preferred_element_type=jnp.float32)
    norm_term_first, gain_first, shift_first = norm_backward(
        grad_hidden_first, plain_first, inv_first, column_set[:, 0]
    )
    grad_inputs = (grad_residual + norm_term_first).astype(jnp.bfloat16).reshape(inputs.shape)
    grad_columns = jnp.stack(
        [
            gain_first,
            shift_first,
            grad_query_bias,
            grad_value_bias,
            grad_out_bias,
            gain_second,
            shift_second,
            grad_down_bias,
        ],
        axis=1,
    )
    small_grads = jnp.concatenate(
        [
            grad_columns,
            grad_bias_term.reshape(model_width, -1),
            jnp.zeros((model_width, 128 - 12), jnp.float32),
        ],
        axis=1,
    )
    owned_first = tree_reduce_scatter(
        jnp.concatenate([grad_in_term, small_grads], axis=1),
        (896, 768, 768),
        rotated_orders,
        (bit_count, core_bit),
    )[0]
    owned_in = owned_first[:, :wide_in]
    owned_vectors = owned_first[:, wide_in : wide_in + vectors.shape[1]]
    owned_bias = owned_first[:, wide_in + vectors.shape[1] : wide_in + 12].reshape(-1)
    owned_shrink = owned_late[:, :ff_width].reshape(shrink_weight.shape)
    owned_expand = owned_late[:, ff_width : 2 * ff_width]
    owned_out = owned_late[:, 2 * ff_width :]
    new_in, mom_in = adam_step(project_in, moments_in, owned_in)
    new_out, mom_out = adam_step(project_out, moments_out, owned_out)
    new_expand, mom_expand = adam_step(expand_weight, moments_expand, owned_expand)
    new_shrink, mom_shrink = adam_step(shrink_weight, moments_shrink, owned_shrink)
    new_bias, mom_bias = adam_step(expand_bias, moments_bias, owned_bias)
    new_vectors, mom_vectors = adam_step(vectors, moments_vectors, owned_vectors)
    return (
        output,
        grad_inputs,
        owned_in,
        owned_out,
        owned_expand,
        owned_shrink,
        owned_bias,
        owned_vectors,
        new_in,
        new_out,
        new_expand,
        new_shrink,
        new_bias,
        new_vectors,
        mom_in,
        mom_out,
        mom_expand,
        mom_shrink,
        mom_bias,
        mom_vectors,
    )


def solution(mesh):
    in_specs = (
        P("clip", "frame", None),
        P("clip", "frame", None),
        P(("clip", "frame"), None),
        P(("clip", "frame"), None),
        P(("clip", "frame"), None),
        P(("clip", "frame"), None),
        P(("clip", "frame")),
        P(("clip", "frame"), None),
        P(None, ("clip", "frame"), None),
        P(None, ("clip", "frame"), None),
        P(None, ("clip", "frame"), None),
        P(None, ("clip", "frame"), None),
        P(None, ("clip", "frame")),
        P(None, ("clip", "frame"), None),
    )
    out_specs = (
        P("clip", "frame", None),
        P("clip", "frame", None),
        P(("clip", "frame"), None),
        P(("clip", "frame"), None),
        P(("clip", "frame"), None),
        P(("clip", "frame"), None),
        P(("clip", "frame")),
        P(("clip", "frame"), None),
        P(("clip", "frame"), None),
        P(("clip", "frame"), None),
        P(("clip", "frame"), None),
        P(("clip", "frame"), None),
        P(("clip", "frame")),
        P(("clip", "frame"), None),
        P(None, ("clip", "frame"), None),
        P(None, ("clip", "frame"), None),
        P(None, ("clip", "frame"), None),
        P(None, ("clip", "frame"), None),
        P(None, ("clip", "frame")),
        P(None, ("clip", "frame"), None),
    )
    return jax.shard_map(
        functools.partial(body, link_plan(mesh)),
        mesh=mesh,
        in_specs=in_specs,
        out_specs=out_specs,
        check_vma=False,
    )
```

```python
import functools
import math

import jax
import jax.numpy as jnp
from jax import lax
from jax.experimental import pallas as pl
from jax.experimental.pallas import tpu as pltpu
from jax.sharding import PartitionSpec as P

HEADS = 12
ADAM_STEP = 4


epsilon_norm = 1e-05
beta_first = 0.9
beta_second = 0.99
learn_rate = 0.03
decay_rate = 0.01
epsilon_adam = 1e-08
root_half = 0.7071067811865476
inv_root_two_pi = 0.3989422804014327


def norm_parts(inputs, norm_gain, norm_shift):
    average = jnp.mean(inputs, axis=-1, keepdims=True)
    centered = inputs - average
    spread = jnp.mean(centered * centered, axis=-1, keepdims=True)
    inv_std = lax.rsqrt(spread + epsilon_norm)
    normed = centered * inv_std
    return (normed * norm_gain + norm_shift, normed, inv_std)


def norm_backward(grad_normed, normed, inv_std, norm_gain):
    grad_gain = jnp.sum(grad_normed * normed, axis=0)
    grad_shift = jnp.sum(grad_normed, axis=0)
    scaled = grad_normed * norm_gain
    grad_input = inv_std * (
        scaled
        - jnp.mean(scaled, axis=-1, keepdims=True)
        - normed * jnp.mean(scaled * normed, axis=-1, keepdims=True)
    )
    return (grad_input, grad_gain, grad_shift)


def gelu_exact(inputs):
    return 0.5 * inputs * (1.0 + jax.scipy.special.erf(inputs * root_half))


def gelu_slope(inputs):
    return (
        0.5 * (1.0 + jax.scipy.special.erf(inputs * root_half))
        + inputs * jnp.exp(-0.5 * inputs * inputs) * inv_root_two_pi
    )


QUERY_CHUNK = 256
MASKED = -1e30


def attention_forward_kernel(q_ref, k_ref, v_ref, kbias_ref, o_ref, l_ref):
    head_size = q_ref.shape[1] // 2
    rows = q_ref.shape[0]
    kbias = kbias_ref[...]
    lane = lax.broadcasted_iota(jnp.int32, (QUERY_CHUNK, 2 * head_size), 1)
    for chunk in range(rows // QUERY_CHUNK):
        span = pl.ds(chunk * QUERY_CHUNK, QUERY_CHUNK)
        mixed_parts = []
        totals = []
        for half in range(2):
            cols = pl.ds(half * head_size, head_size)
            query = q_ref[span, cols]
            key = k_ref[:, cols]
            value = v_ref[:, cols]
            scores = (
                lax.dot_general(
                    query, key, (((1,), (1,)), ((), ())), preferred_element_type=jnp.float32
                )
                + kbias
            )
            highest = jnp.max(scores, axis=1, keepdims=True)
            exponent = jnp.exp(scores - highest)
            denominator = jnp.sum(exponent, axis=1, keepdims=True)
            weights = (exponent * (1.0 / denominator)).astype(jnp.bfloat16)
            mixed_parts.append(jnp.dot(weights, value, preferred_element_type=jnp.float32))
            totals.append(highest + jnp.log(denominator))
        o_ref[span, :] = jnp.concatenate(mixed_parts, axis=1).astype(o_ref.dtype)
        l_ref[span, :] = jnp.where(lane < head_size, totals[0], totals[1])


def attention_backward_kernel(
    q_ref, k_ref, v_ref, do_ref, l_ref, kbias_ref, dq_ref, dk_ref, dv_ref
):
    head_size = q_ref.shape[1] // 2
    rows = q_ref.shape[0]
    kbias = kbias_ref[...]
    for half in range(2):
        cols = pl.ds(half * head_size, head_size)
        key = k_ref[:, cols]
        value = v_ref[:, cols]
        grad_key = None
        grad_value = None
        for chunk in range(rows // QUERY_CHUNK):
            span = pl.ds(chunk * QUERY_CHUNK, QUERY_CHUNK)
            query = q_ref[span, cols]
            grad_out = do_ref[span, cols]
            total = l_ref[span, pl.ds(half * head_size, 1)]
            scores = (
                lax.dot_general(
                    query, key, (((1,), (1,)), ((), ())), preferred_element_type=jnp.float32
                )
                + kbias
            )
            weights = jnp.exp(scores - total)
            grad_weights = lax.dot_general(
                grad_out, value, (((1,), (1,)), ((), ())), preferred_element_type=jnp.float32
            )
            delta = jnp.sum(weights * grad_weights, axis=1, keepdims=True)
            grad_scores = (weights * (grad_weights - delta)).astype(jnp.bfloat16)
            dq_ref[span, cols] = jnp.dot(
                grad_scores, key, preferred_element_type=jnp.float32
            ).astype(dq_ref.dtype)
            key_part = lax.dot_general(
                grad_scores, query, (((0,), (0,)), ((), ())), preferred_element_type=jnp.float32
            )
            value_part = lax.dot_general(
                weights.astype(jnp.bfloat16),
                grad_out,
                (((0,), (0,)), ((), ())),
                preferred_element_type=jnp.float32,
            )
            grad_key = key_part if grad_key is None else grad_key + key_part
            grad_value = value_part if grad_value is None else grad_value + value_part
        dk_ref[:, cols] = grad_key
        dv_ref[:, cols] = grad_value


def pad_rows(values, rows):
    return jnp.pad(values, ((0, rows - values.shape[0]), (0, 0)))


def attention_pallas(queries, pairs, grad_out=None, totals=None, first_pair=0, pair_span=None):
    query_rows, model_width = queries.shape
    key_rows = pairs.shape[0]
    padded_q = -(-query_rows // QUERY_CHUNK) * QUERY_CHUNK
    padded_k = -(-key_rows // 128) * 128
    pair_count = model_width // 128
    q_pad = pad_rows(queries, padded_q)
    kv_pad = pad_rows(pairs, padded_k)
    kbias = jnp.where(jnp.arange(padded_k) < key_rows, 0.0, MASKED).astype(jnp.float32)[None, :]
    q_spec = pl.BlockSpec((padded_q, 128), lambda j: (0, j))
    k_spec = pl.BlockSpec((padded_k, 128), lambda j: (0, j))
    v_spec = pl.BlockSpec((padded_k, 128), lambda j: (0, j + pair_count))
    b_spec = pl.BlockSpec((1, padded_k), lambda j: (0, 0))
    params = pltpu.CompilerParams(vmem_limit_bytes=48 * 1024 * 1024)
    if grad_out is None:
        mixed, log_totals = pl.pallas_call(
            attention_forward_kernel,
            grid=(pair_count,),
            in_specs=[q_spec, k_spec, v_spec, b_spec],
            out_specs=[q_spec, q_spec],
            out_shape=[
                jax.ShapeDtypeStruct((padded_q, model_width), jnp.bfloat16),
                jax.ShapeDtypeStruct((padded_q, model_width), jnp.float32),
            ],
            compiler_params=params,
        )(q_pad, kv_pad, kv_pad, kbias)
        return mixed[:query_rows], log_totals
    do_pad = pad_rows(grad_out, padded_q)
    span = pair_count if pair_span is None else pair_span
    qi_spec = pl.BlockSpec((padded_q, 128), lambda j: (0, j + first_pair))
    ki_spec = pl.BlockSpec((padded_k, 128), lambda j: (0, j + first_pair))
    vi_spec = pl.BlockSpec((padded_k, 128), lambda j: (0, j + first_pair + pair_count))
    qo_spec = pl.BlockSpec((padded_q, 128), lambda j: (0, j))
    ko_spec = pl.BlockSpec((padded_k, 128), lambda j: (0, j))
    dq, dk, dv = pl.pallas_call(
        attention_backward_kernel,
        grid=(span,),
        in_specs=[qi_spec, ki_spec, vi_spec, qi_spec, qi_spec, b_spec],
        out_specs=[qo_spec, ko_spec, ko_spec],
        out_shape=[
            jax.ShapeDtypeStruct((padded_q, 128 * span), jnp.float32),
            jax.ShapeDtypeStruct((padded_k, 128 * span), jnp.float32),
            jax.ShapeDtypeStruct((padded_k, 128 * span), jnp.float32),
        ],
        compiler_params=params,
    )(q_pad, kv_pad, kv_pad, do_pad, totals, kbias)
    return dq[:query_rows], dk[:key_rows], dv[:key_rows]


def attend_forward(queries, keys_values, head_count):
    model_width = queries.shape[2]
    head_size = model_width // head_count
    score_scale = 1.0 / math.sqrt(head_size)

    def one_head(head_index):
        offset = head_index * head_size
        query_block = lax.dynamic_slice_in_dim(queries, offset, head_size, 2)
        key_block = lax.dynamic_slice_in_dim(keys_values, offset, head_size, 2)
        value_block = lax.dynamic_slice_in_dim(keys_values, model_width + offset, head_size, 2)
        scores = (
            jnp.einsum("cqd,ckd->cqk", query_block, key_block, preferred_element_type=jnp.float32)
            * score_scale
        )
        highest = jnp.max(scores, axis=-1, keepdims=True)
        exponent = jnp.exp(scores - highest)
        denominator = jnp.sum(exponent, axis=-1, keepdims=True)
        weights_soft = (exponent / denominator).astype(jnp.bfloat16)
        mixed = jnp.einsum(
            "cqk,ckd->cqd", weights_soft, value_block, preferred_element_type=jnp.float32
        )
        return (mixed, (highest + jnp.log(denominator))[..., 0])

    mixed, log_totals = lax.map(one_head, jnp.arange(head_count))
    clip_count, frame_count = (queries.shape[0], queries.shape[1])
    mixed = jnp.transpose(mixed, (1, 2, 0, 3)).reshape(clip_count, frame_count, model_width)
    return (mixed, log_totals)


def attend_backward(queries, keys_values, grad_mixed, log_totals, head_count):
    model_width = queries.shape[2]
    head_size = model_width // head_count
    score_scale = 1.0 / math.sqrt(head_size)

    def one_head_back(head_index):
        offset = head_index * head_size
        query_block = lax.dynamic_slice_in_dim(queries, offset, head_size, 2)
        key_block = lax.dynamic_slice_in_dim(keys_values, offset, head_size, 2)
        value_block = lax.dynamic_slice_in_dim(keys_values, model_width + offset, head_size, 2)
        grad_block = lax.dynamic_slice_in_dim(grad_mixed, offset, head_size, 2)
        totals = lax.dynamic_index_in_dim(log_totals, head_index, 0, keepdims=False)
        scores = (
            jnp.einsum("cqd,ckd->cqk", query_block, key_block, preferred_element_type=jnp.float32)
            * score_scale
        )
        weights_soft = jnp.exp(scores - totals[..., None])
        grad_weights = jnp.einsum(
            "cqd,ckd->cqk", grad_block, value_block, preferred_element_type=jnp.float32
        )
        delta = jnp.sum(weights_soft * grad_weights, axis=-1, keepdims=True)
        grad_scores = (weights_soft * (grad_weights - delta)).astype(jnp.bfloat16)
        grad_query = (
            jnp.einsum("cqk,ckd->cqd", grad_scores, key_block, preferred_element_type=jnp.float32)
            * score_scale
        )
        grad_key = (
            jnp.einsum("cqk,cqd->ckd", grad_scores, query_block, preferred_element_type=jnp.float32)
            * score_scale
        )
        grad_value = jnp.einsum(
            "cqk,cqd->ckd",
            weights_soft.astype(jnp.bfloat16),
            grad_block,
            preferred_element_type=jnp.float32,
        )
        return (grad_query, delta[..., 0], grad_key, grad_value)

    pieces = lax.map(one_head_back, jnp.arange(head_count))
    clip_count, frame_count = (queries.shape[0], queries.shape[1])
    clip_frames = keys_values.shape[1]
    grad_query = jnp.transpose(pieces[0], (1, 2, 0, 3)).reshape(
        clip_count, frame_count, model_width
    )
    grad_key = jnp.transpose(pieces[2], (1, 2, 0, 3)).reshape(clip_count, clip_frames, model_width)
    grad_value = jnp.transpose(pieces[3], (1, 2, 0, 3)).reshape(
        clip_count, clip_frames, model_width
    )
    return (grad_query, pieces[1], jnp.concatenate([grad_key, grad_value], axis=2))


def link_plan(mesh):
    devices = list(mesh.devices.reshape(-1))
    bit_count = len(devices).bit_length() - 1
    core_bit = 1
    for bit in range(bit_count):
        first, other = devices[0], devices[1 << bit]
        if getattr(first, "coords", None) is not None and tuple(first.coords) == tuple(other.coords):
            core_bit = bit
    others = [bit for bit in range(bit_count) if bit != core_bit]
    near, far = others[:-1], others[-1:]
    rotated = tuple(tuple(near[k:] + near[:k] + far) for k in range(3))
    inner = [bit for bit in near if bit != 0]
    late = tuple(tuple(inner[k:] + inner[:k] + [0] + far) for k in range(2))
    return bit_count, core_bit, rotated, late


def tree_reduce_scatter(terms, orders, plan_bits, hooks=None):
    hooks = dict(hooks or {})
    tied = {}
    bit_count, core_bit = plan_bits
    device = lax.axis_index("clip") * lax.axis_size("frame") + lax.axis_index("frame")
    blocks = 1 << bit_count
    parts = []
    for term in terms:
        shape = (2,) * bit_count + (term.shape[0] // blocks, term.shape[1])
        parts.append((term.reshape(shape), list(range(bit_count - 1, -1, -1))))
    plans = [(core_bit,) + tuple(order) for order in orders]
    for stage in range(len(plans[0])):
        new_parts = []
        for (part, part_bits), plan in zip(parts, plans):
            bit = plan[stage]
            axis = part_bits.index(bit)
            mine = (device >> bit) & 1
            keep = lax.dynamic_index_in_dim(part, mine, axis=axis, keepdims=False)
            send = lax.dynamic_index_in_dim(part, 1 - mine, axis=axis, keepdims=False)
            pairs = [(index, index ^ (1 << bit)) for index in range(blocks)]
            got = lax.ppermute(send.astype(jnp.bfloat16), ("clip", "frame"), pairs)
            new_parts.append(
                (keep.astype(jnp.float32) + got.astype(jnp.float32), [b for b in part_bits if b != bit])
            )
        if stage in hooks:
            values, tied[stage] = lax.optimization_barrier(
                ([part for part, _ in new_parts], hooks[stage](tied))
            )
            new_parts = [(value, part_bits) for value, (_, part_bits) in zip(values, new_parts)]
        parts = new_parts
    return [part for part, _ in parts], tied


def tree_all_gather(local, part_columns, orders, plan_bits):
    bit_count, core_bit = plan_bits
    device = lax.axis_index("clip") * lax.axis_size("frame") + lax.axis_index("frame")
    canonical = list(range(bit_count - 1, -1, -1))

    def double(data, bits, bit):
        mine = (device >> bit) & 1
        pairs = [(index, index ^ (1 << bit)) for index in range(1 << bit_count)]
        got = lax.ppermute(data, ("clip", "frame"), pairs)
        new_bits = sorted(bits + [bit], reverse=True)
        axis = new_bits.index(bit)
        low_first = jnp.stack([data, got], axis=axis)
        high_first = jnp.stack([got, data], axis=axis)
        return jnp.where(mine == 0, low_first, high_first), new_bits

    parts = []
    offset = 0
    for width in part_columns:
        parts.append((local[:, offset : offset + width], []))
        offset += width
    reversed_orders = [list(reversed(order)) for order in orders]
    for stage in range(len(reversed_orders[0])):
        parts = [double(part, bits, order[stage]) for (part, bits), order in zip(parts, reversed_orders)]
    whole = jnp.concatenate([part for part, _ in parts], axis=-1)
    whole, bits = double(whole, parts[0][1], core_bit)
    assert bits == canonical
    return whole.reshape((1 << bit_count) * local.shape[0], local.shape[1])


def adam_step(weight, moments, gradient):
    first = beta_first * moments[0] + (1.0 - beta_first) * gradient
    second = beta_second * moments[1] + (1.0 - beta_second) * gradient * gradient
    first_hat = first / (1.0 - beta_first**ADAM_STEP)
    second_hat = second / (1.0 - beta_second**ADAM_STEP)
    change = -learn_rate * (first_hat / (jnp.sqrt(second_hat) + epsilon_adam) + decay_rate * weight)
    return (change, jnp.stack([first, second]))


def body(
    plan,
    inputs,
    cotangent,
    project_in,
    project_out,
    expand_weight,
    shrink_weight,
    expand_bias,
    vectors,
    moments_in,
    moments_out,
    moments_expand,
    moments_shrink,
    moments_bias,
    moments_vectors,
):
    clip_count, frame_count, model_width = inputs.shape
    row_count = clip_count * frame_count
    head_count = HEADS
    shard_rows = project_in.shape[0]
    wide_in = project_in.shape[1]
    ff_width = expand_weight.shape[1]
    swap = [(0, 1), (1, 0)]
    everyone = ("clip", "frame")

    small = jnp.concatenate(
        [
            vectors,
            expand_bias.reshape(shard_rows, -1),
            jnp.zeros((shard_rows, 128 - vectors.shape[1] - expand_bias.shape[0] // shard_rows), jnp.float32),
        ],
        axis=1,
    )
    first_pack = jnp.concatenate([project_in, small], axis=1).astype(jnp.bfloat16)
    second_pack = jnp.concatenate(
        [project_out, expand_weight, shrink_weight.reshape(shard_rows, -1)], axis=1
    ).astype(jnp.bfloat16)
    bit_count, core_bit, rotated_orders, late_orders = plan
    first_full = tree_all_gather(first_pack, (896, 768, 768), rotated_orders, (bit_count, core_bit))
    second_full = lax.all_gather(second_pack, everyone, axis=0, tiled=True)
    full_in = first_full[:, :wide_in]
    small_full = first_full[:, wide_in:].astype(jnp.float32)
    column_set = small_full[:, : vectors.shape[1]]
    full_bias = small_full[:, vectors.shape[1] : vectors.shape[1] + ff_width // model_width].reshape(-1)
    full_out = second_full[:, :model_width]
    full_expand = second_full[:, model_width : model_width + ff_width]
    full_shrink = second_full[:, model_width + ff_width :].reshape(ff_width, model_width)

    frames_rows = inputs.reshape(row_count, model_width).astype(jnp.float32)
    normed_first, plain_first, inv_first = norm_parts(
        frames_rows, column_set[:, 0], column_set[:, 1]
    )
    hidden_first = normed_first.astype(jnp.bfloat16)
    partner_rows = lax.ppermute(inputs, "frame", swap).reshape(row_count, model_width)
    hidden_partner = norm_parts(
        partner_rows.astype(jnp.float32), column_set[:, 0], column_set[:, 1]
    )[0].astype(jnp.bfloat16)
    bias_in = jnp.concatenate(
        [column_set[:, 2], jnp.zeros((model_width,), jnp.float32), column_set[:, 3]]
    )
    projected = (
        jnp.dot(hidden_first, full_in, preferred_element_type=jnp.float32) + bias_in
    ).astype(jnp.bfloat16)
    partner_pairs = (
        jnp.dot(hidden_partner, full_in[:, model_width:], preferred_element_type=jnp.float32)
        + bias_in[model_width:]
    ).astype(jnp.bfloat16)
    queries = projected[:, :model_width].reshape(clip_count, frame_count, model_width)
    clip_pairs = jnp.concatenate([projected[:, model_width:], partner_pairs], axis=0).reshape(
        clip_count, 2 * frame_count, 2 * model_width
    )
    score_scale = 1.0 / math.sqrt(model_width // head_count)
    scaled_queries = (projected[:, :model_width] * score_scale).astype(jnp.bfloat16)
    pair_rows = clip_pairs.reshape(2 * row_count, 2 * model_width)
    mixed_low, log_totals = attention_pallas(scaled_queries, pair_rows)
    attended = jnp.dot(mixed_low, full_out, preferred_element_type=jnp.float32) + column_set[:, 4]
    residual = frames_rows + attended
    normed_second, plain_second, inv_second = norm_parts(
        residual, column_set[:, 5], column_set[:, 6]
    )
    hidden_second = normed_second.astype(jnp.bfloat16)
    preact = jnp.dot(hidden_second, full_expand, preferred_element_type=jnp.float32) + full_bias
    activated = gelu_exact(preact).astype(jnp.bfloat16)
    result = (
        residual
        + jnp.dot(activated, full_shrink, preferred_element_type=jnp.float32)
        + column_set[:, 7]
    )
    output = result.astype(jnp.bfloat16).reshape(inputs.shape)

    grad_result = cotangent.reshape(row_count, model_width)
    grad_shrink_term = jnp.dot(
        activated.T, grad_result, preferred_element_type=jnp.float32
    ).astype(jnp.bfloat16)
    grad_down_bias = jnp.sum(grad_result.astype(jnp.float32), axis=0)
    grad_activated = jnp.dot(grad_result, full_shrink.T, preferred_element_type=jnp.float32)
    grad_preact = (grad_activated * gelu_slope(preact)).astype(jnp.bfloat16)
    grad_expand_term = jnp.dot(
        hidden_second.T, grad_preact, preferred_element_type=jnp.float32
    ).astype(jnp.bfloat16)
    grad_bias_term = jnp.sum(grad_preact.astype(jnp.float32), axis=0)
    grad_hidden_second = jnp.dot(grad_preact, full_expand.T, preferred_element_type=jnp.float32)
    norm_term_second, gain_second, shift_second = norm_backward(
        grad_hidden_second, plain_second, inv_second, column_set[:, 5]
    )
    grad_residual = grad_result.astype(jnp.float32) + norm_term_second
    grad_attended = grad_residual.astype(jnp.bfloat16)
    grad_out_term = jnp.dot(
        mixed_low.T, grad_attended, preferred_element_type=jnp.float32
    ).astype(jnp.bfloat16)
    grad_out_bias = jnp.sum(grad_attended.astype(jnp.float32), axis=0)
    late_terms = [grad_shrink_term.reshape(model_width, -1), grad_expand_term, grad_out_term]
    grad_mixed = jnp.dot(grad_attended, full_out.T, preferred_element_type=jnp.float32).astype(
        jnp.bfloat16
    )
    piece_pairs = 2
    piece_count = model_width // 128 // piece_pairs

    def run_piece(index, mixed_grads):
        return attention_pallas(
            scaled_queries, pair_rows, mixed_grads, log_totals, index * piece_pairs, piece_pairs
        )

    def piece_hook(index):
        return lambda tied: (run_piece(index, tied[index - 1][1]), tied[index - 1][1])

    hooks = {0: lambda tied: ((), grad_mixed)}
    hooks.update({index: piece_hook(index) for index in range(1, piece_count)})
    pieces = [run_piece(0, grad_mixed)]
    owned_late, tied = tree_reduce_scatter(
        late_terms, [late_orders[index % len(late_orders)] for index in range(3)], (bit_count, core_bit), hooks
    )
    pieces += [tied[index][0] for index in range(1, piece_count)]
    finished = []
    for grad_query, grad_keys, grad_values in pieces:
        terms = jnp.concatenate([grad_keys, grad_values], axis=1)
        returned = lax.ppermute(terms[row_count:].astype(jnp.bfloat16), "frame", swap)
        finished.append((grad_query, terms[:row_count] + returned.astype(jnp.float32)))
    piece_width = finished[0][0].shape[1]
    grad_query_all = (jnp.concatenate([query for query, _ in finished], axis=1) * score_scale).astype(
        jnp.bfloat16
    )
    grad_key_all = jnp.concatenate([pair[:, :piece_width] for _, pair in finished], axis=1).astype(
        jnp.bfloat16
    )
    grad_value_all = jnp.concatenate([pair[:, piece_width:] for _, pair in finished], axis=1).astype(
        jnp.bfloat16
    )
    grad_blocks = (grad_query_all, grad_key_all, grad_value_all)
    grad_in_terms = [
        jnp.dot(hidden_first.T, block, preferred_element_type=jnp.float32).astype(jnp.bfloat16)
        for block in grad_blocks
    ]
    grad_query_bias = jnp.sum(grad_query_all.astype(jnp.float32), axis=0)
    grad_value_bias = jnp.sum(grad_value_all.astype(jnp.float32), axis=0)
    grad_hidden_first = sum(
        jnp.dot(
            block,
            full_in[:, index * model_width : (index + 1) * model_width].T,
            preferred_element_type=jnp.float32,
        )
        for index, block in enumerate(grad_blocks)
    )
    norm_term_first, gain_first, shift_first = norm_backward(
        grad_hidden_first, plain_first, inv_first, column_set[:, 0]
    )
    grad_inputs = (grad_residual + norm_term_first).astype(jnp.bfloat16).reshape(inputs.shape)
    grad_columns = jnp.stack(
        [
            gain_first,
            shift_first,
            grad_query_bias,
            grad_value_bias,
            grad_out_bias,
            gain_second,
            shift_second,
            grad_down_bias,
        ],
        axis=1,
    )
    small_grads = jnp.concatenate(
        [
            grad_columns,
            grad_bias_term.reshape(model_width, -1),
            jnp.zeros((model_width, 128 - 12), jnp.float32),
        ],
        axis=1,
    )
    owned_first = tree_reduce_scatter(
        grad_in_terms + [small_grads],
        [rotated_orders[index % len(rotated_orders)] for index in range(4)],
        (bit_count, core_bit),
    )[0]
    owned_in = jnp.concatenate(owned_first[:3], axis=1)
    owned_vectors = owned_first[3][:, : vectors.shape[1]]
    owned_bias = owned_first[3][:, vectors.shape[1] : 12].reshape(-1)
    owned_shrink = owned_late[0].reshape(shrink_weight.shape)
    owned_expand = owned_late[1]
    owned_out = owned_late[2]
    new_in, mom_in = adam_step(project_in, moments_in, owned_in)
    new_out, mom_out = adam_step(project_out, moments_out, owned_out)
    new_expand, mom_expand = adam_step(expand_weight, moments_expand, owned_expand)
    new_shrink, mom_shrink = adam_step(shrink_weight, moments_shrink, owned_shrink)
    new_bias, mom_bias = adam_step(expand_bias, moments_bias, owned_bias)
    new_vectors, mom_vectors = adam_step(vectors, moments_vectors, owned_vectors)
    return (
        output,
        grad_inputs,
        owned_in,
        owned_out,
        owned_expand,
        owned_shrink,
        owned_bias,
        owned_vectors,
        new_in,
        new_out,
        new_expand,
        new_shrink,
        new_bias,
        new_vectors,
        mom_in,
        mom_out,
        mom_expand,
        mom_shrink,
        mom_bias,
        mom_vectors,
    )


def solution(mesh):
    in_specs = (
        P("clip", "frame", None),
        P("clip", "frame", None),
        P(("clip", "frame"), None),
        P(("clip", "frame"), None),
        P(("clip", "frame"), None),
        P(("clip", "frame"), None),
        P(("clip", "frame")),
        P(("clip", "frame"), None),
        P(None, ("clip", "frame"), None),
        P(None, ("clip", "frame"), None),
        P(None, ("clip", "frame"), None),
        P(None, ("clip", "frame"), None),
        P(None, ("clip", "frame")),
        P(None, ("clip", "frame"), None),
    )
    out_specs = (
        P("clip", "frame", None),
        P("clip", "frame", None),
        P(("clip", "frame"), None),
        P(("clip", "frame"), None),
        P(("clip", "frame"), None),
        P(("clip", "frame"), None),
        P(("clip", "frame")),
        P(("clip", "frame"), None),
        P(("clip", "frame"), None),
        P(("clip", "frame"), None),
        P(("clip", "frame"), None),
        P(("clip", "frame"), None),
        P(("clip", "frame")),
        P(("clip", "frame"), None),
        P(None, ("clip", "frame"), None),
        P(None, ("clip", "frame"), None),
        P(None, ("clip", "frame"), None),
        P(None, ("clip", "frame"), None),
        P(None, ("clip", "frame")),
        P(None, ("clip", "frame"), None),
    )
    return jax.shard_map(
        functools.partial(body, link_plan(mesh)),
        mesh=mesh,
        in_specs=in_specs,
        out_specs=out_specs,
        check_vma=False,
    )
```

```python
import functools
import math

import jax
import jax.numpy as jnp
from jax import lax
from jax.experimental import pallas as pl
from jax.experimental.pallas import tpu as pltpu
from jax.sharding import PartitionSpec as P

HEADS = 12
ADAM_STEP = 4


epsilon_norm = 1e-05
beta_first = 0.9
beta_second = 0.99
learn_rate = 0.03
decay_rate = 0.01
epsilon_adam = 1e-08
root_half = 0.7071067811865476
inv_root_two_pi = 0.3989422804014327


def norm_parts(inputs, norm_gain, norm_shift):
    average = jnp.mean(inputs, axis=-1, keepdims=True)
    centered = inputs - average
    spread = jnp.mean(centered * centered, axis=-1, keepdims=True)
    inv_std = lax.rsqrt(spread + epsilon_norm)
    normed = centered * inv_std
    return (normed * norm_gain + norm_shift, normed, inv_std)


def norm_backward(grad_normed, normed, inv_std, norm_gain):
    grad_gain = jnp.sum(grad_normed * normed, axis=0)
    grad_shift = jnp.sum(grad_normed, axis=0)
    scaled = grad_normed * norm_gain
    grad_input = inv_std * (
        scaled
        - jnp.mean(scaled, axis=-1, keepdims=True)
        - normed * jnp.mean(scaled * normed, axis=-1, keepdims=True)
    )
    return (grad_input, grad_gain, grad_shift)


def gelu_exact(inputs):
    return 0.5 * inputs * (1.0 + jax.scipy.special.erf(inputs * root_half))


def gelu_slope(inputs):
    return (
        0.5 * (1.0 + jax.scipy.special.erf(inputs * root_half))
        + inputs * jnp.exp(-0.5 * inputs * inputs) * inv_root_two_pi
    )


QUERY_CHUNK = 256
MASKED = -1e30


def attention_forward_kernel(q_ref, k_ref, v_ref, kbias_ref, o_ref, l_ref):
    head_size = q_ref.shape[1] // 2
    rows = q_ref.shape[0]
    kbias = kbias_ref[...]
    lane = lax.broadcasted_iota(jnp.int32, (QUERY_CHUNK, 2 * head_size), 1)
    for chunk in range(rows // QUERY_CHUNK):
        span = pl.ds(chunk * QUERY_CHUNK, QUERY_CHUNK)
        mixed_parts = []
        totals = []
        for half in range(2):
            cols = pl.ds(half * head_size, head_size)
            query = q_ref[span, cols]
            key = k_ref[:, cols]
            value = v_ref[:, cols]
            scores = (
                lax.dot_general(
                    query, key, (((1,), (1,)), ((), ())), preferred_element_type=jnp.float32
                )
                + kbias
            )
            highest = jnp.max(scores, axis=1, keepdims=True)
            exponent = jnp.exp(scores - highest)
            denominator = jnp.sum(exponent, axis=1, keepdims=True)
            weights = (exponent * (1.0 / denominator)).astype(jnp.bfloat16)
            mixed_parts.append(jnp.dot(weights, value, preferred_element_type=jnp.float32))
            totals.append(highest + jnp.log(denominator))
        o_ref[span, :] = jnp.concatenate(mixed_parts, axis=1).astype(o_ref.dtype)
        l_ref[span, :] = jnp.where(lane < head_size, totals[0], totals[1])


def attention_backward_kernel(
    q_ref, k_ref, v_ref, do_ref, l_ref, kbias_ref, dq_ref, dk_ref, dv_ref
):
    head_size = q_ref.shape[1] // 2
    rows = q_ref.shape[0]
    kbias = kbias_ref[...]
    for half in range(2):
        cols = pl.ds(half * head_size, head_size)
        key = k_ref[:, cols]
        value = v_ref[:, cols]
        grad_key = None
        grad_value = None
        for chunk in range(rows // QUERY_CHUNK):
            span = pl.ds(chunk * QUERY_CHUNK, QUERY_CHUNK)
            query = q_ref[span, cols]
            grad_out = do_ref[span, cols]
            total = l_ref[span, pl.ds(half * head_size, 1)]
            scores = (
                lax.dot_general(
                    query, key, (((1,), (1,)), ((), ())), preferred_element_type=jnp.float32
                )
                + kbias
            )
            weights = jnp.exp(scores - total)
            grad_weights = lax.dot_general(
                grad_out, value, (((1,), (1,)), ((), ())), preferred_element_type=jnp.float32
            )
            delta = jnp.sum(weights * grad_weights, axis=1, keepdims=True)
            grad_scores = (weights * (grad_weights - delta)).astype(jnp.bfloat16)
            dq_ref[span, cols] = jnp.dot(
                grad_scores, key, preferred_element_type=jnp.float32
            ).astype(dq_ref.dtype)
            key_part = lax.dot_general(
                grad_scores, query, (((0,), (0,)), ((), ())), preferred_element_type=jnp.float32
            )
            value_part = lax.dot_general(
                weights.astype(jnp.bfloat16),
                grad_out,
                (((0,), (0,)), ((), ())),
                preferred_element_type=jnp.float32,
            )
            grad_key = key_part if grad_key is None else grad_key + key_part
            grad_value = value_part if grad_value is None else grad_value + value_part
        dk_ref[:, cols] = grad_key
        dv_ref[:, cols] = grad_value


def pad_rows(values, rows):
    return jnp.pad(values, ((0, rows - values.shape[0]), (0, 0)))


def attention_pallas(queries, pairs, grad_out=None, totals=None, first_pair=0, pair_span=None):
    query_rows, model_width = queries.shape
    key_rows = pairs.shape[0]
    padded_q = -(-query_rows // QUERY_CHUNK) * QUERY_CHUNK
    padded_k = -(-key_rows // 128) * 128
    pair_count = model_width // 128
    q_pad = pad_rows(queries, padded_q)
    kv_pad = pad_rows(pairs, padded_k)
    kbias = jnp.where(jnp.arange(padded_k) < key_rows, 0.0, MASKED).astype(jnp.float32)[None, :]
    q_spec = pl.BlockSpec((padded_q, 128), lambda j: (0, j))
    k_spec = pl.BlockSpec((padded_k, 128), lambda j: (0, j))
    v_spec = pl.BlockSpec((padded_k, 128), lambda j: (0, j + pair_count))
    b_spec = pl.BlockSpec((1, padded_k), lambda j: (0, 0))
    params = pltpu.CompilerParams(vmem_limit_bytes=48 * 1024 * 1024)
    if grad_out is None:
        mixed, log_totals = pl.pallas_call(
            attention_forward_kernel,
            grid=(pair_count,),
            in_specs=[q_spec, k_spec, v_spec, b_spec],
            out_specs=[q_spec, q_spec],
            out_shape=[
                jax.ShapeDtypeStruct((padded_q, model_width), jnp.bfloat16),
                jax.ShapeDtypeStruct((padded_q, model_width), jnp.float32),
            ],
            compiler_params=params,
        )(q_pad, kv_pad, kv_pad, kbias)
        return mixed[:query_rows], log_totals
    do_pad = pad_rows(grad_out, padded_q)
    span = pair_count if pair_span is None else pair_span
    qi_spec = pl.BlockSpec((padded_q, 128), lambda j: (0, j + first_pair))
    ki_spec = pl.BlockSpec((padded_k, 128), lambda j: (0, j + first_pair))
    vi_spec = pl.BlockSpec((padded_k, 128), lambda j: (0, j + first_pair + pair_count))
    qo_spec = pl.BlockSpec((padded_q, 128), lambda j: (0, j))
    ko_spec = pl.BlockSpec((padded_k, 128), lambda j: (0, j))
    dq, dk, dv = pl.pallas_call(
        attention_backward_kernel,
        grid=(span,),
        in_specs=[qi_spec, ki_spec, vi_spec, qi_spec, qi_spec, b_spec],
        out_specs=[qo_spec, ko_spec, ko_spec],
        out_shape=[
            jax.ShapeDtypeStruct((padded_q, 128 * span), jnp.float32),
            jax.ShapeDtypeStruct((padded_k, 128 * span), jnp.float32),
            jax.ShapeDtypeStruct((padded_k, 128 * span), jnp.float32),
        ],
        compiler_params=params,
    )(q_pad, kv_pad, kv_pad, do_pad, totals, kbias)
    return dq[:query_rows], dk[:key_rows], dv[:key_rows]


def attend_forward(queries, keys_values, head_count):
    model_width = queries.shape[2]
    head_size = model_width // head_count
    score_scale = 1.0 / math.sqrt(head_size)

    def one_head(head_index):
        offset = head_index * head_size
        query_block = lax.dynamic_slice_in_dim(queries, offset, head_size, 2)
        key_block = lax.dynamic_slice_in_dim(keys_values, offset, head_size, 2)
        value_block = lax.dynamic_slice_in_dim(keys_values, model_width + offset, head_size, 2)
        scores = (
            jnp.einsum("cqd,ckd->cqk", query_block, key_block, preferred_element_type=jnp.float32)
            * score_scale
        )
        highest = jnp.max(scores, axis=-1, keepdims=True)
        exponent = jnp.exp(scores - highest)
        denominator = jnp.sum(exponent, axis=-1, keepdims=True)
        weights_soft = (exponent / denominator).astype(jnp.bfloat16)
        mixed = jnp.einsum(
            "cqk,ckd->cqd", weights_soft, value_block, preferred_element_type=jnp.float32
        )
        return (mixed, (highest + jnp.log(denominator))[..., 0])

    mixed, log_totals = lax.map(one_head, jnp.arange(head_count))
    clip_count, frame_count = (queries.shape[0], queries.shape[1])
    mixed = jnp.transpose(mixed, (1, 2, 0, 3)).reshape(clip_count, frame_count, model_width)
    return (mixed, log_totals)


def attend_backward(queries, keys_values, grad_mixed, log_totals, head_count):
    model_width = queries.shape[2]
    head_size = model_width // head_count
    score_scale = 1.0 / math.sqrt(head_size)

    def one_head_back(head_index):
        offset = head_index * head_size
        query_block = lax.dynamic_slice_in_dim(queries, offset, head_size, 2)
        key_block = lax.dynamic_slice_in_dim(keys_values, offset, head_size, 2)
        value_block = lax.dynamic_slice_in_dim(keys_values, model_width + offset, head_size, 2)
        grad_block = lax.dynamic_slice_in_dim(grad_mixed, offset, head_size, 2)
        totals = lax.dynamic_index_in_dim(log_totals, head_index, 0, keepdims=False)
        scores = (
            jnp.einsum("cqd,ckd->cqk", query_block, key_block, preferred_element_type=jnp.float32)
            * score_scale
        )
        weights_soft = jnp.exp(scores - totals[..., None])
        grad_weights = jnp.einsum(
            "cqd,ckd->cqk", grad_block, value_block, preferred_element_type=jnp.float32
        )
        delta = jnp.sum(weights_soft * grad_weights, axis=-1, keepdims=True)
        grad_scores = (weights_soft * (grad_weights - delta)).astype(jnp.bfloat16)
        grad_query = (
            jnp.einsum("cqk,ckd->cqd", grad_scores, key_block, preferred_element_type=jnp.float32)
            * score_scale
        )
        grad_key = (
            jnp.einsum("cqk,cqd->ckd", grad_scores, query_block, preferred_element_type=jnp.float32)
            * score_scale
        )
        grad_value = jnp.einsum(
            "cqk,cqd->ckd",
            weights_soft.astype(jnp.bfloat16),
            grad_block,
            preferred_element_type=jnp.float32,
        )
        return (grad_query, delta[..., 0], grad_key, grad_value)

    pieces = lax.map(one_head_back, jnp.arange(head_count))
    clip_count, frame_count = (queries.shape[0], queries.shape[1])
    clip_frames = keys_values.shape[1]
    grad_query = jnp.transpose(pieces[0], (1, 2, 0, 3)).reshape(
        clip_count, frame_count, model_width
    )
    grad_key = jnp.transpose(pieces[2], (1, 2, 0, 3)).reshape(clip_count, clip_frames, model_width)
    grad_value = jnp.transpose(pieces[3], (1, 2, 0, 3)).reshape(
        clip_count, clip_frames, model_width
    )
    return (grad_query, pieces[1], jnp.concatenate([grad_key, grad_value], axis=2))


def link_plan(mesh):
    devices = list(mesh.devices.reshape(-1))
    bit_count = len(devices).bit_length() - 1
    core_bit = 1
    for bit in range(bit_count):
        first, other = devices[0], devices[1 << bit]
        if getattr(first, "coords", None) is not None and tuple(first.coords) == tuple(other.coords):
            core_bit = bit
    others = [bit for bit in range(bit_count) if bit != core_bit]
    near, far = others[:-1], others[-1:]
    rotated = tuple(tuple(near[k:] + near[:k] + far) for k in range(3))
    inner = [bit for bit in near if bit != 0]
    late = tuple(tuple(inner[k:] + inner[:k] + [0] + far) for k in range(2))
    return bit_count, core_bit, rotated, late


def tree_reduce_scatter(terms, part_columns, orders, plan_bits, hooks=None):
    hooks = dict(hooks or {})
    tied = {}
    bit_count, core_bit = plan_bits
    device = lax.axis_index("clip") * lax.axis_size("frame") + lax.axis_index("frame")
    blocks = 1 << bit_count
    block_rows = terms.shape[0] // blocks
    data = terms.reshape((2,) * bit_count + (block_rows, terms.shape[1]))
    parts = [(data, list(range(bit_count - 1, -1, -1)))]
    plan = [(core_bit,)] + [tuple(order[stage] for order in orders) for stage in range(len(orders[0]))]
    for stage, stage_bits in enumerate(plan):
        if stage == 1:
            whole, bits = parts[0]
            parts = []
            offset = 0
            for width in part_columns:
                parts.append((whole[..., offset : offset + width], bits))
                offset += width
        keeps, sends = [], []
        for (part, part_bits), bit in zip(parts, stage_bits):
            axis = part_bits.index(bit)
            mine = (device >> bit) & 1
            keeps.append(lax.dynamic_index_in_dim(part, mine, axis=axis, keepdims=False))
            sends.append(
                lax.dynamic_index_in_dim(part, 1 - mine, axis=axis, keepdims=False).astype(jnp.bfloat16)
            )
        new_parts = []
        for keep, send, (part, part_bits), bit in zip(keeps, sends, parts, stage_bits):
            pairs = [(index, index ^ (1 << bit)) for index in range(blocks)]
            got = lax.ppermute(send, ("clip", "frame"), pairs)
            new_parts.append((keep + got.astype(jnp.float32), [b for b in part_bits if b != bit]))
        if stage in hooks:
            values, tied[stage] = lax.optimization_barrier(
                ([part for part, _ in new_parts], hooks[stage](tied))
            )
            new_parts = [(value, part_bits) for value, (_, part_bits) in zip(values, new_parts)]
        parts = new_parts
    return jnp.concatenate([part for part, _ in parts], axis=-1).astype(jnp.float32), tied


def tree_reduce_scatter_parts(terms, orders, plan_bits, hooks=None):
    hooks = dict(hooks or {})
    tied = {}
    bit_count, core_bit = plan_bits
    device = lax.axis_index("clip") * lax.axis_size("frame") + lax.axis_index("frame")
    blocks = 1 << bit_count
    parts = []
    for term in terms:
        shape = (2,) * bit_count + (term.shape[0] // blocks, term.shape[1])
        parts.append((term.reshape(shape), list(range(bit_count - 1, -1, -1))))
    plans = [(core_bit,) + tuple(order) for order in orders]
    for stage in range(len(plans[0])):
        new_parts = []
        for (part, part_bits), plan in zip(parts, plans):
            bit = plan[stage]
            axis = part_bits.index(bit)
            mine = (device >> bit) & 1
            keep = lax.dynamic_index_in_dim(part, mine, axis=axis, keepdims=False)
            send = lax.dynamic_index_in_dim(part, 1 - mine, axis=axis, keepdims=False)
            pairs = [(index, index ^ (1 << bit)) for index in range(blocks)]
            got = lax.ppermute(send.astype(jnp.bfloat16), ("clip", "frame"), pairs)
            new_parts.append(
                (keep.astype(jnp.float32) + got.astype(jnp.float32), [b for b in part_bits if b != bit])
            )
        if stage in hooks:
            values, tied[stage] = lax.optimization_barrier(
                ([part for part, _ in new_parts], hooks[stage](tied))
            )
            new_parts = [(value, part_bits) for value, (_, part_bits) in zip(values, new_parts)]
        parts = new_parts
    return [part for part, _ in parts], tied


def tree_all_gather(local, part_columns, orders, plan_bits):
    bit_count, core_bit = plan_bits
    device = lax.axis_index("clip") * lax.axis_size("frame") + lax.axis_index("frame")
    canonical = list(range(bit_count - 1, -1, -1))

    def double(data, bits, bit):
        mine = (device >> bit) & 1
        pairs = [(index, index ^ (1 << bit)) for index in range(1 << bit_count)]
        got = lax.ppermute(data, ("clip", "frame"), pairs)
        new_bits = sorted(bits + [bit], reverse=True)
        axis = new_bits.index(bit)
        low_first = jnp.stack([data, got], axis=axis)
        high_first = jnp.stack([got, data], axis=axis)
        return jnp.where(mine == 0, low_first, high_first), new_bits

    parts = []
    offset = 0
    for width in part_columns:
        parts.append((local[:, offset : offset + width], []))
        offset += width
    reversed_orders = [list(reversed(order)) for order in orders]
    for stage in range(len(reversed_orders[0])):
        parts = [double(part, bits, order[stage]) for (part, bits), order in zip(parts, reversed_orders)]
    whole = jnp.concatenate([part for part, _ in parts], axis=-1)
    whole, bits = double(whole, parts[0][1], core_bit)
    assert bits == canonical
    return whole.reshape((1 << bit_count) * local.shape[0], local.shape[1])


def adam_step(weight, moments, gradient):
    first = beta_first * moments[0] + (1.0 - beta_first) * gradient
    second = beta_second * moments[1] + (1.0 - beta_second) * gradient * gradient
    first_hat = first / (1.0 - beta_first**ADAM_STEP)
    second_hat = second / (1.0 - beta_second**ADAM_STEP)
    change = -learn_rate * (first_hat / (jnp.sqrt(second_hat) + epsilon_adam) + decay_rate * weight)
    return (change, jnp.stack([first, second]))


def body(
    plan,
    inputs,
    cotangent,
    project_in,
    project_out,
    expand_weight,
    shrink_weight,
    expand_bias,
    vectors,
    moments_in,
    moments_out,
    moments_expand,
    moments_shrink,
    moments_bias,
    moments_vectors,
):
    clip_count, frame_count, model_width = inputs.shape
    row_count = clip_count * frame_count
    head_count = HEADS
    shard_rows = project_in.shape[0]
    wide_in = project_in.shape[1]
    ff_width = expand_weight.shape[1]
    swap = [(0, 1), (1, 0)]
    everyone = ("clip", "frame")

    small = jnp.concatenate(
        [
            vectors,
            expand_bias.reshape(shard_rows, -1),
            jnp.zeros((shard_rows, 128 - vectors.shape[1] - expand_bias.shape[0] // shard_rows), jnp.float32),
        ],
        axis=1,
    )
    first_pack = jnp.concatenate([project_in, small], axis=1).astype(jnp.bfloat16)
    second_pack = jnp.concatenate(
        [project_out, expand_weight, shrink_weight.reshape(shard_rows, -1)], axis=1
    ).astype(jnp.bfloat16)
    bit_count, core_bit, rotated_orders, late_orders = plan
    first_full = tree_all_gather(first_pack, (896, 768, 768), rotated_orders, (bit_count, core_bit))
    second_full = lax.all_gather(second_pack, everyone, axis=0, tiled=True)
    full_in = first_full[:, :wide_in]
    small_full = first_full[:, wide_in:].astype(jnp.float32)
    column_set = small_full[:, : vectors.shape[1]]
    full_bias = small_full[:, vectors.shape[1] : vectors.shape[1] + ff_width // model_width].reshape(-1)
    full_out = second_full[:, :model_width]
    full_expand = second_full[:, model_width : model_width + ff_width]
    full_shrink = second_full[:, model_width + ff_width :].reshape(ff_width, model_width)

    frames_rows = inputs.reshape(row_count, model_width).astype(jnp.float32)
    normed_first, plain_first, inv_first = norm_parts(
        frames_rows, column_set[:, 0], column_set[:, 1]
    )
    hidden_first = normed_first.astype(jnp.bfloat16)
    partner_rows = lax.ppermute(inputs, "frame", swap).reshape(row_count, model_width)
    hidden_partner = norm_parts(
        partner_rows.astype(jnp.float32), column_set[:, 0], column_set[:, 1]
    )[0].astype(jnp.bfloat16)
    bias_in = jnp.concatenate(
        [column_set[:, 2], jnp.zeros((model_width,), jnp.float32), column_set[:, 3]]
    )
    projected = (
        jnp.dot(hidden_first, full_in, preferred_element_type=jnp.float32) + bias_in
    ).astype(jnp.bfloat16)
    partner_pairs = (
        jnp.dot(hidden_partner, full_in[:, model_width:], preferred_element_type=jnp.float32)
        + bias_in[model_width:]
    ).astype(jnp.bfloat16)
    queries = projected[:, :model_width].reshape(clip_count, frame_count, model_width)
    clip_pairs = jnp.concatenate([projected[:, model_width:], partner_pairs], axis=0).reshape(
        clip_count, 2 * frame_count, 2 * model_width
    )
    score_scale = 1.0 / math.sqrt(model_width // head_count)
    scaled_queries = (projected[:, :model_width] * score_scale).astype(jnp.bfloat16)
    pair_rows = clip_pairs.reshape(2 * row_count, 2 * model_width)
    mixed_low, log_totals = attention_pallas(scaled_queries, pair_rows)
    attended = jnp.dot(mixed_low, full_out, preferred_element_type=jnp.float32) + column_set[:, 4]
    residual = frames_rows + attended
    normed_second, plain_second, inv_second = norm_parts(
        residual, column_set[:, 5], column_set[:, 6]
    )
    hidden_second = normed_second.astype(jnp.bfloat16)
    preact = jnp.dot(hidden_second, full_expand, preferred_element_type=jnp.float32) + full_bias
    activated = gelu_exact(preact).astype(jnp.bfloat16)
    result = (
        residual
        + jnp.dot(activated, full_shrink, preferred_element_type=jnp.float32)
        + column_set[:, 7]
    )
    output = result.astype(jnp.bfloat16).reshape(inputs.shape)

    grad_result = cotangent.reshape(row_count, model_width)
    grad_shrink_term = jnp.dot(
        activated.T, grad_result, preferred_element_type=jnp.float32
    ).astype(jnp.bfloat16)
    grad_down_bias = jnp.sum(grad_result.astype(jnp.float32), axis=0)
    grad_activated = jnp.dot(grad_result, full_shrink.T, preferred_element_type=jnp.float32)
    grad_preact = (grad_activated * gelu_slope(preact)).astype(jnp.bfloat16)
    grad_expand_term = jnp.dot(
        hidden_second.T, grad_preact, preferred_element_type=jnp.float32
    ).astype(jnp.bfloat16)
    grad_bias_term = jnp.sum(grad_preact.astype(jnp.float32), axis=0)
    grad_hidden_second = jnp.dot(grad_preact, full_expand.T, preferred_element_type=jnp.float32)
    norm_term_second, gain_second, shift_second = norm_backward(
        grad_hidden_second, plain_second, inv_second, column_set[:, 5]
    )
    grad_residual = grad_result.astype(jnp.float32) + norm_term_second
    grad_attended = grad_residual.astype(jnp.bfloat16)
    grad_out_term = jnp.dot(
        mixed_low.T, grad_attended, preferred_element_type=jnp.float32
    ).astype(jnp.bfloat16)
    grad_out_bias = jnp.sum(grad_attended.astype(jnp.float32), axis=0)
    late_terms = jnp.concatenate(
        [grad_shrink_term.reshape(model_width, -1), grad_expand_term, grad_out_term], axis=1
    )
    grad_mixed = jnp.dot(grad_attended, full_out.T, preferred_element_type=jnp.float32).astype(
        jnp.bfloat16
    )
    piece_pairs = 2
    piece_count = model_width // 128 // piece_pairs

    def run_piece(index, mixed_grads):
        return attention_pallas(
            scaled_queries, pair_rows, mixed_grads, log_totals, index * piece_pairs, piece_pairs
        )

    def piece_hook(index):
        return lambda tied: (run_piece(index, tied[index - 1][1]), tied[index - 1][1])

    hooks = {0: lambda tied: ((), grad_mixed)}
    hooks.update({index: piece_hook(index) for index in range(1, piece_count)})
    pieces = [run_piece(0, grad_mixed)]
    owned_late, tied = tree_reduce_scatter(
        late_terms, (3456, 3456), late_orders, (bit_count, core_bit), hooks
    )
    pieces += [tied[index][0] for index in range(1, piece_count)]
    finished = []
    for grad_query, grad_keys, grad_values in pieces:
        terms = jnp.concatenate([grad_keys, grad_values], axis=1)
        returned = lax.ppermute(terms[row_count:].astype(jnp.bfloat16), "frame", swap)
        finished.append((grad_query, terms[:row_count] + returned.astype(jnp.float32)))
    piece_width = finished[0][0].shape[1]
    grad_query_all = (jnp.concatenate([query for query, _ in finished], axis=1) * score_scale).astype(
        jnp.bfloat16
    )
    grad_key_all = jnp.concatenate([pair[:, :piece_width] for _, pair in finished], axis=1).astype(
        jnp.bfloat16
    )
    grad_value_all = jnp.concatenate([pair[:, piece_width:] for _, pair in finished], axis=1).astype(
        jnp.bfloat16
    )
    grad_blocks = (grad_query_all, grad_key_all, grad_value_all)
    grad_in_terms = [
        jnp.dot(hidden_first.T, block, preferred_element_type=jnp.float32).astype(jnp.bfloat16)
        for block in grad_blocks
    ]
    grad_query_bias = jnp.sum(grad_query_all.astype(jnp.float32), axis=0)
    grad_value_bias = jnp.sum(grad_value_all.astype(jnp.float32), axis=0)
    grad_hidden_first = sum(
        jnp.dot(
            block,
            full_in[:, index * model_width : (index + 1) * model_width].T,
            preferred_element_type=jnp.float32,
        )
        for index, block in enumerate(grad_blocks)
    )
    norm_term_first, gain_first, shift_first = norm_backward(
        grad_hidden_first, plain_first, inv_first, column_set[:, 0]
    )
    grad_inputs = (grad_residual + norm_term_first).astype(jnp.bfloat16).reshape(inputs.shape)
    grad_columns = jnp.stack(
        [
            gain_first,
            shift_first,
            grad_query_bias,
            grad_value_bias,
            grad_out_bias,
            gain_second,
            shift_second,
            grad_down_bias,
        ],
        axis=1,
    )
    small_grads = jnp.concatenate(
        [
            grad_columns,
            grad_bias_term.reshape(model_width, -1),
            jnp.zeros((model_width, 128 - 12), jnp.float32),
        ],
        axis=1,
    )
    owned_first = tree_reduce_scatter_parts(
        grad_in_terms + [small_grads],
        [rotated_orders[index % len(rotated_orders)] for index in range(4)],
        (bit_count, core_bit),
    )[0]
    owned_in = jnp.concatenate(owned_first[:3], axis=1)
    owned_vectors = owned_first[3][:, : vectors.shape[1]]
    owned_bias = owned_first[3][:, vectors.shape[1] : 12].reshape(-1)
    owned_shrink = owned_late[:, :ff_width].reshape(shrink_weight.shape)
    owned_expand = owned_late[:, ff_width : 2 * ff_width]
    owned_out = owned_late[:, 2 * ff_width :]
    new_in, mom_in = adam_step(project_in, moments_in, owned_in)
    new_out, mom_out = adam_step(project_out, moments_out, owned_out)
    new_expand, mom_expand = adam_step(expand_weight, moments_expand, owned_expand)
    new_shrink, mom_shrink = adam_step(shrink_weight, moments_shrink, owned_shrink)
    new_bias, mom_bias = adam_step(expand_bias, moments_bias, owned_bias)
    new_vectors, mom_vectors = adam_step(vectors, moments_vectors, owned_vectors)
    return (
        output,
        grad_inputs,
        owned_in,
        owned_out,
        owned_expand,
        owned_shrink,
        owned_bias,
        owned_vectors,
        new_in,
        new_out,
        new_expand,
        new_shrink,
        new_bias,
        new_vectors,
        mom_in,
        mom_out,
        mom_expand,
        mom_shrink,
        mom_bias,
        mom_vectors,
    )


def solution(mesh):
    in_specs = (
        P("clip", "frame", None),
        P("clip", "frame", None),
        P(("clip", "frame"), None),
        P(("clip", "frame"), None),
        P(("clip", "frame"), None),
        P(("clip", "frame"), None),
        P(("clip", "frame")),
        P(("clip", "frame"), None),
        P(None, ("clip", "frame"), None),
        P(None, ("clip", "frame"), None),
        P(None, ("clip", "frame"), None),
        P(None, ("clip", "frame"), None),
        P(None, ("clip", "frame")),
        P(None, ("clip", "frame"), None),
    )
    out_specs = (
        P("clip", "frame", None),
        P("clip", "frame", None),
        P(("clip", "frame"), None),
        P(("clip", "frame"), None),
        P(("clip", "frame"), None),
        P(("clip", "frame"), None),
        P(("clip", "frame")),
        P(("clip", "frame"), None),
        P(("clip", "frame"), None),
        P(("clip", "frame"), None),
        P(("clip", "frame"), None),
        P(("clip", "frame"), None),
        P(("clip", "frame")),
        P(("clip", "frame"), None),
        P(None, ("clip", "frame"), None),
        P(None, ("clip", "frame"), None),
        P(None, ("clip", "frame"), None),
        P(None, ("clip", "frame"), None),
        P(None, ("clip", "frame")),
        P(None, ("clip", "frame"), None),
    )
    return jax.shard_map(
        functools.partial(body, link_plan(mesh)),
        mesh=mesh,
        in_specs=in_specs,
        out_specs=out_specs,
        check_vma=False,
    )
```

```python
import functools
import math

import jax
import jax.numpy as jnp
from jax import lax
from jax.experimental import pallas as pl
from jax.experimental.pallas import tpu as pltpu
from jax.sharding import PartitionSpec as P

HEADS = 12
ADAM_STEP = 4


epsilon_norm = 1e-05
beta_first = 0.9
beta_second = 0.99
learn_rate = 0.03
decay_rate = 0.01
epsilon_adam = 1e-08
root_half = 0.7071067811865476
inv_root_two_pi = 0.3989422804014327


def norm_parts(inputs, norm_gain, norm_shift):
    average = jnp.mean(inputs, axis=-1, keepdims=True)
    centered = inputs - average
    spread = jnp.mean(centered * centered, axis=-1, keepdims=True)
    inv_std = lax.rsqrt(spread + epsilon_norm)
    normed = centered * inv_std
    return (normed * norm_gain + norm_shift, normed, inv_std)


def norm_backward(grad_normed, normed, inv_std, norm_gain):
    grad_gain = jnp.sum(grad_normed * normed, axis=0)
    grad_shift = jnp.sum(grad_normed, axis=0)
    scaled = grad_normed * norm_gain
    grad_input = inv_std * (
        scaled
        - jnp.mean(scaled, axis=-1, keepdims=True)
        - normed * jnp.mean(scaled * normed, axis=-1, keepdims=True)
    )
    return (grad_input, grad_gain, grad_shift)


def gelu_exact(inputs):
    return 0.5 * inputs * (1.0 + jax.scipy.special.erf(inputs * root_half))


def gelu_slope(inputs):
    return (
        0.5 * (1.0 + jax.scipy.special.erf(inputs * root_half))
        + inputs * jnp.exp(-0.5 * inputs * inputs) * inv_root_two_pi
    )


QUERY_CHUNK = 256
MASKED = -1e30


def attention_forward_kernel(q_ref, k_ref, v_ref, kbias_ref, o_ref, l_ref):
    head_size = q_ref.shape[1] // 2
    rows = q_ref.shape[0]
    kbias = kbias_ref[...]
    lane = lax.broadcasted_iota(jnp.int32, (QUERY_CHUNK, 2 * head_size), 1)

    def chunk_body(chunk, carry):
        span = pl.ds(pl.multiple_of(chunk * QUERY_CHUNK, QUERY_CHUNK), QUERY_CHUNK)
        mixed_parts = []
        totals = []
        for half in range(2):
            cols = pl.ds(half * head_size, head_size)
            query = q_ref[span, cols]
            key = k_ref[:, cols]
            value = v_ref[:, cols]
            scores = (
                lax.dot_general(
                    query, key, (((1,), (1,)), ((), ())), preferred_element_type=jnp.float32
                )
                + kbias
            )
            highest = jnp.max(scores, axis=1, keepdims=True)
            exponent = jnp.exp(scores - highest)
            denominator = jnp.sum(exponent, axis=1, keepdims=True)
            weights = (exponent * (1.0 / denominator)).astype(jnp.bfloat16)
            mixed_parts.append(jnp.dot(weights, value, preferred_element_type=jnp.float32))
            totals.append(highest + jnp.log(denominator))
        o_ref[span, :] = jnp.concatenate(mixed_parts, axis=1).astype(o_ref.dtype)
        l_ref[span, :] = jnp.where(lane < head_size, totals[0], totals[1])
        return carry

    lax.fori_loop(0, rows // QUERY_CHUNK, chunk_body, 0)


def attention_backward_kernel(
    q_ref, k_ref, v_ref, do_ref, l_ref, kbias_ref, dq_ref, dk_ref, dv_ref
):
    head_size = q_ref.shape[1] // 2
    rows = q_ref.shape[0]
    kbias = kbias_ref[...]
    dk_ref[...] = jnp.zeros_like(dk_ref)
    dv_ref[...] = jnp.zeros_like(dv_ref)
    for half in range(2):
        cols = pl.ds(half * head_size, head_size)

        def chunk_body(chunk, carry, cols=cols, half=half):
            span = pl.ds(pl.multiple_of(chunk * QUERY_CHUNK, QUERY_CHUNK), QUERY_CHUNK)
            key = k_ref[:, cols]
            value = v_ref[:, cols]
            query = q_ref[span, cols]
            grad_out = do_ref[span, cols]
            total = l_ref[span, pl.ds(half * head_size, 1)]
            scores = (
                lax.dot_general(
                    query, key, (((1,), (1,)), ((), ())), preferred_element_type=jnp.float32
                )
                + kbias
            )
            weights = jnp.exp(scores - total)
            grad_weights = lax.dot_general(
                grad_out, value, (((1,), (1,)), ((), ())), preferred_element_type=jnp.float32
            )
            delta = jnp.sum(weights * grad_weights, axis=1, keepdims=True)
            grad_scores = (weights * (grad_weights - delta)).astype(jnp.bfloat16)
            dq_ref[span, cols] = jnp.dot(
                grad_scores, key, preferred_element_type=jnp.float32
            ).astype(dq_ref.dtype)
            dk_ref[:, cols] += lax.dot_general(
                grad_scores, query, (((0,), (0,)), ((), ())), preferred_element_type=jnp.float32
            )
            dv_ref[:, cols] += lax.dot_general(
                weights.astype(jnp.bfloat16),
                grad_out,
                (((0,), (0,)), ((), ())),
                preferred_element_type=jnp.float32,
            )
            return carry

        lax.fori_loop(0, rows // QUERY_CHUNK, chunk_body, 0)


def pad_rows(values, rows):
    return jnp.pad(values, ((0, rows - values.shape[0]), (0, 0)))


def attention_pallas(queries, pairs, grad_out=None, totals=None, first_pair=0, pair_span=None):
    query_rows, model_width = queries.shape
    key_rows = pairs.shape[0]
    padded_q = -(-query_rows // QUERY_CHUNK) * QUERY_CHUNK
    padded_k = -(-key_rows // 128) * 128
    pair_count = model_width // 128
    q_pad = pad_rows(queries, padded_q)
    kv_pad = pad_rows(pairs, padded_k)
    kbias = jnp.where(jnp.arange(padded_k) < key_rows, 0.0, MASKED).astype(jnp.float32)[None, :]
    q_spec = pl.BlockSpec((padded_q, 128), lambda j: (0, j))
    k_spec = pl.BlockSpec((padded_k, 128), lambda j: (0, j))
    v_spec = pl.BlockSpec((padded_k, 128), lambda j: (0, j + pair_count))
    b_spec = pl.BlockSpec((1, padded_k), lambda j: (0, 0))
    params = pltpu.CompilerParams(vmem_limit_bytes=48 * 1024 * 1024)
    if grad_out is None:
        mixed, log_totals = pl.pallas_call(
            attention_forward_kernel,
            grid=(pair_count,),
            in_specs=[q_spec, k_spec, v_spec, b_spec],
            out_specs=[q_spec, q_spec],
            out_shape=[
                jax.ShapeDtypeStruct((padded_q, model_width), jnp.bfloat16),
                jax.ShapeDtypeStruct((padded_q, model_width), jnp.float32),
            ],
            compiler_params=params,
        )(q_pad, kv_pad, kv_pad, kbias)
        return mixed[:query_rows], log_totals
    do_pad = pad_rows(grad_out, padded_q)
    span = pair_count if pair_span is None else pair_span
    qi_spec = pl.BlockSpec((padded_q, 128), lambda j: (0, j + first_pair))
    ki_spec = pl.BlockSpec((padded_k, 128), lambda j: (0, j + first_pair))
    vi_spec = pl.BlockSpec((padded_k, 128), lambda j: (0, j + first_pair + pair_count))
    qo_spec = pl.BlockSpec((padded_q, 128), lambda j: (0, j))
    ko_spec = pl.BlockSpec((padded_k, 128), lambda j: (0, j))
    dq, dk, dv = pl.pallas_call(
        attention_backward_kernel,
        grid=(span,),
        in_specs=[qi_spec, ki_spec, vi_spec, qi_spec, qi_spec, b_spec],
        out_specs=[qo_spec, ko_spec, ko_spec],
        out_shape=[
            jax.ShapeDtypeStruct((padded_q, 128 * span), jnp.float32),
            jax.ShapeDtypeStruct((padded_k, 128 * span), jnp.float32),
            jax.ShapeDtypeStruct((padded_k, 128 * span), jnp.float32),
        ],
        compiler_params=params,
    )(q_pad, kv_pad, kv_pad, do_pad, totals, kbias)
    return dq[:query_rows], dk[:key_rows], dv[:key_rows]


def attend_forward(queries, keys_values, head_count):
    model_width = queries.shape[2]
    head_size = model_width // head_count
    score_scale = 1.0 / math.sqrt(head_size)

    def one_head(head_index):
        offset = head_index * head_size
        query_block = lax.dynamic_slice_in_dim(queries, offset, head_size, 2)
        key_block = lax.dynamic_slice_in_dim(keys_values, offset, head_size, 2)
        value_block = lax.dynamic_slice_in_dim(keys_values, model_width + offset, head_size, 2)
        scores = (
            jnp.einsum("cqd,ckd->cqk", query_block, key_block, preferred_element_type=jnp.float32)
            * score_scale
        )
        highest = jnp.max(scores, axis=-1, keepdims=True)
        exponent = jnp.exp(scores - highest)
        denominator = jnp.sum(exponent, axis=-1, keepdims=True)
        weights_soft = (exponent / denominator).astype(jnp.bfloat16)
        mixed = jnp.einsum(
            "cqk,ckd->cqd", weights_soft, value_block, preferred_element_type=jnp.float32
        )
        return (mixed, (highest + jnp.log(denominator))[..., 0])

    mixed, log_totals = lax.map(one_head, jnp.arange(head_count))
    clip_count, frame_count = (queries.shape[0], queries.shape[1])
    mixed = jnp.transpose(mixed, (1, 2, 0, 3)).reshape(clip_count, frame_count, model_width)
    return (mixed, log_totals)


def attend_backward(queries, keys_values, grad_mixed, log_totals, head_count):
    model_width = queries.shape[2]
    head_size = model_width // head_count
    score_scale = 1.0 / math.sqrt(head_size)

    def one_head_back(head_index):
        offset = head_index * head_size
        query_block = lax.dynamic_slice_in_dim(queries, offset, head_size, 2)
        key_block = lax.dynamic_slice_in_dim(keys_values, offset, head_size, 2)
        value_block = lax.dynamic_slice_in_dim(keys_values, model_width + offset, head_size, 2)
        grad_block = lax.dynamic_slice_in_dim(grad_mixed, offset, head_size, 2)
        totals = lax.dynamic_index_in_dim(log_totals, head_index, 0, keepdims=False)
        scores = (
            jnp.einsum("cqd,ckd->cqk", query_block, key_block, preferred_element_type=jnp.float32)
            * score_scale
        )
        weights_soft = jnp.exp(scores - totals[..., None])
        grad_weights = jnp.einsum(
            "cqd,ckd->cqk", grad_block, value_block, preferred_element_type=jnp.float32
        )
        delta = jnp.sum(weights_soft * grad_weights, axis=-1, keepdims=True)
        grad_scores = (weights_soft * (grad_weights - delta)).astype(jnp.bfloat16)
        grad_query = (
            jnp.einsum("cqk,ckd->cqd", grad_scores, key_block, preferred_element_type=jnp.float32)
            * score_scale
        )
        grad_key = (
            jnp.einsum("cqk,cqd->ckd", grad_scores, query_block, preferred_element_type=jnp.float32)
            * score_scale
        )
        grad_value = jnp.einsum(
            "cqk,cqd->ckd",
            weights_soft.astype(jnp.bfloat16),
            grad_block,
            preferred_element_type=jnp.float32,
        )
        return (grad_query, delta[..., 0], grad_key, grad_value)

    pieces = lax.map(one_head_back, jnp.arange(head_count))
    clip_count, frame_count = (queries.shape[0], queries.shape[1])
    clip_frames = keys_values.shape[1]
    grad_query = jnp.transpose(pieces[0], (1, 2, 0, 3)).reshape(
        clip_count, frame_count, model_width
    )
    grad_key = jnp.transpose(pieces[2], (1, 2, 0, 3)).reshape(clip_count, clip_frames, model_width)
    grad_value = jnp.transpose(pieces[3], (1, 2, 0, 3)).reshape(
        clip_count, clip_frames, model_width
    )
    return (grad_query, pieces[1], jnp.concatenate([grad_key, grad_value], axis=2))


def link_plan(mesh):
    devices = list(mesh.devices.reshape(-1))
    bit_count = len(devices).bit_length() - 1
    core_bit = 1
    for bit in range(bit_count):
        first, other = devices[0], devices[1 << bit]
        if getattr(first, "coords", None) is not None and tuple(first.coords) == tuple(other.coords):
            core_bit = bit
    others = [bit for bit in range(bit_count) if bit != core_bit]
    near, far = others[:-1], others[-1:]
    rotated = tuple(tuple(near[k:] + near[:k] + far) for k in range(3))
    inner = [bit for bit in near if bit != 0]
    late = tuple(tuple(inner[k:] + inner[:k] + [0] + far) for k in range(2))
    return bit_count, core_bit, rotated, late


def tree_reduce_scatter(terms, part_columns, orders, plan_bits, hooks=None):
    hooks = dict(hooks or {})
    tied = {}
    bit_count, core_bit = plan_bits
    device = lax.axis_index("clip") * lax.axis_size("frame") + lax.axis_index("frame")
    blocks = 1 << bit_count
    block_rows = terms.shape[0] // blocks
    data = terms.reshape((2,) * bit_count + (block_rows, terms.shape[1]))
    parts = [(data, list(range(bit_count - 1, -1, -1)))]
    plan = [(core_bit,)] + [tuple(order[stage] for order in orders) for stage in range(len(orders[0]))]
    for stage, stage_bits in enumerate(plan):
        if stage == 1:
            whole, bits = parts[0]
            parts = []
            offset = 0
            for width in part_columns:
                parts.append((whole[..., offset : offset + width], bits))
                offset += width
        keeps, sends = [], []
        for (part, part_bits), bit in zip(parts, stage_bits):
            axis = part_bits.index(bit)
            mine = (device >> bit) & 1
            keeps.append(lax.dynamic_index_in_dim(part, mine, axis=axis, keepdims=False))
            sends.append(
                lax.dynamic_index_in_dim(part, 1 - mine, axis=axis, keepdims=False).astype(jnp.bfloat16)
            )
        new_parts = []
        for keep, send, (part, part_bits), bit in zip(keeps, sends, parts, stage_bits):
            pairs = [(index, index ^ (1 << bit)) for index in range(blocks)]
            got = lax.ppermute(send, ("clip", "frame"), pairs)
            new_parts.append((keep + got.astype(jnp.float32), [b for b in part_bits if b != bit]))
        if stage in hooks:
            values, tied[stage] = lax.optimization_barrier(
                ([part for part, _ in new_parts], hooks[stage](tied))
            )
            new_parts = [(value, part_bits) for value, (_, part_bits) in zip(values, new_parts)]
        parts = new_parts
    return jnp.concatenate([part for part, _ in parts], axis=-1).astype(jnp.float32), tied


def tree_all_gather(local, part_columns, orders, plan_bits):
    bit_count, core_bit = plan_bits
    device = lax.axis_index("clip") * lax.axis_size("frame") + lax.axis_index("frame")
    canonical = list(range(bit_count - 1, -1, -1))

    def double(data, bits, bit):
        mine = (device >> bit) & 1
        pairs = [(index, index ^ (1 << bit)) for index in range(1 << bit_count)]
        got = lax.ppermute(data, ("clip", "frame"), pairs)
        new_bits = sorted(bits + [bit], reverse=True)
        axis = new_bits.index(bit)
        low_first = jnp.stack([data, got], axis=axis)
        high_first = jnp.stack([got, data], axis=axis)
        return jnp.where(mine == 0, low_first, high_first), new_bits

    parts = []
    offset = 0
    for width in part_columns:
        parts.append((local[:, offset : offset + width], []))
        offset += width
    reversed_orders = [list(reversed(order)) for order in orders]
    for stage in range(len(reversed_orders[0])):
        parts = [double(part, bits, order[stage]) for (part, bits), order in zip(parts, reversed_orders)]
    whole = jnp.concatenate([part for part, _ in parts], axis=-1)
    whole, bits = double(whole, parts[0][1], core_bit)
    assert bits == canonical
    return whole.reshape((1 << bit_count) * local.shape[0], local.shape[1])


def adam_step(weight, moments, gradient):
    first = beta_first * moments[0] + (1.0 - beta_first) * gradient
    second = beta_second * moments[1] + (1.0 - beta_second) * gradient * gradient
    first_hat = first / (1.0 - beta_first**ADAM_STEP)
    second_hat = second / (1.0 - beta_second**ADAM_STEP)
    change = -learn_rate * (first_hat / (jnp.sqrt(second_hat) + epsilon_adam) + decay_rate * weight)
    return (change, jnp.stack([first, second]))


def body(
    plan,
    inputs,
    cotangent,
    project_in,
    project_out,
    expand_weight,
    shrink_weight,
    expand_bias,
    vectors,
    moments_in,
    moments_out,
    moments_expand,
    moments_shrink,
    moments_bias,
    moments_vectors,
):
    clip_count, frame_count, model_width = inputs.shape
    row_count = clip_count * frame_count
    head_count = HEADS
    shard_rows = project_in.shape[0]
    wide_in = project_in.shape[1]
    ff_width = expand_weight.shape[1]
    swap = [(0, 1), (1, 0)]
    everyone = ("clip", "frame")

    small = jnp.concatenate(
        [
            vectors,
            expand_bias.reshape(shard_rows, -1),
            jnp.zeros((shard_rows, 128 - vectors.shape[1] - expand_bias.shape[0] // shard_rows), jnp.float32),
        ],
        axis=1,
    )
    first_pack = jnp.concatenate([project_in, small], axis=1).astype(jnp.bfloat16)
    second_pack = jnp.concatenate(
        [project_out, expand_weight, shrink_weight.reshape(shard_rows, -1)], axis=1
    ).astype(jnp.bfloat16)
    bit_count, core_bit, rotated_orders, late_orders = plan
    first_full = tree_all_gather(first_pack, (896, 768, 768), rotated_orders, (bit_count, core_bit))
    second_full = lax.all_gather(second_pack, everyone, axis=0, tiled=True)
    full_in = first_full[:, :wide_in]
    small_full = first_full[:, wide_in:].astype(jnp.float32)
    column_set = small_full[:, : vectors.shape[1]]
    full_bias = small_full[:, vectors.shape[1] : vectors.shape[1] + ff_width // model_width].reshape(-1)
    full_out = second_full[:, :model_width]
    full_expand = second_full[:, model_width : model_width + ff_width]
    full_shrink = second_full[:, model_width + ff_width :].reshape(ff_width, model_width)

    frames_rows = inputs.reshape(row_count, model_width).astype(jnp.float32)
    normed_first, plain_first, inv_first = norm_parts(
        frames_rows, column_set[:, 0], column_set[:, 1]
    )
    hidden_first = normed_first.astype(jnp.bfloat16)
    partner_rows = lax.ppermute(inputs, "frame", swap).reshape(row_count, model_width)
    hidden_partner = norm_parts(
        partner_rows.astype(jnp.float32), column_set[:, 0], column_set[:, 1]
    )[0].astype(jnp.bfloat16)
    bias_in = jnp.concatenate(
        [column_set[:, 2], jnp.zeros((model_width,), jnp.float32), column_set[:, 3]]
    )
    projected = (
        jnp.dot(hidden_first, full_in, preferred_element_type=jnp.float32) + bias_in
    ).astype(jnp.bfloat16)
    partner_pairs = (
        jnp.dot(hidden_partner, full_in[:, model_width:], preferred_element_type=jnp.float32)
        + bias_in[model_width:]
    ).astype(jnp.bfloat16)
    queries = projected[:, :model_width].reshape(clip_count, frame_count, model_width)
    clip_pairs = jnp.concatenate([projected[:, model_width:], partner_pairs], axis=0).reshape(
        clip_count, 2 * frame_count, 2 * model_width
    )
    score_scale = 1.0 / math.sqrt(model_width // head_count)
    scaled_queries = (projected[:, :model_width] * score_scale).astype(jnp.bfloat16)
    pair_rows = clip_pairs.reshape(2 * row_count, 2 * model_width)
    mixed_low, log_totals = attention_pallas(scaled_queries, pair_rows)
    attended = jnp.dot(mixed_low, full_out, preferred_element_type=jnp.float32) + column_set[:, 4]
    residual = frames_rows + attended
    normed_second, plain_second, inv_second = norm_parts(
        residual, column_set[:, 5], column_set[:, 6]
    )
    hidden_second = normed_second.astype(jnp.bfloat16)
    preact = jnp.dot(hidden_second, full_expand, preferred_element_type=jnp.float32) + full_bias
    activated = gelu_exact(preact).astype(jnp.bfloat16)
    result = (
        residual
        + jnp.dot(activated, full_shrink, preferred_element_type=jnp.float32)
        + column_set[:, 7]
    )
    output = result.astype(jnp.bfloat16).reshape(inputs.shape)

    grad_result = cotangent.reshape(row_count, model_width)
    grad_shrink_term = jnp.dot(
        activated.T, grad_result, preferred_element_type=jnp.float32
    ).astype(jnp.bfloat16)
    grad_down_bias = jnp.sum(grad_result.astype(jnp.float32), axis=0)
    grad_activated = jnp.dot(grad_result, full_shrink.T, preferred_element_type=jnp.float32)
    grad_preact = (grad_activated * gelu_slope(preact)).astype(jnp.bfloat16)
    grad_expand_term = jnp.dot(
        hidden_second.T, grad_preact, preferred_element_type=jnp.float32
    ).astype(jnp.bfloat16)
    grad_bias_term = jnp.sum(grad_preact.astype(jnp.float32), axis=0)
    grad_hidden_second = jnp.dot(grad_preact, full_expand.T, preferred_element_type=jnp.float32)
    norm_term_second, gain_second, shift_second = norm_backward(
        grad_hidden_second, plain_second, inv_second, column_set[:, 5]
    )
    grad_residual = grad_result.astype(jnp.float32) + norm_term_second
    grad_attended = grad_residual.astype(jnp.bfloat16)
    grad_out_term = jnp.dot(
        mixed_low.T, grad_attended, preferred_element_type=jnp.float32
    ).astype(jnp.bfloat16)
    grad_out_bias = jnp.sum(grad_attended.astype(jnp.float32), axis=0)
    late_terms = jnp.concatenate(
        [grad_shrink_term.reshape(model_width, -1), grad_expand_term, grad_out_term], axis=1
    )
    grad_mixed = jnp.dot(grad_attended, full_out.T, preferred_element_type=jnp.float32).astype(
        jnp.bfloat16
    )
    piece_pairs = 2
    piece_count = model_width // 128 // piece_pairs

    def run_piece(index, mixed_grads):
        return attention_pallas(
            scaled_queries, pair_rows, mixed_grads, log_totals, index * piece_pairs, piece_pairs
        )

    def piece_hook(index):
        return lambda tied: (run_piece(index, tied[index - 1][1]), tied[index - 1][1])

    hooks = {0: lambda tied: ((), grad_mixed)}
    hooks.update({index: piece_hook(index) for index in range(1, piece_count)})
    pieces = [run_piece(0, grad_mixed)]
    owned_late, tied = tree_reduce_scatter(
        late_terms, (3456, 3456), late_orders, (bit_count, core_bit), hooks
    )
    pieces += [tied[index][0] for index in range(1, piece_count)]
    finished = []
    for grad_query, grad_keys, grad_values in pieces:
        terms = jnp.concatenate([grad_keys, grad_values], axis=1)
        returned = lax.ppermute(terms[row_count:].astype(jnp.bfloat16), "frame", swap)
        finished.append((grad_query, terms[:row_count] + returned.astype(jnp.float32)))
    piece_width = finished[0][0].shape[1]
    grad_projected = jnp.concatenate(
        [
            (jnp.concatenate([query for query, _ in finished], axis=1) * score_scale).astype(
                jnp.bfloat16
            ),
            jnp.concatenate(
                [pair[:, :piece_width] for _, pair in finished]
                + [pair[:, piece_width:] for _, pair in finished],
                axis=1,
            ).astype(jnp.bfloat16),
        ],
        axis=1,
    )
    grad_in_term = jnp.dot(
        hidden_first.T, grad_projected, preferred_element_type=jnp.float32
    ).astype(jnp.bfloat16)
    projected_sums = jnp.sum(grad_projected.astype(jnp.float32), axis=0)
    grad_query_bias = projected_sums[:model_width]
    grad_value_bias = projected_sums[2 * model_width :]
    grad_hidden_first = jnp.dot(grad_projected, full_in.T, preferred_element_type=jnp.float32)
    norm_term_first, gain_first, shift_first = norm_backward(
        grad_hidden_first, plain_first, inv_first, column_set[:, 0]
    )
    grad_inputs = (grad_residual + norm_term_first).astype(jnp.bfloat16).reshape(inputs.shape)
    grad_columns = jnp.stack(
        [
            gain_first,
            shift_first,
            grad_query_bias,
            grad_value_bias,
            grad_out_bias,
            gain_second,
            shift_second,
            grad_down_bias,
        ],
        axis=1,
    )
    small_grads = jnp.concatenate(
        [
            grad_columns,
            grad_bias_term.reshape(model_width, -1),
            jnp.zeros((model_width, 128 - 12), jnp.float32),
        ],
        axis=1,
    ).astype(jnp.bfloat16)
    owned_first = tree_reduce_scatter(
        jnp.concatenate([grad_in_term, small_grads], axis=1),
        (896, 768, 768),
        rotated_orders,
        (bit_count, core_bit),
    )[0]
    owned_in = owned_first[:, :wide_in]
    owned_vectors = owned_first[:, wide_in : wide_in + vectors.shape[1]]
    owned_bias = owned_first[:, wide_in + vectors.shape[1] : wide_in + 12].reshape(-1)
    owned_shrink = owned_late[:, :ff_width].reshape(shrink_weight.shape)
    owned_expand = owned_late[:, ff_width : 2 * ff_width]
    owned_out = owned_late[:, 2 * ff_width :]
    new_in, mom_in = adam_step(project_in, moments_in, owned_in)
    new_out, mom_out = adam_step(project_out, moments_out, owned_out)
    new_expand, mom_expand = adam_step(expand_weight, moments_expand, owned_expand)
    new_shrink, mom_shrink = adam_step(shrink_weight, moments_shrink, owned_shrink)
    new_bias, mom_bias = adam_step(expand_bias, moments_bias, owned_bias)
    new_vectors, mom_vectors = adam_step(vectors, moments_vectors, owned_vectors)
    return (
        output,
        grad_inputs,
        owned_in,
        owned_out,
        owned_expand,
        owned_shrink,
        owned_bias,
        owned_vectors,
        new_in,
        new_out,
        new_expand,
        new_shrink,
        new_bias,
        new_vectors,
        mom_in,
        mom_out,
        mom_expand,
        mom_shrink,
        mom_bias,
        mom_vectors,
    )


def solution(mesh):
    in_specs = (
        P("clip", "frame", None),
        P("clip", "frame", None),
        P(("clip", "frame"), None),
        P(("clip", "frame"), None),
        P(("clip", "frame"), None),
        P(("clip", "frame"), None),
        P(("clip", "frame")),
        P(("clip", "frame"), None),
        P(None, ("clip", "frame"), None),
        P(None, ("clip", "frame"), None),
        P(None, ("clip", "frame"), None),
        P(None, ("clip", "frame"), None),
        P(None, ("clip", "frame")),
        P(None, ("clip", "frame"), None),
    )
    out_specs = (
        P("clip", "frame", None),
        P("clip", "frame", None),
        P(("clip", "frame"), None),
        P(("clip", "frame"), None),
        P(("clip", "frame"), None),
        P(("clip", "frame"), None),
        P(("clip", "frame")),
        P(("clip", "frame"), None),
        P(("clip", "frame"), None),
        P(("clip", "frame"), None),
        P(("clip", "frame"), None),
        P(("clip", "frame"), None),
        P(("clip", "frame")),
        P(("clip", "frame"), None),
        P(None, ("clip", "frame"), None),
        P(None, ("clip", "frame"), None),
        P(None, ("clip", "frame"), None),
        P(None, ("clip", "frame"), None),
        P(None, ("clip", "frame")),
        P(None, ("clip", "frame"), None),
    )
    return jax.shard_map(
        functools.partial(body, link_plan(mesh)),
        mesh=mesh,
        in_specs=in_specs,
        out_specs=out_specs,
        check_vma=False,
    )
```

```python
import functools
import math

import jax
import jax.numpy as jnp
from jax import lax
from jax.experimental import pallas as pl
from jax.experimental.pallas import tpu as pltpu
from jax.sharding import PartitionSpec as P

HEADS = 12
ADAM_STEP = 4


epsilon_norm = 1e-05
beta_first = 0.9
beta_second = 0.99
learn_rate = 0.03
decay_rate = 0.01
epsilon_adam = 1e-08
root_half = 0.7071067811865476
inv_root_two_pi = 0.3989422804014327


def norm_parts(inputs, norm_gain, norm_shift):
    average = jnp.mean(inputs, axis=-1, keepdims=True)
    centered = inputs - average
    spread = jnp.mean(centered * centered, axis=-1, keepdims=True)
    inv_std = lax.rsqrt(spread + epsilon_norm)
    normed = centered * inv_std
    return (normed * norm_gain + norm_shift, normed, inv_std)


def norm_backward(grad_normed, normed, inv_std, norm_gain):
    grad_gain = jnp.sum(grad_normed * normed, axis=0)
    grad_shift = jnp.sum(grad_normed, axis=0)
    scaled = grad_normed * norm_gain
    grad_input = inv_std * (
        scaled
        - jnp.mean(scaled, axis=-1, keepdims=True)
        - normed * jnp.mean(scaled * normed, axis=-1, keepdims=True)
    )
    return (grad_input, grad_gain, grad_shift)


def gelu_exact(inputs):
    return 0.5 * inputs * (1.0 + jax.scipy.special.erf(inputs * root_half))


def gelu_slope(inputs):
    return (
        0.5 * (1.0 + jax.scipy.special.erf(inputs * root_half))
        + inputs * jnp.exp(-0.5 * inputs * inputs) * inv_root_two_pi
    )


QUERY_CHUNK = 256
MASKED = -1e30


def attention_forward_kernel(q_ref, k_ref, v_ref, kbias_ref, o_ref, l_ref):
    head_size = q_ref.shape[1] // 2
    rows = q_ref.shape[0]
    kbias = kbias_ref[...]
    lane = lax.broadcasted_iota(jnp.int32, (QUERY_CHUNK, 2 * head_size), 1)

    def chunk_body(chunk, carry):
        span = pl.ds(pl.multiple_of(chunk * QUERY_CHUNK, QUERY_CHUNK), QUERY_CHUNK)
        mixed_parts = []
        totals = []
        for half in range(2):
            cols = pl.ds(half * head_size, head_size)
            query = q_ref[span, cols]
            key = k_ref[:, cols]
            value = v_ref[:, cols]
            scores = (
                lax.dot_general(
                    query, key, (((1,), (1,)), ((), ())), preferred_element_type=jnp.float32
                )
                + kbias
            )
            highest = jnp.max(scores, axis=1, keepdims=True)
            exponent = jnp.exp(scores - highest)
            denominator = jnp.sum(exponent, axis=1, keepdims=True)
            weights = (exponent * (1.0 / denominator)).astype(jnp.bfloat16)
            mixed_parts.append(jnp.dot(weights, value, preferred_element_type=jnp.float32))
            totals.append(highest + jnp.log(denominator))
        o_ref[span, :] = jnp.concatenate(mixed_parts, axis=1).astype(o_ref.dtype)
        l_ref[span, :] = jnp.where(lane < head_size, totals[0], totals[1])
        return carry

    lax.fori_loop(0, rows // QUERY_CHUNK, chunk_body, 0)


def attention_backward_kernel(
    q_ref, k_ref, v_ref, do_ref, l_ref, kbias_ref, dq_ref, dk_ref, dv_ref
):
    head_size = q_ref.shape[1] // 2
    rows = q_ref.shape[0]
    kbias = kbias_ref[...]
    dk_ref[...] = jnp.zeros_like(dk_ref)
    dv_ref[...] = jnp.zeros_like(dv_ref)
    for half in range(2):
        cols = pl.ds(half * head_size, head_size)

        def chunk_body(chunk, carry, cols=cols, half=half):
            span = pl.ds(pl.multiple_of(chunk * QUERY_CHUNK, QUERY_CHUNK), QUERY_CHUNK)
            key = k_ref[:, cols]
            value = v_ref[:, cols]
            query = q_ref[span, cols]
            grad_out = do_ref[span, cols]
            total = l_ref[span, pl.ds(half * head_size, 1)]
            scores = (
                lax.dot_general(
                    query, key, (((1,), (1,)), ((), ())), preferred_element_type=jnp.float32
                )
                + kbias
            )
            weights = jnp.exp(scores - total)
            grad_weights = lax.dot_general(
                grad_out, value, (((1,), (1,)), ((), ())), preferred_element_type=jnp.float32
            )
            delta = jnp.sum(weights * grad_weights, axis=1, keepdims=True)
            grad_scores = (weights * (grad_weights - delta)).astype(jnp.bfloat16)
            dq_ref[span, cols] = jnp.dot(
                grad_scores, key, preferred_element_type=jnp.float32
            ).astype(dq_ref.dtype)
            dk_ref[:, cols] += lax.dot_general(
                grad_scores, query, (((0,), (0,)), ((), ())), preferred_element_type=jnp.float32
            )
            dv_ref[:, cols] += lax.dot_general(
                weights.astype(jnp.bfloat16),
                grad_out,
                (((0,), (0,)), ((), ())),
                preferred_element_type=jnp.float32,
            )
            return carry

        lax.fori_loop(0, rows // QUERY_CHUNK, chunk_body, 0)


def pad_rows(values, rows):
    return jnp.pad(values, ((0, rows - values.shape[0]), (0, 0)))


def attention_pallas(queries, pairs, grad_out=None, totals=None, first_pair=0, pair_span=None):
    query_rows, model_width = queries.shape
    key_rows = pairs.shape[0]
    padded_q = -(-query_rows // QUERY_CHUNK) * QUERY_CHUNK
    padded_k = -(-key_rows // 128) * 128
    pair_count = model_width // 128
    q_pad = pad_rows(queries, padded_q)
    kv_pad = pad_rows(pairs, padded_k)
    kbias = jnp.where(jnp.arange(padded_k) < key_rows, 0.0, MASKED).astype(jnp.float32)[None, :]
    q_spec = pl.BlockSpec((padded_q, 128), lambda j: (0, j))
    k_spec = pl.BlockSpec((padded_k, 128), lambda j: (0, j))
    v_spec = pl.BlockSpec((padded_k, 128), lambda j: (0, j + pair_count))
    b_spec = pl.BlockSpec((1, padded_k), lambda j: (0, 0))
    params = pltpu.CompilerParams(vmem_limit_bytes=48 * 1024 * 1024)
    if grad_out is None:
        mixed, log_totals = pl.pallas_call(
            attention_forward_kernel,
            grid=(pair_count,),
            in_specs=[q_spec, k_spec, v_spec, b_spec],
            out_specs=[q_spec, q_spec],
            out_shape=[
                jax.ShapeDtypeStruct((padded_q, model_width), jnp.bfloat16),
                jax.ShapeDtypeStruct((padded_q, model_width), jnp.float32),
            ],
            compiler_params=params,
        )(q_pad, kv_pad, kv_pad, kbias)
        return mixed[:query_rows], log_totals
    do_pad = pad_rows(grad_out, padded_q)
    span = pair_count if pair_span is None else pair_span
    qi_spec = pl.BlockSpec((padded_q, 128), lambda j: (0, j + first_pair))
    ki_spec = pl.BlockSpec((padded_k, 128), lambda j: (0, j + first_pair))
    vi_spec = pl.BlockSpec((padded_k, 128), lambda j: (0, j + first_pair + pair_count))
    qo_spec = pl.BlockSpec((padded_q, 128), lambda j: (0, j))
    ko_spec = pl.BlockSpec((padded_k, 128), lambda j: (0, j))
    dq, dk, dv = pl.pallas_call(
        attention_backward_kernel,
        grid=(span,),
        in_specs=[qi_spec, ki_spec, vi_spec, qi_spec, qi_spec, b_spec],
        out_specs=[qo_spec, ko_spec, ko_spec],
        out_shape=[
            jax.ShapeDtypeStruct((padded_q, 128 * span), jnp.float32),
            jax.ShapeDtypeStruct((padded_k, 128 * span), jnp.float32),
            jax.ShapeDtypeStruct((padded_k, 128 * span), jnp.float32),
        ],
        compiler_params=params,
    )(q_pad, kv_pad, kv_pad, do_pad, totals, kbias)
    return dq[:query_rows], dk[:key_rows], dv[:key_rows]


def attend_forward(queries, keys_values, head_count):
    model_width = queries.shape[2]
    head_size = model_width // head_count
    score_scale = 1.0 / math.sqrt(head_size)

    def one_head(head_index):
        offset = head_index * head_size
        query_block = lax.dynamic_slice_in_dim(queries, offset, head_size, 2)
        key_block = lax.dynamic_slice_in_dim(keys_values, offset, head_size, 2)
        value_block = lax.dynamic_slice_in_dim(keys_values, model_width + offset, head_size, 2)
        scores = (
            jnp.einsum("cqd,ckd->cqk", query_block, key_block, preferred_element_type=jnp.float32)
            * score_scale
        )
        highest = jnp.max(scores, axis=-1, keepdims=True)
        exponent = jnp.exp(scores - highest)
        denominator = jnp.sum(exponent, axis=-1, keepdims=True)
        weights_soft = (exponent / denominator).astype(jnp.bfloat16)
        mixed = jnp.einsum(
            "cqk,ckd->cqd", weights_soft, value_block, preferred_element_type=jnp.float32
        )
        return (mixed, (highest + jnp.log(denominator))[..., 0])

    mixed, log_totals = lax.map(one_head, jnp.arange(head_count))
    clip_count, frame_count = (queries.shape[0], queries.shape[1])
    mixed = jnp.transpose(mixed, (1, 2, 0, 3)).reshape(clip_count, frame_count, model_width)
    return (mixed, log_totals)


def attend_backward(queries, keys_values, grad_mixed, log_totals, head_count):
    model_width = queries.shape[2]
    head_size = model_width // head_count
    score_scale = 1.0 / math.sqrt(head_size)

    def one_head_back(head_index):
        offset = head_index * head_size
        query_block = lax.dynamic_slice_in_dim(queries, offset, head_size, 2)
        key_block = lax.dynamic_slice_in_dim(keys_values, offset, head_size, 2)
        value_block = lax.dynamic_slice_in_dim(keys_values, model_width + offset, head_size, 2)
        grad_block = lax.dynamic_slice_in_dim(grad_mixed, offset, head_size, 2)
        totals = lax.dynamic_index_in_dim(log_totals, head_index, 0, keepdims=False)
        scores = (
            jnp.einsum("cqd,ckd->cqk", query_block, key_block, preferred_element_type=jnp.float32)
            * score_scale
        )
        weights_soft = jnp.exp(scores - totals[..., None])
        grad_weights = jnp.einsum(
            "cqd,ckd->cqk", grad_block, value_block, preferred_element_type=jnp.float32
        )
        delta = jnp.sum(weights_soft * grad_weights, axis=-1, keepdims=True)
        grad_scores = (weights_soft * (grad_weights - delta)).astype(jnp.bfloat16)
        grad_query = (
            jnp.einsum("cqk,ckd->cqd", grad_scores, key_block, preferred_element_type=jnp.float32)
            * score_scale
        )
        grad_key = (
            jnp.einsum("cqk,cqd->ckd", grad_scores, query_block, preferred_element_type=jnp.float32)
            * score_scale
        )
        grad_value = jnp.einsum(
            "cqk,cqd->ckd",
            weights_soft.astype(jnp.bfloat16),
            grad_block,
            preferred_element_type=jnp.float32,
        )
        return (grad_query, delta[..., 0], grad_key, grad_value)

    pieces = lax.map(one_head_back, jnp.arange(head_count))
    clip_count, frame_count = (queries.shape[0], queries.shape[1])
    clip_frames = keys_values.shape[1]
    grad_query = jnp.transpose(pieces[0], (1, 2, 0, 3)).reshape(
        clip_count, frame_count, model_width
    )
    grad_key = jnp.transpose(pieces[2], (1, 2, 0, 3)).reshape(clip_count, clip_frames, model_width)
    grad_value = jnp.transpose(pieces[3], (1, 2, 0, 3)).reshape(
        clip_count, clip_frames, model_width
    )
    return (grad_query, pieces[1], jnp.concatenate([grad_key, grad_value], axis=2))


def link_plan(mesh):
    devices = list(mesh.devices.reshape(-1))
    bit_count = len(devices).bit_length() - 1
    core_bit = 1
    for bit in range(bit_count):
        first, other = devices[0], devices[1 << bit]
        if getattr(first, "coords", None) is not None and tuple(first.coords) == tuple(other.coords):
            core_bit = bit
    others = [bit for bit in range(bit_count) if bit != core_bit]
    near, far = others[:-1], others[-1:]
    rotated = tuple(tuple(near[k:] + near[:k] + far) for k in range(3))
    inner = [bit for bit in near if bit != 0]
    late = tuple(tuple(inner[k:] + inner[:k] + [0] + far) for k in range(2))
    return bit_count, core_bit, rotated, late


def tree_reduce_scatter(terms, part_columns, orders, plan_bits, hooks=None):
    hooks = dict(hooks or {})
    tied = {}
    bit_count, core_bit = plan_bits
    device = lax.axis_index("clip") * lax.axis_size("frame") + lax.axis_index("frame")
    blocks = 1 << bit_count
    block_rows = terms.shape[0] // blocks
    data = terms.reshape((2,) * bit_count + (block_rows, terms.shape[1]))
    parts = [(data, list(range(bit_count - 1, -1, -1)))]
    plan = [(core_bit,)] + [tuple(order[stage] for order in orders) for stage in range(len(orders[0]))]
    for stage, stage_bits in enumerate(plan):
        if stage == 1:
            whole, bits = parts[0]
            parts = []
            offset = 0
            for width in part_columns:
                parts.append((whole[..., offset : offset + width], bits))
                offset += width
        keeps, sends = [], []
        for (part, part_bits), bit in zip(parts, stage_bits):
            axis = part_bits.index(bit)
            mine = (device >> bit) & 1
            keeps.append(lax.dynamic_index_in_dim(part, mine, axis=axis, keepdims=False))
            sends.append(
                lax.dynamic_index_in_dim(part, 1 - mine, axis=axis, keepdims=False).astype(jnp.bfloat16)
            )
        new_parts = []
        for keep, send, (part, part_bits), bit in zip(keeps, sends, parts, stage_bits):
            pairs = [(index, index ^ (1 << bit)) for index in range(blocks)]
            got = lax.ppermute(send, ("clip", "frame"), pairs)
            new_parts.append((keep + got.astype(jnp.float32), [b for b in part_bits if b != bit]))
        if stage in hooks:
            values, tied[stage] = lax.optimization_barrier(
                ([part for part, _ in new_parts], hooks[stage](tied))
            )
            new_parts = [(value, part_bits) for value, (_, part_bits) in zip(values, new_parts)]
        parts = new_parts
    return jnp.concatenate([part for part, _ in parts], axis=-1).astype(jnp.float32), tied


def tree_all_gather(local, part_columns, orders, plan_bits):
    bit_count, core_bit = plan_bits
    device = lax.axis_index("clip") * lax.axis_size("frame") + lax.axis_index("frame")
    canonical = list(range(bit_count - 1, -1, -1))

    def double(data, bits, bit):
        mine = (device >> bit) & 1
        pairs = [(index, index ^ (1 << bit)) for index in range(1 << bit_count)]
        got = lax.ppermute(data, ("clip", "frame"), pairs)
        new_bits = sorted(bits + [bit], reverse=True)
        axis = new_bits.index(bit)
        low_first = jnp.stack([data, got], axis=axis)
        high_first = jnp.stack([got, data], axis=axis)
        return jnp.where(mine == 0, low_first, high_first), new_bits

    parts = []
    offset = 0
    for width in part_columns:
        parts.append((local[:, offset : offset + width], []))
        offset += width
    reversed_orders = [list(reversed(order)) for order in orders]
    for stage in range(len(reversed_orders[0])):
        parts = [double(part, bits, order[stage]) for (part, bits), order in zip(parts, reversed_orders)]
    whole = jnp.concatenate([part for part, _ in parts], axis=-1)
    whole, bits = double(whole, parts[0][1], core_bit)
    assert bits == canonical
    return whole.reshape((1 << bit_count) * local.shape[0], local.shape[1])


def adam_step(weight, moments, gradient):
    first = beta_first * moments[0] + (1.0 - beta_first) * gradient
    second = beta_second * moments[1] + (1.0 - beta_second) * gradient * gradient
    first_hat = first / (1.0 - beta_first**ADAM_STEP)
    second_hat = second / (1.0 - beta_second**ADAM_STEP)
    change = -learn_rate * (first_hat / (jnp.sqrt(second_hat) + epsilon_adam) + decay_rate * weight)
    return (change, jnp.stack([first, second]))


def body(
    plan,
    inputs,
    cotangent,
    project_in,
    project_out,
    expand_weight,
    shrink_weight,
    expand_bias,
    vectors,
    moments_in,
    moments_out,
    moments_expand,
    moments_shrink,
    moments_bias,
    moments_vectors,
):
    clip_count, frame_count, model_width = inputs.shape
    row_count = clip_count * frame_count
    head_count = HEADS
    shard_rows = project_in.shape[0]
    wide_in = project_in.shape[1]
    ff_width = expand_weight.shape[1]
    swap = [(0, 1), (1, 0)]
    everyone = ("clip", "frame")

    small = jnp.concatenate(
        [
            vectors,
            expand_bias.reshape(shard_rows, -1),
            jnp.zeros((shard_rows, 128 - vectors.shape[1] - expand_bias.shape[0] // shard_rows), jnp.float32),
        ],
        axis=1,
    )
    first_pack = jnp.concatenate([project_in, small], axis=1).astype(jnp.bfloat16)
    second_pack = jnp.concatenate(
        [project_out, expand_weight, shrink_weight.reshape(shard_rows, -1)], axis=1
    ).astype(jnp.bfloat16)
    bit_count, core_bit, rotated_orders, late_orders = plan
    first_full = tree_all_gather(first_pack, (896, 768, 768), rotated_orders, (bit_count, core_bit))
    second_full = lax.all_gather(second_pack, everyone, axis=0, tiled=True)
    full_in = first_full[:, :wide_in]
    small_full = first_full[:, wide_in:].astype(jnp.float32)
    column_set = small_full[:, : vectors.shape[1]]
    full_bias = small_full[:, vectors.shape[1] : vectors.shape[1] + ff_width // model_width].reshape(-1)
    full_out = second_full[:, :model_width]
    full_expand = second_full[:, model_width : model_width + ff_width]
    full_shrink = second_full[:, model_width + ff_width :].reshape(ff_width, model_width)

    frames_rows = inputs.reshape(row_count, model_width).astype(jnp.float32)
    normed_first, plain_first, inv_first = norm_parts(
        frames_rows, column_set[:, 0], column_set[:, 1]
    )
    hidden_first = normed_first.astype(jnp.bfloat16)
    partner_rows = lax.ppermute(inputs, "frame", swap).reshape(row_count, model_width)
    hidden_partner = norm_parts(
        partner_rows.astype(jnp.float32), column_set[:, 0], column_set[:, 1]
    )[0].astype(jnp.bfloat16)
    bias_in = jnp.concatenate(
        [column_set[:, 2], jnp.zeros((model_width,), jnp.float32), column_set[:, 3]]
    )
    projected = (
        jnp.dot(hidden_first, full_in, preferred_element_type=jnp.float32) + bias_in
    ).astype(jnp.bfloat16)
    partner_pairs = (
        jnp.dot(hidden_partner, full_in[:, model_width:], preferred_element_type=jnp.float32)
        + bias_in[model_width:]
    ).astype(jnp.bfloat16)
    queries = projected[:, :model_width].reshape(clip_count, frame_count, model_width)
    clip_pairs = jnp.concatenate([projected[:, model_width:], partner_pairs], axis=0).reshape(
        clip_count, 2 * frame_count, 2 * model_width
    )
    score_scale = 1.0 / math.sqrt(model_width // head_count)
    scaled_queries = (projected[:, :model_width] * score_scale).astype(jnp.bfloat16)
    pair_rows = clip_pairs.reshape(2 * row_count, 2 * model_width)
    mixed_low, log_totals = attention_pallas(scaled_queries, pair_rows)
    attended = jnp.dot(mixed_low, full_out, preferred_element_type=jnp.float32) + column_set[:, 4]
    residual = frames_rows + attended
    normed_second, plain_second, inv_second = norm_parts(
        residual, column_set[:, 5], column_set[:, 6]
    )
    hidden_second = normed_second.astype(jnp.bfloat16)
    preact = jnp.dot(hidden_second, full_expand, preferred_element_type=jnp.float32) + full_bias
    activated = gelu_exact(preact).astype(jnp.bfloat16)
    result = (
        residual
        + jnp.dot(activated, full_shrink, preferred_element_type=jnp.float32)
        + column_set[:, 7]
    )
    output = result.astype(jnp.bfloat16).reshape(inputs.shape)

    grad_result = cotangent.reshape(row_count, model_width)
    grad_shrink_term = jnp.dot(
        activated.T, grad_result, preferred_element_type=jnp.float32
    ).astype(jnp.bfloat16)
    grad_down_bias = jnp.sum(grad_result.astype(jnp.float32), axis=0)
    grad_activated = jnp.dot(grad_result, full_shrink.T, preferred_element_type=jnp.float32)
    grad_preact = (grad_activated * gelu_slope(preact)).astype(jnp.bfloat16)
    grad_expand_term = jnp.dot(
        hidden_second.T, grad_preact, preferred_element_type=jnp.float32
    ).astype(jnp.bfloat16)
    grad_bias_term = jnp.sum(grad_preact.astype(jnp.float32), axis=0)
    grad_hidden_second = jnp.dot(grad_preact, full_expand.T, preferred_element_type=jnp.float32)
    norm_term_second, gain_second, shift_second = norm_backward(
        grad_hidden_second, plain_second, inv_second, column_set[:, 5]
    )
    grad_residual = grad_result.astype(jnp.float32) + norm_term_second
    grad_attended = grad_residual.astype(jnp.bfloat16)
    grad_out_term = jnp.dot(
        mixed_low.T, grad_attended, preferred_element_type=jnp.float32
    ).astype(jnp.bfloat16)
    grad_out_bias = jnp.sum(grad_attended.astype(jnp.float32), axis=0)
    late_terms = jnp.concatenate(
        [grad_shrink_term.reshape(model_width, -1), grad_expand_term, grad_out_term], axis=1
    )
    grad_mixed = jnp.dot(grad_attended, full_out.T, preferred_element_type=jnp.float32).astype(
        jnp.bfloat16
    )
    piece_pairs = 1
    piece_count = model_width // 128 // piece_pairs
    stage_count = 1 + len(late_orders[0])
    hooked = list(range(1, min(piece_count, stage_count)))

    def run_piece(index, mixed_grads):
        return attention_pallas(
            scaled_queries, pair_rows, mixed_grads, log_totals, index * piece_pairs, piece_pairs
        )

    def piece_hook(index):
        return lambda tied: (run_piece(index, tied[index - 1][1]), tied[index - 1][1])

    hooks = {0: lambda tied: ((), grad_mixed)}
    hooks.update({index: piece_hook(index) for index in hooked})
    pieces = [run_piece(0, grad_mixed)]
    owned_late, tied = tree_reduce_scatter(
        late_terms, (3456, 3456), late_orders, (bit_count, core_bit), hooks
    )
    pieces += [tied[index][0] for index in hooked]
    last_mixed = tied[hooked[-1]][1] if hooked else grad_mixed
    pieces += [run_piece(index, last_mixed) for index in range(len(hooked) + 1, piece_count)]
    finished = []
    for grad_query, grad_keys, grad_values in pieces:
        terms = jnp.concatenate([grad_keys, grad_values], axis=1)
        returned = lax.ppermute(terms[row_count:].astype(jnp.bfloat16), "frame", swap)
        finished.append((grad_query, terms[:row_count] + returned.astype(jnp.float32)))
    piece_width = finished[0][0].shape[1]
    grad_projected = jnp.concatenate(
        [
            (jnp.concatenate([query for query, _ in finished], axis=1) * score_scale).astype(
                jnp.bfloat16
            ),
            jnp.concatenate(
                [pair[:, :piece_width] for _, pair in finished]
                + [pair[:, piece_width:] for _, pair in finished],
                axis=1,
            ).astype(jnp.bfloat16),
        ],
        axis=1,
    )
    grad_in_term = jnp.dot(
        hidden_first.T, grad_projected, preferred_element_type=jnp.float32
    ).astype(jnp.bfloat16)
    projected_sums = jnp.sum(grad_projected.astype(jnp.float32), axis=0)
    grad_query_bias = projected_sums[:model_width]
    grad_value_bias = projected_sums[2 * model_width :]
    grad_hidden_first = jnp.dot(grad_projected, full_in.T, preferred_element_type=jnp.float32)
    norm_term_first, gain_first, shift_first = norm_backward(
        grad_hidden_first, plain_first, inv_first, column_set[:, 0]
    )
    grad_inputs = (grad_residual + norm_term_first).astype(jnp.bfloat16).reshape(inputs.shape)
    grad_columns = jnp.stack(
        [
            gain_first,
            shift_first,
            grad_query_bias,
            grad_value_bias,
            grad_out_bias,
            gain_second,
            shift_second,
            grad_down_bias,
        ],
        axis=1,
    )
    small_grads = jnp.concatenate(
        [
            grad_columns,
            grad_bias_term.reshape(model_width, -1),
            jnp.zeros((model_width, 128 - 12), jnp.float32),
        ],
        axis=1,
    ).astype(jnp.bfloat16)
    owned_first = tree_reduce_scatter(
        jnp.concatenate([grad_in_term, small_grads], axis=1),
        (896, 768, 768),
        rotated_orders,
        (bit_count, core_bit),
    )[0]
    owned_in = owned_first[:, :wide_in]
    owned_vectors = owned_first[:, wide_in : wide_in + vectors.shape[1]]
    owned_bias = owned_first[:, wide_in + vectors.shape[1] : wide_in + 12].reshape(-1)
    owned_shrink = owned_late[:, :ff_width].reshape(shrink_weight.shape)
    owned_expand = owned_late[:, ff_width : 2 * ff_width]
    owned_out = owned_late[:, 2 * ff_width :]
    new_in, mom_in = adam_step(project_in, moments_in, owned_in)
    new_out, mom_out = adam_step(project_out, moments_out, owned_out)
    new_expand, mom_expand = adam_step(expand_weight, moments_expand, owned_expand)
    new_shrink, mom_shrink = adam_step(shrink_weight, moments_shrink, owned_shrink)
    new_bias, mom_bias = adam_step(expand_bias, moments_bias, owned_bias)
    new_vectors, mom_vectors = adam_step(vectors, moments_vectors, owned_vectors)
    return (
        output,
        grad_inputs,
        owned_in,
        owned_out,
        owned_expand,
        owned_shrink,
        owned_bias,
        owned_vectors,
        new_in,
        new_out,
        new_expand,
        new_shrink,
        new_bias,
        new_vectors,
        mom_in,
        mom_out,
        mom_expand,
        mom_shrink,
        mom_bias,
        mom_vectors,
    )


def solution(mesh):
    in_specs = (
        P("clip", "frame", None),
        P("clip", "frame", None),
        P(("clip", "frame"), None),
        P(("clip", "frame"), None),
        P(("clip", "frame"), None),
        P(("clip", "frame"), None),
        P(("clip", "frame")),
        P(("clip", "frame"), None),
        P(None, ("clip", "frame"), None),
        P(None, ("clip", "frame"), None),
        P(None, ("clip", "frame"), None),
        P(None, ("clip", "frame"), None),
        P(None, ("clip", "frame")),
        P(None, ("clip", "frame"), None),
    )
    out_specs = (
        P("clip", "frame", None),
        P("clip", "frame", None),
        P(("clip", "frame"), None),
        P(("clip", "frame"), None),
        P(("clip", "frame"), None),
        P(("clip", "frame"), None),
        P(("clip", "frame")),
        P(("clip", "frame"), None),
        P(("clip", "frame"), None),
        P(("clip", "frame"), None),
        P(("clip", "frame"), None),
        P(("clip", "frame"), None),
        P(("clip", "frame")),
        P(("clip", "frame"), None),
        P(None, ("clip", "frame"), None),
        P(None, ("clip", "frame"), None),
        P(None, ("clip", "frame"), None),
        P(None, ("clip", "frame"), None),
        P(None, ("clip", "frame")),
        P(None, ("clip", "frame"), None),
    )
    return jax.shard_map(
        functools.partial(body, link_plan(mesh)),
        mesh=mesh,
        in_specs=in_specs,
        out_specs=out_specs,
        check_vma=False,
    )
```

```python
import functools
import math

import jax
import jax.numpy as jnp
from jax import lax
from jax.experimental import pallas as pl
from jax.experimental.pallas import tpu as pltpu
from jax.sharding import PartitionSpec as P

HEADS = 12
ADAM_STEP = 4


epsilon_norm = 1e-05
beta_first = 0.9
beta_second = 0.99
learn_rate = 0.03
decay_rate = 0.01
epsilon_adam = 1e-08
root_half = 0.7071067811865476
inv_root_two_pi = 0.3989422804014327


def norm_parts(inputs, norm_gain, norm_shift):
    average = jnp.mean(inputs, axis=-1, keepdims=True)
    centered = inputs - average
    spread = jnp.mean(centered * centered, axis=-1, keepdims=True)
    inv_std = lax.rsqrt(spread + epsilon_norm)
    normed = centered * inv_std
    return (normed * norm_gain + norm_shift, normed, inv_std)


def norm_backward(grad_normed, normed, inv_std, norm_gain):
    grad_gain = jnp.sum(grad_normed * normed, axis=0)
    grad_shift = jnp.sum(grad_normed, axis=0)
    scaled = grad_normed * norm_gain
    grad_input = inv_std * (
        scaled
        - jnp.mean(scaled, axis=-1, keepdims=True)
        - normed * jnp.mean(scaled * normed, axis=-1, keepdims=True)
    )
    return (grad_input, grad_gain, grad_shift)


def gelu_exact(inputs):
    return 0.5 * inputs * (1.0 + jax.scipy.special.erf(inputs * root_half))


def gelu_slope(inputs):
    return (
        0.5 * (1.0 + jax.scipy.special.erf(inputs * root_half))
        + inputs * jnp.exp(-0.5 * inputs * inputs) * inv_root_two_pi
    )


QUERY_CHUNK = 256
MASKED = -1e30


def attention_forward_kernel(q_ref, k_ref, v_ref, kbias_ref, o_ref, l_ref):
    head_size = q_ref.shape[1] // 2
    rows = q_ref.shape[0]
    kbias = kbias_ref[...]
    lane = lax.broadcasted_iota(jnp.int32, (QUERY_CHUNK, 2 * head_size), 1)

    def chunk_body(chunk, carry):
        span = pl.ds(pl.multiple_of(chunk * QUERY_CHUNK, QUERY_CHUNK), QUERY_CHUNK)
        mixed_parts = []
        totals = []
        for half in range(2):
            cols = pl.ds(half * head_size, head_size)
            query = q_ref[span, cols]
            key = k_ref[:, cols]
            value = v_ref[:, cols]
            scores = (
                lax.dot_general(
                    query, key, (((1,), (1,)), ((), ())), preferred_element_type=jnp.float32
                )
                + kbias
            )
            highest = jnp.max(scores, axis=1, keepdims=True)
            exponent = jnp.exp(scores - highest)
            denominator = jnp.sum(exponent, axis=1, keepdims=True)
            weights = (exponent * (1.0 / denominator)).astype(jnp.bfloat16)
            mixed_parts.append(jnp.dot(weights, value, preferred_element_type=jnp.float32))
            totals.append(highest + jnp.log(denominator))
        o_ref[span, :] = jnp.concatenate(mixed_parts, axis=1).astype(o_ref.dtype)
        l_ref[span, :] = jnp.where(lane < head_size, totals[0], totals[1])
        return carry

    lax.fori_loop(0, rows // QUERY_CHUNK, chunk_body, 0)


def attention_backward_kernel(
    q_ref, k_ref, v_ref, do_ref, l_ref, kbias_ref, dq_ref, dk_ref, dv_ref
):
    head_size = q_ref.shape[1] // 2
    rows = q_ref.shape[0]
    kbias = kbias_ref[...]
    dk_ref[...] = jnp.zeros_like(dk_ref)
    dv_ref[...] = jnp.zeros_like(dv_ref)
    for half in range(2):
        cols = pl.ds(half * head_size, head_size)

        def chunk_body(chunk, carry, cols=cols, half=half):
            span = pl.ds(pl.multiple_of(chunk * QUERY_CHUNK, QUERY_CHUNK), QUERY_CHUNK)
            key = k_ref[:, cols]
            value = v_ref[:, cols]
            query = q_ref[span, cols]
            grad_out = do_ref[span, cols]
            total = l_ref[span, pl.ds(half * head_size, 1)]
            scores = (
                lax.dot_general(
                    query, key, (((1,), (1,)), ((), ())), preferred_element_type=jnp.float32
                )
                + kbias
            )
            weights = jnp.exp(scores - total)
            grad_weights = lax.dot_general(
                grad_out, value, (((1,), (1,)), ((), ())), preferred_element_type=jnp.float32
            )
            delta = jnp.sum(weights * grad_weights, axis=1, keepdims=True)
            grad_scores = (weights * (grad_weights - delta)).astype(jnp.bfloat16)
            dq_ref[span, cols] = jnp.dot(
                grad_scores, key, preferred_element_type=jnp.float32
            ).astype(dq_ref.dtype)
            dk_ref[:, cols] += lax.dot_general(
                grad_scores, query, (((0,), (0,)), ((), ())), preferred_element_type=jnp.float32
            )
            dv_ref[:, cols] += lax.dot_general(
                weights.astype(jnp.bfloat16),
                grad_out,
                (((0,), (0,)), ((), ())),
                preferred_element_type=jnp.float32,
            )
            return carry

        lax.fori_loop(0, rows // QUERY_CHUNK, chunk_body, 0)


def pad_rows(values, rows):
    return jnp.pad(values, ((0, rows - values.shape[0]), (0, 0)))


def attention_pallas(queries, pairs, grad_out=None, totals=None, first_pair=0, pair_span=None):
    query_rows, model_width = queries.shape
    key_rows = pairs.shape[0]
    padded_q = -(-query_rows // QUERY_CHUNK) * QUERY_CHUNK
    padded_k = -(-key_rows // 128) * 128
    pair_count = model_width // 128
    q_pad = pad_rows(queries, padded_q)
    kv_pad = pad_rows(pairs, padded_k)
    kbias = jnp.where(jnp.arange(padded_k) < key_rows, 0.0, MASKED).astype(jnp.float32)[None, :]
    q_spec = pl.BlockSpec((padded_q, 128), lambda j: (0, j))
    k_spec = pl.BlockSpec((padded_k, 128), lambda j: (0, j))
    v_spec = pl.BlockSpec((padded_k, 128), lambda j: (0, j + pair_count))
    b_spec = pl.BlockSpec((1, padded_k), lambda j: (0, 0))
    params = pltpu.CompilerParams(vmem_limit_bytes=48 * 1024 * 1024)
    if grad_out is None:
        mixed, log_totals = pl.pallas_call(
            attention_forward_kernel,
            grid=(pair_count,),
            in_specs=[q_spec, k_spec, v_spec, b_spec],
            out_specs=[q_spec, q_spec],
            out_shape=[
                jax.ShapeDtypeStruct((padded_q, model_width), jnp.bfloat16),
                jax.ShapeDtypeStruct((padded_q, model_width), jnp.float32),
            ],
            compiler_params=params,
        )(q_pad, kv_pad, kv_pad, kbias)
        return mixed[:query_rows], log_totals
    do_pad = pad_rows(grad_out, padded_q)
    span = pair_count if pair_span is None else pair_span
    qi_spec = pl.BlockSpec((padded_q, 128), lambda j: (0, j + first_pair))
    ki_spec = pl.BlockSpec((padded_k, 128), lambda j: (0, j + first_pair))
    vi_spec = pl.BlockSpec((padded_k, 128), lambda j: (0, j + first_pair + pair_count))
    qo_spec = pl.BlockSpec((padded_q, 128), lambda j: (0, j))
    ko_spec = pl.BlockSpec((padded_k, 128), lambda j: (0, j))
    dq, dk, dv = pl.pallas_call(
        attention_backward_kernel,
        grid=(span,),
        in_specs=[qi_spec, ki_spec, vi_spec, qi_spec, qi_spec, b_spec],
        out_specs=[qo_spec, ko_spec, ko_spec],
        out_shape=[
            jax.ShapeDtypeStruct((padded_q, 128 * span), jnp.float32),
            jax.ShapeDtypeStruct((padded_k, 128 * span), jnp.float32),
            jax.ShapeDtypeStruct((padded_k, 128 * span), jnp.float32),
        ],
        compiler_params=params,
    )(q_pad, kv_pad, kv_pad, do_pad, totals, kbias)
    return dq[:query_rows], dk[:key_rows], dv[:key_rows]


def attend_forward(queries, keys_values, head_count):
    model_width = queries.shape[2]
    head_size = model_width // head_count
    score_scale = 1.0 / math.sqrt(head_size)

    def one_head(head_index):
        offset = head_index * head_size
        query_block = lax.dynamic_slice_in_dim(queries, offset, head_size, 2)
        key_block = lax.dynamic_slice_in_dim(keys_values, offset, head_size, 2)
        value_block = lax.dynamic_slice_in_dim(keys_values, model_width + offset, head_size, 2)
        scores = (
            jnp.einsum("cqd,ckd->cqk", query_block, key_block, preferred_element_type=jnp.float32)
            * score_scale
        )
        highest = jnp.max(scores, axis=-1, keepdims=True)
        exponent = jnp.exp(scores - highest)
        denominator = jnp.sum(exponent, axis=-1, keepdims=True)
        weights_soft = (exponent / denominator).astype(jnp.bfloat16)
        mixed = jnp.einsum(
            "cqk,ckd->cqd", weights_soft, value_block, preferred_element_type=jnp.float32
        )
        return (mixed, (highest + jnp.log(denominator))[..., 0])

    mixed, log_totals = lax.map(one_head, jnp.arange(head_count))
    clip_count, frame_count = (queries.shape[0], queries.shape[1])
    mixed = jnp.transpose(mixed, (1, 2, 0, 3)).reshape(clip_count, frame_count, model_width)
    return (mixed, log_totals)


def attend_backward(queries, keys_values, grad_mixed, log_totals, head_count):
    model_width = queries.shape[2]
    head_size = model_width // head_count
    score_scale = 1.0 / math.sqrt(head_size)

    def one_head_back(head_index):
        offset = head_index * head_size
        query_block = lax.dynamic_slice_in_dim(queries, offset, head_size, 2)
        key_block = lax.dynamic_slice_in_dim(keys_values, offset, head_size, 2)
        value_block = lax.dynamic_slice_in_dim(keys_values, model_width + offset, head_size, 2)
        grad_block = lax.dynamic_slice_in_dim(grad_mixed, offset, head_size, 2)
        totals = lax.dynamic_index_in_dim(log_totals, head_index, 0, keepdims=False)
        scores = (
            jnp.einsum("cqd,ckd->cqk", query_block, key_block, preferred_element_type=jnp.float32)
            * score_scale
        )
        weights_soft = jnp.exp(scores - totals[..., None])
        grad_weights = jnp.einsum(
            "cqd,ckd->cqk", grad_block, value_block, preferred_element_type=jnp.float32
        )
        delta = jnp.sum(weights_soft * grad_weights, axis=-1, keepdims=True)
        grad_scores = (weights_soft * (grad_weights - delta)).astype(jnp.bfloat16)
        grad_query = (
            jnp.einsum("cqk,ckd->cqd", grad_scores, key_block, preferred_element_type=jnp.float32)
            * score_scale
        )
        grad_key = (
            jnp.einsum("cqk,cqd->ckd", grad_scores, query_block, preferred_element_type=jnp.float32)
            * score_scale
        )
        grad_value = jnp.einsum(
            "cqk,cqd->ckd",
            weights_soft.astype(jnp.bfloat16),
            grad_block,
            preferred_element_type=jnp.float32,
        )
        return (grad_query, delta[..., 0], grad_key, grad_value)

    pieces = lax.map(one_head_back, jnp.arange(head_count))
    clip_count, frame_count = (queries.shape[0], queries.shape[1])
    clip_frames = keys_values.shape[1]
    grad_query = jnp.transpose(pieces[0], (1, 2, 0, 3)).reshape(
        clip_count, frame_count, model_width
    )
    grad_key = jnp.transpose(pieces[2], (1, 2, 0, 3)).reshape(clip_count, clip_frames, model_width)
    grad_value = jnp.transpose(pieces[3], (1, 2, 0, 3)).reshape(
        clip_count, clip_frames, model_width
    )
    return (grad_query, pieces[1], jnp.concatenate([grad_key, grad_value], axis=2))


def link_plan(mesh):
    devices = list(mesh.devices.reshape(-1))
    bit_count = len(devices).bit_length() - 1
    core_bit = 1
    for bit in range(bit_count):
        first, other = devices[0], devices[1 << bit]
        if getattr(first, "coords", None) is not None and tuple(first.coords) == tuple(other.coords):
            core_bit = bit
    others = [bit for bit in range(bit_count) if bit != core_bit]
    near, far = others[:-1], others[-1:]
    rotated = tuple(tuple(near[k:] + near[:k] + far) for k in range(3))
    inner = [bit for bit in near if bit != 0]
    late = tuple(tuple(inner[k:] + inner[:k] + [0] + far) for k in range(2))
    return bit_count, core_bit, rotated, late


def tree_reduce_scatter(terms, part_columns, orders, plan_bits, hooks=None):
    hooks = dict(hooks or {})
    tied = {}
    bit_count, core_bit = plan_bits
    device = lax.axis_index("clip") * lax.axis_size("frame") + lax.axis_index("frame")
    blocks = 1 << bit_count
    block_rows = terms.shape[0] // blocks
    data = terms.reshape((2,) * bit_count + (block_rows, terms.shape[1]))
    parts = [(data, list(range(bit_count - 1, -1, -1)))]
    plan = [(core_bit,)] + [tuple(order[stage] for order in orders) for stage in range(len(orders[0]))]
    for stage, stage_bits in enumerate(plan):
        if stage == 1:
            whole, bits = parts[0]
            parts = []
            offset = 0
            for width in part_columns:
                parts.append((whole[..., offset : offset + width], bits))
                offset += width
        keeps, sends = [], []
        for (part, part_bits), bit in zip(parts, stage_bits):
            axis = part_bits.index(bit)
            mine = (device >> bit) & 1
            keeps.append(lax.dynamic_index_in_dim(part, mine, axis=axis, keepdims=False))
            sends.append(
                lax.dynamic_index_in_dim(part, 1 - mine, axis=axis, keepdims=False).astype(jnp.bfloat16)
            )
        new_parts = []
        for keep, send, (part, part_bits), bit in zip(keeps, sends, parts, stage_bits):
            pairs = [(index, index ^ (1 << bit)) for index in range(blocks)]
            got = lax.ppermute(send, ("clip", "frame"), pairs)
            new_parts.append((keep + got.astype(jnp.float32), [b for b in part_bits if b != bit]))
        if stage in hooks:
            values, tied[stage] = lax.optimization_barrier(
                ([part for part, _ in new_parts], hooks[stage](tied))
            )
            new_parts = [(value, part_bits) for value, (_, part_bits) in zip(values, new_parts)]
        parts = new_parts
    return jnp.concatenate([part for part, _ in parts], axis=-1).astype(jnp.float32), tied


def tree_all_gather(local, part_columns, orders, plan_bits):
    bit_count, core_bit = plan_bits
    device = lax.axis_index("clip") * lax.axis_size("frame") + lax.axis_index("frame")
    canonical = list(range(bit_count - 1, -1, -1))

    def double(data, bits, bit):
        mine = (device >> bit) & 1
        pairs = [(index, index ^ (1 << bit)) for index in range(1 << bit_count)]
        got = lax.ppermute(data, ("clip", "frame"), pairs)
        new_bits = sorted(bits + [bit], reverse=True)
        axis = new_bits.index(bit)
        low_first = jnp.stack([data, got], axis=axis)
        high_first = jnp.stack([got, data], axis=axis)
        return jnp.where(mine == 0, low_first, high_first), new_bits

    parts = []
    offset = 0
    for width in part_columns:
        parts.append((local[:, offset : offset + width], []))
        offset += width
    reversed_orders = [list(reversed(order)) for order in orders]
    for stage in range(len(reversed_orders[0])):
        parts = [double(part, bits, order[stage]) for (part, bits), order in zip(parts, reversed_orders)]
    whole = jnp.concatenate([part for part, _ in parts], axis=-1)
    whole, bits = double(whole, parts[0][1], core_bit)
    assert bits == canonical
    return whole.reshape((1 << bit_count) * local.shape[0], local.shape[1])


def adam_step(weight, moments, gradient):
    first = beta_first * moments[0] + (1.0 - beta_first) * gradient
    second = beta_second * moments[1] + (1.0 - beta_second) * gradient * gradient
    first_hat = first / (1.0 - beta_first**ADAM_STEP)
    second_hat = second / (1.0 - beta_second**ADAM_STEP)
    change = -learn_rate * (first_hat / (jnp.sqrt(second_hat) + epsilon_adam) + decay_rate * weight)
    return (change, jnp.stack([first, second]))


def body(
    plan,
    inputs,
    cotangent,
    project_in,
    project_out,
    expand_weight,
    shrink_weight,
    expand_bias,
    vectors,
    moments_in,
    moments_out,
    moments_expand,
    moments_shrink,
    moments_bias,
    moments_vectors,
):
    clip_count, frame_count, model_width = inputs.shape
    row_count = clip_count * frame_count
    head_count = HEADS
    shard_rows = project_in.shape[0]
    wide_in = project_in.shape[1]
    ff_width = expand_weight.shape[1]
    swap = [(0, 1), (1, 0)]
    everyone = ("clip", "frame")

    small = jnp.concatenate(
        [
            vectors,
            expand_bias.reshape(shard_rows, -1),
            jnp.zeros((shard_rows, 128 - vectors.shape[1] - expand_bias.shape[0] // shard_rows), jnp.float32),
        ],
        axis=1,
    )
    first_pack = jnp.concatenate([project_in, small], axis=1).astype(jnp.bfloat16)
    second_pack = jnp.concatenate(
        [project_out, expand_weight, shrink_weight.reshape(shard_rows, -1)], axis=1
    ).astype(jnp.bfloat16)
    bit_count, core_bit, rotated_orders, late_orders = plan
    first_full = tree_all_gather(first_pack, (896, 768, 768), rotated_orders, (bit_count, core_bit))
    second_full = lax.all_gather(second_pack, everyone, axis=0, tiled=True)
    full_in = first_full[:, :wide_in]
    small_full = first_full[:, wide_in:].astype(jnp.float32)
    column_set = small_full[:, : vectors.shape[1]]
    full_bias = small_full[:, vectors.shape[1] : vectors.shape[1] + ff_width // model_width].reshape(-1)
    full_out = second_full[:, :model_width]
    full_expand = second_full[:, model_width : model_width + ff_width]
    full_shrink = second_full[:, model_width + ff_width :].reshape(ff_width, model_width)

    frames_rows = inputs.reshape(row_count, model_width).astype(jnp.float32)
    normed_first, plain_first, inv_first = norm_parts(
        frames_rows, column_set[:, 0], column_set[:, 1]
    )
    hidden_first = normed_first.astype(jnp.bfloat16)
    partner_rows = lax.ppermute(inputs, "frame", swap).reshape(row_count, model_width)
    hidden_partner = norm_parts(
        partner_rows.astype(jnp.float32), column_set[:, 0], column_set[:, 1]
    )[0].astype(jnp.bfloat16)
    bias_in = jnp.concatenate(
        [column_set[:, 2], jnp.zeros((model_width,), jnp.float32), column_set[:, 3]]
    )
    projected = (
        jnp.dot(hidden_first, full_in, preferred_element_type=jnp.float32) + bias_in
    ).astype(jnp.bfloat16)
    partner_pairs = (
        jnp.dot(hidden_partner, full_in[:, model_width:], preferred_element_type=jnp.float32)
        + bias_in[model_width:]
    ).astype(jnp.bfloat16)
    queries = projected[:, :model_width].reshape(clip_count, frame_count, model_width)
    clip_pairs = jnp.concatenate([projected[:, model_width:], partner_pairs], axis=0).reshape(
        clip_count, 2 * frame_count, 2 * model_width
    )
    score_scale = 1.0 / math.sqrt(model_width // head_count)
    scaled_queries = (projected[:, :model_width] * score_scale).astype(jnp.bfloat16)
    pair_rows = clip_pairs.reshape(2 * row_count, 2 * model_width)
    mixed_low, log_totals = attention_pallas(scaled_queries, pair_rows)
    attended = jnp.dot(mixed_low, full_out, preferred_element_type=jnp.float32) + column_set[:, 4]
    residual = frames_rows + attended
    normed_second, plain_second, inv_second = norm_parts(
        residual, column_set[:, 5], column_set[:, 6]
    )
    hidden_second = normed_second.astype(jnp.bfloat16)
    preact = jnp.dot(hidden_second, full_expand, preferred_element_type=jnp.float32) + full_bias
    activated = gelu_exact(preact).astype(jnp.bfloat16)
    result = (
        residual
        + jnp.dot(activated, full_shrink, preferred_element_type=jnp.float32)
        + column_set[:, 7]
    )
    output = result.astype(jnp.bfloat16).reshape(inputs.shape)

    grad_result = cotangent.reshape(row_count, model_width)
    grad_shrink_term = jnp.dot(
        activated.T, grad_result, preferred_element_type=jnp.float32
    ).astype(jnp.bfloat16)
    grad_down_bias = jnp.sum(grad_result.astype(jnp.float32), axis=0)
    grad_activated = jnp.dot(grad_result, full_shrink.T, preferred_element_type=jnp.float32)
    grad_preact = (grad_activated * gelu_slope(preact)).astype(jnp.bfloat16)
    grad_expand_term = jnp.dot(
        hidden_second.T, grad_preact, preferred_element_type=jnp.float32
    ).astype(jnp.bfloat16)
    grad_bias_term = jnp.sum(grad_preact.astype(jnp.float32), axis=0)
    grad_hidden_second = jnp.dot(grad_preact, full_expand.T, preferred_element_type=jnp.float32)
    norm_term_second, gain_second, shift_second = norm_backward(
        grad_hidden_second, plain_second, inv_second, column_set[:, 5]
    )
    grad_residual = grad_result.astype(jnp.float32) + norm_term_second
    grad_attended = grad_residual.astype(jnp.bfloat16)
    grad_out_term = jnp.dot(
        mixed_low.T, grad_attended, preferred_element_type=jnp.float32
    ).astype(jnp.bfloat16)
    grad_out_bias = jnp.sum(grad_attended.astype(jnp.float32), axis=0)
    late_terms = jnp.concatenate(
        [grad_shrink_term.reshape(model_width, -1), grad_expand_term, grad_out_term], axis=1
    )
    grad_mixed = jnp.dot(grad_attended, full_out.T, preferred_element_type=jnp.float32).astype(
        jnp.bfloat16
    )
    piece_pairs = 1
    piece_count = model_width // 128 // piece_pairs
    stage_count = 1 + len(late_orders[0])
    hooked = list(range(1, min(piece_count, stage_count)))

    def run_piece(index, mixed_grads):
        return attention_pallas(
            scaled_queries, pair_rows, mixed_grads, log_totals, index * piece_pairs, piece_pairs
        )

    def piece_hook(index):
        return lambda tied: (run_piece(index, tied[index - 1][1]), tied[index - 1][1])

    hooks = {0: lambda tied: ((), grad_mixed)}
    hooks.update({index: piece_hook(index) for index in hooked})
    pieces = [run_piece(0, grad_mixed)]
    owned_late, tied = tree_reduce_scatter(
        late_terms, (3456, 3456), late_orders, (bit_count, core_bit), hooks
    )
    pieces += [tied[index][0] for index in hooked]
    last_mixed = tied[hooked[-1]][1] if hooked else grad_mixed
    pieces += [run_piece(index, last_mixed) for index in range(len(hooked) + 1, piece_count)]
    finished = []
    for grad_query, grad_keys, grad_values in pieces:
        terms = jnp.concatenate([grad_keys, grad_values], axis=1)
        returned = lax.ppermute(terms[row_count:].astype(jnp.bfloat16), "frame", swap)
        finished.append((grad_query, terms[:row_count] + returned.astype(jnp.float32)))
    piece_width = finished[0][0].shape[1]
    grad_projected = jnp.concatenate(
        [
            (jnp.concatenate([query for query, _ in finished], axis=1) * score_scale).astype(
                jnp.bfloat16
            ),
            jnp.concatenate(
                [pair[:, :piece_width] for _, pair in finished]
                + [pair[:, piece_width:] for _, pair in finished],
                axis=1,
            ).astype(jnp.bfloat16),
        ],
        axis=1,
    )
    grad_in_term = jnp.dot(
        hidden_first.T, grad_projected, preferred_element_type=jnp.float32
    ).astype(jnp.bfloat16)
    projected_sums = jnp.sum(grad_projected.astype(jnp.float32), axis=0)
    grad_query_bias = projected_sums[:model_width]
    grad_value_bias = projected_sums[2 * model_width :]
    grad_hidden_first = jnp.dot(grad_projected, full_in.T, preferred_element_type=jnp.float32)
    norm_term_first, gain_first, shift_first = norm_backward(
        grad_hidden_first, plain_first, inv_first, column_set[:, 0]
    )
    grad_inputs = (grad_residual + norm_term_first).astype(jnp.bfloat16).reshape(inputs.shape)
    grad_columns = jnp.stack(
        [
            gain_first,
            shift_first,
            grad_query_bias,
            grad_value_bias,
            grad_out_bias,
            gain_second,
            shift_second,
            grad_down_bias,
        ],
        axis=1,
    )
    small_grads = jnp.concatenate(
        [
            grad_columns,
            grad_bias_term.reshape(model_width, -1),
            jnp.zeros((model_width, 128 - 12), jnp.float32),
        ],
        axis=1,
    ).astype(jnp.bfloat16)
    owned_in = tree_reduce_scatter(
        grad_in_term, (768, 768, 768), rotated_orders, (bit_count, core_bit)
    )[0]
    owned_small = tree_reduce_scatter(
        small_grads, (small_grads.shape[1],), rotated_orders[:1], (bit_count, core_bit)
    )[0]
    owned_vectors = owned_small[:, : vectors.shape[1]]
    owned_bias = owned_small[:, vectors.shape[1] : 12].reshape(-1)
    owned_shrink = owned_late[:, :ff_width].reshape(shrink_weight.shape)
    owned_expand = owned_late[:, ff_width : 2 * ff_width]
    owned_out = owned_late[:, 2 * ff_width :]
    new_in, mom_in = adam_step(project_in, moments_in, owned_in)
    new_out, mom_out = adam_step(project_out, moments_out, owned_out)
    new_expand, mom_expand = adam_step(expand_weight, moments_expand, owned_expand)
    new_shrink, mom_shrink = adam_step(shrink_weight, moments_shrink, owned_shrink)
    new_bias, mom_bias = adam_step(expand_bias, moments_bias, owned_bias)
    new_vectors, mom_vectors = adam_step(vectors, moments_vectors, owned_vectors)
    return (
        output,
        grad_inputs,
        owned_in,
        owned_out,
        owned_expand,
        owned_shrink,
        owned_bias,
        owned_vectors,
        new_in,
        new_out,
        new_expand,
        new_shrink,
        new_bias,
        new_vectors,
        mom_in,
        mom_out,
        mom_expand,
        mom_shrink,
        mom_bias,
        mom_vectors,
    )


def solution(mesh):
    in_specs = (
        P("clip", "frame", None),
        P("clip", "frame", None),
        P(("clip", "frame"), None),
        P(("clip", "frame"), None),
        P(("clip", "frame"), None),
        P(("clip", "frame"), None),
        P(("clip", "frame")),
        P(("clip", "frame"), None),
        P(None, ("clip", "frame"), None),
        P(None, ("clip", "frame"), None),
        P(None, ("clip", "frame"), None),
        P(None, ("clip", "frame"), None),
        P(None, ("clip", "frame")),
        P(None, ("clip", "frame"), None),
    )
    out_specs = (
        P("clip", "frame", None),
        P("clip", "frame", None),
        P(("clip", "frame"), None),
        P(("clip", "frame"), None),
        P(("clip", "frame"), None),
        P(("clip", "frame"), None),
        P(("clip", "frame")),
        P(("clip", "frame"), None),
        P(("clip", "frame"), None),
        P(("clip", "frame"), None),
        P(("clip", "frame"), None),
        P(("clip", "frame"), None),
        P(("clip", "frame")),
        P(("clip", "frame"), None),
        P(None, ("clip", "frame"), None),
        P(None, ("clip", "frame"), None),
        P(None, ("clip", "frame"), None),
        P(None, ("clip", "frame"), None),
        P(None, ("clip", "frame")),
        P(None, ("clip", "frame"), None),
    )
    return jax.shard_map(
        functools.partial(body, link_plan(mesh)),
        mesh=mesh,
        in_specs=in_specs,
        out_specs=out_specs,
        check_vma=False,
    )
```

```python
import functools
import math

import jax
import jax.numpy as jnp
from jax import lax
from jax.experimental import pallas as pl
from jax.experimental.pallas import tpu as pltpu
from jax.sharding import PartitionSpec as P

HEADS = 12
ADAM_STEP = 4


epsilon_norm = 1e-05
beta_first = 0.9
beta_second = 0.99
learn_rate = 0.03
decay_rate = 0.01
epsilon_adam = 1e-08
root_half = 0.7071067811865476
inv_root_two_pi = 0.3989422804014327


def norm_parts(inputs, norm_gain, norm_shift):
    average = jnp.mean(inputs, axis=-1, keepdims=True)
    centered = inputs - average
    spread = jnp.mean(centered * centered, axis=-1, keepdims=True)
    inv_std = lax.rsqrt(spread + epsilon_norm)
    normed = centered * inv_std
    return (normed * norm_gain + norm_shift, normed, inv_std)


def norm_backward(grad_normed, normed, inv_std, norm_gain):
    grad_gain = jnp.sum(grad_normed * normed, axis=0)
    grad_shift = jnp.sum(grad_normed, axis=0)
    scaled = grad_normed * norm_gain
    grad_input = inv_std * (
        scaled
        - jnp.mean(scaled, axis=-1, keepdims=True)
        - normed * jnp.mean(scaled * normed, axis=-1, keepdims=True)
    )
    return (grad_input, grad_gain, grad_shift)


def gelu_exact(inputs):
    return 0.5 * inputs * (1.0 + jax.scipy.special.erf(inputs * root_half))


def gelu_slope(inputs):
    return (
        0.5 * (1.0 + jax.scipy.special.erf(inputs * root_half))
        + inputs * jnp.exp(-0.5 * inputs * inputs) * inv_root_two_pi
    )


QUERY_CHUNK = 256
MASKED = -1e30


def attention_forward_kernel(q_ref, k_ref, v_ref, kbias_ref, o_ref, l_ref):
    head_size = q_ref.shape[1] // 2
    rows = q_ref.shape[0]
    kbias = kbias_ref[...]
    lane = lax.broadcasted_iota(jnp.int32, (QUERY_CHUNK, 2 * head_size), 1)

    def chunk_body(chunk, carry):
        span = pl.ds(pl.multiple_of(chunk * QUERY_CHUNK, QUERY_CHUNK), QUERY_CHUNK)
        mixed_parts = []
        totals = []
        for half in range(2):
            cols = pl.ds(half * head_size, head_size)
            query = q_ref[span, cols]
            key = k_ref[:, cols]
            value = v_ref[:, cols]
            scores = (
                lax.dot_general(
                    query, key, (((1,), (1,)), ((), ())), preferred_element_type=jnp.float32
                )
                + kbias
            )
            highest = jnp.max(scores, axis=1, keepdims=True)
            exponent = jnp.exp(scores - highest)
            denominator = jnp.sum(exponent, axis=1, keepdims=True)
            weights = (exponent * (1.0 / denominator)).astype(jnp.bfloat16)
            mixed_parts.append(jnp.dot(weights, value, preferred_element_type=jnp.float32))
            totals.append(highest + jnp.log(denominator))
        o_ref[span, :] = jnp.concatenate(mixed_parts, axis=1).astype(o_ref.dtype)
        l_ref[span, :] = jnp.where(lane < head_size, totals[0], totals[1])
        return carry

    lax.fori_loop(0, rows // QUERY_CHUNK, chunk_body, 0)


def attention_backward_kernel(
    q_ref, k_ref, v_ref, do_ref, l_ref, kbias_ref, dq_ref, dk_ref, dv_ref
):
    head_size = q_ref.shape[1] // 2
    rows = q_ref.shape[0]
    kbias = kbias_ref[...]
    dk_ref[...] = jnp.zeros_like(dk_ref)
    dv_ref[...] = jnp.zeros_like(dv_ref)
    for half in range(2):
        cols = pl.ds(half * head_size, head_size)

        def chunk_body(chunk, carry, cols=cols, half=half):
            span = pl.ds(pl.multiple_of(chunk * QUERY_CHUNK, QUERY_CHUNK), QUERY_CHUNK)
            key = k_ref[:, cols]
            value = v_ref[:, cols]
            query = q_ref[span, cols]
            grad_out = do_ref[span, cols]
            total = l_ref[span, pl.ds(half * head_size, 1)]
            scores = (
                lax.dot_general(
                    query, key, (((1,), (1,)), ((), ())), preferred_element_type=jnp.float32
                )
                + kbias
            )
            weights = jnp.exp(scores - total)
            grad_weights = lax.dot_general(
                grad_out, value, (((1,), (1,)), ((), ())), preferred_element_type=jnp.float32
            )
            delta = jnp.sum(weights * grad_weights, axis=1, keepdims=True)
            grad_scores = (weights * (grad_weights - delta)).astype(jnp.bfloat16)
            dq_ref[span, cols] = jnp.dot(
                grad_scores, key, preferred_element_type=jnp.float32
            ).astype(dq_ref.dtype)
            dk_ref[:, cols] += lax.dot_general(
                grad_scores, query, (((0,), (0,)), ((), ())), preferred_element_type=jnp.float32
            )
            dv_ref[:, cols] += lax.dot_general(
                weights.astype(jnp.bfloat16),
                grad_out,
                (((0,), (0,)), ((), ())),
                preferred_element_type=jnp.float32,
            )
            return carry

        lax.fori_loop(0, rows // QUERY_CHUNK, chunk_body, 0)


def pad_rows(values, rows):
    return jnp.pad(values, ((0, rows - values.shape[0]), (0, 0)))


def attention_pallas(queries, pairs, grad_out=None, totals=None, first_pair=0, pair_span=None):
    query_rows, model_width = queries.shape
    key_rows = pairs.shape[0]
    padded_q = -(-query_rows // QUERY_CHUNK) * QUERY_CHUNK
    padded_k = -(-key_rows // 128) * 128
    pair_count = model_width // 128
    q_pad = pad_rows(queries, padded_q)
    kv_pad = pad_rows(pairs, padded_k)
    kbias = jnp.where(jnp.arange(padded_k) < key_rows, 0.0, MASKED).astype(jnp.float32)[None, :]
    q_spec = pl.BlockSpec((padded_q, 128), lambda j: (0, j))
    k_spec = pl.BlockSpec((padded_k, 128), lambda j: (0, j))
    v_spec = pl.BlockSpec((padded_k, 128), lambda j: (0, j + pair_count))
    b_spec = pl.BlockSpec((1, padded_k), lambda j: (0, 0))
    params = pltpu.CompilerParams(vmem_limit_bytes=48 * 1024 * 1024)
    if grad_out is None:
        mixed, log_totals = pl.pallas_call(
            attention_forward_kernel,
            grid=(pair_count,),
            in_specs=[q_spec, k_spec, v_spec, b_spec],
            out_specs=[q_spec, q_spec],
            out_shape=[
                jax.ShapeDtypeStruct((padded_q, model_width), jnp.bfloat16),
                jax.ShapeDtypeStruct((padded_q, model_width), jnp.float32),
            ],
            compiler_params=params,
        )(q_pad, kv_pad, kv_pad, kbias)
        return mixed[:query_rows], log_totals
    do_pad = pad_rows(grad_out, padded_q)
    span = pair_count if pair_span is None else pair_span
    qi_spec = pl.BlockSpec((padded_q, 128), lambda j: (0, j + first_pair))
    ki_spec = pl.BlockSpec((padded_k, 128), lambda j: (0, j + first_pair))
    vi_spec = pl.BlockSpec((padded_k, 128), lambda j: (0, j + first_pair + pair_count))
    qo_spec = pl.BlockSpec((padded_q, 128), lambda j: (0, j))
    ko_spec = pl.BlockSpec((padded_k, 128), lambda j: (0, j))
    dq, dk, dv = pl.pallas_call(
        attention_backward_kernel,
        grid=(span,),
        in_specs=[qi_spec, ki_spec, vi_spec, qi_spec, qi_spec, b_spec],
        out_specs=[qo_spec, ko_spec, ko_spec],
        out_shape=[
            jax.ShapeDtypeStruct((padded_q, 128 * span), jnp.float32),
            jax.ShapeDtypeStruct((padded_k, 128 * span), jnp.float32),
            jax.ShapeDtypeStruct((padded_k, 128 * span), jnp.float32),
        ],
        compiler_params=params,
    )(q_pad, kv_pad, kv_pad, do_pad, totals, kbias)
    return dq[:query_rows], dk[:key_rows], dv[:key_rows]


def attend_forward(queries, keys_values, head_count):
    model_width = queries.shape[2]
    head_size = model_width // head_count
    score_scale = 1.0 / math.sqrt(head_size)

    def one_head(head_index):
        offset = head_index * head_size
        query_block = lax.dynamic_slice_in_dim(queries, offset, head_size, 2)
        key_block = lax.dynamic_slice_in_dim(keys_values, offset, head_size, 2)
        value_block = lax.dynamic_slice_in_dim(keys_values, model_width + offset, head_size, 2)
        scores = (
            jnp.einsum("cqd,ckd->cqk", query_block, key_block, preferred_element_type=jnp.float32)
            * score_scale
        )
        highest = jnp.max(scores, axis=-1, keepdims=True)
        exponent = jnp.exp(scores - highest)
        denominator = jnp.sum(exponent, axis=-1, keepdims=True)
        weights_soft = (exponent / denominator).astype(jnp.bfloat16)
        mixed = jnp.einsum(
            "cqk,ckd->cqd", weights_soft, value_block, preferred_element_type=jnp.float32
        )
        return (mixed, (highest + jnp.log(denominator))[..., 0])

    mixed, log_totals = lax.map(one_head, jnp.arange(head_count))
    clip_count, frame_count = (queries.shape[0], queries.shape[1])
    mixed = jnp.transpose(mixed, (1, 2, 0, 3)).reshape(clip_count, frame_count, model_width)
    return (mixed, log_totals)


def attend_backward(queries, keys_values, grad_mixed, log_totals, head_count):
    model_width = queries.shape[2]
    head_size = model_width // head_count
    score_scale = 1.0 / math.sqrt(head_size)

    def one_head_back(head_index):
        offset = head_index * head_size
        query_block = lax.dynamic_slice_in_dim(queries, offset, head_size, 2)
        key_block = lax.dynamic_slice_in_dim(keys_values, offset, head_size, 2)
        value_block = lax.dynamic_slice_in_dim(keys_values, model_width + offset, head_size, 2)
        grad_block = lax.dynamic_slice_in_dim(grad_mixed, offset, head_size, 2)
        totals = lax.dynamic_index_in_dim(log_totals, head_index, 0, keepdims=False)
        scores = (
            jnp.einsum("cqd,ckd->cqk", query_block, key_block, preferred_element_type=jnp.float32)
            * score_scale
        )
        weights_soft = jnp.exp(scores - totals[..., None])
        grad_weights = jnp.einsum(
            "cqd,ckd->cqk", grad_block, value_block, preferred_element_type=jnp.float32
        )
        delta = jnp.sum(weights_soft * grad_weights, axis=-1, keepdims=True)
        grad_scores = (weights_soft * (grad_weights - delta)).astype(jnp.bfloat16)
        grad_query = (
            jnp.einsum("cqk,ckd->cqd", grad_scores, key_block, preferred_element_type=jnp.float32)
            * score_scale
        )
        grad_key = (
            jnp.einsum("cqk,cqd->ckd", grad_scores, query_block, preferred_element_type=jnp.float32)
            * score_scale
        )
        grad_value = jnp.einsum(
            "cqk,cqd->ckd",
            weights_soft.astype(jnp.bfloat16),
            grad_block,
            preferred_element_type=jnp.float32,
        )
        return (grad_query, delta[..., 0], grad_key, grad_value)

    pieces = lax.map(one_head_back, jnp.arange(head_count))
    clip_count, frame_count = (queries.shape[0], queries.shape[1])
    clip_frames = keys_values.shape[1]
    grad_query = jnp.transpose(pieces[0], (1, 2, 0, 3)).reshape(
        clip_count, frame_count, model_width
    )
    grad_key = jnp.transpose(pieces[2], (1, 2, 0, 3)).reshape(clip_count, clip_frames, model_width)
    grad_value = jnp.transpose(pieces[3], (1, 2, 0, 3)).reshape(
        clip_count, clip_frames, model_width
    )
    return (grad_query, pieces[1], jnp.concatenate([grad_key, grad_value], axis=2))


def link_plan(mesh):
    devices = list(mesh.devices.reshape(-1))
    bit_count = len(devices).bit_length() - 1
    core_bit = 1
    for bit in range(bit_count):
        first, other = devices[0], devices[1 << bit]
        if getattr(first, "coords", None) is not None and tuple(first.coords) == tuple(other.coords):
            core_bit = bit
    others = [bit for bit in range(bit_count) if bit != core_bit]
    near, far = others[:-1], others[-1:]
    rotated = tuple(tuple(near[k:] + near[:k] + far) for k in range(3))
    inner = [bit for bit in near if bit != 0]
    late = tuple(tuple(inner[k:] + inner[:k] + [0] + far) for k in range(2))
    return bit_count, core_bit, rotated, late


def tree_reduce_scatter(terms, part_columns, orders, plan_bits, hooks=None):
    hooks = dict(hooks or {})
    tied = {}
    bit_count, core_bit = plan_bits
    device = lax.axis_index("clip") * lax.axis_size("frame") + lax.axis_index("frame")
    blocks = 1 << bit_count
    block_rows = terms.shape[0] // blocks
    data = terms.reshape((2,) * bit_count + (block_rows, terms.shape[1]))
    parts = [(data, list(range(bit_count - 1, -1, -1)))]
    plan = [(core_bit,)] + [tuple(order[stage] for order in orders) for stage in range(len(orders[0]))]
    for stage, stage_bits in enumerate(plan):
        if stage == 1:
            whole, bits = parts[0]
            parts = []
            offset = 0
            for width in part_columns:
                parts.append((whole[..., offset : offset + width], bits))
                offset += width
        keeps, sends = [], []
        for (part, part_bits), bit in zip(parts, stage_bits):
            axis = part_bits.index(bit)
            mine = (device >> bit) & 1
            keeps.append(lax.dynamic_index_in_dim(part, mine, axis=axis, keepdims=False))
            sends.append(
                lax.dynamic_index_in_dim(part, 1 - mine, axis=axis, keepdims=False).astype(jnp.bfloat16)
            )
        new_parts = []
        for keep, send, (part, part_bits), bit in zip(keeps, sends, parts, stage_bits):
            pairs = [(index, index ^ (1 << bit)) for index in range(blocks)]
            got = lax.ppermute(send, ("clip", "frame"), pairs)
            new_parts.append((keep + got.astype(jnp.float32), [b for b in part_bits if b != bit]))
        if stage in hooks:
            values, tied[stage] = lax.optimization_barrier(
                ([part for part, _ in new_parts], hooks[stage](tied))
            )
            new_parts = [(value, part_bits) for value, (_, part_bits) in zip(values, new_parts)]
        parts = new_parts
    return jnp.concatenate([part for part, _ in parts], axis=-1).astype(jnp.float32), tied


def tree_all_gather(local, part_columns, orders, plan_bits):
    bit_count, core_bit = plan_bits
    device = lax.axis_index("clip") * lax.axis_size("frame") + lax.axis_index("frame")
    canonical = list(range(bit_count - 1, -1, -1))

    def double(data, bits, bit):
        mine = (device >> bit) & 1
        pairs = [(index, index ^ (1 << bit)) for index in range(1 << bit_count)]
        got = lax.ppermute(data, ("clip", "frame"), pairs)
        new_bits = sorted(bits + [bit], reverse=True)
        axis = new_bits.index(bit)
        low_first = jnp.stack([data, got], axis=axis)
        high_first = jnp.stack([got, data], axis=axis)
        return jnp.where(mine == 0, low_first, high_first), new_bits

    parts = []
    offset = 0
    for width in part_columns:
        parts.append((local[:, offset : offset + width], []))
        offset += width
    reversed_orders = [list(reversed(order)) for order in orders]
    for stage in range(len(reversed_orders[0])):
        parts = [double(part, bits, order[stage]) for (part, bits), order in zip(parts, reversed_orders)]
    whole = jnp.concatenate([part for part, _ in parts], axis=-1)
    whole, bits = double(whole, parts[0][1], core_bit)
    assert bits == canonical
    return whole.reshape((1 << bit_count) * local.shape[0], local.shape[1])


def adam_step(weight, moments, gradient):
    first = beta_first * moments[0] + (1.0 - beta_first) * gradient
    second = beta_second * moments[1] + (1.0 - beta_second) * gradient * gradient
    first_hat = first / (1.0 - beta_first**ADAM_STEP)
    second_hat = second / (1.0 - beta_second**ADAM_STEP)
    change = -learn_rate * (first_hat / (jnp.sqrt(second_hat) + epsilon_adam) + decay_rate * weight)
    return (change, jnp.stack([first, second]))


def body(
    plan,
    inputs,
    cotangent,
    project_in,
    project_out,
    expand_weight,
    shrink_weight,
    expand_bias,
    vectors,
    moments_in,
    moments_out,
    moments_expand,
    moments_shrink,
    moments_bias,
    moments_vectors,
):
    clip_count, frame_count, model_width = inputs.shape
    row_count = clip_count * frame_count
    head_count = HEADS
    shard_rows = project_in.shape[0]
    wide_in = project_in.shape[1]
    ff_width = expand_weight.shape[1]
    swap = [(0, 1), (1, 0)]
    everyone = ("clip", "frame")

    small = jnp.concatenate(
        [
            vectors,
            expand_bias.reshape(shard_rows, -1),
            jnp.zeros((shard_rows, 128 - vectors.shape[1] - expand_bias.shape[0] // shard_rows), jnp.float32),
        ],
        axis=1,
    )
    first_pack = jnp.concatenate([project_in, small], axis=1).astype(jnp.bfloat16)
    ff_group = ff_width // model_width
    expand_local = jnp.swapaxes(
        expand_weight.reshape(shard_rows, ff_width // ff_group, ff_group), 1, 2
    ).reshape(shard_rows, ff_width)
    second_pack = jnp.concatenate(
        [project_out, expand_local, shrink_weight.reshape(shard_rows, -1)], axis=1
    ).astype(jnp.bfloat16)
    bit_count, core_bit, rotated_orders, late_orders = plan
    first_full = tree_all_gather(first_pack, (896, 768, 768), rotated_orders, (bit_count, core_bit))
    second_full = lax.all_gather(second_pack, everyone, axis=0, tiled=True)
    full_in = first_full[:, :wide_in]
    small_full = first_full[:, wide_in:].astype(jnp.float32)
    column_set = small_full[:, : vectors.shape[1]]
    full_bias = small_full[:, vectors.shape[1] : vectors.shape[1] + ff_width // model_width].T.reshape(-1)
    full_out = second_full[:, :model_width]
    full_expand = second_full[:, model_width : model_width + ff_width]
    shrink_rows = second_full[:, model_width + ff_width :]
    ff_block = ff_width // ff_group

    def ff_cols(values, group):
        return values[:, group * ff_block : (group + 1) * ff_block]


    frames_rows = inputs.reshape(row_count, model_width).astype(jnp.float32)
    normed_first, plain_first, inv_first = norm_parts(
        frames_rows, column_set[:, 0], column_set[:, 1]
    )
    hidden_first = normed_first.astype(jnp.bfloat16)
    partner_rows = lax.ppermute(inputs, "frame", swap).reshape(row_count, model_width)
    hidden_partner = norm_parts(
        partner_rows.astype(jnp.float32), column_set[:, 0], column_set[:, 1]
    )[0].astype(jnp.bfloat16)
    bias_in = jnp.concatenate(
        [column_set[:, 2], jnp.zeros((model_width,), jnp.float32), column_set[:, 3]]
    )
    projected = (
        jnp.dot(hidden_first, full_in, preferred_element_type=jnp.float32) + bias_in
    ).astype(jnp.bfloat16)
    partner_pairs = (
        jnp.dot(hidden_partner, full_in[:, model_width:], preferred_element_type=jnp.float32)
        + bias_in[model_width:]
    ).astype(jnp.bfloat16)
    queries = projected[:, :model_width].reshape(clip_count, frame_count, model_width)
    clip_pairs = jnp.concatenate([projected[:, model_width:], partner_pairs], axis=0).reshape(
        clip_count, 2 * frame_count, 2 * model_width
    )
    score_scale = 1.0 / math.sqrt(model_width // head_count)
    scaled_queries = (projected[:, :model_width] * score_scale).astype(jnp.bfloat16)
    pair_rows = clip_pairs.reshape(2 * row_count, 2 * model_width)
    mixed_low, log_totals = attention_pallas(scaled_queries, pair_rows)
    attended = jnp.dot(mixed_low, full_out, preferred_element_type=jnp.float32) + column_set[:, 4]
    residual = frames_rows + attended
    normed_second, plain_second, inv_second = norm_parts(
        residual, column_set[:, 5], column_set[:, 6]
    )
    hidden_second = normed_second.astype(jnp.bfloat16)
    preact = jnp.dot(hidden_second, full_expand, preferred_element_type=jnp.float32) + full_bias
    activated = gelu_exact(preact).astype(jnp.bfloat16)
    result = (
        residual
        + sum(
            jnp.dot(ff_cols(activated, group), ff_cols(shrink_rows, group), preferred_element_type=jnp.float32)
            for group in range(ff_group)
        )
        + column_set[:, 7]
    )
    output = result.astype(jnp.bfloat16).reshape(inputs.shape)

    grad_result = cotangent.reshape(row_count, model_width)
    grad_shrink_term = jnp.concatenate(
        [
            jnp.dot(ff_cols(activated, group).T, grad_result, preferred_element_type=jnp.float32)
            for group in range(ff_group)
        ],
        axis=1,
    ).astype(jnp.bfloat16)
    grad_down_bias = jnp.sum(grad_result.astype(jnp.float32), axis=0)
    grad_activated = jnp.concatenate(
        [
            jnp.dot(grad_result, ff_cols(shrink_rows, group).T, preferred_element_type=jnp.float32)
            for group in range(ff_group)
        ],
        axis=1,
    )
    grad_preact = (grad_activated * gelu_slope(preact)).astype(jnp.bfloat16)
    grad_expand_term = jnp.dot(
        hidden_second.T, grad_preact, preferred_element_type=jnp.float32
    ).astype(jnp.bfloat16)
    grad_bias_term = jnp.sum(grad_preact.astype(jnp.float32), axis=0)
    grad_hidden_second = jnp.dot(grad_preact, full_expand.T, preferred_element_type=jnp.float32)
    norm_term_second, gain_second, shift_second = norm_backward(
        grad_hidden_second, plain_second, inv_second, column_set[:, 5]
    )
    grad_residual = grad_result.astype(jnp.float32) + norm_term_second
    grad_attended = grad_residual.astype(jnp.bfloat16)
    grad_out_term = jnp.dot(
        mixed_low.T, grad_attended, preferred_element_type=jnp.float32
    ).astype(jnp.bfloat16)
    grad_out_bias = jnp.sum(grad_attended.astype(jnp.float32), axis=0)
    late_terms = jnp.concatenate(
        [grad_shrink_term.reshape(model_width, -1), grad_expand_term, grad_out_term], axis=1
    )
    grad_mixed = jnp.dot(grad_attended, full_out.T, preferred_element_type=jnp.float32).astype(
        jnp.bfloat16
    )
    piece_pairs = 1
    piece_count = model_width // 128 // piece_pairs
    stage_count = 1 + len(late_orders[0])
    hooked = list(range(1, min(piece_count, stage_count)))

    def run_piece(index, mixed_grads):
        return attention_pallas(
            scaled_queries, pair_rows, mixed_grads, log_totals, index * piece_pairs, piece_pairs
        )

    def piece_hook(index):
        return lambda tied: (run_piece(index, tied[index - 1][1]), tied[index - 1][1])

    hooks = {0: lambda tied: ((), grad_mixed)}
    hooks.update({index: piece_hook(index) for index in hooked})
    pieces = [run_piece(0, grad_mixed)]
    owned_late, tied = tree_reduce_scatter(
        late_terms, (3456, 3456), late_orders, (bit_count, core_bit), hooks
    )
    pieces += [tied[index][0] for index in hooked]
    last_mixed = tied[hooked[-1]][1] if hooked else grad_mixed
    pieces += [run_piece(index, last_mixed) for index in range(len(hooked) + 1, piece_count)]
    finished = []
    for grad_query, grad_keys, grad_values in pieces:
        terms = jnp.concatenate([grad_keys, grad_values], axis=1)
        returned = lax.ppermute(terms[row_count:].astype(jnp.bfloat16), "frame", swap)
        finished.append((grad_query, terms[:row_count] + returned.astype(jnp.float32)))
    piece_width = finished[0][0].shape[1]
    grad_projected = jnp.concatenate(
        [
            (jnp.concatenate([query for query, _ in finished], axis=1) * score_scale).astype(
                jnp.bfloat16
            ),
            jnp.concatenate(
                [pair[:, :piece_width] for _, pair in finished]
                + [pair[:, piece_width:] for _, pair in finished],
                axis=1,
            ).astype(jnp.bfloat16),
        ],
        axis=1,
    )
    grad_in_term = jnp.dot(
        hidden_first.T, grad_projected, preferred_element_type=jnp.float32
    ).astype(jnp.bfloat16)
    projected_sums = jnp.sum(grad_projected.astype(jnp.float32), axis=0)
    grad_query_bias = projected_sums[:model_width]
    grad_value_bias = projected_sums[2 * model_width :]
    grad_hidden_first = jnp.dot(grad_projected, full_in.T, preferred_element_type=jnp.float32)
    norm_term_first, gain_first, shift_first = norm_backward(
        grad_hidden_first, plain_first, inv_first, column_set[:, 0]
    )
    grad_inputs = (grad_residual + norm_term_first).astype(jnp.bfloat16).reshape(inputs.shape)
    grad_columns = jnp.stack(
        [
            gain_first,
            shift_first,
            grad_query_bias,
            grad_value_bias,
            grad_out_bias,
            gain_second,
            shift_second,
            grad_down_bias,
        ],
        axis=1,
    )
    small_grads = jnp.concatenate(
        [
            grad_columns,
            grad_bias_term.reshape(ff_group, -1).T,
            jnp.zeros((model_width, 128 - 12), jnp.float32),
        ],
        axis=1,
    ).astype(jnp.bfloat16)
    owned_first = tree_reduce_scatter(
        jnp.concatenate([grad_in_term, small_grads], axis=1),
        (896, 768, 768),
        rotated_orders,
        (bit_count, core_bit),
    )[0]
    owned_in = owned_first[:, :wide_in]
    owned_vectors = owned_first[:, wide_in : wide_in + vectors.shape[1]]
    owned_bias = owned_first[:, wide_in + vectors.shape[1] : wide_in + 12].reshape(-1)
    owned_shrink = owned_late[:, :ff_width].reshape(shrink_weight.shape)
    owned_expand = jnp.swapaxes(
        owned_late[:, ff_width : 2 * ff_width].reshape(shard_rows, ff_group, ff_block), 1, 2
    ).reshape(shard_rows, ff_width)
    owned_out = owned_late[:, 2 * ff_width :]
    new_in, mom_in = adam_step(project_in, moments_in, owned_in)
    new_out, mom_out = adam_step(project_out, moments_out, owned_out)
    new_expand, mom_expand = adam_step(expand_weight, moments_expand, owned_expand)
    new_shrink, mom_shrink = adam_step(shrink_weight, moments_shrink, owned_shrink)
    new_bias, mom_bias = adam_step(expand_bias, moments_bias, owned_bias)
    new_vectors, mom_vectors = adam_step(vectors, moments_vectors, owned_vectors)
    return (
        output,
        grad_inputs,
        owned_in,
        owned_out,
        owned_expand,
        owned_shrink,
        owned_bias,
        owned_vectors,
        new_in,
        new_out,
        new_expand,
        new_shrink,
        new_bias,
        new_vectors,
        mom_in,
        mom_out,
        mom_expand,
        mom_shrink,
        mom_bias,
        mom_vectors,
    )


def solution(mesh):
    in_specs = (
        P("clip", "frame", None),
        P("clip", "frame", None),
        P(("clip", "frame"), None),
        P(("clip", "frame"), None),
        P(("clip", "frame"), None),
        P(("clip", "frame"), None),
        P(("clip", "frame")),
        P(("clip", "frame"), None),
        P(None, ("clip", "frame"), None),
        P(None, ("clip", "frame"), None),
        P(None, ("clip", "frame"), None),
        P(None, ("clip", "frame"), None),
        P(None, ("clip", "frame")),
        P(None, ("clip", "frame"), None),
    )
    out_specs = (
        P("clip", "frame", None),
        P("clip", "frame", None),
        P(("clip", "frame"), None),
        P(("clip", "frame"), None),
        P(("clip", "frame"), None),
        P(("clip", "frame"), None),
        P(("clip", "frame")),
        P(("clip", "frame"), None),
        P(("clip", "frame"), None),
        P(("clip", "frame"), None),
        P(("clip", "frame"), None),
        P(("clip", "frame"), None),
        P(("clip", "frame")),
        P(("clip", "frame"), None),
        P(None, ("clip", "frame"), None),
        P(None, ("clip", "frame"), None),
        P(None, ("clip", "frame"), None),
        P(None, ("clip", "frame"), None),
        P(None, ("clip", "frame")),
        P(None, ("clip", "frame"), None),
    )
    return jax.shard_map(
        functools.partial(body, link_plan(mesh)),
        mesh=mesh,
        in_specs=in_specs,
        out_specs=out_specs,
        check_vma=False,
    )
```

```python
import functools
import math

import jax
import jax.numpy as jnp
from jax import lax
from jax.experimental import pallas as pl
from jax.experimental.pallas import tpu as pltpu
from jax.sharding import PartitionSpec as P

HEADS = 12
ADAM_STEP = 4


epsilon_norm = 1e-05
beta_first = 0.9
beta_second = 0.99
learn_rate = 0.03
decay_rate = 0.01
epsilon_adam = 1e-08
root_half = 0.7071067811865476
inv_root_two_pi = 0.3989422804014327


def norm_parts(inputs, norm_gain, norm_shift):
    average = jnp.mean(inputs, axis=-1, keepdims=True)
    centered = inputs - average
    spread = jnp.mean(centered * centered, axis=-1, keepdims=True)
    inv_std = lax.rsqrt(spread + epsilon_norm)
    normed = centered * inv_std
    return (normed * norm_gain + norm_shift, normed, inv_std)


def norm_backward(grad_normed, normed, inv_std, norm_gain):
    grad_gain = jnp.sum(grad_normed * normed, axis=0)
    grad_shift = jnp.sum(grad_normed, axis=0)
    scaled = grad_normed * norm_gain
    grad_input = inv_std * (
        scaled
        - jnp.mean(scaled, axis=-1, keepdims=True)
        - normed * jnp.mean(scaled * normed, axis=-1, keepdims=True)
    )
    return (grad_input, grad_gain, grad_shift)


def gelu_exact(inputs):
    return 0.5 * inputs * (1.0 + jax.scipy.special.erf(inputs * root_half))


def gelu_slope(inputs):
    return (
        0.5 * (1.0 + jax.scipy.special.erf(inputs * root_half))
        + inputs * jnp.exp(-0.5 * inputs * inputs) * inv_root_two_pi
    )


QUERY_CHUNK = 256
MASKED = -1e30


def attention_forward_kernel(q_ref, k_ref, v_ref, kbias_ref, o_ref, l_ref):
    head_size = q_ref.shape[1] // 2
    rows = q_ref.shape[0]
    kbias = kbias_ref[...]
    lane = lax.broadcasted_iota(jnp.int32, (QUERY_CHUNK, 2 * head_size), 1)
    for chunk in range(rows // QUERY_CHUNK):
        span = pl.ds(chunk * QUERY_CHUNK, QUERY_CHUNK)
        mixed_parts = []
        totals = []
        for half in range(2):
            cols = pl.ds(half * head_size, head_size)
            query = q_ref[span, cols]
            key = k_ref[:, cols]
            value = v_ref[:, cols]
            scores = (
                lax.dot_general(
                    query, key, (((1,), (1,)), ((), ())), preferred_element_type=jnp.float32
                )
                + kbias
            )
            highest = jnp.max(scores, axis=1, keepdims=True)
            exponent = jnp.exp(scores - highest)
            denominator = jnp.sum(exponent, axis=1, keepdims=True)
            weights = (exponent * (1.0 / denominator)).astype(jnp.bfloat16)
            mixed_parts.append(jnp.dot(weights, value, preferred_element_type=jnp.float32))
            totals.append(highest + jnp.log(denominator))
        o_ref[span, :] = jnp.concatenate(mixed_parts, axis=1).astype(o_ref.dtype)
        l_ref[span, :] = jnp.where(lane < head_size, totals[0], totals[1])


def attention_backward_kernel(
    q_ref, k_ref, v_ref, do_ref, l_ref, kbias_ref, dq_ref, dk_ref, dv_ref
):
    head_size = q_ref.shape[1] // 2
    rows = q_ref.shape[0]
    kbias = kbias_ref[...]
    for half in range(2):
        cols = pl.ds(half * head_size, head_size)
        key = k_ref[:, cols]
        value = v_ref[:, cols]
        grad_key = None
        grad_value = None
        for chunk in range(rows // QUERY_CHUNK):
            span = pl.ds(chunk * QUERY_CHUNK, QUERY_CHUNK)
            query = q_ref[span, cols]
            grad_out = do_ref[span, cols]
            total = l_ref[span, pl.ds(half * head_size, 1)]
            scores = (
                lax.dot_general(
                    query, key, (((1,), (1,)), ((), ())), preferred_element_type=jnp.float32
                )
                + kbias
            )
            weights = jnp.exp(scores - total)
            grad_weights = lax.dot_general(
                grad_out, value, (((1,), (1,)), ((), ())), preferred_element_type=jnp.float32
            )
            delta = jnp.sum(weights * grad_weights, axis=1, keepdims=True)
            grad_scores = (weights * (grad_weights - delta)).astype(jnp.bfloat16)
            dq_ref[span, cols] = jnp.dot(
                grad_scores, key, preferred_element_type=jnp.float32
            ).astype(dq_ref.dtype)
            key_part = lax.dot_general(
                grad_scores, query, (((0,), (0,)), ((), ())), preferred_element_type=jnp.float32
            )
            value_part = lax.dot_general(
                weights.astype(jnp.bfloat16),
                grad_out,
                (((0,), (0,)), ((), ())),
                preferred_element_type=jnp.float32,
            )
            grad_key = key_part if grad_key is None else grad_key + key_part
            grad_value = value_part if grad_value is None else grad_value + value_part
        dk_ref[:, cols] = grad_key
        dv_ref[:, cols] = grad_value


def pad_rows(values, rows):
    return jnp.pad(values, ((0, rows - values.shape[0]), (0, 0)))


def attention_pallas(queries, pairs, grad_out=None, totals=None, first_pair=0, pair_span=None):
    query_rows, model_width = queries.shape
    key_rows = pairs.shape[0]
    padded_q = -(-query_rows // QUERY_CHUNK) * QUERY_CHUNK
    padded_k = -(-key_rows // 128) * 128
    pair_count = model_width // 128
    q_pad = pad_rows(queries, padded_q)
    kv_pad = pad_rows(pairs, padded_k)
    kbias = jnp.where(jnp.arange(padded_k) < key_rows, 0.0, MASKED).astype(jnp.float32)[None, :]
    q_spec = pl.BlockSpec((padded_q, 128), lambda j: (0, j))
    k_spec = pl.BlockSpec((padded_k, 128), lambda j: (0, j))
    v_spec = pl.BlockSpec((padded_k, 128), lambda j: (0, j + pair_count))
    b_spec = pl.BlockSpec((1, padded_k), lambda j: (0, 0))
    params = pltpu.CompilerParams(vmem_limit_bytes=48 * 1024 * 1024)
    if grad_out is None:
        mixed, log_totals = pl.pallas_call(
            attention_forward_kernel,
            grid=(pair_count,),
            in_specs=[q_spec, k_spec, v_spec, b_spec],
            out_specs=[q_spec, q_spec],
            out_shape=[
                jax.ShapeDtypeStruct((padded_q, model_width), jnp.bfloat16),
                jax.ShapeDtypeStruct((padded_q, model_width), jnp.float32),
            ],
            compiler_params=params,
        )(q_pad, kv_pad, kv_pad, kbias)
        return mixed[:query_rows], log_totals
    do_pad = pad_rows(grad_out, padded_q)
    span = pair_count if pair_span is None else pair_span
    qi_spec = pl.BlockSpec((padded_q, 128), lambda j: (0, j + first_pair))
    ki_spec = pl.BlockSpec((padded_k, 128), lambda j: (0, j + first_pair))
    vi_spec = pl.BlockSpec((padded_k, 128), lambda j: (0, j + first_pair + pair_count))
    qo_spec = pl.BlockSpec((padded_q, 128), lambda j: (0, j))
    ko_spec = pl.BlockSpec((padded_k, 128), lambda j: (0, j))
    dq, dk, dv = pl.pallas_call(
        attention_backward_kernel,
        grid=(span,),
        in_specs=[qi_spec, ki_spec, vi_spec, qi_spec, qi_spec, b_spec],
        out_specs=[qo_spec, ko_spec, ko_spec],
        out_shape=[
            jax.ShapeDtypeStruct((padded_q, 128 * span), jnp.float32),
            jax.ShapeDtypeStruct((padded_k, 128 * span), jnp.float32),
            jax.ShapeDtypeStruct((padded_k, 128 * span), jnp.float32),
        ],
        compiler_params=params,
    )(q_pad, kv_pad, kv_pad, do_pad, totals, kbias)
    return dq[:query_rows], dk[:key_rows], dv[:key_rows]


def attend_forward(queries, keys_values, head_count):
    model_width = queries.shape[2]
    head_size = model_width // head_count
    score_scale = 1.0 / math.sqrt(head_size)

    def one_head(head_index):
        offset = head_index * head_size
        query_block = lax.dynamic_slice_in_dim(queries, offset, head_size, 2)
        key_block = lax.dynamic_slice_in_dim(keys_values, offset, head_size, 2)
        value_block = lax.dynamic_slice_in_dim(keys_values, model_width + offset, head_size, 2)
        scores = (
            jnp.einsum("cqd,ckd->cqk", query_block, key_block, preferred_element_type=jnp.float32)
            * score_scale
        )
        highest = jnp.max(scores, axis=-1, keepdims=True)
        exponent = jnp.exp(scores - highest)
        denominator = jnp.sum(exponent, axis=-1, keepdims=True)
        weights_soft = (exponent / denominator).astype(jnp.bfloat16)
        mixed = jnp.einsum(
            "cqk,ckd->cqd", weights_soft, value_block, preferred_element_type=jnp.float32
        )
        return (mixed, (highest + jnp.log(denominator))[..., 0])

    mixed, log_totals = lax.map(one_head, jnp.arange(head_count))
    clip_count, frame_count = (queries.shape[0], queries.shape[1])
    mixed = jnp.transpose(mixed, (1, 2, 0, 3)).reshape(clip_count, frame_count, model_width)
    return (mixed, log_totals)


def attend_backward(queries, keys_values, grad_mixed, log_totals, head_count):
    model_width = queries.shape[2]
    head_size = model_width // head_count
    score_scale = 1.0 / math.sqrt(head_size)

    def one_head_back(head_index):
        offset = head_index * head_size
        query_block = lax.dynamic_slice_in_dim(queries, offset, head_size, 2)
        key_block = lax.dynamic_slice_in_dim(keys_values, offset, head_size, 2)
        value_block = lax.dynamic_slice_in_dim(keys_values, model_width + offset, head_size, 2)
        grad_block = lax.dynamic_slice_in_dim(grad_mixed, offset, head_size, 2)
        totals = lax.dynamic_index_in_dim(log_totals, head_index, 0, keepdims=False)
        scores = (
            jnp.einsum("cqd,ckd->cqk", query_block, key_block, preferred_element_type=jnp.float32)
            * score_scale
        )
        weights_soft = jnp.exp(scores - totals[..., None])
        grad_weights = jnp.einsum(
            "cqd,ckd->cqk", grad_block, value_block, preferred_element_type=jnp.float32
        )
        delta = jnp.sum(weights_soft * grad_weights, axis=-1, keepdims=True)
        grad_scores = (weights_soft * (grad_weights - delta)).astype(jnp.bfloat16)
        grad_query = (
            jnp.einsum("cqk,ckd->cqd", grad_scores, key_block, preferred_element_type=jnp.float32)
            * score_scale
        )
        grad_key = (
            jnp.einsum("cqk,cqd->ckd", grad_scores, query_block, preferred_element_type=jnp.float32)
            * score_scale
        )
        grad_value = jnp.einsum(
            "cqk,cqd->ckd",
            weights_soft.astype(jnp.bfloat16),
            grad_block,
            preferred_element_type=jnp.float32,
        )
        return (grad_query, delta[..., 0], grad_key, grad_value)

    pieces = lax.map(one_head_back, jnp.arange(head_count))
    clip_count, frame_count = (queries.shape[0], queries.shape[1])
    clip_frames = keys_values.shape[1]
    grad_query = jnp.transpose(pieces[0], (1, 2, 0, 3)).reshape(
        clip_count, frame_count, model_width
    )
    grad_key = jnp.transpose(pieces[2], (1, 2, 0, 3)).reshape(clip_count, clip_frames, model_width)
    grad_value = jnp.transpose(pieces[3], (1, 2, 0, 3)).reshape(
        clip_count, clip_frames, model_width
    )
    return (grad_query, pieces[1], jnp.concatenate([grad_key, grad_value], axis=2))


def link_plan(mesh):
    devices = list(mesh.devices.reshape(-1))
    bit_count = len(devices).bit_length() - 1
    core_bit = 1
    for bit in range(bit_count):
        first, other = devices[0], devices[1 << bit]
        if getattr(first, "coords", None) is not None and tuple(first.coords) == tuple(other.coords):
            core_bit = bit
    others = [bit for bit in range(bit_count) if bit != core_bit]
    near, far = others[:-1], others[-1:]
    rotated = tuple(tuple(near[k:] + near[:k] + far) for k in range(3))
    inner = [bit for bit in near if bit != 0]
    late = tuple(tuple(inner[k:] + inner[:k] + [0] + far) for k in range(2))
    return bit_count, core_bit, rotated, late


def tree_reduce_scatter(terms, part_columns, orders, plan_bits, hooks=None):
    hooks = dict(hooks or {})
    tied = {}
    bit_count, core_bit = plan_bits
    device = lax.axis_index("clip") * lax.axis_size("frame") + lax.axis_index("frame")
    blocks = 1 << bit_count
    block_rows = terms.shape[0] // blocks
    data = terms.reshape((2,) * bit_count + (block_rows, terms.shape[1]))
    parts = [(data, list(range(bit_count - 1, -1, -1)))]
    plan = [(core_bit,)] + [tuple(order[stage] for order in orders) for stage in range(len(orders[0]))]
    for stage, stage_bits in enumerate(plan):
        if stage == 1:
            whole, bits = parts[0]
            parts = []
            offset = 0
            for width in part_columns:
                parts.append((whole[..., offset : offset + width], bits))
                offset += width
        keeps, sends = [], []
        for (part, part_bits), bit in zip(parts, stage_bits):
            axis = part_bits.index(bit)
            mine = (device >> bit) & 1
            keeps.append(lax.dynamic_index_in_dim(part, mine, axis=axis, keepdims=False))
            sends.append(
                lax.dynamic_index_in_dim(part, 1 - mine, axis=axis, keepdims=False).astype(jnp.bfloat16)
            )
        new_parts = []
        for keep, send, (part, part_bits), bit in zip(keeps, sends, parts, stage_bits):
            pairs = [(index, index ^ (1 << bit)) for index in range(blocks)]
            got = lax.ppermute(send, ("clip", "frame"), pairs)
            new_parts.append((keep + got.astype(jnp.float32), [b for b in part_bits if b != bit]))
        if stage in hooks:
            values, tied[stage] = lax.optimization_barrier(
                ([part for part, _ in new_parts], hooks[stage](tied))
            )
            new_parts = [(value, part_bits) for value, (_, part_bits) in zip(values, new_parts)]
        parts = new_parts
    return jnp.concatenate([part for part, _ in parts], axis=-1).astype(jnp.float32), tied


def tree_all_gather(local, part_columns, orders, plan_bits):
    bit_count, core_bit = plan_bits
    device = lax.axis_index("clip") * lax.axis_size("frame") + lax.axis_index("frame")
    canonical = list(range(bit_count - 1, -1, -1))

    def double(data, bits, bit):
        mine = (device >> bit) & 1
        pairs = [(index, index ^ (1 << bit)) for index in range(1 << bit_count)]
        got = lax.ppermute(data, ("clip", "frame"), pairs)
        new_bits = sorted(bits + [bit], reverse=True)
        axis = new_bits.index(bit)
        low_first = jnp.stack([data, got], axis=axis)
        high_first = jnp.stack([got, data], axis=axis)
        return jnp.where(mine == 0, low_first, high_first), new_bits

    parts = []
    offset = 0
    for width in part_columns:
        parts.append((local[:, offset : offset + width], []))
        offset += width
    reversed_orders = [list(reversed(order)) for order in orders]
    for stage in range(len(reversed_orders[0])):
        parts = [double(part, bits, order[stage]) for (part, bits), order in zip(parts, reversed_orders)]
    whole = jnp.concatenate([part for part, _ in parts], axis=-1)
    whole, bits = double(whole, parts[0][1], core_bit)
    assert bits == canonical
    return whole.reshape((1 << bit_count) * local.shape[0], local.shape[1])


def adam_step(weight, moments, gradient):
    first = beta_first * moments[0] + (1.0 - beta_first) * gradient
    second = beta_second * moments[1] + (1.0 - beta_second) * gradient * gradient
    first_hat = first / (1.0 - beta_first**ADAM_STEP)
    second_hat = second / (1.0 - beta_second**ADAM_STEP)
    change = -learn_rate * (first_hat / (jnp.sqrt(second_hat) + epsilon_adam) + decay_rate * weight)
    return (change, jnp.stack([first, second]))


def body(
    plan,
    inputs,
    cotangent,
    project_in,
    project_out,
    expand_weight,
    shrink_weight,
    expand_bias,
    vectors,
    moments_in,
    moments_out,
    moments_expand,
    moments_shrink,
    moments_bias,
    moments_vectors,
):
    clip_count, frame_count, model_width = inputs.shape
    row_count = clip_count * frame_count
    head_count = HEADS
    shard_rows = project_in.shape[0]
    wide_in = project_in.shape[1]
    ff_width = expand_weight.shape[1]
    swap = [(0, 1), (1, 0)]
    everyone = ("clip", "frame")

    small = jnp.concatenate(
        [
            vectors,
            expand_bias.reshape(shard_rows, -1),
            jnp.zeros((shard_rows, 128 - vectors.shape[1] - expand_bias.shape[0] // shard_rows), jnp.float32),
        ],
        axis=1,
    )
    first_pack = jnp.concatenate([project_in, small], axis=1).astype(jnp.bfloat16)
    second_pack = jnp.concatenate(
        [project_out, expand_weight, shrink_weight.reshape(shard_rows, -1)], axis=1
    ).astype(jnp.bfloat16)
    bit_count, core_bit, rotated_orders, late_orders = plan
    first_full = tree_all_gather(first_pack, (896, 768, 768), rotated_orders, (bit_count, core_bit))
    second_full = lax.all_gather(second_pack, everyone, axis=0, tiled=True)
    full_in = first_full[:, :wide_in]
    small_full = first_full[:, wide_in:].astype(jnp.float32)
    column_set = small_full[:, : vectors.shape[1]]
    full_bias = small_full[:, vectors.shape[1] : vectors.shape[1] + ff_width // model_width].reshape(-1)
    full_out = second_full[:, :model_width]
    full_expand = second_full[:, model_width : model_width + ff_width]
    full_shrink = second_full[:, model_width + ff_width :].reshape(ff_width, model_width)

    frames_rows = inputs.reshape(row_count, model_width).astype(jnp.float32)
    normed_first, plain_first, inv_first = norm_parts(
        frames_rows, column_set[:, 0], column_set[:, 1]
    )
    hidden_first = normed_first.astype(jnp.bfloat16)
    partner_rows = lax.ppermute(inputs, "frame", swap).reshape(row_count, model_width)
    hidden_partner = norm_parts(
        partner_rows.astype(jnp.float32), column_set[:, 0], column_set[:, 1]
    )[0].astype(jnp.bfloat16)
    bias_in = jnp.concatenate(
        [column_set[:, 2], jnp.zeros((model_width,), jnp.float32), column_set[:, 3]]
    )
    projected = (
        jnp.dot(hidden_first, full_in, preferred_element_type=jnp.float32) + bias_in
    ).astype(jnp.bfloat16)
    partner_pairs = (
        jnp.dot(hidden_partner, full_in[:, model_width:], preferred_element_type=jnp.float32)
        + bias_in[model_width:]
    ).astype(jnp.bfloat16)
    queries = projected[:, :model_width].reshape(clip_count, frame_count, model_width)
    clip_pairs = jnp.concatenate([projected[:, model_width:], partner_pairs], axis=0).reshape(
        clip_count, 2 * frame_count, 2 * model_width
    )
    score_scale = 1.0 / math.sqrt(model_width // head_count)
    scaled_queries = (projected[:, :model_width] * score_scale).astype(jnp.bfloat16)
    pair_rows = clip_pairs.reshape(2 * row_count, 2 * model_width)
    mixed_low, log_totals = attention_pallas(scaled_queries, pair_rows)
    attended = jnp.dot(mixed_low, full_out, preferred_element_type=jnp.float32) + column_set[:, 4]
    residual = frames_rows + attended
    normed_second, plain_second, inv_second = norm_parts(
        residual, column_set[:, 5], column_set[:, 6]
    )
    hidden_second = normed_second.astype(jnp.bfloat16)
    preact = jnp.dot(hidden_second, full_expand, preferred_element_type=jnp.float32) + full_bias
    activated = gelu_exact(preact).astype(jnp.bfloat16)
    result = (
        residual
        + jnp.dot(activated, full_shrink, preferred_element_type=jnp.float32)
        + column_set[:, 7]
    )
    output = result.astype(jnp.bfloat16).reshape(inputs.shape)

    grad_result = cotangent.reshape(row_count, model_width)
    grad_shrink_term = jnp.dot(
        activated.T, grad_result, preferred_element_type=jnp.float32
    ).astype(jnp.bfloat16)
    grad_down_bias = jnp.sum(grad_result.astype(jnp.float32), axis=0)
    grad_activated = jnp.dot(grad_result, full_shrink.T, preferred_element_type=jnp.float32)
    grad_preact = (grad_activated * gelu_slope(preact)).astype(jnp.bfloat16)
    grad_expand_term = jnp.dot(
        hidden_second.T, grad_preact, preferred_element_type=jnp.float32
    ).astype(jnp.bfloat16)
    grad_bias_term = jnp.sum(grad_preact.astype(jnp.float32), axis=0)
    grad_hidden_second = jnp.dot(grad_preact, full_expand.T, preferred_element_type=jnp.float32)
    norm_term_second, gain_second, shift_second = norm_backward(
        grad_hidden_second, plain_second, inv_second, column_set[:, 5]
    )
    grad_residual = grad_result.astype(jnp.float32) + norm_term_second
    grad_attended = grad_residual.astype(jnp.bfloat16)
    grad_out_term = jnp.dot(
        mixed_low.T, grad_attended, preferred_element_type=jnp.float32
    ).astype(jnp.bfloat16)
    grad_out_bias = jnp.sum(grad_attended.astype(jnp.float32), axis=0)
    late_terms = jnp.concatenate(
        [grad_shrink_term.reshape(model_width, -1), grad_expand_term, grad_out_term], axis=1
    )
    grad_mixed = jnp.dot(grad_attended, full_out.T, preferred_element_type=jnp.float32).astype(
        jnp.bfloat16
    )
    piece_pairs = 1
    piece_count = model_width // 128 // piece_pairs
    stage_count = 1 + len(late_orders[0])
    hooked = list(range(1, min(piece_count, stage_count)))

    def run_piece(index, mixed_grads):
        return attention_pallas(
            scaled_queries, pair_rows, mixed_grads, log_totals, index * piece_pairs, piece_pairs
        )

    def piece_hook(index):
        return lambda tied: (run_piece(index, tied[index - 1][1]), tied[index - 1][1])

    hooks = {0: lambda tied: ((), grad_mixed)}
    hooks.update({index: piece_hook(index) for index in hooked})
    pieces = [run_piece(0, grad_mixed)]
    owned_late, tied = tree_reduce_scatter(
        late_terms, (3456, 3456), late_orders, (bit_count, core_bit), hooks
    )
    pieces += [tied[index][0] for index in hooked]
    last_mixed = tied[hooked[-1]][1] if hooked else grad_mixed
    pieces += [run_piece(index, last_mixed) for index in range(len(hooked) + 1, piece_count)]
    finished = []
    for grad_query, grad_keys, grad_values in pieces:
        terms = jnp.concatenate([grad_keys, grad_values], axis=1)
        returned = lax.ppermute(terms[row_count:].astype(jnp.bfloat16), "frame", swap)
        finished.append((grad_query, terms[:row_count] + returned.astype(jnp.float32)))
    piece_width = finished[0][0].shape[1]
    grad_projected = jnp.concatenate(
        [
            (jnp.concatenate([query for query, _ in finished], axis=1) * score_scale).astype(
                jnp.bfloat16
            ),
            jnp.concatenate(
                [pair[:, :piece_width] for _, pair in finished]
                + [pair[:, piece_width:] for _, pair in finished],
                axis=1,
            ).astype(jnp.bfloat16),
        ],
        axis=1,
    )
    grad_in_term = jnp.dot(
        hidden_first.T, grad_projected, preferred_element_type=jnp.float32
    ).astype(jnp.bfloat16)
    projected_sums = jnp.sum(grad_projected.astype(jnp.float32), axis=0)
    grad_query_bias = projected_sums[:model_width]
    grad_value_bias = projected_sums[2 * model_width :]
    grad_hidden_first = jnp.dot(grad_projected, full_in.T, preferred_element_type=jnp.float32)
    norm_term_first, gain_first, shift_first = norm_backward(
        grad_hidden_first, plain_first, inv_first, column_set[:, 0]
    )
    grad_inputs = (grad_residual + norm_term_first).astype(jnp.bfloat16).reshape(inputs.shape)
    grad_columns = jnp.stack(
        [
            gain_first,
            shift_first,
            grad_query_bias,
            grad_value_bias,
            grad_out_bias,
            gain_second,
            shift_second,
            grad_down_bias,
        ],
        axis=1,
    )
    small_grads = jnp.concatenate(
        [
            grad_columns,
            grad_bias_term.reshape(model_width, -1),
            jnp.zeros((model_width, 128 - 12), jnp.float32),
        ],
        axis=1,
    ).astype(jnp.bfloat16)
    owned_first = tree_reduce_scatter(
        jnp.concatenate([grad_in_term, small_grads], axis=1),
        (896, 768, 768),
        rotated_orders,
        (bit_count, core_bit),
    )[0]
    owned_in = owned_first[:, :wide_in]
    owned_vectors = owned_first[:, wide_in : wide_in + vectors.shape[1]]
    owned_bias = owned_first[:, wide_in + vectors.shape[1] : wide_in + 12].reshape(-1)
    owned_shrink = owned_late[:, :ff_width].reshape(shrink_weight.shape)
    owned_expand = owned_late[:, ff_width : 2 * ff_width]
    owned_out = owned_late[:, 2 * ff_width :]
    new_in, mom_in = adam_step(project_in, moments_in, owned_in)
    new_out, mom_out = adam_step(project_out, moments_out, owned_out)
    new_expand, mom_expand = adam_step(expand_weight, moments_expand, owned_expand)
    new_shrink, mom_shrink = adam_step(shrink_weight, moments_shrink, owned_shrink)
    new_bias, mom_bias = adam_step(expand_bias, moments_bias, owned_bias)
    new_vectors, mom_vectors = adam_step(vectors, moments_vectors, owned_vectors)
    return (
        output,
        grad_inputs,
        owned_in,
        owned_out,
        owned_expand,
        owned_shrink,
        owned_bias,
        owned_vectors,
        new_in,
        new_out,
        new_expand,
        new_shrink,
        new_bias,
        new_vectors,
        mom_in,
        mom_out,
        mom_expand,
        mom_shrink,
        mom_bias,
        mom_vectors,
    )


def solution(mesh):
    in_specs = (
        P("clip", "frame", None),
        P("clip", "frame", None),
        P(("clip", "frame"), None),
        P(("clip", "frame"), None),
        P(("clip", "frame"), None),
        P(("clip", "frame"), None),
        P(("clip", "frame")),
        P(("clip", "frame"), None),
        P(None, ("clip", "frame"), None),
        P(None, ("clip", "frame"), None),
        P(None, ("clip", "frame"), None),
        P(None, ("clip", "frame"), None),
        P(None, ("clip", "frame")),
        P(None, ("clip", "frame"), None),
    )
    out_specs = (
        P("clip", "frame", None),
        P("clip", "frame", None),
        P(("clip", "frame"), None),
        P(("clip", "frame"), None),
        P(("clip", "frame"), None),
        P(("clip", "frame"), None),
        P(("clip", "frame")),
        P(("clip", "frame"), None),
        P(("clip", "frame"), None),
        P(("clip", "frame"), None),
        P(("clip", "frame"), None),
        P(("clip", "frame"), None),
        P(("clip", "frame")),
        P(("clip", "frame"), None),
        P(None, ("clip", "frame"), None),
        P(None, ("clip", "frame"), None),
        P(None, ("clip", "frame"), None),
        P(None, ("clip", "frame"), None),
        P(None, ("clip", "frame")),
        P(None, ("clip", "frame"), None),
    )
    return jax.shard_map(
        functools.partial(body, link_plan(mesh)),
        mesh=mesh,
        in_specs=in_specs,
        out_specs=out_specs,
        check_vma=False,
    )
```

```python
import functools
import math

import jax
import jax.numpy as jnp
from jax import lax
from jax.experimental import pallas as pl
from jax.experimental.pallas import tpu as pltpu
from jax.sharding import PartitionSpec as P

HEADS = 12
ADAM_STEP = 4


epsilon_norm = 1e-05
beta_first = 0.9
beta_second = 0.99
learn_rate = 0.03
decay_rate = 0.01
epsilon_adam = 1e-08
root_half = 0.7071067811865476
inv_root_two_pi = 0.3989422804014327


def norm_parts(inputs, norm_gain, norm_shift):
    average = jnp.mean(inputs, axis=-1, keepdims=True)
    centered = inputs - average
    spread = jnp.mean(centered * centered, axis=-1, keepdims=True)
    inv_std = lax.rsqrt(spread + epsilon_norm)
    normed = centered * inv_std
    return (normed * norm_gain + norm_shift, normed, inv_std)


def norm_backward(grad_normed, normed, inv_std, norm_gain):
    grad_gain = jnp.sum(grad_normed * normed, axis=0)
    grad_shift = jnp.sum(grad_normed, axis=0)
    scaled = grad_normed * norm_gain
    grad_input = inv_std * (
        scaled
        - jnp.mean(scaled, axis=-1, keepdims=True)
        - normed * jnp.mean(scaled * normed, axis=-1, keepdims=True)
    )
    return (grad_input, grad_gain, grad_shift)


def gelu_exact(inputs):
    return 0.5 * inputs * (1.0 + jax.scipy.special.erf(inputs * root_half))


def gelu_slope(inputs):
    return (
        0.5 * (1.0 + jax.scipy.special.erf(inputs * root_half))
        + inputs * jnp.exp(-0.5 * inputs * inputs) * inv_root_two_pi
    )


QUERY_CHUNK = 256
MASKED = -1e30


def attention_forward_kernel(q_ref, k_ref, v_ref, kbias_ref, o_ref, l_ref):
    head_size = q_ref.shape[1] // 2
    rows = q_ref.shape[0]
    kbias = kbias_ref[...]
    lane = lax.broadcasted_iota(jnp.int32, (QUERY_CHUNK, 2 * head_size), 1)

    def chunk_body(chunk, carry):
        span = pl.ds(pl.multiple_of(chunk * QUERY_CHUNK, QUERY_CHUNK), QUERY_CHUNK)
        mixed_parts = []
        totals = []
        for half in range(2):
            cols = pl.ds(half * head_size, head_size)
            query = q_ref[span, cols]
            key = k_ref[:, cols]
            value = v_ref[:, cols]
            scores = (
                lax.dot_general(
                    query, key, (((1,), (1,)), ((), ())), preferred_element_type=jnp.float32
                )
                + kbias
            )
            highest = jnp.max(scores, axis=1, keepdims=True)
            exponent = jnp.exp(scores - highest)
            denominator = jnp.sum(exponent, axis=1, keepdims=True)
            weights = (exponent * (1.0 / denominator)).astype(jnp.bfloat16)
            mixed_parts.append(jnp.dot(weights, value, preferred_element_type=jnp.float32))
            totals.append(highest + jnp.log(denominator))
        o_ref[span, :] = jnp.concatenate(mixed_parts, axis=1).astype(o_ref.dtype)
        l_ref[span, :] = jnp.where(lane < head_size, totals[0], totals[1])
        return carry

    lax.fori_loop(0, rows // QUERY_CHUNK, chunk_body, 0)


def attention_backward_kernel(
    q_ref, k_ref, v_ref, do_ref, l_ref, kbias_ref, dq_ref, dk_ref, dv_ref
):
    head_size = q_ref.shape[1] // 2
    rows = q_ref.shape[0]
    kbias = kbias_ref[...]
    dk_ref[...] = jnp.zeros_like(dk_ref)
    dv_ref[...] = jnp.zeros_like(dv_ref)
    for half in range(2):
        cols = pl.ds(half * head_size, head_size)

        def chunk_body(chunk, carry, cols=cols, half=half):
            span = pl.ds(pl.multiple_of(chunk * QUERY_CHUNK, QUERY_CHUNK), QUERY_CHUNK)
            key = k_ref[:, cols]
            value = v_ref[:, cols]
            query = q_ref[span, cols]
            grad_out = do_ref[span, cols]
            total = l_ref[span, pl.ds(half * head_size, 1)]
            scores = (
                lax.dot_general(
                    query, key, (((1,), (1,)), ((), ())), preferred_element_type=jnp.float32
                )
                + kbias
            )
            weights = jnp.exp(scores - total)
            grad_weights = lax.dot_general(
                grad_out, value, (((1,), (1,)), ((), ())), preferred_element_type=jnp.float32
            )
            delta = jnp.sum(weights * grad_weights, axis=1, keepdims=True)
            grad_scores = (weights * (grad_weights - delta)).astype(jnp.bfloat16)
            dq_ref[span, cols] = jnp.dot(
                grad_scores, key, preferred_element_type=jnp.float32
            ).astype(dq_ref.dtype)
            dk_ref[:, cols] += lax.dot_general(
                grad_scores, query, (((0,), (0,)), ((), ())), preferred_element_type=jnp.float32
            )
            dv_ref[:, cols] += lax.dot_general(
                weights.astype(jnp.bfloat16),
                grad_out,
                (((0,), (0,)), ((), ())),
                preferred_element_type=jnp.float32,
            )
            return carry

        lax.fori_loop(0, rows // QUERY_CHUNK, chunk_body, 0)


def pad_rows(values, rows):
    return jnp.pad(values, ((0, rows - values.shape[0]), (0, 0)))


def attention_pallas(queries, pairs, grad_out=None, totals=None, first_pair=0, pair_span=None):
    query_rows, model_width = queries.shape
    key_rows = pairs.shape[0]
    padded_q = -(-query_rows // QUERY_CHUNK) * QUERY_CHUNK
    padded_k = -(-key_rows // 128) * 128
    pair_count = model_width // 128
    q_pad = pad_rows(queries, padded_q)
    kv_pad = pad_rows(pairs, padded_k)
    kbias = jnp.where(jnp.arange(padded_k) < key_rows, 0.0, MASKED).astype(jnp.float32)[None, :]
    q_spec = pl.BlockSpec((padded_q, 128), lambda j: (0, j))
    k_spec = pl.BlockSpec((padded_k, 128), lambda j: (0, j))
    v_spec = pl.BlockSpec((padded_k, 128), lambda j: (0, j + pair_count))
    b_spec = pl.BlockSpec((1, padded_k), lambda j: (0, 0))
    params = pltpu.CompilerParams(vmem_limit_bytes=48 * 1024 * 1024)
    if grad_out is None:
        mixed, log_totals = pl.pallas_call(
            attention_forward_kernel,
            grid=(pair_count,),
            in_specs=[q_spec, k_spec, v_spec, b_spec],
            out_specs=[q_spec, q_spec],
            out_shape=[
                jax.ShapeDtypeStruct((padded_q, model_width), jnp.bfloat16),
                jax.ShapeDtypeStruct((padded_q, model_width), jnp.float32),
            ],
            compiler_params=params,
        )(q_pad, kv_pad, kv_pad, kbias)
        return mixed[:query_rows], log_totals
    do_pad = pad_rows(grad_out, padded_q)
    span = pair_count if pair_span is None else pair_span
    qi_spec = pl.BlockSpec((padded_q, 128), lambda j: (0, j + first_pair))
    ki_spec = pl.BlockSpec((padded_k, 128), lambda j: (0, j + first_pair))
    vi_spec = pl.BlockSpec((padded_k, 128), lambda j: (0, j + first_pair + pair_count))
    qo_spec = pl.BlockSpec((padded_q, 128), lambda j: (0, j))
    ko_spec = pl.BlockSpec((padded_k, 128), lambda j: (0, j))
    dq, dk, dv = pl.pallas_call(
        attention_backward_kernel,
        grid=(span,),
        in_specs=[qi_spec, ki_spec, vi_spec, qi_spec, qi_spec, b_spec],
        out_specs=[qo_spec, ko_spec, ko_spec],
        out_shape=[
            jax.ShapeDtypeStruct((padded_q, 128 * span), jnp.float32),
            jax.ShapeDtypeStruct((padded_k, 128 * span), jnp.float32),
            jax.ShapeDtypeStruct((padded_k, 128 * span), jnp.float32),
        ],
        compiler_params=params,
    )(q_pad, kv_pad, kv_pad, do_pad, totals, kbias)
    return dq[:query_rows], dk[:key_rows], dv[:key_rows]


def attend_forward(queries, keys_values, head_count):
    model_width = queries.shape[2]
    head_size = model_width // head_count
    score_scale = 1.0 / math.sqrt(head_size)

    def one_head(head_index):
        offset = head_index * head_size
        query_block = lax.dynamic_slice_in_dim(queries, offset, head_size, 2)
        key_block = lax.dynamic_slice_in_dim(keys_values, offset, head_size, 2)
        value_block = lax.dynamic_slice_in_dim(keys_values, model_width + offset, head_size, 2)
        scores = (
            jnp.einsum("cqd,ckd->cqk", query_block, key_block, preferred_element_type=jnp.float32)
            * score_scale
        )
        highest = jnp.max(scores, axis=-1, keepdims=True)
        exponent = jnp.exp(scores - highest)
        denominator = jnp.sum(exponent, axis=-1, keepdims=True)
        weights_soft = (exponent / denominator).astype(jnp.bfloat16)
        mixed = jnp.einsum(
            "cqk,ckd->cqd", weights_soft, value_block, preferred_element_type=jnp.float32
        )
        return (mixed, (highest + jnp.log(denominator))[..., 0])

    mixed, log_totals = lax.map(one_head, jnp.arange(head_count))
    clip_count, frame_count = (queries.shape[0], queries.shape[1])
    mixed = jnp.transpose(mixed, (1, 2, 0, 3)).reshape(clip_count, frame_count, model_width)
    return (mixed, log_totals)


def attend_backward(queries, keys_values, grad_mixed, log_totals, head_count):
    model_width = queries.shape[2]
    head_size = model_width // head_count
    score_scale = 1.0 / math.sqrt(head_size)

    def one_head_back(head_index):
        offset = head_index * head_size
        query_block = lax.dynamic_slice_in_dim(queries, offset, head_size, 2)
        key_block = lax.dynamic_slice_in_dim(keys_values, offset, head_size, 2)
        value_block = lax.dynamic_slice_in_dim(keys_values, model_width + offset, head_size, 2)
        grad_block = lax.dynamic_slice_in_dim(grad_mixed, offset, head_size, 2)
        totals = lax.dynamic_index_in_dim(log_totals, head_index, 0, keepdims=False)
        scores = (
            jnp.einsum("cqd,ckd->cqk", query_block, key_block, preferred_element_type=jnp.float32)
            * score_scale
        )
        weights_soft = jnp.exp(scores - totals[..., None])
        grad_weights = jnp.einsum(
            "cqd,ckd->cqk", grad_block, value_block, preferred_element_type=jnp.float32
        )
        delta = jnp.sum(weights_soft * grad_weights, axis=-1, keepdims=True)
        grad_scores = (weights_soft * (grad_weights - delta)).astype(jnp.bfloat16)
        grad_query = (
            jnp.einsum("cqk,ckd->cqd", grad_scores, key_block, preferred_element_type=jnp.float32)
            * score_scale
        )
        grad_key = (
            jnp.einsum("cqk,cqd->ckd", grad_scores, query_block, preferred_element_type=jnp.float32)
            * score_scale
        )
        grad_value = jnp.einsum(
            "cqk,cqd->ckd",
            weights_soft.astype(jnp.bfloat16),
            grad_block,
            preferred_element_type=jnp.float32,
        )
        return (grad_query, delta[..., 0], grad_key, grad_value)

    pieces = lax.map(one_head_back, jnp.arange(head_count))
    clip_count, frame_count = (queries.shape[0], queries.shape[1])
    clip_frames = keys_values.shape[1]
    grad_query = jnp.transpose(pieces[0], (1, 2, 0, 3)).reshape(
        clip_count, frame_count, model_width
    )
    grad_key = jnp.transpose(pieces[2], (1, 2, 0, 3)).reshape(clip_count, clip_frames, model_width)
    grad_value = jnp.transpose(pieces[3], (1, 2, 0, 3)).reshape(
        clip_count, clip_frames, model_width
    )
    return (grad_query, pieces[1], jnp.concatenate([grad_key, grad_value], axis=2))


def link_plan(mesh):
    devices = list(mesh.devices.reshape(-1))
    bit_count = len(devices).bit_length() - 1
    core_bit = 1
    for bit in range(bit_count):
        first, other = devices[0], devices[1 << bit]
        if getattr(first, "coords", None) is not None and tuple(first.coords) == tuple(other.coords):
            core_bit = bit
    others = [bit for bit in range(bit_count) if bit != core_bit]
    near, far = others[:-1], others[-1:]
    rotated = tuple(tuple(near[k:] + near[:k] + far) for k in range(3))
    inner = [bit for bit in near if bit != 0]
    late = tuple(tuple(inner[k:] + inner[:k] + [0] + far) for k in range(2))
    return bit_count, core_bit, rotated, late


def tree_reduce_scatter(terms, part_columns, orders, plan_bits, hooks=None):
    hooks = dict(hooks or {})
    tied = {}
    bit_count, core_bit = plan_bits
    device = lax.axis_index("clip") * lax.axis_size("frame") + lax.axis_index("frame")
    blocks = 1 << bit_count
    block_rows = terms.shape[0] // blocks
    data = terms.reshape((2,) * bit_count + (block_rows, terms.shape[1]))
    parts = [(data, list(range(bit_count - 1, -1, -1)))]
    plan = [(core_bit,)] + [tuple(order[stage] for order in orders) for stage in range(len(orders[0]))]
    for stage, stage_bits in enumerate(plan):
        if stage == 1:
            whole, bits = parts[0]
            parts = []
            offset = 0
            for width in part_columns:
                parts.append((whole[..., offset : offset + width], bits))
                offset += width
        keeps, sends = [], []
        for (part, part_bits), bit in zip(parts, stage_bits):
            axis = part_bits.index(bit)
            mine = (device >> bit) & 1
            keeps.append(lax.dynamic_index_in_dim(part, mine, axis=axis, keepdims=False))
            sends.append(
                lax.dynamic_index_in_dim(part, 1 - mine, axis=axis, keepdims=False).astype(jnp.bfloat16)
            )
        new_parts = []
        for keep, send, (part, part_bits), bit in zip(keeps, sends, parts, stage_bits):
            pairs = [(index, index ^ (1 << bit)) for index in range(blocks)]
            got = lax.ppermute(send, ("clip", "frame"), pairs)
            new_parts.append((keep + got.astype(jnp.float32), [b for b in part_bits if b != bit]))
        if stage in hooks:
            values, tied[stage] = lax.optimization_barrier(
                ([part for part, _ in new_parts], hooks[stage](tied))
            )
            new_parts = [(value, part_bits) for value, (_, part_bits) in zip(values, new_parts)]
        parts = new_parts
    return jnp.concatenate([part for part, _ in parts], axis=-1).astype(jnp.float32), tied


def tree_all_gather(local, part_columns, orders, plan_bits):
    bit_count, core_bit = plan_bits
    device = lax.axis_index("clip") * lax.axis_size("frame") + lax.axis_index("frame")
    canonical = list(range(bit_count - 1, -1, -1))

    def double(data, bits, bit):
        mine = (device >> bit) & 1
        pairs = [(index, index ^ (1 << bit)) for index in range(1 << bit_count)]
        got = lax.ppermute(data, ("clip", "frame"), pairs)
        new_bits = sorted(bits + [bit], reverse=True)
        axis = new_bits.index(bit)
        low_first = jnp.stack([data, got], axis=axis)
        high_first = jnp.stack([got, data], axis=axis)
        return jnp.where(mine == 0, low_first, high_first), new_bits

    parts = []
    offset = 0
    for width in part_columns:
        parts.append((local[:, offset : offset + width], []))
        offset += width
    reversed_orders = [list(reversed(order)) for order in orders]
    for stage in range(len(reversed_orders[0])):
        parts = [double(part, bits, order[stage]) for (part, bits), order in zip(parts, reversed_orders)]
    whole = jnp.concatenate([part for part, _ in parts], axis=-1)
    whole, bits = double(whole, parts[0][1], core_bit)
    assert bits == canonical
    return whole.reshape((1 << bit_count) * local.shape[0], local.shape[1])


def adam_step(weight, moments, gradient):
    first = beta_first * moments[0] + (1.0 - beta_first) * gradient
    second = beta_second * moments[1] + (1.0 - beta_second) * gradient * gradient
    first_hat = first / (1.0 - beta_first**ADAM_STEP)
    second_hat = second / (1.0 - beta_second**ADAM_STEP)
    change = -learn_rate * (first_hat / (jnp.sqrt(second_hat) + epsilon_adam) + decay_rate * weight)
    return (change, jnp.stack([first, second]))


def body(
    plan,
    inputs,
    cotangent,
    project_in,
    project_out,
    expand_weight,
    shrink_weight,
    expand_bias,
    vectors,
    moments_in,
    moments_out,
    moments_expand,
    moments_shrink,
    moments_bias,
    moments_vectors,
):
    clip_count, frame_count, model_width = inputs.shape
    row_count = clip_count * frame_count
    head_count = HEADS
    shard_rows = project_in.shape[0]
    wide_in = project_in.shape[1]
    ff_width = expand_weight.shape[1]
    swap = [(0, 1), (1, 0)]
    everyone = ("clip", "frame")

    small = jnp.concatenate(
        [
            vectors,
            expand_bias.reshape(shard_rows, -1),
            jnp.zeros((shard_rows, 128 - vectors.shape[1] - expand_bias.shape[0] // shard_rows), jnp.float32),
        ],
        axis=1,
    )
    first_pack = jnp.concatenate([project_in, small], axis=1).astype(jnp.bfloat16)
    second_pack = jnp.concatenate(
        [project_out, expand_weight, shrink_weight.reshape(shard_rows, -1)], axis=1
    ).astype(jnp.bfloat16)
    bit_count, core_bit, rotated_orders, late_orders = plan
    first_full = tree_all_gather(first_pack, (896, 768, 768), rotated_orders, (bit_count, core_bit))
    partner_send, first_full = lax.optimization_barrier((inputs, first_full))
    second_full = lax.all_gather(second_pack, everyone, axis=0, tiled=True)
    full_in = first_full[:, :wide_in]
    small_full = first_full[:, wide_in:].astype(jnp.float32)
    column_set = small_full[:, : vectors.shape[1]]
    full_bias = small_full[:, vectors.shape[1] : vectors.shape[1] + ff_width // model_width].reshape(-1)
    full_out = second_full[:, :model_width]
    full_expand = second_full[:, model_width : model_width + ff_width]
    full_shrink = second_full[:, model_width + ff_width :].reshape(ff_width, model_width)

    frames_rows = inputs.reshape(row_count, model_width).astype(jnp.float32)
    normed_first, plain_first, inv_first = norm_parts(
        frames_rows, column_set[:, 0], column_set[:, 1]
    )
    hidden_first = normed_first.astype(jnp.bfloat16)
    partner_rows = lax.ppermute(partner_send, "frame", swap).reshape(row_count, model_width)
    hidden_partner = norm_parts(
        partner_rows.astype(jnp.float32), column_set[:, 0], column_set[:, 1]
    )[0].astype(jnp.bfloat16)
    bias_in = jnp.concatenate(
        [column_set[:, 2], jnp.zeros((model_width,), jnp.float32), column_set[:, 3]]
    )
    projected = (
        jnp.dot(hidden_first, full_in, preferred_element_type=jnp.float32) + bias_in
    ).astype(jnp.bfloat16)
    partner_pairs = (
        jnp.dot(hidden_partner, full_in[:, model_width:], preferred_element_type=jnp.float32)
        + bias_in[model_width:]
    ).astype(jnp.bfloat16)
    queries = projected[:, :model_width].reshape(clip_count, frame_count, model_width)
    clip_pairs = jnp.concatenate([projected[:, model_width:], partner_pairs], axis=0).reshape(
        clip_count, 2 * frame_count, 2 * model_width
    )
    score_scale = 1.0 / math.sqrt(model_width // head_count)
    scaled_queries = (projected[:, :model_width] * score_scale).astype(jnp.bfloat16)
    pair_rows = clip_pairs.reshape(2 * row_count, 2 * model_width)
    mixed_low, log_totals = attention_pallas(scaled_queries, pair_rows)
    attended = jnp.dot(mixed_low, full_out, preferred_element_type=jnp.float32) + column_set[:, 4]
    residual = frames_rows + attended
    normed_second, plain_second, inv_second = norm_parts(
        residual, column_set[:, 5], column_set[:, 6]
    )
    hidden_second = normed_second.astype(jnp.bfloat16)
    preact = jnp.dot(hidden_second, full_expand, preferred_element_type=jnp.float32) + full_bias
    activated = gelu_exact(preact).astype(jnp.bfloat16)
    result = (
        residual
        + jnp.dot(activated, full_shrink, preferred_element_type=jnp.float32)
        + column_set[:, 7]
    )
    output = result.astype(jnp.bfloat16).reshape(inputs.shape)

    grad_result = cotangent.reshape(row_count, model_width)
    grad_shrink_term = jnp.dot(
        activated.T, grad_result, preferred_element_type=jnp.float32
    ).astype(jnp.bfloat16)
    grad_down_bias = jnp.sum(grad_result.astype(jnp.float32), axis=0)
    grad_activated = jnp.dot(grad_result, full_shrink.T, preferred_element_type=jnp.float32)
    grad_preact = (grad_activated * gelu_slope(preact)).astype(jnp.bfloat16)
    grad_expand_term = jnp.dot(
        hidden_second.T, grad_preact, preferred_element_type=jnp.float32
    ).astype(jnp.bfloat16)
    grad_bias_term = jnp.sum(grad_preact.astype(jnp.float32), axis=0)
    grad_hidden_second = jnp.dot(grad_preact, full_expand.T, preferred_element_type=jnp.float32)
    norm_term_second, gain_second, shift_second = norm_backward(
        grad_hidden_second, plain_second, inv_second, column_set[:, 5]
    )
    grad_residual = grad_result.astype(jnp.float32) + norm_term_second
    grad_attended = grad_residual.astype(jnp.bfloat16)
    grad_out_term = jnp.dot(
        mixed_low.T, grad_attended, preferred_element_type=jnp.float32
    ).astype(jnp.bfloat16)
    grad_out_bias = jnp.sum(grad_attended.astype(jnp.float32), axis=0)
    late_terms = jnp.concatenate(
        [grad_shrink_term.reshape(model_width, -1), grad_expand_term, grad_out_term], axis=1
    )
    grad_mixed = jnp.dot(grad_attended, full_out.T, preferred_element_type=jnp.float32).astype(
        jnp.bfloat16
    )
    piece_pairs = 1
    piece_count = model_width // 128 // piece_pairs
    stage_count = 1 + len(late_orders[0])
    hooked = list(range(1, min(piece_count, stage_count)))

    def run_piece(index, mixed_grads):
        return attention_pallas(
            scaled_queries, pair_rows, mixed_grads, log_totals, index * piece_pairs, piece_pairs
        )

    def piece_hook(index):
        return lambda tied: (run_piece(index, tied[index - 1][1]), tied[index - 1][1])

    hooks = {0: lambda tied: ((), grad_mixed)}
    hooks.update({index: piece_hook(index) for index in hooked})
    pieces = [run_piece(0, grad_mixed)]
    owned_late, tied = tree_reduce_scatter(
        late_terms, (3456, 3456), late_orders, (bit_count, core_bit), hooks
    )
    pieces += [tied[index][0] for index in hooked]
    last_mixed = tied[hooked[-1]][1] if hooked else grad_mixed
    pieces += [run_piece(index, last_mixed) for index in range(len(hooked) + 1, piece_count)]
    finished = []
    for grad_query, grad_keys, grad_values in pieces:
        terms = jnp.concatenate([grad_keys, grad_values], axis=1)
        returned = lax.ppermute(terms[row_count:].astype(jnp.bfloat16), "frame", swap)
        finished.append((grad_query, terms[:row_count] + returned.astype(jnp.float32)))
    piece_width = finished[0][0].shape[1]
    grad_projected = jnp.concatenate(
        [
            (jnp.concatenate([query for query, _ in finished], axis=1) * score_scale).astype(
                jnp.bfloat16
            ),
            jnp.concatenate(
                [pair[:, :piece_width] for _, pair in finished]
                + [pair[:, piece_width:] for _, pair in finished],
                axis=1,
            ).astype(jnp.bfloat16),
        ],
        axis=1,
    )
    grad_in_term = jnp.dot(
        hidden_first.T, grad_projected, preferred_element_type=jnp.float32
    ).astype(jnp.bfloat16)
    projected_sums = jnp.sum(grad_projected.astype(jnp.float32), axis=0)
    grad_query_bias = projected_sums[:model_width]
    grad_value_bias = projected_sums[2 * model_width :]
    grad_hidden_first = jnp.dot(grad_projected, full_in.T, preferred_element_type=jnp.float32)
    norm_term_first, gain_first, shift_first = norm_backward(
        grad_hidden_first, plain_first, inv_first, column_set[:, 0]
    )
    grad_inputs = (grad_residual + norm_term_first).astype(jnp.bfloat16).reshape(inputs.shape)
    grad_columns = jnp.stack(
        [
            gain_first,
            shift_first,
            grad_query_bias,
            grad_value_bias,
            grad_out_bias,
            gain_second,
            shift_second,
            grad_down_bias,
        ],
        axis=1,
    )
    small_grads = jnp.concatenate(
        [
            grad_columns,
            grad_bias_term.reshape(model_width, -1),
            jnp.zeros((model_width, 128 - 12), jnp.float32),
        ],
        axis=1,
    ).astype(jnp.bfloat16)
    owned_first = tree_reduce_scatter(
        jnp.concatenate([grad_in_term, small_grads], axis=1),
        (896, 768, 768),
        rotated_orders,
        (bit_count, core_bit),
    )[0]
    owned_in = owned_first[:, :wide_in]
    owned_vectors = owned_first[:, wide_in : wide_in + vectors.shape[1]]
    owned_bias = owned_first[:, wide_in + vectors.shape[1] : wide_in + 12].reshape(-1)
    owned_shrink = owned_late[:, :ff_width].reshape(shrink_weight.shape)
    owned_expand = owned_late[:, ff_width : 2 * ff_width]
    owned_out = owned_late[:, 2 * ff_width :]
    new_in, mom_in = adam_step(project_in, moments_in, owned_in)
    new_out, mom_out = adam_step(project_out, moments_out, owned_out)
    new_expand, mom_expand = adam_step(expand_weight, moments_expand, owned_expand)
    new_shrink, mom_shrink = adam_step(shrink_weight, moments_shrink, owned_shrink)
    new_bias, mom_bias = adam_step(expand_bias, moments_bias, owned_bias)
    new_vectors, mom_vectors = adam_step(vectors, moments_vectors, owned_vectors)
    return (
        output,
        grad_inputs,
        owned_in,
        owned_out,
        owned_expand,
        owned_shrink,
        owned_bias,
        owned_vectors,
        new_in,
        new_out,
        new_expand,
        new_shrink,
        new_bias,
        new_vectors,
        mom_in,
        mom_out,
        mom_expand,
        mom_shrink,
        mom_bias,
        mom_vectors,
    )


def solution(mesh):
    in_specs = (
        P("clip", "frame", None),
        P("clip", "frame", None),
        P(("clip", "frame"), None),
        P(("clip", "frame"), None),
        P(("clip", "frame"), None),
        P(("clip", "frame"), None),
        P(("clip", "frame")),
        P(("clip", "frame"), None),
        P(None, ("clip", "frame"), None),
        P(None, ("clip", "frame"), None),
        P(None, ("clip", "frame"), None),
        P(None, ("clip", "frame"), None),
        P(None, ("clip", "frame")),
        P(None, ("clip", "frame"), None),
    )
    out_specs = (
        P("clip", "frame", None),
        P("clip", "frame", None),
        P(("clip", "frame"), None),
        P(("clip", "frame"), None),
        P(("clip", "frame"), None),
        P(("clip", "frame"), None),
        P(("clip", "frame")),
        P(("clip", "frame"), None),
        P(("clip", "frame"), None),
        P(("clip", "frame"), None),
        P(("clip", "frame"), None),
        P(("clip", "frame"), None),
        P(("clip", "frame")),
        P(("clip", "frame"), None),
        P(None, ("clip", "frame"), None),
        P(None, ("clip", "frame"), None),
        P(None, ("clip", "frame"), None),
        P(None, ("clip", "frame"), None),
        P(None, ("clip", "frame")),
        P(None, ("clip", "frame"), None),
    )
    return jax.shard_map(
        functools.partial(body, link_plan(mesh)),
        mesh=mesh,
        in_specs=in_specs,
        out_specs=out_specs,
        check_vma=False,
    )
```

```python
import functools
import math

import jax
import jax.numpy as jnp
from jax import lax
from jax.experimental import pallas as pl
from jax.experimental.pallas import tpu as pltpu
from jax.sharding import PartitionSpec as P

HEADS = 12
ADAM_STEP = 4


epsilon_norm = 1e-05
beta_first = 0.9
beta_second = 0.99
learn_rate = 0.03
decay_rate = 0.01
epsilon_adam = 1e-08
root_half = 0.7071067811865476
inv_root_two_pi = 0.3989422804014327


def norm_parts(inputs, norm_gain, norm_shift):
    average = jnp.mean(inputs, axis=-1, keepdims=True)
    centered = inputs - average
    spread = jnp.mean(centered * centered, axis=-1, keepdims=True)
    inv_std = lax.rsqrt(spread + epsilon_norm)
    normed = centered * inv_std
    return (normed * norm_gain + norm_shift, normed, inv_std)


def norm_backward(grad_normed, normed, inv_std, norm_gain):
    grad_gain = jnp.sum(grad_normed * normed, axis=0)
    grad_shift = jnp.sum(grad_normed, axis=0)
    scaled = grad_normed * norm_gain
    grad_input = inv_std * (
        scaled
        - jnp.mean(scaled, axis=-1, keepdims=True)
        - normed * jnp.mean(scaled * normed, axis=-1, keepdims=True)
    )
    return (grad_input, grad_gain, grad_shift)


def gelu_exact(inputs):
    return 0.5 * inputs * (1.0 + jax.scipy.special.erf(inputs * root_half))


def gelu_slope(inputs):
    return (
        0.5 * (1.0 + jax.scipy.special.erf(inputs * root_half))
        + inputs * jnp.exp(-0.5 * inputs * inputs) * inv_root_two_pi
    )


QUERY_CHUNK = 128
MASKED = -1e30


def attention_forward_kernel(q_ref, k_ref, v_ref, kbias_ref, o_ref, l_ref):
    head_size = q_ref.shape[1] // 2
    rows = q_ref.shape[0]
    kbias = kbias_ref[...]
    lane = lax.broadcasted_iota(jnp.int32, (QUERY_CHUNK, 2 * head_size), 1)

    def chunk_body(chunk, carry):
        span = pl.ds(pl.multiple_of(chunk * QUERY_CHUNK, QUERY_CHUNK), QUERY_CHUNK)
        mixed_parts = []
        totals = []
        for half in range(2):
            cols = pl.ds(half * head_size, head_size)
            query = q_ref[span, cols]
            key = k_ref[:, cols]
            value = v_ref[:, cols]
            scores = (
                lax.dot_general(
                    query, key, (((1,), (1,)), ((), ())), preferred_element_type=jnp.float32
                )
                + kbias
            )
            highest = jnp.max(scores, axis=1, keepdims=True)
            exponent = jnp.exp(scores - highest)
            denominator = jnp.sum(exponent, axis=1, keepdims=True)
            weights = (exponent * (1.0 / denominator)).astype(jnp.bfloat16)
            mixed_parts.append(jnp.dot(weights, value, preferred_element_type=jnp.float32))
            totals.append(highest + jnp.log(denominator))
        o_ref[span, :] = jnp.concatenate(mixed_parts, axis=1).astype(o_ref.dtype)
        l_ref[span, :] = jnp.where(lane < head_size, totals[0], totals[1])
        return carry

    lax.fori_loop(0, rows // QUERY_CHUNK, chunk_body, 0)


def attention_backward_kernel(
    q_ref, k_ref, v_ref, do_ref, l_ref, kbias_ref, dq_ref, dk_ref, dv_ref
):
    head_size = q_ref.shape[1] // 2
    rows = q_ref.shape[0]
    kbias = kbias_ref[...]
    dk_ref[...] = jnp.zeros_like(dk_ref)
    dv_ref[...] = jnp.zeros_like(dv_ref)
    for half in range(2):
        cols = pl.ds(half * head_size, head_size)

        def chunk_body(chunk, carry, cols=cols, half=half):
            span = pl.ds(pl.multiple_of(chunk * QUERY_CHUNK, QUERY_CHUNK), QUERY_CHUNK)
            key = k_ref[:, cols]
            value = v_ref[:, cols]
            query = q_ref[span, cols]
            grad_out = do_ref[span, cols]
            total = l_ref[span, pl.ds(half * head_size, 1)]
            scores = (
                lax.dot_general(
                    query, key, (((1,), (1,)), ((), ())), preferred_element_type=jnp.float32
                )
                + kbias
            )
            weights = jnp.exp(scores - total)
            grad_weights = lax.dot_general(
                grad_out, value, (((1,), (1,)), ((), ())), preferred_element_type=jnp.float32
            )
            delta = jnp.sum(weights * grad_weights, axis=1, keepdims=True)
            grad_scores = (weights * (grad_weights - delta)).astype(jnp.bfloat16)
            dq_ref[span, cols] = jnp.dot(
                grad_scores, key, preferred_element_type=jnp.float32
            ).astype(dq_ref.dtype)
            dk_ref[:, cols] += lax.dot_general(
                grad_scores, query, (((0,), (0,)), ((), ())), preferred_element_type=jnp.float32
            )
            dv_ref[:, cols] += lax.dot_general(
                weights.astype(jnp.bfloat16),
                grad_out,
                (((0,), (0,)), ((), ())),
                preferred_element_type=jnp.float32,
            )
            return carry

        lax.fori_loop(0, rows // QUERY_CHUNK, chunk_body, 0)


def pad_rows(values, rows):
    return jnp.pad(values, ((0, rows - values.shape[0]), (0, 0)))


def attention_pallas(queries, pairs, grad_out=None, totals=None, first_pair=0, pair_span=None):
    query_rows, model_width = queries.shape
    key_rows = pairs.shape[0]
    padded_q = -(-query_rows // QUERY_CHUNK) * QUERY_CHUNK
    padded_k = -(-key_rows // 128) * 128
    pair_count = model_width // 128
    q_pad = pad_rows(queries, padded_q)
    kv_pad = pad_rows(pairs, padded_k)
    kbias = jnp.where(jnp.arange(padded_k) < key_rows, 0.0, MASKED).astype(jnp.float32)[None, :]
    q_spec = pl.BlockSpec((padded_q, 128), lambda j: (0, j))
    k_spec = pl.BlockSpec((padded_k, 128), lambda j: (0, j))
    v_spec = pl.BlockSpec((padded_k, 128), lambda j: (0, j + pair_count))
    b_spec = pl.BlockSpec((1, padded_k), lambda j: (0, 0))
    params = pltpu.CompilerParams(vmem_limit_bytes=48 * 1024 * 1024)
    if grad_out is None:
        mixed, log_totals = pl.pallas_call(
            attention_forward_kernel,
            grid=(pair_count,),
            in_specs=[q_spec, k_spec, v_spec, b_spec],
            out_specs=[q_spec, q_spec],
            out_shape=[
                jax.ShapeDtypeStruct((padded_q, model_width), jnp.bfloat16),
                jax.ShapeDtypeStruct((padded_q, model_width), jnp.float32),
            ],
            compiler_params=params,
        )(q_pad, kv_pad, kv_pad, kbias)
        return mixed[:query_rows], log_totals
    do_pad = pad_rows(grad_out, padded_q)
    span = pair_count if pair_span is None else pair_span
    qi_spec = pl.BlockSpec((padded_q, 128), lambda j: (0, j + first_pair))
    ki_spec = pl.BlockSpec((padded_k, 128), lambda j: (0, j + first_pair))
    vi_spec = pl.BlockSpec((padded_k, 128), lambda j: (0, j + first_pair + pair_count))
    qo_spec = pl.BlockSpec((padded_q, 128), lambda j: (0, j))
    ko_spec = pl.BlockSpec((padded_k, 128), lambda j: (0, j))
    dq, dk, dv = pl.pallas_call(
        attention_backward_kernel,
        grid=(span,),
        in_specs=[qi_spec, ki_spec, vi_spec, qi_spec, qi_spec, b_spec],
        out_specs=[qo_spec, ko_spec, ko_spec],
        out_shape=[
            jax.ShapeDtypeStruct((padded_q, 128 * span), jnp.float32),
            jax.ShapeDtypeStruct((padded_k, 128 * span), jnp.float32),
            jax.ShapeDtypeStruct((padded_k, 128 * span), jnp.float32),
        ],
        compiler_params=params,
    )(q_pad, kv_pad, kv_pad, do_pad, totals, kbias)
    return dq[:query_rows], dk[:key_rows], dv[:key_rows]


def attend_forward(queries, keys_values, head_count):
    model_width = queries.shape[2]
    head_size = model_width // head_count
    score_scale = 1.0 / math.sqrt(head_size)

    def one_head(head_index):
        offset = head_index * head_size
        query_block = lax.dynamic_slice_in_dim(queries, offset, head_size, 2)
        key_block = lax.dynamic_slice_in_dim(keys_values, offset, head_size, 2)
        value_block = lax.dynamic_slice_in_dim(keys_values, model_width + offset, head_size, 2)
        scores = (
            jnp.einsum("cqd,ckd->cqk", query_block, key_block, preferred_element_type=jnp.float32)
            * score_scale
        )
        highest = jnp.max(scores, axis=-1, keepdims=True)
        exponent = jnp.exp(scores - highest)
        denominator = jnp.sum(exponent, axis=-1, keepdims=True)
        weights_soft = (exponent / denominator).astype(jnp.bfloat16)
        mixed = jnp.einsum(
            "cqk,ckd->cqd", weights_soft, value_block, preferred_element_type=jnp.float32
        )
        return (mixed, (highest + jnp.log(denominator))[..., 0])

    mixed, log_totals = lax.map(one_head, jnp.arange(head_count))
    clip_count, frame_count = (queries.shape[0], queries.shape[1])
    mixed = jnp.transpose(mixed, (1, 2, 0, 3)).reshape(clip_count, frame_count, model_width)
    return (mixed, log_totals)


def attend_backward(queries, keys_values, grad_mixed, log_totals, head_count):
    model_width = queries.shape[2]
    head_size = model_width // head_count
    score_scale = 1.0 / math.sqrt(head_size)

    def one_head_back(head_index):
        offset = head_index * head_size
        query_block = lax.dynamic_slice_in_dim(queries, offset, head_size, 2)
        key_block = lax.dynamic_slice_in_dim(keys_values, offset, head_size, 2)
        value_block = lax.dynamic_slice_in_dim(keys_values, model_width + offset, head_size, 2)
        grad_block = lax.dynamic_slice_in_dim(grad_mixed, offset, head_size, 2)
        totals = lax.dynamic_index_in_dim(log_totals, head_index, 0, keepdims=False)
        scores = (
            jnp.einsum("cqd,ckd->cqk", query_block, key_block, preferred_element_type=jnp.float32)
            * score_scale
        )
        weights_soft = jnp.exp(scores - totals[..., None])
        grad_weights = jnp.einsum(
            "cqd,ckd->cqk", grad_block, value_block, preferred_element_type=jnp.float32
        )
        delta = jnp.sum(weights_soft * grad_weights, axis=-1, keepdims=True)
        grad_scores = (weights_soft * (grad_weights - delta)).astype(jnp.bfloat16)
        grad_query = (
            jnp.einsum("cqk,ckd->cqd", grad_scores, key_block, preferred_element_type=jnp.float32)
            * score_scale
        )
        grad_key = (
            jnp.einsum("cqk,cqd->ckd", grad_scores, query_block, preferred_element_type=jnp.float32)
            * score_scale
        )
        grad_value = jnp.einsum(
            "cqk,cqd->ckd",
            weights_soft.astype(jnp.bfloat16),
            grad_block,
            preferred_element_type=jnp.float32,
        )
        return (grad_query, delta[..., 0], grad_key, grad_value)

    pieces = lax.map(one_head_back, jnp.arange(head_count))
    clip_count, frame_count = (queries.shape[0], queries.shape[1])
    clip_frames = keys_values.shape[1]
    grad_query = jnp.transpose(pieces[0], (1, 2, 0, 3)).reshape(
        clip_count, frame_count, model_width
    )
    grad_key = jnp.transpose(pieces[2], (1, 2, 0, 3)).reshape(clip_count, clip_frames, model_width)
    grad_value = jnp.transpose(pieces[3], (1, 2, 0, 3)).reshape(
        clip_count, clip_frames, model_width
    )
    return (grad_query, pieces[1], jnp.concatenate([grad_key, grad_value], axis=2))


def link_plan(mesh):
    devices = list(mesh.devices.reshape(-1))
    bit_count = len(devices).bit_length() - 1
    core_bit = 1
    for bit in range(bit_count):
        first, other = devices[0], devices[1 << bit]
        if getattr(first, "coords", None) is not None and tuple(first.coords) == tuple(other.coords):
            core_bit = bit
    others = [bit for bit in range(bit_count) if bit != core_bit]
    near, far = others[:-1], others[-1:]
    rotated = tuple(tuple(near[k:] + near[:k] + far) for k in range(3))
    inner = [bit for bit in near if bit != 0]
    late = tuple(tuple(inner[k:] + inner[:k] + [0] + far) for k in range(2))
    return bit_count, core_bit, rotated, late


def tree_reduce_scatter(terms, part_columns, orders, plan_bits, hooks=None):
    hooks = dict(hooks or {})
    tied = {}
    bit_count, core_bit = plan_bits
    device = lax.axis_index("clip") * lax.axis_size("frame") + lax.axis_index("frame")
    blocks = 1 << bit_count
    block_rows = terms.shape[0] // blocks
    data = terms.reshape((2,) * bit_count + (block_rows, terms.shape[1]))
    parts = [(data, list(range(bit_count - 1, -1, -1)))]
    plan = [(core_bit,)] + [tuple(order[stage] for order in orders) for stage in range(len(orders[0]))]
    for stage, stage_bits in enumerate(plan):
        if stage == 1:
            whole, bits = parts[0]
            parts = []
            offset = 0
            for width in part_columns:
                parts.append((whole[..., offset : offset + width], bits))
                offset += width
        keeps, sends = [], []
        for (part, part_bits), bit in zip(parts, stage_bits):
            axis = part_bits.index(bit)
            mine = (device >> bit) & 1
            keeps.append(lax.dynamic_index_in_dim(part, mine, axis=axis, keepdims=False))
            sends.append(
                lax.dynamic_index_in_dim(part, 1 - mine, axis=axis, keepdims=False).astype(jnp.bfloat16)
            )
        new_parts = []
        for keep, send, (part, part_bits), bit in zip(keeps, sends, parts, stage_bits):
            pairs = [(index, index ^ (1 << bit)) for index in range(blocks)]
            got = lax.ppermute(send, ("clip", "frame"), pairs)
            new_parts.append((keep + got.astype(jnp.float32), [b for b in part_bits if b != bit]))
        if stage in hooks:
            values, tied[stage] = lax.optimization_barrier(
                ([part for part, _ in new_parts], hooks[stage](tied))
            )
            new_parts = [(value, part_bits) for value, (_, part_bits) in zip(values, new_parts)]
        parts = new_parts
    return jnp.concatenate([part for part, _ in parts], axis=-1).astype(jnp.float32), tied


def tree_all_gather(local, part_columns, orders, plan_bits):
    bit_count, core_bit = plan_bits
    device = lax.axis_index("clip") * lax.axis_size("frame") + lax.axis_index("frame")
    canonical = list(range(bit_count - 1, -1, -1))

    def double(data, bits, bit):
        mine = (device >> bit) & 1
        pairs = [(index, index ^ (1 << bit)) for index in range(1 << bit_count)]
        got = lax.ppermute(data, ("clip", "frame"), pairs)
        new_bits = sorted(bits + [bit], reverse=True)
        axis = new_bits.index(bit)
        low_first = jnp.stack([data, got], axis=axis)
        high_first = jnp.stack([got, data], axis=axis)
        return jnp.where(mine == 0, low_first, high_first), new_bits

    parts = []
    offset = 0
    for width in part_columns:
        parts.append((local[:, offset : offset + width], []))
        offset += width
    reversed_orders = [list(reversed(order)) for order in orders]
    for stage in range(len(reversed_orders[0])):
        parts = [double(part, bits, order[stage]) for (part, bits), order in zip(parts, reversed_orders)]
    whole = jnp.concatenate([part for part, _ in parts], axis=-1)
    whole, bits = double(whole, parts[0][1], core_bit)
    assert bits == canonical
    return whole.reshape((1 << bit_count) * local.shape[0], local.shape[1])


def adam_step(weight, moments, gradient):
    first = beta_first * moments[0] + (1.0 - beta_first) * gradient
    second = beta_second * moments[1] + (1.0 - beta_second) * gradient * gradient
    first_hat = first / (1.0 - beta_first**ADAM_STEP)
    second_hat = second / (1.0 - beta_second**ADAM_STEP)
    change = -learn_rate * (first_hat / (jnp.sqrt(second_hat) + epsilon_adam) + decay_rate * weight)
    return (change, jnp.stack([first, second]))


def body(
    plan,
    inputs,
    cotangent,
    project_in,
    project_out,
    expand_weight,
    shrink_weight,
    expand_bias,
    vectors,
    moments_in,
    moments_out,
    moments_expand,
    moments_shrink,
    moments_bias,
    moments_vectors,
):
    clip_count, frame_count, model_width = inputs.shape
    row_count = clip_count * frame_count
    head_count = HEADS
    shard_rows = project_in.shape[0]
    wide_in = project_in.shape[1]
    ff_width = expand_weight.shape[1]
    swap = [(0, 1), (1, 0)]
    everyone = ("clip", "frame")

    small = jnp.concatenate(
        [
            vectors,
            expand_bias.reshape(shard_rows, -1),
            jnp.zeros((shard_rows, 128 - vectors.shape[1] - expand_bias.shape[0] // shard_rows), jnp.float32),
        ],
        axis=1,
    )
    first_pack = jnp.concatenate([project_in, small], axis=1).astype(jnp.bfloat16)
    second_pack = jnp.concatenate(
        [project_out, expand_weight, shrink_weight.reshape(shard_rows, -1)], axis=1
    ).astype(jnp.bfloat16)
    bit_count, core_bit, rotated_orders, late_orders = plan
    first_full = tree_all_gather(first_pack, (896, 768, 768), rotated_orders, (bit_count, core_bit))
    second_full = lax.all_gather(second_pack, everyone, axis=0, tiled=True)
    full_in = first_full[:, :wide_in]
    small_full = first_full[:, wide_in:].astype(jnp.float32)
    column_set = small_full[:, : vectors.shape[1]]
    full_bias = small_full[:, vectors.shape[1] : vectors.shape[1] + ff_width // model_width].reshape(-1)
    full_out = second_full[:, :model_width]
    full_expand = second_full[:, model_width : model_width + ff_width]
    full_shrink = second_full[:, model_width + ff_width :].reshape(ff_width, model_width)

    frames_rows = inputs.reshape(row_count, model_width).astype(jnp.float32)
    normed_first, plain_first, inv_first = norm_parts(
        frames_rows, column_set[:, 0], column_set[:, 1]
    )
    hidden_first = normed_first.astype(jnp.bfloat16)
    partner_rows = lax.ppermute(inputs, "frame", swap).reshape(row_count, model_width)
    hidden_partner = norm_parts(
        partner_rows.astype(jnp.float32), column_set[:, 0], column_set[:, 1]
    )[0].astype(jnp.bfloat16)
    bias_in = jnp.concatenate(
        [column_set[:, 2], jnp.zeros((model_width,), jnp.float32), column_set[:, 3]]
    )
    projected = (
        jnp.dot(hidden_first, full_in, preferred_element_type=jnp.float32) + bias_in
    ).astype(jnp.bfloat16)
    partner_pairs = (
        jnp.dot(hidden_partner, full_in[:, model_width:], preferred_element_type=jnp.float32)
        + bias_in[model_width:]
    ).astype(jnp.bfloat16)
    queries = projected[:, :model_width].reshape(clip_count, frame_count, model_width)
    clip_pairs = jnp.concatenate([projected[:, model_width:], partner_pairs], axis=0).reshape(
        clip_count, 2 * frame_count, 2 * model_width
    )
    score_scale = 1.0 / math.sqrt(model_width // head_count)
    scaled_queries = (projected[:, :model_width] * score_scale).astype(jnp.bfloat16)
    pair_rows = clip_pairs.reshape(2 * row_count, 2 * model_width)
    mixed_low, log_totals = attention_pallas(scaled_queries, pair_rows)
    attended = jnp.dot(mixed_low, full_out, preferred_element_type=jnp.float32) + column_set[:, 4]
    residual = frames_rows + attended
    normed_second, plain_second, inv_second = norm_parts(
        residual, column_set[:, 5], column_set[:, 6]
    )
    hidden_second = normed_second.astype(jnp.bfloat16)
    preact = jnp.dot(hidden_second, full_expand, preferred_element_type=jnp.float32) + full_bias
    activated = gelu_exact(preact).astype(jnp.bfloat16)
    result = (
        residual
        + jnp.dot(activated, full_shrink, preferred_element_type=jnp.float32)
        + column_set[:, 7]
    )
    output = result.astype(jnp.bfloat16).reshape(inputs.shape)

    grad_result = cotangent.reshape(row_count, model_width)
    grad_shrink_term = jnp.dot(
        activated.T, grad_result, preferred_element_type=jnp.float32
    ).astype(jnp.bfloat16)
    grad_down_bias = jnp.sum(grad_result.astype(jnp.float32), axis=0)
    grad_activated = jnp.dot(grad_result, full_shrink.T, preferred_element_type=jnp.float32)
    grad_preact = (grad_activated * gelu_slope(preact)).astype(jnp.bfloat16)
    grad_expand_term = jnp.dot(
        hidden_second.T, grad_preact, preferred_element_type=jnp.float32
    ).astype(jnp.bfloat16)
    grad_bias_term = jnp.sum(grad_preact.astype(jnp.float32), axis=0)
    grad_hidden_second = jnp.dot(grad_preact, full_expand.T, preferred_element_type=jnp.float32)
    norm_term_second, gain_second, shift_second = norm_backward(
        grad_hidden_second, plain_second, inv_second, column_set[:, 5]
    )
    grad_residual = grad_result.astype(jnp.float32) + norm_term_second
    grad_attended = grad_residual.astype(jnp.bfloat16)
    grad_out_term = jnp.dot(
        mixed_low.T, grad_attended, preferred_element_type=jnp.float32
    ).astype(jnp.bfloat16)
    grad_out_bias = jnp.sum(grad_attended.astype(jnp.float32), axis=0)
    late_terms = jnp.concatenate(
        [grad_shrink_term.reshape(model_width, -1), grad_expand_term, grad_out_term], axis=1
    )
    grad_mixed = jnp.dot(grad_attended, full_out.T, preferred_element_type=jnp.float32).astype(
        jnp.bfloat16
    )
    piece_pairs = 1
    piece_count = model_width // 128 // piece_pairs
    stage_count = 1 + len(late_orders[0])
    hooked = list(range(1, min(piece_count, stage_count)))

    def run_piece(index, mixed_grads):
        return attention_pallas(
            scaled_queries, pair_rows, mixed_grads, log_totals, index * piece_pairs, piece_pairs
        )

    def piece_hook(index):
        return lambda tied: (run_piece(index, tied[index - 1][1]), tied[index - 1][1])

    hooks = {0: lambda tied: ((), grad_mixed)}
    hooks.update({index: piece_hook(index) for index in hooked})
    pieces = [run_piece(0, grad_mixed)]
    owned_late, tied = tree_reduce_scatter(
        late_terms, (3456, 3456), late_orders, (bit_count, core_bit), hooks
    )
    pieces += [tied[index][0] for index in hooked]
    last_mixed = tied[hooked[-1]][1] if hooked else grad_mixed
    pieces += [run_piece(index, last_mixed) for index in range(len(hooked) + 1, piece_count)]
    finished = []
    for grad_query, grad_keys, grad_values in pieces:
        terms = jnp.concatenate([grad_keys, grad_values], axis=1)
        returned = lax.ppermute(terms[row_count:].astype(jnp.bfloat16), "frame", swap)
        finished.append((grad_query, terms[:row_count] + returned.astype(jnp.float32)))
    piece_width = finished[0][0].shape[1]
    grad_projected = jnp.concatenate(
        [
            (jnp.concatenate([query for query, _ in finished], axis=1) * score_scale).astype(
                jnp.bfloat16
            ),
            jnp.concatenate(
                [pair[:, :piece_width] for _, pair in finished]
                + [pair[:, piece_width:] for _, pair in finished],
                axis=1,
            ).astype(jnp.bfloat16),
        ],
        axis=1,
    )
    grad_in_term = jnp.dot(
        hidden_first.T, grad_projected, preferred_element_type=jnp.float32
    ).astype(jnp.bfloat16)
    projected_sums = jnp.sum(grad_projected.astype(jnp.float32), axis=0)
    grad_query_bias = projected_sums[:model_width]
    grad_value_bias = projected_sums[2 * model_width :]
    grad_hidden_first = jnp.dot(grad_projected, full_in.T, preferred_element_type=jnp.float32)
    norm_term_first, gain_first, shift_first = norm_backward(
        grad_hidden_first, plain_first, inv_first, column_set[:, 0]
    )
    grad_inputs = (grad_residual + norm_term_first).astype(jnp.bfloat16).reshape(inputs.shape)
    grad_columns = jnp.stack(
        [
            gain_first,
            shift_first,
            grad_query_bias,
            grad_value_bias,
            grad_out_bias,
            gain_second,
            shift_second,
            grad_down_bias,
        ],
        axis=1,
    )
    small_grads = jnp.concatenate(
        [
            grad_columns,
            grad_bias_term.reshape(model_width, -1),
            jnp.zeros((model_width, 128 - 12), jnp.float32),
        ],
        axis=1,
    ).astype(jnp.bfloat16)
    owned_first = tree_reduce_scatter(
        jnp.concatenate([grad_in_term, small_grads], axis=1),
        (896, 768, 768),
        rotated_orders,
        (bit_count, core_bit),
    )[0]
    owned_in = owned_first[:, :wide_in]
    owned_vectors = owned_first[:, wide_in : wide_in + vectors.shape[1]]
    owned_bias = owned_first[:, wide_in + vectors.shape[1] : wide_in + 12].reshape(-1)
    owned_shrink = owned_late[:, :ff_width].reshape(shrink_weight.shape)
    owned_expand = owned_late[:, ff_width : 2 * ff_width]
    owned_out = owned_late[:, 2 * ff_width :]
    new_in, mom_in = adam_step(project_in, moments_in, owned_in)
    new_out, mom_out = adam_step(project_out, moments_out, owned_out)
    new_expand, mom_expand = adam_step(expand_weight, moments_expand, owned_expand)
    new_shrink, mom_shrink = adam_step(shrink_weight, moments_shrink, owned_shrink)
    new_bias, mom_bias = adam_step(expand_bias, moments_bias, owned_bias)
    new_vectors, mom_vectors = adam_step(vectors, moments_vectors, owned_vectors)
    return (
        output,
        grad_inputs,
        owned_in,
        owned_out,
        owned_expand,
        owned_shrink,
        owned_bias,
        owned_vectors,
        new_in,
        new_out,
        new_expand,
        new_shrink,
        new_bias,
        new_vectors,
        mom_in,
        mom_out,
        mom_expand,
        mom_shrink,
        mom_bias,
        mom_vectors,
    )


def solution(mesh):
    in_specs = (
        P("clip", "frame", None),
        P("clip", "frame", None),
        P(("clip", "frame"), None),
        P(("clip", "frame"), None),
        P(("clip", "frame"), None),
        P(("clip", "frame"), None),
        P(("clip", "frame")),
        P(("clip", "frame"), None),
        P(None, ("clip", "frame"), None),
        P(None, ("clip", "frame"), None),
        P(None, ("clip", "frame"), None),
        P(None, ("clip", "frame"), None),
        P(None, ("clip", "frame")),
        P(None, ("clip", "frame"), None),
    )
    out_specs = (
        P("clip", "frame", None),
        P("clip", "frame", None),
        P(("clip", "frame"), None),
        P(("clip", "frame"), None),
        P(("clip", "frame"), None),
        P(("clip", "frame"), None),
        P(("clip", "frame")),
        P(("clip", "frame"), None),
        P(("clip", "frame"), None),
        P(("clip", "frame"), None),
        P(("clip", "frame"), None),
        P(("clip", "frame"), None),
        P(("clip", "frame")),
        P(("clip", "frame"), None),
        P(None, ("clip", "frame"), None),
        P(None, ("clip", "frame"), None),
        P(None, ("clip", "frame"), None),
        P(None, ("clip", "frame"), None),
        P(None, ("clip", "frame")),
        P(None, ("clip", "frame"), None),
    )
    return jax.shard_map(
        functools.partial(body, link_plan(mesh)),
        mesh=mesh,
        in_specs=in_specs,
        out_specs=out_specs,
        check_vma=False,
    )
```

```python
import functools
import math

import jax
import jax.numpy as jnp
from jax import lax
from jax.experimental import pallas as pl
from jax.experimental.pallas import tpu as pltpu
from jax.sharding import PartitionSpec as P

HEADS = 12
ADAM_STEP = 4


epsilon_norm = 1e-05
beta_first = 0.9
beta_second = 0.99
learn_rate = 0.03
decay_rate = 0.01
epsilon_adam = 1e-08
root_half = 0.7071067811865476
inv_root_two_pi = 0.3989422804014327


def norm_parts(inputs, norm_gain, norm_shift):
    average = jnp.mean(inputs, axis=-1, keepdims=True)
    centered = inputs - average
    spread = jnp.mean(centered * centered, axis=-1, keepdims=True)
    inv_std = lax.rsqrt(spread + epsilon_norm)
    normed = centered * inv_std
    return (normed * norm_gain + norm_shift, normed, inv_std)


def norm_backward(grad_normed, normed, inv_std, norm_gain):
    grad_gain = jnp.sum(grad_normed * normed, axis=0)
    grad_shift = jnp.sum(grad_normed, axis=0)
    scaled = grad_normed * norm_gain
    grad_input = inv_std * (
        scaled
        - jnp.mean(scaled, axis=-1, keepdims=True)
        - normed * jnp.mean(scaled * normed, axis=-1, keepdims=True)
    )
    return (grad_input, grad_gain, grad_shift)


def gelu_exact(inputs):
    return 0.5 * inputs * (1.0 + jax.scipy.special.erf(inputs * root_half))


def gelu_slope(inputs):
    return (
        0.5 * (1.0 + jax.scipy.special.erf(inputs * root_half))
        + inputs * jnp.exp(-0.5 * inputs * inputs) * inv_root_two_pi
    )


QUERY_CHUNK = 384
MASKED = -1e30


def attention_forward_kernel(q_ref, k_ref, v_ref, kbias_ref, o_ref, l_ref):
    head_size = q_ref.shape[1] // 2
    rows = q_ref.shape[0]
    kbias = kbias_ref[...]
    lane = lax.broadcasted_iota(jnp.int32, (QUERY_CHUNK, 2 * head_size), 1)

    def chunk_body(chunk, carry):
        span = pl.ds(pl.multiple_of(chunk * QUERY_CHUNK, QUERY_CHUNK), QUERY_CHUNK)
        mixed_parts = []
        totals = []
        for half in range(2):
            cols = pl.ds(half * head_size, head_size)
            query = q_ref[span, cols]
            key = k_ref[:, cols]
            value = v_ref[:, cols]
            scores = (
                lax.dot_general(
                    query, key, (((1,), (1,)), ((), ())), preferred_element_type=jnp.float32
                )
                + kbias
            )
            highest = jnp.max(scores, axis=1, keepdims=True)
            exponent = jnp.exp(scores - highest)
            denominator = jnp.sum(exponent, axis=1, keepdims=True)
            weights = (exponent * (1.0 / denominator)).astype(jnp.bfloat16)
            mixed_parts.append(jnp.dot(weights, value, preferred_element_type=jnp.float32))
            totals.append(highest + jnp.log(denominator))
        o_ref[span, :] = jnp.concatenate(mixed_parts, axis=1).astype(o_ref.dtype)
        l_ref[span, :] = jnp.where(lane < head_size, totals[0], totals[1])
        return carry

    lax.fori_loop(0, rows // QUERY_CHUNK, chunk_body, 0)


def attention_backward_kernel(
    q_ref, k_ref, v_ref, do_ref, l_ref, kbias_ref, dq_ref, dk_ref, dv_ref
):
    head_size = q_ref.shape[1] // 2
    rows = q_ref.shape[0]
    kbias = kbias_ref[...]
    dk_ref[...] = jnp.zeros_like(dk_ref)
    dv_ref[...] = jnp.zeros_like(dv_ref)
    for half in range(2):
        cols = pl.ds(half * head_size, head_size)

        def chunk_body(chunk, carry, cols=cols, half=half):
            span = pl.ds(pl.multiple_of(chunk * QUERY_CHUNK, QUERY_CHUNK), QUERY_CHUNK)
            key = k_ref[:, cols]
            value = v_ref[:, cols]
            query = q_ref[span, cols]
            grad_out = do_ref[span, cols]
            total = l_ref[span, pl.ds(half * head_size, 1)]
            scores = (
                lax.dot_general(
                    query, key, (((1,), (1,)), ((), ())), preferred_element_type=jnp.float32
                )
                + kbias
            )
            weights = jnp.exp(scores - total)
            grad_weights = lax.dot_general(
                grad_out, value, (((1,), (1,)), ((), ())), preferred_element_type=jnp.float32
            )
            delta = jnp.sum(weights * grad_weights, axis=1, keepdims=True)
            grad_scores = (weights * (grad_weights - delta)).astype(jnp.bfloat16)
            dq_ref[span, cols] = jnp.dot(
                grad_scores, key, preferred_element_type=jnp.float32
            ).astype(dq_ref.dtype)
            dk_ref[:, cols] += lax.dot_general(
                grad_scores, query, (((0,), (0,)), ((), ())), preferred_element_type=jnp.float32
            )
            dv_ref[:, cols] += lax.dot_general(
                weights.astype(jnp.bfloat16),
                grad_out,
                (((0,), (0,)), ((), ())),
                preferred_element_type=jnp.float32,
            )
            return carry

        lax.fori_loop(0, rows // QUERY_CHUNK, chunk_body, 0)


def pad_rows(values, rows):
    return jnp.pad(values, ((0, rows - values.shape[0]), (0, 0)))


def attention_pallas(queries, pairs, grad_out=None, totals=None, first_pair=0, pair_span=None):
    query_rows, model_width = queries.shape
    key_rows = pairs.shape[0]
    padded_q = -(-query_rows // QUERY_CHUNK) * QUERY_CHUNK
    padded_k = -(-key_rows // 128) * 128
    pair_count = model_width // 128
    q_pad = pad_rows(queries, padded_q)
    kv_pad = pad_rows(pairs, padded_k)
    kbias = jnp.where(jnp.arange(padded_k) < key_rows, 0.0, MASKED).astype(jnp.float32)[None, :]
    q_spec = pl.BlockSpec((padded_q, 128), lambda j: (0, j))
    k_spec = pl.BlockSpec((padded_k, 128), lambda j: (0, j))
    v_spec = pl.BlockSpec((padded_k, 128), lambda j: (0, j + pair_count))
    b_spec = pl.BlockSpec((1, padded_k), lambda j: (0, 0))
    params = pltpu.CompilerParams(vmem_limit_bytes=48 * 1024 * 1024)
    if grad_out is None:
        mixed, log_totals = pl.pallas_call(
            attention_forward_kernel,
            grid=(pair_count,),
            in_specs=[q_spec, k_spec, v_spec, b_spec],
            out_specs=[q_spec, q_spec],
            out_shape=[
                jax.ShapeDtypeStruct((padded_q, model_width), jnp.bfloat16),
                jax.ShapeDtypeStruct((padded_q, model_width), jnp.float32),
            ],
            compiler_params=params,
        )(q_pad, kv_pad, kv_pad, kbias)
        return mixed[:query_rows], log_totals
    do_pad = pad_rows(grad_out, padded_q)
    span = pair_count if pair_span is None else pair_span
    qi_spec = pl.BlockSpec((padded_q, 128), lambda j: (0, j + first_pair))
    ki_spec = pl.BlockSpec((padded_k, 128), lambda j: (0, j + first_pair))
    vi_spec = pl.BlockSpec((padded_k, 128), lambda j: (0, j + first_pair + pair_count))
    qo_spec = pl.BlockSpec((padded_q, 128), lambda j: (0, j))
    ko_spec = pl.BlockSpec((padded_k, 128), lambda j: (0, j))
    dq, dk, dv = pl.pallas_call(
        attention_backward_kernel,
        grid=(span,),
        in_specs=[qi_spec, ki_spec, vi_spec, qi_spec, qi_spec, b_spec],
        out_specs=[qo_spec, ko_spec, ko_spec],
        out_shape=[
            jax.ShapeDtypeStruct((padded_q, 128 * span), jnp.float32),
            jax.ShapeDtypeStruct((padded_k, 128 * span), jnp.float32),
            jax.ShapeDtypeStruct((padded_k, 128 * span), jnp.float32),
        ],
        compiler_params=params,
    )(q_pad, kv_pad, kv_pad, do_pad, totals, kbias)
    return dq[:query_rows], dk[:key_rows], dv[:key_rows]


def attend_forward(queries, keys_values, head_count):
    model_width = queries.shape[2]
    head_size = model_width // head_count
    score_scale = 1.0 / math.sqrt(head_size)

    def one_head(head_index):
        offset = head_index * head_size
        query_block = lax.dynamic_slice_in_dim(queries, offset, head_size, 2)
        key_block = lax.dynamic_slice_in_dim(keys_values, offset, head_size, 2)
        value_block = lax.dynamic_slice_in_dim(keys_values, model_width + offset, head_size, 2)
        scores = (
            jnp.einsum("cqd,ckd->cqk", query_block, key_block, preferred_element_type=jnp.float32)
            * score_scale
        )
        highest = jnp.max(scores, axis=-1, keepdims=True)
        exponent = jnp.exp(scores - highest)
        denominator = jnp.sum(exponent, axis=-1, keepdims=True)
        weights_soft = (exponent / denominator).astype(jnp.bfloat16)
        mixed = jnp.einsum(
            "cqk,ckd->cqd", weights_soft, value_block, preferred_element_type=jnp.float32
        )
        return (mixed, (highest + jnp.log(denominator))[..., 0])

    mixed, log_totals = lax.map(one_head, jnp.arange(head_count))
    clip_count, frame_count = (queries.shape[0], queries.shape[1])
    mixed = jnp.transpose(mixed, (1, 2, 0, 3)).reshape(clip_count, frame_count, model_width)
    return (mixed, log_totals)


def attend_backward(queries, keys_values, grad_mixed, log_totals, head_count):
    model_width = queries.shape[2]
    head_size = model_width // head_count
    score_scale = 1.0 / math.sqrt(head_size)

    def one_head_back(head_index):
        offset = head_index * head_size
        query_block = lax.dynamic_slice_in_dim(queries, offset, head_size, 2)
        key_block = lax.dynamic_slice_in_dim(keys_values, offset, head_size, 2)
        value_block = lax.dynamic_slice_in_dim(keys_values, model_width + offset, head_size, 2)
        grad_block = lax.dynamic_slice_in_dim(grad_mixed, offset, head_size, 2)
        totals = lax.dynamic_index_in_dim(log_totals, head_index, 0, keepdims=False)
        scores = (
            jnp.einsum("cqd,ckd->cqk", query_block, key_block, preferred_element_type=jnp.float32)
            * score_scale
        )
        weights_soft = jnp.exp(scores - totals[..., None])
        grad_weights = jnp.einsum(
            "cqd,ckd->cqk", grad_block, value_block, preferred_element_type=jnp.float32
        )
        delta = jnp.sum(weights_soft * grad_weights, axis=-1, keepdims=True)
        grad_scores = (weights_soft * (grad_weights - delta)).astype(jnp.bfloat16)
        grad_query = (
            jnp.einsum("cqk,ckd->cqd", grad_scores, key_block, preferred_element_type=jnp.float32)
            * score_scale
        )
        grad_key = (
            jnp.einsum("cqk,cqd->ckd", grad_scores, query_block, preferred_element_type=jnp.float32)
            * score_scale
        )
        grad_value = jnp.einsum(
            "cqk,cqd->ckd",
            weights_soft.astype(jnp.bfloat16),
            grad_block,
            preferred_element_type=jnp.float32,
        )
        return (grad_query, delta[..., 0], grad_key, grad_value)

    pieces = lax.map(one_head_back, jnp.arange(head_count))
    clip_count, frame_count = (queries.shape[0], queries.shape[1])
    clip_frames = keys_values.shape[1]
    grad_query = jnp.transpose(pieces[0], (1, 2, 0, 3)).reshape(
        clip_count, frame_count, model_width
    )
    grad_key = jnp.transpose(pieces[2], (1, 2, 0, 3)).reshape(clip_count, clip_frames, model_width)
    grad_value = jnp.transpose(pieces[3], (1, 2, 0, 3)).reshape(
        clip_count, clip_frames, model_width
    )
    return (grad_query, pieces[1], jnp.concatenate([grad_key, grad_value], axis=2))


def link_plan(mesh):
    devices = list(mesh.devices.reshape(-1))
    bit_count = len(devices).bit_length() - 1
    core_bit = 1
    for bit in range(bit_count):
        first, other = devices[0], devices[1 << bit]
        if getattr(first, "coords", None) is not None and tuple(first.coords) == tuple(other.coords):
            core_bit = bit
    others = [bit for bit in range(bit_count) if bit != core_bit]
    near, far = others[:-1], others[-1:]
    rotated = tuple(tuple(near[k:] + near[:k] + far) for k in range(3))
    inner = [bit for bit in near if bit != 0]
    late = tuple(tuple(inner[k:] + inner[:k] + [0] + far) for k in range(2))
    return bit_count, core_bit, rotated, late


def tree_reduce_scatter(terms, part_columns, orders, plan_bits, hooks=None):
    hooks = dict(hooks or {})
    tied = {}
    bit_count, core_bit = plan_bits
    device = lax.axis_index("clip") * lax.axis_size("frame") + lax.axis_index("frame")
    blocks = 1 << bit_count
    block_rows = terms.shape[0] // blocks
    data = terms.reshape((2,) * bit_count + (block_rows, terms.shape[1]))
    parts = [(data, list(range(bit_count - 1, -1, -1)))]
    plan = [(core_bit,)] + [tuple(order[stage] for order in orders) for stage in range(len(orders[0]))]
    for stage, stage_bits in enumerate(plan):
        if stage == 1:
            whole, bits = parts[0]
            parts = []
            offset = 0
            for width in part_columns:
                parts.append((whole[..., offset : offset + width], bits))
                offset += width
        keeps, sends = [], []
        for (part, part_bits), bit in zip(parts, stage_bits):
            axis = part_bits.index(bit)
            mine = (device >> bit) & 1
            keeps.append(lax.dynamic_index_in_dim(part, mine, axis=axis, keepdims=False))
            sends.append(
                lax.dynamic_index_in_dim(part, 1 - mine, axis=axis, keepdims=False).astype(jnp.bfloat16)
            )
        new_parts = []
        for keep, send, (part, part_bits), bit in zip(keeps, sends, parts, stage_bits):
            pairs = [(index, index ^ (1 << bit)) for index in range(blocks)]
            got = lax.ppermute(send, ("clip", "frame"), pairs)
            new_parts.append((keep + got.astype(jnp.float32), [b for b in part_bits if b != bit]))
        if stage in hooks:
            values, tied[stage] = lax.optimization_barrier(
                ([part for part, _ in new_parts], hooks[stage](tied))
            )
            new_parts = [(value, part_bits) for value, (_, part_bits) in zip(values, new_parts)]
        parts = new_parts
    return jnp.concatenate([part for part, _ in parts], axis=-1).astype(jnp.float32), tied


def tree_all_gather(local, part_columns, orders, plan_bits):
    bit_count, core_bit = plan_bits
    device = lax.axis_index("clip") * lax.axis_size("frame") + lax.axis_index("frame")
    canonical = list(range(bit_count - 1, -1, -1))

    def double(data, bits, bit):
        mine = (device >> bit) & 1
        pairs = [(index, index ^ (1 << bit)) for index in range(1 << bit_count)]
        got = lax.ppermute(data, ("clip", "frame"), pairs)
        new_bits = sorted(bits + [bit], reverse=True)
        axis = new_bits.index(bit)
        low_first = jnp.stack([data, got], axis=axis)
        high_first = jnp.stack([got, data], axis=axis)
        return jnp.where(mine == 0, low_first, high_first), new_bits

    parts = []
    offset = 0
    for width in part_columns:
        parts.append((local[:, offset : offset + width], []))
        offset += width
    reversed_orders = [list(reversed(order)) for order in orders]
    for stage in range(len(reversed_orders[0])):
        parts = [double(part, bits, order[stage]) for (part, bits), order in zip(parts, reversed_orders)]
    whole = jnp.concatenate([part for part, _ in parts], axis=-1)
    whole, bits = double(whole, parts[0][1], core_bit)
    assert bits == canonical
    return whole.reshape((1 << bit_count) * local.shape[0], local.shape[1])


def adam_step(weight, moments, gradient):
    first = beta_first * moments[0] + (1.0 - beta_first) * gradient
    second = beta_second * moments[1] + (1.0 - beta_second) * gradient * gradient
    first_hat = first / (1.0 - beta_first**ADAM_STEP)
    second_hat = second / (1.0 - beta_second**ADAM_STEP)
    change = -learn_rate * (first_hat / (jnp.sqrt(second_hat) + epsilon_adam) + decay_rate * weight)
    return (change, jnp.stack([first, second]))


def body(
    plan,
    inputs,
    cotangent,
    project_in,
    project_out,
    expand_weight,
    shrink_weight,
    expand_bias,
    vectors,
    moments_in,
    moments_out,
    moments_expand,
    moments_shrink,
    moments_bias,
    moments_vectors,
):
    clip_count, frame_count, model_width = inputs.shape
    row_count = clip_count * frame_count
    head_count = HEADS
    shard_rows = project_in.shape[0]
    wide_in = project_in.shape[1]
    ff_width = expand_weight.shape[1]
    swap = [(0, 1), (1, 0)]
    everyone = ("clip", "frame")

    small = jnp.concatenate(
        [
            vectors,
            expand_bias.reshape(shard_rows, -1),
            jnp.zeros((shard_rows, 128 - vectors.shape[1] - expand_bias.shape[0] // shard_rows), jnp.float32),
        ],
        axis=1,
    )
    first_pack = jnp.concatenate([project_in, small], axis=1).astype(jnp.bfloat16)
    second_pack = jnp.concatenate(
        [project_out, expand_weight, shrink_weight.reshape(shard_rows, -1)], axis=1
    ).astype(jnp.bfloat16)
    bit_count, core_bit, rotated_orders, late_orders = plan
    first_full = tree_all_gather(first_pack, (896, 768, 768), rotated_orders, (bit_count, core_bit))
    second_full = lax.all_gather(second_pack, everyone, axis=0, tiled=True)
    full_in = first_full[:, :wide_in]
    small_full = first_full[:, wide_in:].astype(jnp.float32)
    column_set = small_full[:, : vectors.shape[1]]
    full_bias = small_full[:, vectors.shape[1] : vectors.shape[1] + ff_width // model_width].reshape(-1)
    full_out = second_full[:, :model_width]
    full_expand = second_full[:, model_width : model_width + ff_width]
    full_shrink = second_full[:, model_width + ff_width :].reshape(ff_width, model_width)

    frames_rows = inputs.reshape(row_count, model_width).astype(jnp.float32)
    normed_first, plain_first, inv_first = norm_parts(
        frames_rows, column_set[:, 0], column_set[:, 1]
    )
    hidden_first = normed_first.astype(jnp.bfloat16)
    partner_rows = lax.ppermute(inputs, "frame", swap).reshape(row_count, model_width)
    hidden_partner = norm_parts(
        partner_rows.astype(jnp.float32), column_set[:, 0], column_set[:, 1]
    )[0].astype(jnp.bfloat16)
    bias_in = jnp.concatenate(
        [column_set[:, 2], jnp.zeros((model_width,), jnp.float32), column_set[:, 3]]
    )
    projected = (
        jnp.dot(hidden_first, full_in, preferred_element_type=jnp.float32) + bias_in
    ).astype(jnp.bfloat16)
    partner_pairs = (
        jnp.dot(hidden_partner, full_in[:, model_width:], preferred_element_type=jnp.float32)
        + bias_in[model_width:]
    ).astype(jnp.bfloat16)
    queries = projected[:, :model_width].reshape(clip_count, frame_count, model_width)
    clip_pairs = jnp.concatenate([projected[:, model_width:], partner_pairs], axis=0).reshape(
        clip_count, 2 * frame_count, 2 * model_width
    )
    score_scale = 1.0 / math.sqrt(model_width // head_count)
    scaled_queries = (projected[:, :model_width] * score_scale).astype(jnp.bfloat16)
    pair_rows = clip_pairs.reshape(2 * row_count, 2 * model_width)
    mixed_low, log_totals = attention_pallas(scaled_queries, pair_rows)
    attended = jnp.dot(mixed_low, full_out, preferred_element_type=jnp.float32) + column_set[:, 4]
    residual = frames_rows + attended
    normed_second, plain_second, inv_second = norm_parts(
        residual, column_set[:, 5], column_set[:, 6]
    )
    hidden_second = normed_second.astype(jnp.bfloat16)
    preact = jnp.dot(hidden_second, full_expand, preferred_element_type=jnp.float32) + full_bias
    activated = gelu_exact(preact).astype(jnp.bfloat16)
    result = (
        residual
        + jnp.dot(activated, full_shrink, preferred_element_type=jnp.float32)
        + column_set[:, 7]
    )
    output = result.astype(jnp.bfloat16).reshape(inputs.shape)

    grad_result = cotangent.reshape(row_count, model_width)
    grad_shrink_term = jnp.dot(
        activated.T, grad_result, preferred_element_type=jnp.float32
    ).astype(jnp.bfloat16)
    grad_down_bias = jnp.sum(grad_result.astype(jnp.float32), axis=0)
    grad_activated = jnp.dot(grad_result, full_shrink.T, preferred_element_type=jnp.float32)
    grad_preact = (grad_activated * gelu_slope(preact)).astype(jnp.bfloat16)
    grad_expand_term = jnp.dot(
        hidden_second.T, grad_preact, preferred_element_type=jnp.float32
    ).astype(jnp.bfloat16)
    grad_bias_term = jnp.sum(grad_preact.astype(jnp.float32), axis=0)
    grad_hidden_second = jnp.dot(grad_preact, full_expand.T, preferred_element_type=jnp.float32)
    norm_term_second, gain_second, shift_second = norm_backward(
        grad_hidden_second, plain_second, inv_second, column_set[:, 5]
    )
    grad_residual = grad_result.astype(jnp.float32) + norm_term_second
    grad_attended = grad_residual.astype(jnp.bfloat16)
    grad_out_term = jnp.dot(
        mixed_low.T, grad_attended, preferred_element_type=jnp.float32
    ).astype(jnp.bfloat16)
    grad_out_bias = jnp.sum(grad_attended.astype(jnp.float32), axis=0)
    late_terms = jnp.concatenate(
        [grad_shrink_term.reshape(model_width, -1), grad_expand_term, grad_out_term], axis=1
    )
    grad_mixed = jnp.dot(grad_attended, full_out.T, preferred_element_type=jnp.float32).astype(
        jnp.bfloat16
    )
    piece_pairs = 1
    piece_count = model_width // 128 // piece_pairs
    stage_count = 1 + len(late_orders[0])
    hooked = list(range(1, min(piece_count, stage_count)))

    def run_piece(index, mixed_grads):
        return attention_pallas(
            scaled_queries, pair_rows, mixed_grads, log_totals, index * piece_pairs, piece_pairs
        )

    def piece_hook(index):
        return lambda tied: (run_piece(index, tied[index - 1][1]), tied[index - 1][1])

    hooks = {0: lambda tied: ((), grad_mixed)}
    hooks.update({index: piece_hook(index) for index in hooked})
    pieces = [run_piece(0, grad_mixed)]
    owned_late, tied = tree_reduce_scatter(
        late_terms, (3456, 3456), late_orders, (bit_count, core_bit), hooks
    )
    pieces += [tied[index][0] for index in hooked]
    last_mixed = tied[hooked[-1]][1] if hooked else grad_mixed
    pieces += [run_piece(index, last_mixed) for index in range(len(hooked) + 1, piece_count)]
    finished = []
    for grad_query, grad_keys, grad_values in pieces:
        terms = jnp.concatenate([grad_keys, grad_values], axis=1)
        returned = lax.ppermute(terms[row_count:].astype(jnp.bfloat16), "frame", swap)
        finished.append((grad_query, terms[:row_count] + returned.astype(jnp.float32)))
    piece_width = finished[0][0].shape[1]
    grad_projected = jnp.concatenate(
        [
            (jnp.concatenate([query for query, _ in finished], axis=1) * score_scale).astype(
                jnp.bfloat16
            ),
            jnp.concatenate(
                [pair[:, :piece_width] for _, pair in finished]
                + [pair[:, piece_width:] for _, pair in finished],
                axis=1,
            ).astype(jnp.bfloat16),
        ],
        axis=1,
    )
    grad_in_term = jnp.dot(
        hidden_first.T, grad_projected, preferred_element_type=jnp.float32
    ).astype(jnp.bfloat16)
    projected_sums = jnp.sum(grad_projected.astype(jnp.float32), axis=0)
    grad_query_bias = projected_sums[:model_width]
    grad_value_bias = projected_sums[2 * model_width :]
    grad_hidden_first = jnp.dot(grad_projected, full_in.T, preferred_element_type=jnp.float32)
    norm_term_first, gain_first, shift_first = norm_backward(
        grad_hidden_first, plain_first, inv_first, column_set[:, 0]
    )
    grad_inputs = (grad_residual + norm_term_first).astype(jnp.bfloat16).reshape(inputs.shape)
    grad_columns = jnp.stack(
        [
            gain_first,
            shift_first,
            grad_query_bias,
            grad_value_bias,
            grad_out_bias,
            gain_second,
            shift_second,
            grad_down_bias,
        ],
        axis=1,
    )
    small_grads = jnp.concatenate(
        [
            grad_columns,
            grad_bias_term.reshape(model_width, -1),
            jnp.zeros((model_width, 128 - 12), jnp.float32),
        ],
        axis=1,
    ).astype(jnp.bfloat16)
    owned_first = tree_reduce_scatter(
        jnp.concatenate([grad_in_term, small_grads], axis=1),
        (896, 768, 768),
        rotated_orders,
        (bit_count, core_bit),
    )[0]
    owned_in = owned_first[:, :wide_in]
    owned_vectors = owned_first[:, wide_in : wide_in + vectors.shape[1]]
    owned_bias = owned_first[:, wide_in + vectors.shape[1] : wide_in + 12].reshape(-1)
    owned_shrink = owned_late[:, :ff_width].reshape(shrink_weight.shape)
    owned_expand = owned_late[:, ff_width : 2 * ff_width]
    owned_out = owned_late[:, 2 * ff_width :]
    new_in, mom_in = adam_step(project_in, moments_in, owned_in)
    new_out, mom_out = adam_step(project_out, moments_out, owned_out)
    new_expand, mom_expand = adam_step(expand_weight, moments_expand, owned_expand)
    new_shrink, mom_shrink = adam_step(shrink_weight, moments_shrink, owned_shrink)
    new_bias, mom_bias = adam_step(expand_bias, moments_bias, owned_bias)
    new_vectors, mom_vectors = adam_step(vectors, moments_vectors, owned_vectors)
    return (
        output,
        grad_inputs,
        owned_in,
        owned_out,
        owned_expand,
        owned_shrink,
        owned_bias,
        owned_vectors,
        new_in,
        new_out,
        new_expand,
        new_shrink,
        new_bias,
        new_vectors,
        mom_in,
        mom_out,
        mom_expand,
        mom_shrink,
        mom_bias,
        mom_vectors,
    )


def solution(mesh):
    in_specs = (
        P("clip", "frame", None),
        P("clip", "frame", None),
        P(("clip", "frame"), None),
        P(("clip", "frame"), None),
        P(("clip", "frame"), None),
        P(("clip", "frame"), None),
        P(("clip", "frame")),
        P(("clip", "frame"), None),
        P(None, ("clip", "frame"), None),
        P(None, ("clip", "frame"), None),
        P(None, ("clip", "frame"), None),
        P(None, ("clip", "frame"), None),
        P(None, ("clip", "frame")),
        P(None, ("clip", "frame"), None),
    )
    out_specs = (
        P("clip", "frame", None),
        P("clip", "frame", None),
        P(("clip", "frame"), None),
        P(("clip", "frame"), None),
        P(("clip", "frame"), None),
        P(("clip", "frame"), None),
        P(("clip", "frame")),
        P(("clip", "frame"), None),
        P(("clip", "frame"), None),
        P(("clip", "frame"), None),
        P(("clip", "frame"), None),
        P(("clip", "frame"), None),
        P(("clip", "frame")),
        P(("clip", "frame"), None),
        P(None, ("clip", "frame"), None),
        P(None, ("clip", "frame"), None),
        P(None, ("clip", "frame"), None),
        P(None, ("clip", "frame"), None),
        P(None, ("clip", "frame")),
        P(None, ("clip", "frame"), None),
    )
    return jax.shard_map(
        functools.partial(body, link_plan(mesh)),
        mesh=mesh,
        in_specs=in_specs,
        out_specs=out_specs,
        check_vma=False,
    )
```

```python
import functools
import math

import jax
import jax.numpy as jnp
from jax import lax
from jax.experimental import pallas as pl
from jax.experimental.pallas import tpu as pltpu
from jax.sharding import PartitionSpec as P

HEADS = 12
ADAM_STEP = 4


epsilon_norm = 1e-05
beta_first = 0.9
beta_second = 0.99
learn_rate = 0.03
decay_rate = 0.01
epsilon_adam = 1e-08
root_half = 0.7071067811865476
inv_root_two_pi = 0.3989422804014327


def norm_parts(inputs, norm_gain, norm_shift):
    average = jnp.mean(inputs, axis=-1, keepdims=True)
    centered = inputs - average
    spread = jnp.mean(centered * centered, axis=-1, keepdims=True)
    inv_std = lax.rsqrt(spread + epsilon_norm)
    normed = centered * inv_std
    return (normed * norm_gain + norm_shift, normed, inv_std)


def norm_backward(grad_normed, normed, inv_std, norm_gain):
    grad_gain = jnp.sum(grad_normed * normed, axis=0)
    grad_shift = jnp.sum(grad_normed, axis=0)
    scaled = grad_normed * norm_gain
    grad_input = inv_std * (
        scaled
        - jnp.mean(scaled, axis=-1, keepdims=True)
        - normed * jnp.mean(scaled * normed, axis=-1, keepdims=True)
    )
    return (grad_input, grad_gain, grad_shift)


def gelu_exact(inputs):
    return 0.5 * inputs * (1.0 + jax.scipy.special.erf(inputs * root_half))


def gelu_slope(inputs):
    return (
        0.5 * (1.0 + jax.scipy.special.erf(inputs * root_half))
        + inputs * jnp.exp(-0.5 * inputs * inputs) * inv_root_two_pi
    )


QUERY_CHUNK = 768
MASKED = -1e30


def attention_forward_kernel(q_ref, k_ref, v_ref, kbias_ref, o_ref, l_ref):
    head_size = q_ref.shape[1] // 2
    rows = q_ref.shape[0]
    kbias = kbias_ref[...]
    lane = lax.broadcasted_iota(jnp.int32, (QUERY_CHUNK, 2 * head_size), 1)

    def chunk_body(chunk, carry):
        span = pl.ds(pl.multiple_of(chunk * QUERY_CHUNK, QUERY_CHUNK), QUERY_CHUNK)
        mixed_parts = []
        totals = []
        for half in range(2):
            cols = pl.ds(half * head_size, head_size)
            query = q_ref[span, cols]
            key = k_ref[:, cols]
            value = v_ref[:, cols]
            scores = (
                lax.dot_general(
                    query, key, (((1,), (1,)), ((), ())), preferred_element_type=jnp.float32
                )
                + kbias
            )
            highest = jnp.max(scores, axis=1, keepdims=True)
            exponent = jnp.exp(scores - highest)
            denominator = jnp.sum(exponent, axis=1, keepdims=True)
            weights = (exponent * (1.0 / denominator)).astype(jnp.bfloat16)
            mixed_parts.append(jnp.dot(weights, value, preferred_element_type=jnp.float32))
            totals.append(highest + jnp.log(denominator))
        o_ref[span, :] = jnp.concatenate(mixed_parts, axis=1).astype(o_ref.dtype)
        l_ref[span, :] = jnp.where(lane < head_size, totals[0], totals[1])
        return carry

    lax.fori_loop(0, rows // QUERY_CHUNK, chunk_body, 0)


def attention_backward_kernel(
    q_ref, k_ref, v_ref, do_ref, l_ref, kbias_ref, dq_ref, dk_ref, dv_ref
):
    head_size = q_ref.shape[1] // 2
    rows = q_ref.shape[0]
    kbias = kbias_ref[...]
    dk_ref[...] = jnp.zeros_like(dk_ref)
    dv_ref[...] = jnp.zeros_like(dv_ref)
    for half in range(2):
        cols = pl.ds(half * head_size, head_size)

        def chunk_body(chunk, carry, cols=cols, half=half):
            span = pl.ds(pl.multiple_of(chunk * QUERY_CHUNK, QUERY_CHUNK), QUERY_CHUNK)
            key = k_ref[:, cols]
            value = v_ref[:, cols]
            query = q_ref[span, cols]
            grad_out = do_ref[span, cols]
            total = l_ref[span, pl.ds(half * head_size, 1)]
            scores = (
                lax.dot_general(
                    query, key, (((1,), (1,)), ((), ())), preferred_element_type=jnp.float32
                )
                + kbias
            )
            weights = jnp.exp(scores - total)
            grad_weights = lax.dot_general(
                grad_out, value, (((1,), (1,)), ((), ())), preferred_element_type=jnp.float32
            )
            delta = jnp.sum(weights * grad_weights, axis=1, keepdims=True)
            grad_scores = (weights * (grad_weights - delta)).astype(jnp.bfloat16)
            dq_ref[span, cols] = jnp.dot(
                grad_scores, key, preferred_element_type=jnp.float32
            ).astype(dq_ref.dtype)
            dk_ref[:, cols] += lax.dot_general(
                grad_scores, query, (((0,), (0,)), ((), ())), preferred_element_type=jnp.float32
            )
            dv_ref[:, cols] += lax.dot_general(
                weights.astype(jnp.bfloat16),
                grad_out,
                (((0,), (0,)), ((), ())),
                preferred_element_type=jnp.float32,
            )
            return carry

        lax.fori_loop(0, rows // QUERY_CHUNK, chunk_body, 0)


def pad_rows(values, rows):
    return jnp.pad(values, ((0, rows - values.shape[0]), (0, 0)))


def attention_pallas(queries, pairs, grad_out=None, totals=None, first_pair=0, pair_span=None):
    query_rows, model_width = queries.shape
    key_rows = pairs.shape[0]
    padded_q = -(-query_rows // QUERY_CHUNK) * QUERY_CHUNK
    padded_k = -(-key_rows // 128) * 128
    pair_count = model_width // 128
    q_pad = pad_rows(queries, padded_q)
    kv_pad = pad_rows(pairs, padded_k)
    kbias = jnp.where(jnp.arange(padded_k) < key_rows, 0.0, MASKED).astype(jnp.float32)[None, :]
    q_spec = pl.BlockSpec((padded_q, 128), lambda j: (0, j))
    k_spec = pl.BlockSpec((padded_k, 128), lambda j: (0, j))
    v_spec = pl.BlockSpec((padded_k, 128), lambda j: (0, j + pair_count))
    b_spec = pl.BlockSpec((1, padded_k), lambda j: (0, 0))
    params = pltpu.CompilerParams(vmem_limit_bytes=48 * 1024 * 1024)
    if grad_out is None:
        mixed, log_totals = pl.pallas_call(
            attention_forward_kernel,
            grid=(pair_count,),
            in_specs=[q_spec, k_spec, v_spec, b_spec],
            out_specs=[q_spec, q_spec],
            out_shape=[
                jax.ShapeDtypeStruct((padded_q, model_width), jnp.bfloat16),
                jax.ShapeDtypeStruct((padded_q, model_width), jnp.float32),
            ],
            compiler_params=params,
        )(q_pad, kv_pad, kv_pad, kbias)
        return mixed[:query_rows], log_totals
    do_pad = pad_rows(grad_out, padded_q)
    span = pair_count if pair_span is None else pair_span
    qi_spec = pl.BlockSpec((padded_q, 128), lambda j: (0, j + first_pair))
    ki_spec = pl.BlockSpec((padded_k, 128), lambda j: (0, j + first_pair))
    vi_spec = pl.BlockSpec((padded_k, 128), lambda j: (0, j + first_pair + pair_count))
    qo_spec = pl.BlockSpec((padded_q, 128), lambda j: (0, j))
    ko_spec = pl.BlockSpec((padded_k, 128), lambda j: (0, j))
    dq, dk, dv = pl.pallas_call(
        attention_backward_kernel,
        grid=(span,),
        in_specs=[qi_spec, ki_spec, vi_spec, qi_spec, qi_spec, b_spec],
        out_specs=[qo_spec, ko_spec, ko_spec],
        out_shape=[
            jax.ShapeDtypeStruct((padded_q, 128 * span), jnp.float32),
            jax.ShapeDtypeStruct((padded_k, 128 * span), jnp.float32),
            jax.ShapeDtypeStruct((padded_k, 128 * span), jnp.float32),
        ],
        compiler_params=params,
    )(q_pad, kv_pad, kv_pad, do_pad, totals, kbias)
    return dq[:query_rows], dk[:key_rows], dv[:key_rows]


def attend_forward(queries, keys_values, head_count):
    model_width = queries.shape[2]
    head_size = model_width // head_count
    score_scale = 1.0 / math.sqrt(head_size)

    def one_head(head_index):
        offset = head_index * head_size
        query_block = lax.dynamic_slice_in_dim(queries, offset, head_size, 2)
        key_block = lax.dynamic_slice_in_dim(keys_values, offset, head_size, 2)
        value_block = lax.dynamic_slice_in_dim(keys_values, model_width + offset, head_size, 2)
        scores = (
            jnp.einsum("cqd,ckd->cqk", query_block, key_block, preferred_element_type=jnp.float32)
            * score_scale
        )
        highest = jnp.max(scores, axis=-1, keepdims=True)
        exponent = jnp.exp(scores - highest)
        denominator = jnp.sum(exponent, axis=-1, keepdims=True)
        weights_soft = (exponent / denominator).astype(jnp.bfloat16)
        mixed = jnp.einsum(
            "cqk,ckd->cqd", weights_soft, value_block, preferred_element_type=jnp.float32
        )
        return (mixed, (highest + jnp.log(denominator))[..., 0])

    mixed, log_totals = lax.map(one_head, jnp.arange(head_count))
    clip_count, frame_count = (queries.shape[0], queries.shape[1])
    mixed = jnp.transpose(mixed, (1, 2, 0, 3)).reshape(clip_count, frame_count, model_width)
    return (mixed, log_totals)


def attend_backward(queries, keys_values, grad_mixed, log_totals, head_count):
    model_width = queries.shape[2]
    head_size = model_width // head_count
    score_scale = 1.0 / math.sqrt(head_size)

    def one_head_back(head_index):
        offset = head_index * head_size
        query_block = lax.dynamic_slice_in_dim(queries, offset, head_size, 2)
        key_block = lax.dynamic_slice_in_dim(keys_values, offset, head_size, 2)
        value_block = lax.dynamic_slice_in_dim(keys_values, model_width + offset, head_size, 2)
        grad_block = lax.dynamic_slice_in_dim(grad_mixed, offset, head_size, 2)
        totals = lax.dynamic_index_in_dim(log_totals, head_index, 0, keepdims=False)
        scores = (
            jnp.einsum("cqd,ckd->cqk", query_block, key_block, preferred_element_type=jnp.float32)
            * score_scale
        )
        weights_soft = jnp.exp(scores - totals[..., None])
        grad_weights = jnp.einsum(
            "cqd,ckd->cqk", grad_block, value_block, preferred_element_type=jnp.float32
        )
        delta = jnp.sum(weights_soft * grad_weights, axis=-1, keepdims=True)
        grad_scores = (weights_soft * (grad_weights - delta)).astype(jnp.bfloat16)
        grad_query = (
            jnp.einsum("cqk,ckd->cqd", grad_scores, key_block, preferred_element_type=jnp.float32)
            * score_scale
        )
        grad_key = (
            jnp.einsum("cqk,cqd->ckd", grad_scores, query_block, preferred_element_type=jnp.float32)
            * score_scale
        )
        grad_value = jnp.einsum(
            "cqk,cqd->ckd",
            weights_soft.astype(jnp.bfloat16),
            grad_block,
            preferred_element_type=jnp.float32,
        )
        return (grad_query, delta[..., 0], grad_key, grad_value)

    pieces = lax.map(one_head_back, jnp.arange(head_count))
    clip_count, frame_count = (queries.shape[0], queries.shape[1])
    clip_frames = keys_values.shape[1]
    grad_query = jnp.transpose(pieces[0], (1, 2, 0, 3)).reshape(
        clip_count, frame_count, model_width
    )
    grad_key = jnp.transpose(pieces[2], (1, 2, 0, 3)).reshape(clip_count, clip_frames, model_width)
    grad_value = jnp.transpose(pieces[3], (1, 2, 0, 3)).reshape(
        clip_count, clip_frames, model_width
    )
    return (grad_query, pieces[1], jnp.concatenate([grad_key, grad_value], axis=2))


def link_plan(mesh):
    devices = list(mesh.devices.reshape(-1))
    bit_count = len(devices).bit_length() - 1
    core_bit = 1
    for bit in range(bit_count):
        first, other = devices[0], devices[1 << bit]
        if getattr(first, "coords", None) is not None and tuple(first.coords) == tuple(other.coords):
            core_bit = bit
    others = [bit for bit in range(bit_count) if bit != core_bit]
    near, far = others[:-1], others[-1:]
    rotated = tuple(tuple(near[k:] + near[:k] + far) for k in range(3))
    inner = [bit for bit in near if bit != 0]
    late = tuple(tuple(inner[k:] + inner[:k] + [0] + far) for k in range(2))
    return bit_count, core_bit, rotated, late


def tree_reduce_scatter(terms, part_columns, orders, plan_bits, hooks=None):
    hooks = dict(hooks or {})
    tied = {}
    bit_count, core_bit = plan_bits
    device = lax.axis_index("clip") * lax.axis_size("frame") + lax.axis_index("frame")
    blocks = 1 << bit_count
    block_rows = terms.shape[0] // blocks
    data = terms.reshape((2,) * bit_count + (block_rows, terms.shape[1]))
    parts = [(data, list(range(bit_count - 1, -1, -1)))]
    plan = [(core_bit,)] + [tuple(order[stage] for order in orders) for stage in range(len(orders[0]))]
    for stage, stage_bits in enumerate(plan):
        if stage == 1:
            whole, bits = parts[0]
            parts = []
            offset = 0
            for width in part_columns:
                parts.append((whole[..., offset : offset + width], bits))
                offset += width
        keeps, sends = [], []
        for (part, part_bits), bit in zip(parts, stage_bits):
            axis = part_bits.index(bit)
            mine = (device >> bit) & 1
            keeps.append(lax.dynamic_index_in_dim(part, mine, axis=axis, keepdims=False))
            sends.append(
                lax.dynamic_index_in_dim(part, 1 - mine, axis=axis, keepdims=False).astype(jnp.bfloat16)
            )
        new_parts = []
        for keep, send, (part, part_bits), bit in zip(keeps, sends, parts, stage_bits):
            pairs = [(index, index ^ (1 << bit)) for index in range(blocks)]
            got = lax.ppermute(send, ("clip", "frame"), pairs)
            new_parts.append((keep + got.astype(jnp.float32), [b for b in part_bits if b != bit]))
        if stage in hooks:
            values, tied[stage] = lax.optimization_barrier(
                ([part for part, _ in new_parts], hooks[stage](tied))
            )
            new_parts = [(value, part_bits) for value, (_, part_bits) in zip(values, new_parts)]
        parts = new_parts
    return jnp.concatenate([part for part, _ in parts], axis=-1).astype(jnp.float32), tied


def tree_all_gather(local, part_columns, orders, plan_bits):
    bit_count, core_bit = plan_bits
    device = lax.axis_index("clip") * lax.axis_size("frame") + lax.axis_index("frame")
    canonical = list(range(bit_count - 1, -1, -1))

    def double(data, bits, bit):
        mine = (device >> bit) & 1
        pairs = [(index, index ^ (1 << bit)) for index in range(1 << bit_count)]
        got = lax.ppermute(data, ("clip", "frame"), pairs)
        new_bits = sorted(bits + [bit], reverse=True)
        axis = new_bits.index(bit)
        low_first = jnp.stack([data, got], axis=axis)
        high_first = jnp.stack([got, data], axis=axis)
        return jnp.where(mine == 0, low_first, high_first), new_bits

    parts = []
    offset = 0
    for width in part_columns:
        parts.append((local[:, offset : offset + width], []))
        offset += width
    reversed_orders = [list(reversed(order)) for order in orders]
    for stage in range(len(reversed_orders[0])):
        parts = [double(part, bits, order[stage]) for (part, bits), order in zip(parts, reversed_orders)]
    whole = jnp.concatenate([part for part, _ in parts], axis=-1)
    whole, bits = double(whole, parts[0][1], core_bit)
    assert bits == canonical
    return whole.reshape((1 << bit_count) * local.shape[0], local.shape[1])


def adam_step(weight, moments, gradient):
    first = beta_first * moments[0] + (1.0 - beta_first) * gradient
    second = beta_second * moments[1] + (1.0 - beta_second) * gradient * gradient
    first_hat = first / (1.0 - beta_first**ADAM_STEP)
    second_hat = second / (1.0 - beta_second**ADAM_STEP)
    change = -learn_rate * (first_hat / (jnp.sqrt(second_hat) + epsilon_adam) + decay_rate * weight)
    return (change, jnp.stack([first, second]))


def body(
    plan,
    inputs,
    cotangent,
    project_in,
    project_out,
    expand_weight,
    shrink_weight,
    expand_bias,
    vectors,
    moments_in,
    moments_out,
    moments_expand,
    moments_shrink,
    moments_bias,
    moments_vectors,
):
    clip_count, frame_count, model_width = inputs.shape
    row_count = clip_count * frame_count
    head_count = HEADS
    shard_rows = project_in.shape[0]
    wide_in = project_in.shape[1]
    ff_width = expand_weight.shape[1]
    swap = [(0, 1), (1, 0)]
    everyone = ("clip", "frame")

    small = jnp.concatenate(
        [
            vectors,
            expand_bias.reshape(shard_rows, -1),
            jnp.zeros((shard_rows, 128 - vectors.shape[1] - expand_bias.shape[0] // shard_rows), jnp.float32),
        ],
        axis=1,
    )
    first_pack = jnp.concatenate([project_in, small], axis=1).astype(jnp.bfloat16)
    second_pack = jnp.concatenate(
        [project_out, expand_weight, shrink_weight.reshape(shard_rows, -1)], axis=1
    ).astype(jnp.bfloat16)
    bit_count, core_bit, rotated_orders, late_orders = plan
    first_full = tree_all_gather(first_pack, (896, 768, 768), rotated_orders, (bit_count, core_bit))
    second_full = lax.all_gather(second_pack, everyone, axis=0, tiled=True)
    full_in = first_full[:, :wide_in]
    small_full = first_full[:, wide_in:].astype(jnp.float32)
    column_set = small_full[:, : vectors.shape[1]]
    full_bias = small_full[:, vectors.shape[1] : vectors.shape[1] + ff_width // model_width].reshape(-1)
    full_out = second_full[:, :model_width]
    full_expand = second_full[:, model_width : model_width + ff_width]
    full_shrink = second_full[:, model_width + ff_width :].reshape(ff_width, model_width)

    frames_rows = inputs.reshape(row_count, model_width).astype(jnp.float32)
    normed_first, plain_first, inv_first = norm_parts(
        frames_rows, column_set[:, 0], column_set[:, 1]
    )
    hidden_first = normed_first.astype(jnp.bfloat16)
    partner_rows = lax.ppermute(inputs, "frame", swap).reshape(row_count, model_width)
    hidden_partner = norm_parts(
        partner_rows.astype(jnp.float32), column_set[:, 0], column_set[:, 1]
    )[0].astype(jnp.bfloat16)
    bias_in = jnp.concatenate(
        [column_set[:, 2], jnp.zeros((model_width,), jnp.float32), column_set[:, 3]]
    )
    projected = (
        jnp.dot(hidden_first, full_in, preferred_element_type=jnp.float32) + bias_in
    ).astype(jnp.bfloat16)
    partner_pairs = (
        jnp.dot(hidden_partner, full_in[:, model_width:], preferred_element_type=jnp.float32)
        + bias_in[model_width:]
    ).astype(jnp.bfloat16)
    queries = projected[:, :model_width].reshape(clip_count, frame_count, model_width)
    clip_pairs = jnp.concatenate([projected[:, model_width:], partner_pairs], axis=0).reshape(
        clip_count, 2 * frame_count, 2 * model_width
    )
    score_scale = 1.0 / math.sqrt(model_width // head_count)
    scaled_queries = (projected[:, :model_width] * score_scale).astype(jnp.bfloat16)
    pair_rows = clip_pairs.reshape(2 * row_count, 2 * model_width)
    mixed_low, log_totals = attention_pallas(scaled_queries, pair_rows)
    attended = jnp.dot(mixed_low, full_out, preferred_element_type=jnp.float32) + column_set[:, 4]
    residual = frames_rows + attended
    normed_second, plain_second, inv_second = norm_parts(
        residual, column_set[:, 5], column_set[:, 6]
    )
    hidden_second = normed_second.astype(jnp.bfloat16)
    preact = jnp.dot(hidden_second, full_expand, preferred_element_type=jnp.float32) + full_bias
    activated = gelu_exact(preact).astype(jnp.bfloat16)
    result = (
        residual
        + jnp.dot(activated, full_shrink, preferred_element_type=jnp.float32)
        + column_set[:, 7]
    )
    output = result.astype(jnp.bfloat16).reshape(inputs.shape)

    grad_result = cotangent.reshape(row_count, model_width)
    grad_shrink_term = jnp.dot(
        activated.T, grad_result, preferred_element_type=jnp.float32
    ).astype(jnp.bfloat16)
    grad_down_bias = jnp.sum(grad_result.astype(jnp.float32), axis=0)
    grad_activated = jnp.dot(grad_result, full_shrink.T, preferred_element_type=jnp.float32)
    grad_preact = (grad_activated * gelu_slope(preact)).astype(jnp.bfloat16)
    grad_expand_term = jnp.dot(
        hidden_second.T, grad_preact, preferred_element_type=jnp.float32
    ).astype(jnp.bfloat16)
    grad_bias_term = jnp.sum(grad_preact.astype(jnp.float32), axis=0)
    grad_hidden_second = jnp.dot(grad_preact, full_expand.T, preferred_element_type=jnp.float32)
    norm_term_second, gain_second, shift_second = norm_backward(
        grad_hidden_second, plain_second, inv_second, column_set[:, 5]
    )
    grad_residual = grad_result.astype(jnp.float32) + norm_term_second
    grad_attended = grad_residual.astype(jnp.bfloat16)
    grad_out_term = jnp.dot(
        mixed_low.T, grad_attended, preferred_element_type=jnp.float32
    ).astype(jnp.bfloat16)
    grad_out_bias = jnp.sum(grad_attended.astype(jnp.float32), axis=0)
    late_terms = jnp.concatenate(
        [grad_shrink_term.reshape(model_width, -1), grad_expand_term, grad_out_term], axis=1
    )
    grad_mixed = jnp.dot(grad_attended, full_out.T, preferred_element_type=jnp.float32).astype(
        jnp.bfloat16
    )
    piece_pairs = 1
    piece_count = model_width // 128 // piece_pairs
    stage_count = 1 + len(late_orders[0])
    hooked = list(range(1, min(piece_count, stage_count)))

    def run_piece(index, mixed_grads):
        return attention_pallas(
            scaled_queries, pair_rows, mixed_grads, log_totals, index * piece_pairs, piece_pairs
        )

    def piece_hook(index):
        return lambda tied: (run_piece(index, tied[index - 1][1]), tied[index - 1][1])

    hooks = {0: lambda tied: ((), grad_mixed)}
    hooks.update({index: piece_hook(index) for index in hooked})
    pieces = [run_piece(0, grad_mixed)]
    owned_late, tied = tree_reduce_scatter(
        late_terms, (3456, 3456), late_orders, (bit_count, core_bit), hooks
    )
    pieces += [tied[index][0] for index in hooked]
    last_mixed = tied[hooked[-1]][1] if hooked else grad_mixed
    pieces += [run_piece(index, last_mixed) for index in range(len(hooked) + 1, piece_count)]
    finished = []
    for grad_query, grad_keys, grad_values in pieces:
        terms = jnp.concatenate([grad_keys, grad_values], axis=1)
        returned = lax.ppermute(terms[row_count:].astype(jnp.bfloat16), "frame", swap)
        finished.append((grad_query, terms[:row_count] + returned.astype(jnp.float32)))
    piece_width = finished[0][0].shape[1]
    grad_projected = jnp.concatenate(
        [
            (jnp.concatenate([query for query, _ in finished], axis=1) * score_scale).astype(
                jnp.bfloat16
            ),
            jnp.concatenate(
                [pair[:, :piece_width] for _, pair in finished]
                + [pair[:, piece_width:] for _, pair in finished],
                axis=1,
            ).astype(jnp.bfloat16),
        ],
        axis=1,
    )
    grad_in_term = jnp.dot(
        hidden_first.T, grad_projected, preferred_element_type=jnp.float32
    ).astype(jnp.bfloat16)
    projected_sums = jnp.sum(grad_projected.astype(jnp.float32), axis=0)
    grad_query_bias = projected_sums[:model_width]
    grad_value_bias = projected_sums[2 * model_width :]
    grad_hidden_first = jnp.dot(grad_projected, full_in.T, preferred_element_type=jnp.float32)
    norm_term_first, gain_first, shift_first = norm_backward(
        grad_hidden_first, plain_first, inv_first, column_set[:, 0]
    )
    grad_inputs = (grad_residual + norm_term_first).astype(jnp.bfloat16).reshape(inputs.shape)
    grad_columns = jnp.stack(
        [
            gain_first,
            shift_first,
            grad_query_bias,
            grad_value_bias,
            grad_out_bias,
            gain_second,
            shift_second,
            grad_down_bias,
        ],
        axis=1,
    )
    small_grads = jnp.concatenate(
        [
            grad_columns,
            grad_bias_term.reshape(model_width, -1),
            jnp.zeros((model_width, 128 - 12), jnp.float32),
        ],
        axis=1,
    ).astype(jnp.bfloat16)
    owned_first = tree_reduce_scatter(
        jnp.concatenate([grad_in_term, small_grads], axis=1),
        (896, 768, 768),
        rotated_orders,
        (bit_count, core_bit),
    )[0]
    owned_in = owned_first[:, :wide_in]
    owned_vectors = owned_first[:, wide_in : wide_in + vectors.shape[1]]
    owned_bias = owned_first[:, wide_in + vectors.shape[1] : wide_in + 12].reshape(-1)
    owned_shrink = owned_late[:, :ff_width].reshape(shrink_weight.shape)
    owned_expand = owned_late[:, ff_width : 2 * ff_width]
    owned_out = owned_late[:, 2 * ff_width :]
    new_in, mom_in = adam_step(project_in, moments_in, owned_in)
    new_out, mom_out = adam_step(project_out, moments_out, owned_out)
    new_expand, mom_expand = adam_step(expand_weight, moments_expand, owned_expand)
    new_shrink, mom_shrink = adam_step(shrink_weight, moments_shrink, owned_shrink)
    new_bias, mom_bias = adam_step(expand_bias, moments_bias, owned_bias)
    new_vectors, mom_vectors = adam_step(vectors, moments_vectors, owned_vectors)
    return (
        output,
        grad_inputs,
        owned_in,
        owned_out,
        owned_expand,
        owned_shrink,
        owned_bias,
        owned_vectors,
        new_in,
        new_out,
        new_expand,
        new_shrink,
        new_bias,
        new_vectors,
        mom_in,
        mom_out,
        mom_expand,
        mom_shrink,
        mom_bias,
        mom_vectors,
    )


def solution(mesh):
    in_specs = (
        P("clip", "frame", None),
        P("clip", "frame", None),
        P(("clip", "frame"), None),
        P(("clip", "frame"), None),
        P(("clip", "frame"), None),
        P(("clip", "frame"), None),
        P(("clip", "frame")),
        P(("clip", "frame"), None),
        P(None, ("clip", "frame"), None),
        P(None, ("clip", "frame"), None),
        P(None, ("clip", "frame"), None),
        P(None, ("clip", "frame"), None),
        P(None, ("clip", "frame")),
        P(None, ("clip", "frame"), None),
    )
    out_specs = (
        P("clip", "frame", None),
        P("clip", "frame", None),
        P(("clip", "frame"), None),
        P(("clip", "frame"), None),
        P(("clip", "frame"), None),
        P(("clip", "frame"), None),
        P(("clip", "frame")),
        P(("clip", "frame"), None),
        P(("clip", "frame"), None),
        P(("clip", "frame"), None),
        P(("clip", "frame"), None),
        P(("clip", "frame"), None),
        P(("clip", "frame")),
        P(("clip", "frame"), None),
        P(None, ("clip", "frame"), None),
        P(None, ("clip", "frame"), None),
        P(None, ("clip", "frame"), None),
        P(None, ("clip", "frame"), None),
        P(None, ("clip", "frame")),
        P(None, ("clip", "frame"), None),
    )
    return jax.shard_map(
        functools.partial(body, link_plan(mesh)),
        mesh=mesh,
        in_specs=in_specs,
        out_specs=out_specs,
        check_vma=False,
    )
```

```python
import functools
import math

import jax
import jax.numpy as jnp
from jax import lax
from jax.experimental import pallas as pl
from jax.experimental.pallas import tpu as pltpu
from jax.sharding import PartitionSpec as P

HEADS = 12
ADAM_STEP = 4


epsilon_norm = 1e-05
beta_first = 0.9
beta_second = 0.99
learn_rate = 0.03
decay_rate = 0.01
epsilon_adam = 1e-08
root_half = 0.7071067811865476
inv_root_two_pi = 0.3989422804014327


def norm_parts(inputs, norm_gain, norm_shift):
    average = jnp.mean(inputs, axis=-1, keepdims=True)
    centered = inputs - average
    spread = jnp.mean(centered * centered, axis=-1, keepdims=True)
    inv_std = lax.rsqrt(spread + epsilon_norm)
    normed = centered * inv_std
    return (normed * norm_gain + norm_shift, normed, inv_std)


def norm_backward(grad_normed, normed, inv_std, norm_gain):
    grad_gain = jnp.sum(grad_normed * normed, axis=0)
    grad_shift = jnp.sum(grad_normed, axis=0)
    scaled = grad_normed * norm_gain
    grad_input = inv_std * (
        scaled
        - jnp.mean(scaled, axis=-1, keepdims=True)
        - normed * jnp.mean(scaled * normed, axis=-1, keepdims=True)
    )
    return (grad_input, grad_gain, grad_shift)


def gelu_exact(inputs):
    return 0.5 * inputs * (1.0 + jax.scipy.special.erf(inputs * root_half))


def gelu_slope(inputs):
    return (
        0.5 * (1.0 + jax.scipy.special.erf(inputs * root_half))
        + inputs * jnp.exp(-0.5 * inputs * inputs) * inv_root_two_pi
    )


QUERY_CHUNK = 384
MASKED = -1e30


def attention_forward_kernel(q_ref, k_ref, v_ref, kbias_ref, o_ref, l_ref):
    head_size = q_ref.shape[1] // 2
    rows = q_ref.shape[0]
    kbias = kbias_ref[...]
    lane = lax.broadcasted_iota(jnp.int32, (QUERY_CHUNK, 2 * head_size), 1)

    def chunk_body(chunk, carry):
        span = pl.ds(pl.multiple_of(chunk * QUERY_CHUNK, QUERY_CHUNK), QUERY_CHUNK)
        mixed_parts = []
        totals = []
        for half in range(2):
            cols = pl.ds(half * head_size, head_size)
            query = q_ref[span, cols]
            key = k_ref[:, cols]
            value = v_ref[:, cols]
            scores = (
                lax.dot_general(
                    query, key, (((1,), (1,)), ((), ())), preferred_element_type=jnp.float32
                )
                + kbias
            )
            highest = jnp.max(scores, axis=1, keepdims=True)
            exponent = jnp.exp(scores - highest)
            denominator = jnp.sum(exponent, axis=1, keepdims=True)
            weights = (exponent * (1.0 / denominator)).astype(jnp.bfloat16)
            mixed_parts.append(jnp.dot(weights, value, preferred_element_type=jnp.float32))
            totals.append(highest + jnp.log(denominator))
        o_ref[span, :] = jnp.concatenate(mixed_parts, axis=1).astype(o_ref.dtype)
        l_ref[span, :] = jnp.where(lane < head_size, totals[0], totals[1])
        return carry

    lax.fori_loop(0, rows // QUERY_CHUNK, chunk_body, 0)


def attention_backward_kernel(
    q_ref, k_ref, v_ref, do_ref, l_ref, kbias_ref, dq_ref, dk_ref, dv_ref
):
    head_size = q_ref.shape[1] // 2
    rows = q_ref.shape[0]
    kbias = kbias_ref[...]
    dk_ref[...] = jnp.zeros_like(dk_ref)
    dv_ref[...] = jnp.zeros_like(dv_ref)
    for half in range(2):
        cols = pl.ds(half * head_size, head_size)

        def chunk_body(chunk, carry, cols=cols, half=half):
            span = pl.ds(pl.multiple_of(chunk * QUERY_CHUNK, QUERY_CHUNK), QUERY_CHUNK)
            key = k_ref[:, cols]
            value = v_ref[:, cols]
            query = q_ref[span, cols]
            grad_out = do_ref[span, cols]
            total = l_ref[span, pl.ds(half * head_size, 1)]
            scores = (
                lax.dot_general(
                    query, key, (((1,), (1,)), ((), ())), preferred_element_type=jnp.float32
                )
                + kbias
            )
            weights = jnp.exp(scores - total)
            grad_weights = lax.dot_general(
                grad_out, value, (((1,), (1,)), ((), ())), preferred_element_type=jnp.float32
            )
            delta = jnp.sum(weights * grad_weights, axis=1, keepdims=True)
            grad_scores = (weights * (grad_weights - delta)).astype(jnp.bfloat16)
            dq_ref[span, cols] = jnp.dot(
                grad_scores, key, preferred_element_type=jnp.float32
            ).astype(dq_ref.dtype)
            dk_ref[:, cols] += lax.dot_general(
                grad_scores, query, (((0,), (0,)), ((), ())), preferred_element_type=jnp.float32
            )
            dv_ref[:, cols] += lax.dot_general(
                weights.astype(jnp.bfloat16),
                grad_out,
                (((0,), (0,)), ((), ())),
                preferred_element_type=jnp.float32,
            )
            return carry

        lax.fori_loop(0, rows // QUERY_CHUNK, chunk_body, 0)


def pad_rows(values, rows):
    return jnp.pad(values, ((0, rows - values.shape[0]), (0, 0)))


def attention_pallas(queries, pairs, grad_out=None, totals=None, first_pair=0, pair_span=None):
    query_rows, model_width = queries.shape
    key_rows = pairs.shape[0]
    padded_q = -(-query_rows // QUERY_CHUNK) * QUERY_CHUNK
    padded_k = -(-key_rows // 128) * 128
    pair_count = model_width // 128
    q_pad = pad_rows(queries, padded_q)
    kv_pad = pad_rows(pairs, padded_k)
    kbias = jnp.where(jnp.arange(padded_k) < key_rows, 0.0, MASKED).astype(jnp.float32)[None, :]
    q_spec = pl.BlockSpec((padded_q, 128), lambda j: (0, j))
    k_spec = pl.BlockSpec((padded_k, 128), lambda j: (0, j))
    v_spec = pl.BlockSpec((padded_k, 128), lambda j: (0, j + pair_count))
    b_spec = pl.BlockSpec((1, padded_k), lambda j: (0, 0))
    params = pltpu.CompilerParams(vmem_limit_bytes=48 * 1024 * 1024)
    if grad_out is None:
        mixed, log_totals = pl.pallas_call(
            attention_forward_kernel,
            grid=(pair_count,),
            in_specs=[q_spec, k_spec, v_spec, b_spec],
            out_specs=[q_spec, q_spec],
            out_shape=[
                jax.ShapeDtypeStruct((padded_q, model_width), jnp.bfloat16),
                jax.ShapeDtypeStruct((padded_q, model_width), jnp.float32),
            ],
            compiler_params=params,
        )(q_pad, kv_pad, kv_pad, kbias)
        return mixed[:query_rows], log_totals
    do_pad = pad_rows(grad_out, padded_q)
    span = pair_count if pair_span is None else pair_span
    qi_spec = pl.BlockSpec((padded_q, 128), lambda j: (0, j + first_pair))
    ki_spec = pl.BlockSpec((padded_k, 128), lambda j: (0, j + first_pair))
    vi_spec = pl.BlockSpec((padded_k, 128), lambda j: (0, j + first_pair + pair_count))
    qo_spec = pl.BlockSpec((padded_q, 128), lambda j: (0, j))
    ko_spec = pl.BlockSpec((padded_k, 128), lambda j: (0, j))
    dq, dk, dv = pl.pallas_call(
        attention_backward_kernel,
        grid=(span,),
        in_specs=[qi_spec, ki_spec, vi_spec, qi_spec, qi_spec, b_spec],
        out_specs=[qo_spec, ko_spec, ko_spec],
        out_shape=[
            jax.ShapeDtypeStruct((padded_q, 128 * span), jnp.float32),
            jax.ShapeDtypeStruct((padded_k, 128 * span), jnp.float32),
            jax.ShapeDtypeStruct((padded_k, 128 * span), jnp.float32),
        ],
        compiler_params=params,
    )(q_pad, kv_pad, kv_pad, do_pad, totals, kbias)
    return dq[:query_rows], dk[:key_rows], dv[:key_rows]


def attend_forward(queries, keys_values, head_count):
    model_width = queries.shape[2]
    head_size = model_width // head_count
    score_scale = 1.0 / math.sqrt(head_size)

    def one_head(head_index):
        offset = head_index * head_size
        query_block = lax.dynamic_slice_in_dim(queries, offset, head_size, 2)
        key_block = lax.dynamic_slice_in_dim(keys_values, offset, head_size, 2)
        value_block = lax.dynamic_slice_in_dim(keys_values, model_width + offset, head_size, 2)
        scores = (
            jnp.einsum("cqd,ckd->cqk", query_block, key_block, preferred_element_type=jnp.float32)
            * score_scale
        )
        highest = jnp.max(scores, axis=-1, keepdims=True)
        exponent = jnp.exp(scores - highest)
        denominator = jnp.sum(exponent, axis=-1, keepdims=True)
        weights_soft = (exponent / denominator).astype(jnp.bfloat16)
        mixed = jnp.einsum(
            "cqk,ckd->cqd", weights_soft, value_block, preferred_element_type=jnp.float32
        )
        return (mixed, (highest + jnp.log(denominator))[..., 0])

    mixed, log_totals = lax.map(one_head, jnp.arange(head_count))
    clip_count, frame_count = (queries.shape[0], queries.shape[1])
    mixed = jnp.transpose(mixed, (1, 2, 0, 3)).reshape(clip_count, frame_count, model_width)
    return (mixed, log_totals)


def attend_backward(queries, keys_values, grad_mixed, log_totals, head_count):
    model_width = queries.shape[2]
    head_size = model_width // head_count
    score_scale = 1.0 / math.sqrt(head_size)

    def one_head_back(head_index):
        offset = head_index * head_size
        query_block = lax.dynamic_slice_in_dim(queries, offset, head_size, 2)
        key_block = lax.dynamic_slice_in_dim(keys_values, offset, head_size, 2)
        value_block = lax.dynamic_slice_in_dim(keys_values, model_width + offset, head_size, 2)
        grad_block = lax.dynamic_slice_in_dim(grad_mixed, offset, head_size, 2)
        totals = lax.dynamic_index_in_dim(log_totals, head_index, 0, keepdims=False)
        scores = (
            jnp.einsum("cqd,ckd->cqk", query_block, key_block, preferred_element_type=jnp.float32)
            * score_scale
        )
        weights_soft = jnp.exp(scores - totals[..., None])
        grad_weights = jnp.einsum(
            "cqd,ckd->cqk", grad_block, value_block, preferred_element_type=jnp.float32
        )
        delta = jnp.sum(weights_soft * grad_weights, axis=-1, keepdims=True)
        grad_scores = (weights_soft * (grad_weights - delta)).astype(jnp.bfloat16)
        grad_query = (
            jnp.einsum("cqk,ckd->cqd", grad_scores, key_block, preferred_element_type=jnp.float32)
            * score_scale
        )
        grad_key = (
            jnp.einsum("cqk,cqd->ckd", grad_scores, query_block, preferred_element_type=jnp.float32)
            * score_scale
        )
        grad_value = jnp.einsum(
            "cqk,cqd->ckd",
            weights_soft.astype(jnp.bfloat16),
            grad_block,
            preferred_element_type=jnp.float32,
        )
        return (grad_query, delta[..., 0], grad_key, grad_value)

    pieces = lax.map(one_head_back, jnp.arange(head_count))
    clip_count, frame_count = (queries.shape[0], queries.shape[1])
    clip_frames = keys_values.shape[1]
    grad_query = jnp.transpose(pieces[0], (1, 2, 0, 3)).reshape(
        clip_count, frame_count, model_width
    )
    grad_key = jnp.transpose(pieces[2], (1, 2, 0, 3)).reshape(clip_count, clip_frames, model_width)
    grad_value = jnp.transpose(pieces[3], (1, 2, 0, 3)).reshape(
        clip_count, clip_frames, model_width
    )
    return (grad_query, pieces[1], jnp.concatenate([grad_key, grad_value], axis=2))


def link_plan(mesh):
    devices = list(mesh.devices.reshape(-1))
    bit_count = len(devices).bit_length() - 1
    core_bit = 1
    for bit in range(bit_count):
        first, other = devices[0], devices[1 << bit]
        if getattr(first, "coords", None) is not None and tuple(first.coords) == tuple(other.coords):
            core_bit = bit
    others = [bit for bit in range(bit_count) if bit != core_bit]
    near, far = others[:-1], others[-1:]
    rotated = tuple(tuple(near[k:] + near[:k] + far) for k in range(3))
    inner = [bit for bit in near if bit != 0]
    late = tuple(tuple(inner[k:] + inner[:k] + [0] + far) for k in range(2))
    return bit_count, core_bit, rotated, late


def tree_reduce_scatter(terms, part_columns, orders, plan_bits, hooks=None):
    hooks = dict(hooks or {})
    tied = {}
    bit_count, core_bit = plan_bits
    device = lax.axis_index("clip") * lax.axis_size("frame") + lax.axis_index("frame")
    blocks = 1 << bit_count
    block_rows = terms.shape[0] // blocks
    data = terms.reshape((2,) * bit_count + (block_rows, terms.shape[1]))
    parts = [(data, list(range(bit_count - 1, -1, -1)))]
    plan = [(core_bit,)] + [tuple(order[stage] for order in orders) for stage in range(len(orders[0]))]
    for stage, stage_bits in enumerate(plan):
        if stage == 1:
            whole, bits = parts[0]
            parts = []
            offset = 0
            for width in part_columns:
                parts.append((whole[..., offset : offset + width], bits))
                offset += width
        keeps, sends = [], []
        for (part, part_bits), bit in zip(parts, stage_bits):
            axis = part_bits.index(bit)
            mine = (device >> bit) & 1
            keeps.append(lax.dynamic_index_in_dim(part, mine, axis=axis, keepdims=False))
            sends.append(
                lax.dynamic_index_in_dim(part, 1 - mine, axis=axis, keepdims=False).astype(jnp.bfloat16)
            )
        new_parts = []
        for keep, send, (part, part_bits), bit in zip(keeps, sends, parts, stage_bits):
            pairs = [(index, index ^ (1 << bit)) for index in range(blocks)]
            got = lax.ppermute(send, ("clip", "frame"), pairs)
            new_parts.append((keep + got.astype(jnp.float32), [b for b in part_bits if b != bit]))
        if stage in hooks:
            values, tied[stage] = lax.optimization_barrier(
                ([part for part, _ in new_parts], hooks[stage](tied))
            )
            new_parts = [(value, part_bits) for value, (_, part_bits) in zip(values, new_parts)]
        parts = new_parts
    return jnp.concatenate([part for part, _ in parts], axis=-1).astype(jnp.float32), tied


def tree_all_gather(local, part_columns, orders, plan_bits):
    bit_count, core_bit = plan_bits
    device = lax.axis_index("clip") * lax.axis_size("frame") + lax.axis_index("frame")
    canonical = list(range(bit_count - 1, -1, -1))

    def double(data, bits, bit):
        mine = (device >> bit) & 1
        pairs = [(index, index ^ (1 << bit)) for index in range(1 << bit_count)]
        got = lax.ppermute(data, ("clip", "frame"), pairs)
        new_bits = sorted(bits + [bit], reverse=True)
        axis = new_bits.index(bit)
        low_first = jnp.stack([data, got], axis=axis)
        high_first = jnp.stack([got, data], axis=axis)
        return jnp.where(mine == 0, low_first, high_first), new_bits

    parts = []
    offset = 0
    for width in part_columns:
        parts.append((local[:, offset : offset + width], []))
        offset += width
    reversed_orders = [list(reversed(order)) for order in orders]
    for stage in range(len(reversed_orders[0])):
        parts = [double(part, bits, order[stage]) for (part, bits), order in zip(parts, reversed_orders)]
    whole = jnp.concatenate([part for part, _ in parts], axis=-1)
    whole, bits = double(whole, parts[0][1], core_bit)
    assert bits == canonical
    return whole.reshape((1 << bit_count) * local.shape[0], local.shape[1])


def adam_step(weight, moments, gradient):
    first = beta_first * moments[0] + (1.0 - beta_first) * gradient
    second = beta_second * moments[1] + (1.0 - beta_second) * gradient * gradient
    first_hat = first / (1.0 - beta_first**ADAM_STEP)
    second_hat = second / (1.0 - beta_second**ADAM_STEP)
    change = -learn_rate * (first_hat / (jnp.sqrt(second_hat) + epsilon_adam) + decay_rate * weight)
    return (change, jnp.stack([first, second]))


def body(
    plan,
    inputs,
    cotangent,
    project_in,
    project_out,
    expand_weight,
    shrink_weight,
    expand_bias,
    vectors,
    moments_in,
    moments_out,
    moments_expand,
    moments_shrink,
    moments_bias,
    moments_vectors,
):
    clip_count, frame_count, model_width = inputs.shape
    row_count = clip_count * frame_count
    head_count = HEADS
    shard_rows = project_in.shape[0]
    wide_in = project_in.shape[1]
    ff_width = expand_weight.shape[1]
    swap = [(0, 1), (1, 0)]
    everyone = ("clip", "frame")

    small = jnp.concatenate(
        [
            vectors,
            expand_bias.reshape(shard_rows, -1),
            jnp.zeros((shard_rows, 128 - vectors.shape[1] - expand_bias.shape[0] // shard_rows), jnp.float32),
        ],
        axis=1,
    )
    first_pack = jnp.concatenate([project_in, small], axis=1).astype(jnp.bfloat16)
    second_pack = jnp.concatenate(
        [project_out, expand_weight, shrink_weight.reshape(shard_rows, -1)], axis=1
    ).astype(jnp.bfloat16)
    bit_count, core_bit, rotated_orders, late_orders = plan
    first_full = tree_all_gather(first_pack, (896, 768, 768), rotated_orders, (bit_count, core_bit))
    second_full = lax.all_gather(second_pack, everyone, axis=0, tiled=True)
    full_in = first_full[:, :wide_in]
    small_full = first_full[:, wide_in:].astype(jnp.float32)
    column_set = small_full[:, : vectors.shape[1]]
    full_bias = small_full[:, vectors.shape[1] : vectors.shape[1] + ff_width // model_width].reshape(-1)
    full_out = second_full[:, :model_width]
    full_expand = second_full[:, model_width : model_width + ff_width]
    full_shrink = second_full[:, model_width + ff_width :].reshape(ff_width, model_width)

    frames_rows = inputs.reshape(row_count, model_width).astype(jnp.float32)
    normed_first, plain_first, inv_first = norm_parts(
        frames_rows, column_set[:, 0], column_set[:, 1]
    )
    hidden_first = normed_first.astype(jnp.bfloat16)
    partner_rows = lax.ppermute(inputs, "frame", swap).reshape(row_count, model_width)
    hidden_partner = norm_parts(
        partner_rows.astype(jnp.float32), column_set[:, 0], column_set[:, 1]
    )[0].astype(jnp.bfloat16)
    bias_in = jnp.concatenate(
        [column_set[:, 2], jnp.zeros((model_width,), jnp.float32), column_set[:, 3]]
    )
    projected = (
        jnp.dot(hidden_first, full_in, preferred_element_type=jnp.float32) + bias_in
    ).astype(jnp.bfloat16)
    partner_pairs = (
        jnp.dot(hidden_partner, full_in[:, model_width:], preferred_element_type=jnp.float32)
        + bias_in[model_width:]
    ).astype(jnp.bfloat16)
    queries = projected[:, :model_width].reshape(clip_count, frame_count, model_width)
    clip_pairs = jnp.concatenate([projected[:, model_width:], partner_pairs], axis=0).reshape(
        clip_count, 2 * frame_count, 2 * model_width
    )
    score_scale = 1.0 / math.sqrt(model_width // head_count)
    scaled_queries = (projected[:, :model_width] * score_scale).astype(jnp.bfloat16)
    pair_rows = clip_pairs.reshape(2 * row_count, 2 * model_width)
    mixed_low, log_totals = attention_pallas(scaled_queries, pair_rows)
    attended = jnp.dot(mixed_low, full_out, preferred_element_type=jnp.float32) + column_set[:, 4]
    residual = frames_rows + attended
    normed_second, plain_second, inv_second = norm_parts(
        residual, column_set[:, 5], column_set[:, 6]
    )
    hidden_second = normed_second.astype(jnp.bfloat16)
    preact = jnp.dot(hidden_second, full_expand, preferred_element_type=jnp.float32) + full_bias
    activated = gelu_exact(preact).astype(jnp.bfloat16)
    result = (
        residual
        + jnp.dot(activated, full_shrink, preferred_element_type=jnp.float32)
        + column_set[:, 7]
    )
    output = result.astype(jnp.bfloat16).reshape(inputs.shape)

    grad_result = cotangent.reshape(row_count, model_width)
    grad_shrink_term = jnp.dot(
        activated.T, grad_result, preferred_element_type=jnp.float32
    ).astype(jnp.bfloat16)
    grad_down_bias = jnp.sum(grad_result.astype(jnp.float32), axis=0)
    grad_activated = jnp.dot(grad_result, full_shrink.T, preferred_element_type=jnp.float32)
    grad_preact = (grad_activated * gelu_slope(preact)).astype(jnp.bfloat16)
    grad_expand_term = jnp.dot(
        hidden_second.T, grad_preact, preferred_element_type=jnp.float32
    ).astype(jnp.bfloat16)
    grad_bias_term = jnp.sum(grad_preact.astype(jnp.float32), axis=0)
    grad_hidden_second = jnp.dot(grad_preact, full_expand.T, preferred_element_type=jnp.float32)
    norm_term_second, gain_second, shift_second = norm_backward(
        grad_hidden_second, plain_second, inv_second, column_set[:, 5]
    )
    grad_residual = grad_result.astype(jnp.float32) + norm_term_second
    grad_attended = grad_residual.astype(jnp.bfloat16)
    grad_out_term = jnp.dot(
        mixed_low.T, grad_attended, preferred_element_type=jnp.float32
    ).astype(jnp.bfloat16)
    grad_out_bias = jnp.sum(grad_attended.astype(jnp.float32), axis=0)
    late_terms = jnp.concatenate(
        [grad_shrink_term.reshape(model_width, -1), grad_expand_term, grad_out_term], axis=1
    )
    grad_mixed = jnp.dot(grad_attended, full_out.T, preferred_element_type=jnp.float32).astype(
        jnp.bfloat16
    )
    piece_pairs = 1
    piece_count = model_width // 128 // piece_pairs
    stage_count = 1 + len(late_orders[0])
    hooked = list(range(1, min(piece_count, stage_count)))

    def run_piece(index, mixed_grads):
        return attention_pallas(
            scaled_queries, pair_rows, mixed_grads, log_totals, index * piece_pairs, piece_pairs
        )

    def piece_hook(index):
        return lambda tied: (run_piece(index, tied[index - 1][1]), tied[index - 1][1])

    hooks = {0: lambda tied: ((), grad_mixed)}
    hooks.update({index: piece_hook(index) for index in hooked})
    pieces = [run_piece(0, grad_mixed)]
    owned_late, tied = tree_reduce_scatter(
        late_terms, (2304, 2304, 2304), rotated_orders, (bit_count, core_bit), hooks
    )
    pieces += [tied[index][0] for index in hooked]
    last_mixed = tied[hooked[-1]][1] if hooked else grad_mixed
    pieces += [run_piece(index, last_mixed) for index in range(len(hooked) + 1, piece_count)]
    finished = []
    for grad_query, grad_keys, grad_values in pieces:
        terms = jnp.concatenate([grad_keys, grad_values], axis=1)
        returned = lax.ppermute(terms[row_count:].astype(jnp.bfloat16), "frame", swap)
        finished.append((grad_query, terms[:row_count] + returned.astype(jnp.float32)))
    piece_width = finished[0][0].shape[1]
    grad_projected = jnp.concatenate(
        [
            (jnp.concatenate([query for query, _ in finished], axis=1) * score_scale).astype(
                jnp.bfloat16
            ),
            jnp.concatenate(
                [pair[:, :piece_width] for _, pair in finished]
                + [pair[:, piece_width:] for _, pair in finished],
                axis=1,
            ).astype(jnp.bfloat16),
        ],
        axis=1,
    )
    grad_in_term = jnp.dot(
        hidden_first.T, grad_projected, preferred_element_type=jnp.float32
    ).astype(jnp.bfloat16)
    projected_sums = jnp.sum(grad_projected.astype(jnp.float32), axis=0)
    grad_query_bias = projected_sums[:model_width]
    grad_value_bias = projected_sums[2 * model_width :]
    grad_hidden_first = jnp.dot(grad_projected, full_in.T, preferred_element_type=jnp.float32)
    norm_term_first, gain_first, shift_first = norm_backward(
        grad_hidden_first, plain_first, inv_first, column_set[:, 0]
    )
    grad_inputs = (grad_residual + norm_term_first).astype(jnp.bfloat16).reshape(inputs.shape)
    grad_columns = jnp.stack(
        [
            gain_first,
            shift_first,
            grad_query_bias,
            grad_value_bias,
            grad_out_bias,
            gain_second,
            shift_second,
            grad_down_bias,
        ],
        axis=1,
    )
    small_grads = jnp.concatenate(
        [
            grad_columns,
            grad_bias_term.reshape(model_width, -1),
            jnp.zeros((model_width, 128 - 12), jnp.float32),
        ],
        axis=1,
    ).astype(jnp.bfloat16)
    owned_first = tree_reduce_scatter(
        jnp.concatenate([grad_in_term, small_grads], axis=1),
        (896, 768, 768),
        rotated_orders,
        (bit_count, core_bit),
    )[0]
    owned_in = owned_first[:, :wide_in]
    owned_vectors = owned_first[:, wide_in : wide_in + vectors.shape[1]]
    owned_bias = owned_first[:, wide_in + vectors.shape[1] : wide_in + 12].reshape(-1)
    owned_shrink = owned_late[:, :ff_width].reshape(shrink_weight.shape)
    owned_expand = owned_late[:, ff_width : 2 * ff_width]
    owned_out = owned_late[:, 2 * ff_width :]
    new_in, mom_in = adam_step(project_in, moments_in, owned_in)
    new_out, mom_out = adam_step(project_out, moments_out, owned_out)
    new_expand, mom_expand = adam_step(expand_weight, moments_expand, owned_expand)
    new_shrink, mom_shrink = adam_step(shrink_weight, moments_shrink, owned_shrink)
    new_bias, mom_bias = adam_step(expand_bias, moments_bias, owned_bias)
    new_vectors, mom_vectors = adam_step(vectors, moments_vectors, owned_vectors)
    return (
        output,
        grad_inputs,
        owned_in,
        owned_out,
        owned_expand,
        owned_shrink,
        owned_bias,
        owned_vectors,
        new_in,
        new_out,
        new_expand,
        new_shrink,
        new_bias,
        new_vectors,
        mom_in,
        mom_out,
        mom_expand,
        mom_shrink,
        mom_bias,
        mom_vectors,
    )


def solution(mesh):
    in_specs = (
        P("clip", "frame", None),
        P("clip", "frame", None),
        P(("clip", "frame"), None),
        P(("clip", "frame"), None),
        P(("clip", "frame"), None),
        P(("clip", "frame"), None),
        P(("clip", "frame")),
        P(("clip", "frame"), None),
        P(None, ("clip", "frame"), None),
        P(None, ("clip", "frame"), None),
        P(None, ("clip", "frame"), None),
        P(None, ("clip", "frame"), None),
        P(None, ("clip", "frame")),
        P(None, ("clip", "frame"), None),
    )
    out_specs = (
        P("clip", "frame", None),
        P("clip", "frame", None),
        P(("clip", "frame"), None),
        P(("clip", "frame"), None),
        P(("clip", "frame"), None),
        P(("clip", "frame"), None),
        P(("clip", "frame")),
        P(("clip", "frame"), None),
        P(("clip", "frame"), None),
        P(("clip", "frame"), None),
        P(("clip", "frame"), None),
        P(("clip", "frame"), None),
        P(("clip", "frame")),
        P(("clip", "frame"), None),
        P(None, ("clip", "frame"), None),
        P(None, ("clip", "frame"), None),
        P(None, ("clip", "frame"), None),
        P(None, ("clip", "frame"), None),
        P(None, ("clip", "frame")),
        P(None, ("clip", "frame"), None),
    )
    return jax.shard_map(
        functools.partial(body, link_plan(mesh)),
        mesh=mesh,
        in_specs=in_specs,
        out_specs=out_specs,
        check_vma=False,
    )
```

```python
import functools
import math

import jax
import jax.numpy as jnp
from jax import lax
from jax.experimental import pallas as pl
from jax.experimental.pallas import tpu as pltpu
from jax.sharding import PartitionSpec as P

HEADS = 12
ADAM_STEP = 4


epsilon_norm = 1e-05
beta_first = 0.9
beta_second = 0.99
learn_rate = 0.03
decay_rate = 0.01
epsilon_adam = 1e-08
root_half = 0.7071067811865476
inv_root_two_pi = 0.3989422804014327


def norm_parts(inputs, norm_gain, norm_shift):
    average = jnp.mean(inputs, axis=-1, keepdims=True)
    centered = inputs - average
    spread = jnp.mean(centered * centered, axis=-1, keepdims=True)
    inv_std = lax.rsqrt(spread + epsilon_norm)
    normed = centered * inv_std
    return (normed * norm_gain + norm_shift, normed, inv_std)


def norm_backward(grad_normed, normed, inv_std, norm_gain):
    grad_gain = jnp.sum(grad_normed * normed, axis=0)
    grad_shift = jnp.sum(grad_normed, axis=0)
    scaled = grad_normed * norm_gain
    grad_input = inv_std * (
        scaled
        - jnp.mean(scaled, axis=-1, keepdims=True)
        - normed * jnp.mean(scaled * normed, axis=-1, keepdims=True)
    )
    return (grad_input, grad_gain, grad_shift)


def gelu_exact(inputs):
    return 0.5 * inputs * (1.0 + jax.scipy.special.erf(inputs * root_half))


def gelu_slope(inputs):
    return (
        0.5 * (1.0 + jax.scipy.special.erf(inputs * root_half))
        + inputs * jnp.exp(-0.5 * inputs * inputs) * inv_root_two_pi
    )


QUERY_CHUNK = 384
MASKED = -1e30


def attention_forward_kernel(q_ref, k_ref, v_ref, kbias_ref, o_ref, l_ref):
    head_size = q_ref.shape[1] // 2
    rows = q_ref.shape[0]
    kbias = kbias_ref[...]
    lane = lax.broadcasted_iota(jnp.int32, (QUERY_CHUNK, 2 * head_size), 1)

    def chunk_body(chunk, carry):
        span = pl.ds(pl.multiple_of(chunk * QUERY_CHUNK, QUERY_CHUNK), QUERY_CHUNK)
        mixed_parts = []
        totals = []
        for half in range(2):
            cols = pl.ds(half * head_size, head_size)
            query = q_ref[span, cols]
            key = k_ref[:, cols]
            value = v_ref[:, cols]
            scores = (
                lax.dot_general(
                    query, key, (((1,), (1,)), ((), ())), preferred_element_type=jnp.float32
                )
                + kbias
            )
            highest = jnp.max(scores, axis=1, keepdims=True)
            exponent = jnp.exp(scores - highest)
            denominator = jnp.sum(exponent, axis=1, keepdims=True)
            weights = (exponent * (1.0 / denominator)).astype(jnp.bfloat16)
            mixed_parts.append(jnp.dot(weights, value, preferred_element_type=jnp.float32))
            totals.append(highest + jnp.log(denominator))
        o_ref[span, :] = jnp.concatenate(mixed_parts, axis=1).astype(o_ref.dtype)
        l_ref[span, :] = jnp.where(lane < head_size, totals[0], totals[1])
        return carry

    lax.fori_loop(0, rows // QUERY_CHUNK, chunk_body, 0)


def attention_backward_kernel(
    q_ref, k_ref, v_ref, do_ref, l_ref, kbias_ref, dq_ref, dk_ref, dv_ref
):
    head_size = q_ref.shape[1] // 2
    rows = q_ref.shape[0]
    kbias = kbias_ref[...]
    dk_ref[...] = jnp.zeros_like(dk_ref)
    dv_ref[...] = jnp.zeros_like(dv_ref)
    for half in range(2):
        cols = pl.ds(half * head_size, head_size)

        def chunk_body(chunk, carry, cols=cols, half=half):
            span = pl.ds(pl.multiple_of(chunk * QUERY_CHUNK, QUERY_CHUNK), QUERY_CHUNK)
            key = k_ref[:, cols]
            value = v_ref[:, cols]
            query = q_ref[span, cols]
            grad_out = do_ref[span, cols]
            total = l_ref[span, pl.ds(half * head_size, 1)]
            scores = (
                lax.dot_general(
                    query, key, (((1,), (1,)), ((), ())), preferred_element_type=jnp.float32
                )
                + kbias
            )
            weights = jnp.exp(scores - total)
            grad_weights = lax.dot_general(
                grad_out, value, (((1,), (1,)), ((), ())), preferred_element_type=jnp.float32
            )
            delta = jnp.sum(weights * grad_weights, axis=1, keepdims=True)
            grad_scores = (weights * (grad_weights - delta)).astype(jnp.bfloat16)
            dq_ref[span, cols] = jnp.dot(
                grad_scores, key, preferred_element_type=jnp.float32
            ).astype(dq_ref.dtype)
            dk_ref[:, cols] += lax.dot_general(
                grad_scores, query, (((0,), (0,)), ((), ())), preferred_element_type=jnp.float32
            )
            dv_ref[:, cols] += lax.dot_general(
                weights.astype(jnp.bfloat16),
                grad_out,
                (((0,), (0,)), ((), ())),
                preferred_element_type=jnp.float32,
            )
            return carry

        lax.fori_loop(0, rows // QUERY_CHUNK, chunk_body, 0)


def pad_rows(values, rows):
    return jnp.pad(values, ((0, rows - values.shape[0]), (0, 0)))


def attention_pallas(queries, pairs, grad_out=None, totals=None, first_pair=0, pair_span=None):
    query_rows, model_width = queries.shape
    key_rows = pairs.shape[0]
    padded_q = -(-query_rows // QUERY_CHUNK) * QUERY_CHUNK
    padded_k = -(-key_rows // 128) * 128
    pair_count = model_width // 128
    q_pad = pad_rows(queries, padded_q)
    kv_pad = pad_rows(pairs, padded_k)
    kbias = jnp.where(jnp.arange(padded_k) < key_rows, 0.0, MASKED).astype(jnp.float32)[None, :]
    q_spec = pl.BlockSpec((padded_q, 128), lambda j: (0, j))
    k_spec = pl.BlockSpec((padded_k, 128), lambda j: (0, j))
    v_spec = pl.BlockSpec((padded_k, 128), lambda j: (0, j + pair_count))
    b_spec = pl.BlockSpec((1, padded_k), lambda j: (0, 0))
    params = pltpu.CompilerParams(vmem_limit_bytes=48 * 1024 * 1024)
    if grad_out is None:
        mixed, log_totals = pl.pallas_call(
            attention_forward_kernel,
            grid=(pair_count,),
            in_specs=[q_spec, k_spec, v_spec, b_spec],
            out_specs=[q_spec, q_spec],
            out_shape=[
                jax.ShapeDtypeStruct((padded_q, model_width), jnp.bfloat16),
                jax.ShapeDtypeStruct((padded_q, model_width), jnp.float32),
            ],
            compiler_params=params,
        )(q_pad, kv_pad, kv_pad, kbias)
        return mixed[:query_rows], log_totals
    do_pad = pad_rows(grad_out, padded_q)
    span = pair_count if pair_span is None else pair_span
    qi_spec = pl.BlockSpec((padded_q, 128), lambda j: (0, j + first_pair))
    ki_spec = pl.BlockSpec((padded_k, 128), lambda j: (0, j + first_pair))
    vi_spec = pl.BlockSpec((padded_k, 128), lambda j: (0, j + first_pair + pair_count))
    qo_spec = pl.BlockSpec((padded_q, 128), lambda j: (0, j))
    ko_spec = pl.BlockSpec((padded_k, 128), lambda j: (0, j))
    dq, dk, dv = pl.pallas_call(
        attention_backward_kernel,
        grid=(span,),
        in_specs=[qi_spec, ki_spec, vi_spec, qi_spec, qi_spec, b_spec],
        out_specs=[qo_spec, ko_spec, ko_spec],
        out_shape=[
            jax.ShapeDtypeStruct((padded_q, 128 * span), jnp.float32),
            jax.ShapeDtypeStruct((padded_k, 128 * span), jnp.float32),
            jax.ShapeDtypeStruct((padded_k, 128 * span), jnp.float32),
        ],
        compiler_params=params,
    )(q_pad, kv_pad, kv_pad, do_pad, totals, kbias)
    return dq[:query_rows], dk[:key_rows], dv[:key_rows]


def attend_forward(queries, keys_values, head_count):
    model_width = queries.shape[2]
    head_size = model_width // head_count
    score_scale = 1.0 / math.sqrt(head_size)

    def one_head(head_index):
        offset = head_index * head_size
        query_block = lax.dynamic_slice_in_dim(queries, offset, head_size, 2)
        key_block = lax.dynamic_slice_in_dim(keys_values, offset, head_size, 2)
        value_block = lax.dynamic_slice_in_dim(keys_values, model_width + offset, head_size, 2)
        scores = (
            jnp.einsum("cqd,ckd->cqk", query_block, key_block, preferred_element_type=jnp.float32)
            * score_scale
        )
        highest = jnp.max(scores, axis=-1, keepdims=True)
        exponent = jnp.exp(scores - highest)
        denominator = jnp.sum(exponent, axis=-1, keepdims=True)
        weights_soft = (exponent / denominator).astype(jnp.bfloat16)
        mixed = jnp.einsum(
            "cqk,ckd->cqd", weights_soft, value_block, preferred_element_type=jnp.float32
        )
        return (mixed, (highest + jnp.log(denominator))[..., 0])

    mixed, log_totals = lax.map(one_head, jnp.arange(head_count))
    clip_count, frame_count = (queries.shape[0], queries.shape[1])
    mixed = jnp.transpose(mixed, (1, 2, 0, 3)).reshape(clip_count, frame_count, model_width)
    return (mixed, log_totals)


def attend_backward(queries, keys_values, grad_mixed, log_totals, head_count):
    model_width = queries.shape[2]
    head_size = model_width // head_count
    score_scale = 1.0 / math.sqrt(head_size)

    def one_head_back(head_index):
        offset = head_index * head_size
        query_block = lax.dynamic_slice_in_dim(queries, offset, head_size, 2)
        key_block = lax.dynamic_slice_in_dim(keys_values, offset, head_size, 2)
        value_block = lax.dynamic_slice_in_dim(keys_values, model_width + offset, head_size, 2)
        grad_block = lax.dynamic_slice_in_dim(grad_mixed, offset, head_size, 2)
        totals = lax.dynamic_index_in_dim(log_totals, head_index, 0, keepdims=False)
        scores = (
            jnp.einsum("cqd,ckd->cqk", query_block, key_block, preferred_element_type=jnp.float32)
            * score_scale
        )
        weights_soft = jnp.exp(scores - totals[..., None])
        grad_weights = jnp.einsum(
            "cqd,ckd->cqk", grad_block, value_block, preferred_element_type=jnp.float32
        )
        delta = jnp.sum(weights_soft * grad_weights, axis=-1, keepdims=True)
        grad_scores = (weights_soft * (grad_weights - delta)).astype(jnp.bfloat16)
        grad_query = (
            jnp.einsum("cqk,ckd->cqd", grad_scores, key_block, preferred_element_type=jnp.float32)
            * score_scale
        )
        grad_key = (
            jnp.einsum("cqk,cqd->ckd", grad_scores, query_block, preferred_element_type=jnp.float32)
            * score_scale
        )
        grad_value = jnp.einsum(
            "cqk,cqd->ckd",
            weights_soft.astype(jnp.bfloat16),
            grad_block,
            preferred_element_type=jnp.float32,
        )
        return (grad_query, delta[..., 0], grad_key, grad_value)

    pieces = lax.map(one_head_back, jnp.arange(head_count))
    clip_count, frame_count = (queries.shape[0], queries.shape[1])
    clip_frames = keys_values.shape[1]
    grad_query = jnp.transpose(pieces[0], (1, 2, 0, 3)).reshape(
        clip_count, frame_count, model_width
    )
    grad_key = jnp.transpose(pieces[2], (1, 2, 0, 3)).reshape(clip_count, clip_frames, model_width)
    grad_value = jnp.transpose(pieces[3], (1, 2, 0, 3)).reshape(
        clip_count, clip_frames, model_width
    )
    return (grad_query, pieces[1], jnp.concatenate([grad_key, grad_value], axis=2))


def link_plan(mesh):
    devices = list(mesh.devices.reshape(-1))
    bit_count = len(devices).bit_length() - 1
    core_bit = 1
    for bit in range(bit_count):
        first, other = devices[0], devices[1 << bit]
        if getattr(first, "coords", None) is not None and tuple(first.coords) == tuple(other.coords):
            core_bit = bit
    others = [bit for bit in range(bit_count) if bit != core_bit]
    near, far = others[:-1], others[-1:]
    rotated = tuple(tuple(near[k:] + near[:k] + far) for k in range(3))
    inner = [bit for bit in near if bit != 0]
    late = tuple(tuple(inner[k:] + inner[:k] + [0] + far) for k in range(2))
    return bit_count, core_bit, rotated, late


def tree_reduce_scatter(terms, part_columns, orders, plan_bits, hooks=None):
    hooks = dict(hooks or {})
    tied = {}
    bit_count, core_bit = plan_bits
    device = lax.axis_index("clip") * lax.axis_size("frame") + lax.axis_index("frame")
    blocks = 1 << bit_count
    block_rows = terms.shape[0] // blocks
    data = terms.reshape((2,) * bit_count + (block_rows, terms.shape[1]))
    parts = [(data, list(range(bit_count - 1, -1, -1)))]
    plan = [(core_bit,)] + [tuple(order[stage] for order in orders) for stage in range(len(orders[0]))]
    for stage, stage_bits in enumerate(plan):
        if stage == 1:
            whole, bits = parts[0]
            parts = []
            offset = 0
            for width in part_columns:
                parts.append((whole[..., offset : offset + width], bits))
                offset += width
        keeps, sends = [], []
        for (part, part_bits), bit in zip(parts, stage_bits):
            axis = part_bits.index(bit)
            mine = (device >> bit) & 1
            keeps.append(lax.dynamic_index_in_dim(part, mine, axis=axis, keepdims=False))
            sends.append(
                lax.dynamic_index_in_dim(part, 1 - mine, axis=axis, keepdims=False).astype(jnp.bfloat16)
            )
        new_parts = []
        for keep, send, (part, part_bits), bit in zip(keeps, sends, parts, stage_bits):
            pairs = [(index, index ^ (1 << bit)) for index in range(blocks)]
            got = lax.ppermute(send, ("clip", "frame"), pairs)
            new_parts.append((keep + got.astype(jnp.float32), [b for b in part_bits if b != bit]))
        if stage in hooks:
            values, tied[stage] = lax.optimization_barrier(
                ([part for part, _ in new_parts], hooks[stage](tied))
            )
            new_parts = [(value, part_bits) for value, (_, part_bits) in zip(values, new_parts)]
        parts = new_parts
    return jnp.concatenate([part for part, _ in parts], axis=-1).astype(jnp.float32), tied


def tree_all_gather(local, part_columns, orders, plan_bits):
    bit_count, core_bit = plan_bits
    device = lax.axis_index("clip") * lax.axis_size("frame") + lax.axis_index("frame")
    canonical = list(range(bit_count - 1, -1, -1))

    def double(data, bits, bit):
        mine = (device >> bit) & 1
        pairs = [(index, index ^ (1 << bit)) for index in range(1 << bit_count)]
        got = lax.ppermute(data, ("clip", "frame"), pairs)
        new_bits = sorted(bits + [bit], reverse=True)
        axis = new_bits.index(bit)
        low_first = jnp.stack([data, got], axis=axis)
        high_first = jnp.stack([got, data], axis=axis)
        return jnp.where(mine == 0, low_first, high_first), new_bits

    parts = []
    offset = 0
    for width in part_columns:
        parts.append((local[:, offset : offset + width], []))
        offset += width
    reversed_orders = [list(reversed(order)) for order in orders]
    for stage in range(len(reversed_orders[0])):
        parts = [double(part, bits, order[stage]) for (part, bits), order in zip(parts, reversed_orders)]
    whole = jnp.concatenate([part for part, _ in parts], axis=-1)
    whole, bits = double(whole, parts[0][1], core_bit)
    assert bits == canonical
    return whole.reshape((1 << bit_count) * local.shape[0], local.shape[1])


def adam_step(weight, moments, gradient):
    first = beta_first * moments[0] + (1.0 - beta_first) * gradient
    second = beta_second * moments[1] + (1.0 - beta_second) * gradient * gradient
    first_hat = first / (1.0 - beta_first**ADAM_STEP)
    second_hat = second / (1.0 - beta_second**ADAM_STEP)
    change = -learn_rate * (first_hat / (jnp.sqrt(second_hat) + epsilon_adam) + decay_rate * weight)
    return (change, jnp.stack([first, second]))


def body(
    plan,
    inputs,
    cotangent,
    project_in,
    project_out,
    expand_weight,
    shrink_weight,
    expand_bias,
    vectors,
    moments_in,
    moments_out,
    moments_expand,
    moments_shrink,
    moments_bias,
    moments_vectors,
):
    clip_count, frame_count, model_width = inputs.shape
    row_count = clip_count * frame_count
    head_count = HEADS
    shard_rows = project_in.shape[0]
    wide_in = project_in.shape[1]
    ff_width = expand_weight.shape[1]
    swap = [(0, 1), (1, 0)]
    everyone = ("clip", "frame")

    small = jnp.concatenate(
        [
            vectors,
            expand_bias.reshape(shard_rows, -1),
            jnp.zeros((shard_rows, 128 - vectors.shape[1] - expand_bias.shape[0] // shard_rows), jnp.float32),
        ],
        axis=1,
    )
    first_pack = jnp.concatenate([project_in, small], axis=1).astype(jnp.bfloat16)
    second_pack = jnp.concatenate(
        [project_out, expand_weight, shrink_weight.reshape(shard_rows, -1)], axis=1
    ).astype(jnp.bfloat16)
    bit_count, core_bit, rotated_orders, late_orders = plan
    first_full = tree_all_gather(first_pack, (896, 768, 768), rotated_orders, (bit_count, core_bit))
    second_full = lax.all_gather(second_pack, everyone, axis=0, tiled=True)
    full_in = first_full[:, :wide_in]
    small_full = first_full[:, wide_in:].astype(jnp.float32)
    column_set = small_full[:, : vectors.shape[1]]
    full_bias = small_full[:, vectors.shape[1] : vectors.shape[1] + ff_width // model_width].reshape(-1)
    full_out = second_full[:, :model_width]
    full_expand = second_full[:, model_width : model_width + ff_width]
    full_shrink = second_full[:, model_width + ff_width :].reshape(ff_width, model_width)

    frames_rows = inputs.reshape(row_count, model_width).astype(jnp.float32)
    normed_first, plain_first, inv_first = norm_parts(
        frames_rows, column_set[:, 0], column_set[:, 1]
    )
    hidden_first = normed_first.astype(jnp.bfloat16)
    partner_rows = lax.ppermute(inputs, "frame", swap).reshape(row_count, model_width)
    hidden_partner = norm_parts(
        partner_rows.astype(jnp.float32), column_set[:, 0], column_set[:, 1]
    )[0].astype(jnp.bfloat16)
    bias_in = jnp.concatenate(
        [column_set[:, 2], jnp.zeros((model_width,), jnp.float32), column_set[:, 3]]
    )
    projected = (
        jnp.dot(hidden_first, full_in, preferred_element_type=jnp.float32) + bias_in
    ).astype(jnp.bfloat16)
    partner_pairs = (
        jnp.dot(hidden_partner, full_in[:, model_width:], preferred_element_type=jnp.float32)
        + bias_in[model_width:]
    ).astype(jnp.bfloat16)
    queries = projected[:, :model_width].reshape(clip_count, frame_count, model_width)
    clip_pairs = jnp.concatenate([projected[:, model_width:], partner_pairs], axis=0).reshape(
        clip_count, 2 * frame_count, 2 * model_width
    )
    score_scale = 1.0 / math.sqrt(model_width // head_count)
    scaled_queries = (projected[:, :model_width] * score_scale).astype(jnp.bfloat16)
    pair_rows = clip_pairs.reshape(2 * row_count, 2 * model_width)
    mixed_low, log_totals = attention_pallas(scaled_queries, pair_rows)
    attended = jnp.dot(mixed_low, full_out, preferred_element_type=jnp.float32) + column_set[:, 4]
    residual = frames_rows + attended
    normed_second, plain_second, inv_second = norm_parts(
        residual, column_set[:, 5], column_set[:, 6]
    )
    hidden_second = normed_second.astype(jnp.bfloat16)
    preact = jnp.dot(hidden_second, full_expand, preferred_element_type=jnp.float32) + full_bias
    activated = gelu_exact(preact).astype(jnp.bfloat16)
    result = (
        residual
        + jnp.dot(activated, full_shrink, preferred_element_type=jnp.float32)
        + column_set[:, 7]
    )
    output = result.astype(jnp.bfloat16).reshape(inputs.shape)

    grad_result = cotangent.reshape(row_count, model_width)
    grad_shrink_term = jnp.dot(
        activated.T, grad_result, preferred_element_type=jnp.float32
    ).astype(jnp.bfloat16)
    grad_down_bias = jnp.sum(grad_result.astype(jnp.float32), axis=0)
    grad_activated = jnp.dot(grad_result, full_shrink.T, preferred_element_type=jnp.float32)
    grad_preact = (grad_activated * gelu_slope(preact)).astype(jnp.bfloat16)
    grad_expand_term = jnp.dot(
        hidden_second.T, grad_preact, preferred_element_type=jnp.float32
    ).astype(jnp.bfloat16)
    grad_bias_term = jnp.sum(grad_preact.astype(jnp.float32), axis=0)
    grad_hidden_second = jnp.dot(grad_preact, full_expand.T, preferred_element_type=jnp.float32)
    norm_term_second, gain_second, shift_second = norm_backward(
        grad_hidden_second, plain_second, inv_second, column_set[:, 5]
    )
    grad_residual = grad_result.astype(jnp.float32) + norm_term_second
    grad_attended = grad_residual.astype(jnp.bfloat16)
    grad_out_term = jnp.dot(
        mixed_low.T, grad_attended, preferred_element_type=jnp.float32
    ).astype(jnp.bfloat16)
    grad_out_bias = jnp.sum(grad_attended.astype(jnp.float32), axis=0)
    late_terms = jnp.concatenate(
        [grad_shrink_term.reshape(model_width, -1), grad_expand_term, grad_out_term], axis=1
    )
    grad_mixed = jnp.dot(grad_attended, full_out.T, preferred_element_type=jnp.float32).astype(
        jnp.bfloat16
    )
    piece_pairs = 1
    piece_count = model_width // 128 // piece_pairs
    stage_count = 1 + len(late_orders[0])
    hooked = list(range(1, min(piece_count, stage_count)))

    def run_piece(index, mixed_grads):
        return attention_pallas(
            scaled_queries, pair_rows, mixed_grads, log_totals, index * piece_pairs, piece_pairs
        )

    def piece_hook(index):
        return lambda tied: (run_piece(index, tied[index - 1][1]), tied[index - 1][1])

    hooks = {0: lambda tied: ((), grad_mixed)}
    hooks.update({index: piece_hook(index) for index in hooked})
    pieces = [run_piece(0, grad_mixed)]
    owned_late, tied = tree_reduce_scatter(
        late_terms, (1152,) * 6, rotated_orders * 2, (bit_count, core_bit), hooks
    )
    pieces += [tied[index][0] for index in hooked]
    last_mixed = tied[hooked[-1]][1] if hooked else grad_mixed
    pieces += [run_piece(index, last_mixed) for index in range(len(hooked) + 1, piece_count)]
    finished = []
    for grad_query, grad_keys, grad_values in pieces:
        terms = jnp.concatenate([grad_keys, grad_values], axis=1)
        returned = lax.ppermute(terms[row_count:].astype(jnp.bfloat16), "frame", swap)
        finished.append((grad_query, terms[:row_count] + returned.astype(jnp.float32)))
    piece_width = finished[0][0].shape[1]
    grad_projected = jnp.concatenate(
        [
            (jnp.concatenate([query for query, _ in finished], axis=1) * score_scale).astype(
                jnp.bfloat16
            ),
            jnp.concatenate(
                [pair[:, :piece_width] for _, pair in finished]
                + [pair[:, piece_width:] for _, pair in finished],
                axis=1,
            ).astype(jnp.bfloat16),
        ],
        axis=1,
    )
    grad_in_term = jnp.dot(
        hidden_first.T, grad_projected, preferred_element_type=jnp.float32
    ).astype(jnp.bfloat16)
    projected_sums = jnp.sum(grad_projected.astype(jnp.float32), axis=0)
    grad_query_bias = projected_sums[:model_width]
    grad_value_bias = projected_sums[2 * model_width :]
    grad_hidden_first = jnp.dot(grad_projected, full_in.T, preferred_element_type=jnp.float32)
    norm_term_first, gain_first, shift_first = norm_backward(
        grad_hidden_first, plain_first, inv_first, column_set[:, 0]
    )
    grad_inputs = (grad_residual + norm_term_first).astype(jnp.bfloat16).reshape(inputs.shape)
    grad_columns = jnp.stack(
        [
            gain_first,
            shift_first,
            grad_query_bias,
            grad_value_bias,
            grad_out_bias,
            gain_second,
            shift_second,
            grad_down_bias,
        ],
        axis=1,
    )
    small_grads = jnp.concatenate(
        [
            grad_columns,
            grad_bias_term.reshape(model_width, -1),
            jnp.zeros((model_width, 128 - 12), jnp.float32),
        ],
        axis=1,
    ).astype(jnp.bfloat16)
    owned_first = tree_reduce_scatter(
        jnp.concatenate([grad_in_term, small_grads], axis=1),
        (896, 768, 768),
        rotated_orders,
        (bit_count, core_bit),
    )[0]
    owned_in = owned_first[:, :wide_in]
    owned_vectors = owned_first[:, wide_in : wide_in + vectors.shape[1]]
    owned_bias = owned_first[:, wide_in + vectors.shape[1] : wide_in + 12].reshape(-1)
    owned_shrink = owned_late[:, :ff_width].reshape(shrink_weight.shape)
    owned_expand = owned_late[:, ff_width : 2 * ff_width]
    owned_out = owned_late[:, 2 * ff_width :]
    new_in, mom_in = adam_step(project_in, moments_in, owned_in)
    new_out, mom_out = adam_step(project_out, moments_out, owned_out)
    new_expand, mom_expand = adam_step(expand_weight, moments_expand, owned_expand)
    new_shrink, mom_shrink = adam_step(shrink_weight, moments_shrink, owned_shrink)
    new_bias, mom_bias = adam_step(expand_bias, moments_bias, owned_bias)
    new_vectors, mom_vectors = adam_step(vectors, moments_vectors, owned_vectors)
    return (
        output,
        grad_inputs,
        owned_in,
        owned_out,
        owned_expand,
        owned_shrink,
        owned_bias,
        owned_vectors,
        new_in,
        new_out,
        new_expand,
        new_shrink,
        new_bias,
        new_vectors,
        mom_in,
        mom_out,
        mom_expand,
        mom_shrink,
        mom_bias,
        mom_vectors,
    )


def solution(mesh):
    in_specs = (
        P("clip", "frame", None),
        P("clip", "frame", None),
        P(("clip", "frame"), None),
        P(("clip", "frame"), None),
        P(("clip", "frame"), None),
        P(("clip", "frame"), None),
        P(("clip", "frame")),
        P(("clip", "frame"), None),
        P(None, ("clip", "frame"), None),
        P(None, ("clip", "frame"), None),
        P(None, ("clip", "frame"), None),
        P(None, ("clip", "frame"), None),
        P(None, ("clip", "frame")),
        P(None, ("clip", "frame"), None),
    )
    out_specs = (
        P("clip", "frame", None),
        P("clip", "frame", None),
        P(("clip", "frame"), None),
        P(("clip", "frame"), None),
        P(("clip", "frame"), None),
        P(("clip", "frame"), None),
        P(("clip", "frame")),
        P(("clip", "frame"), None),
        P(("clip", "frame"), None),
        P(("clip", "frame"), None),
        P(("clip", "frame"), None),
        P(("clip", "frame"), None),
        P(("clip", "frame")),
        P(("clip", "frame"), None),
        P(None, ("clip", "frame"), None),
        P(None, ("clip", "frame"), None),
        P(None, ("clip", "frame"), None),
        P(None, ("clip", "frame"), None),
        P(None, ("clip", "frame")),
        P(None, ("clip", "frame"), None),
    )
    return jax.shard_map(
        functools.partial(body, link_plan(mesh)),
        mesh=mesh,
        in_specs=in_specs,
        out_specs=out_specs,
        check_vma=False,
    )
```
